32 devices in a mesh: expert: 16 (over z, y, x), hidden: 2 (over core).
Axes of the slice: x: 2, y: 2, z: 4, core: 2. Of those that a mesh axis runs over, the one named last changes fastest.
Arguments:
- tokens: bfloat16 [16384, 1024], P(('expert', 'hidden')), may hold values from -6 to 6
- lengths: int32 [2, 128], replicated, may hold values from 32 to 64, as said below
- deal: int32 [2, 128], replicated, may hold values from 0 to 127, each once within a row
- routes: int32 [16384, 1], P(('expert', 'hidden')), may hold values from 0 to 15
- slot_order: int32 [16384, 1], P(('expert', 'hidden')), may hold values from 0 to 63, as said below
- gain_attn: bfloat16 [1024], P(('expert', 'hidden')), may hold values from 0.25 to 1.75
- gain_ffn: bfloat16 [1024], P(('expert', 'hidden')), may hold values from 0.25 to 1.75
- w_qkv: bfloat16 [1024, 3072], P(('expert', 'hidden')), may hold values from -0.1875 to 0.1875
- w_out: bfloat16 [1024, 1024], P(('expert', 'hidden')), may hold values from -2 to 2
- centroids: bfloat16 [16, 1024], P('expert'), may hold values from -0.125 to 0.125
- expert_in: bfloat16 [16, 1024, 4096], P('expert', None, 'hidden'), may hold values from -0.1875 to 0.1875
- expert_out: bfloat16 [16, 4096, 1024], P('expert', 'hidden'), may hold values from -0.1875 to 0.1875
- second_in: bfloat16 [16, 1024, 4096], P('expert', None, 'hidden'), may hold values from -0.1875 to 0.1875
- second_out: bfloat16 [16, 4096, 1024], P('expert', 'hidden'), may hold values from -0.1875 to 0.1875
- cotangent: bfloat16 [16384, 1024], P(('expert', 'hidden')), may hold values from -6 to 6
Outputs:
- output: bfloat16 [16384, 1024], P(('expert', 'hidden'))
- input_grad: float32 [16384, 1024], P(('expert', 'hidden'))
- grad_gain_attn: float32 [1024], P(('expert', 'hidden'))
- grad_gain_ffn: float32 [1024], P(('expert', 'hidden'))
- grad_w_qkv: float32 [1024, 3072], P(('expert', 'hidden'))
- grad_w_out: float32 [1024, 1024], P(('expert', 'hidden'))
- grad_centroids: float32 [16, 1024], P('expert')
- grad_expert_in: float32 [16, 1024, 4096], P('expert', None, 'hidden')
- grad_expert_out: float32 [16, 4096, 1024], P('expert', 'hidden')
- grad_second_in: float32 [16, 1024, 4096], P('expert', None, 'hidden')
- grad_second_out: float32 [16, 4096, 1024], P('expert', 'hidden')
The draws below stay inside these ranges and needn't reach their ends.
Inputs may be any that keep to these rules, and one draw needn't show every extreme that they name: `lengths`: some sequence is full and some has exactly 32 real tokens. `deal`: each row is a permutation of 0 to 127. `slot_order`: within each sequence the values are a permutation of 0 to 63.
All inputs are finite; a program needn't handle non-finite values.
Results may differ from the reference program's by a relative error of at most 0.015.
Values may be sent and summed in bfloat16 or wider, within the bound.
A program may use at most 320 MiB of HBM per device.

```python
import jax
import jax.numpy as jnp
from jax import lax

D = 1024
HEADS = 16
HEAD = 64
FF = 4096
MICRO = 4
PER = 2
SEQ = 64
EXPERTS = 16
SETS = 2
GROUP = 128
PIECE = 4
CAP = 9
TOKENS = 16384


def draw_lengths(key, part):
    entries = SETS * GROUP
    drawn = jax.random.randint(jax.random.fold_in(key, 11), (entries,), SEQ // 2, SEQ + 1)
    largest_at = jax.random.randint(jax.random.fold_in(key, 12), (), 0, entries)
    offset_draw = jax.random.randint(jax.random.fold_in(key, 13), (), 1, entries)
    shortest_at = (largest_at + offset_draw) % entries
    positions = jnp.arange(entries)
    drawn = jnp.where(positions == largest_at, SEQ, drawn)
    drawn = jnp.where(positions == shortest_at, SEQ // 2, drawn)
    return drawn.reshape(SETS, GROUP).astype(jnp.int32)


def draw_slot_order(key, part):
    random_bits = jax.random.randint(jax.random.fold_in(key, 21), (SETS * GROUP, SEQ), 0, 1048576)
    distinct = random_bits * SEQ + jnp.arange(SEQ, dtype=jnp.int32)[None, :]
    ranks = jnp.argsort(jnp.argsort(distinct, axis=1, stable=True), axis=1, stable=True)
    blocks = ranks.reshape(SETS, GROUP, EXPERTS, PIECE)
    return blocks.transpose(2, 0, 1, 3).reshape(TOKENS, 1).astype(jnp.int32)


def levels(rng, dims, cuts, smallest, largest):
    def one(position, blocks):
        draws = jax.random.uniform(jax.random.fold_in(jax.random.fold_in(rng, 6), position), (blocks,), jnp.float32, smallest / len(cuts), largest / len(cuts))
        return jnp.repeat(jnp.exp(draws), dims[position] // blocks).reshape((-1,) + (1,) * (len(dims) - position - 1))

    factor_of = one(*cuts[0])
    for cut in cuts[1:]:
        factor_of = factor_of * one(*cut)
    return factor_of


def different_ones(stream_key, rows, count, top, lift):
    ranking = jax.random.permutation(jax.random.fold_in(stream_key, 1), count)
    favour = ranking
    for power in range(3):
        favour = favour * favour // count
    favour = favour * lift // count
    lots = jax.random.randint(jax.random.fold_in(stream_key, 2), (rows, count), 0, 4096) + favour
    fixed_rows = jax.random.permutation(jax.random.fold_in(stream_key, 3), rows)[jnp.arange(count) % rows]
    lots = jnp.where(jnp.arange(rows)[:, None] == fixed_rows[None, :], 1 << 14, lots)
    merit = lots * count + jnp.arange(count)
    return lax.top_k(merit.astype(jnp.int32), top)[1].astype(jnp.int32)


def bell_draw(stream_key, extent, scale, reach, pieces=(), kind=jnp.bfloat16):
    level = levels(stream_key, extent, pieces, -0.22, 0.18) if pieces else 1.0
    values = jax.random.normal(stream_key, extent, jnp.float32) * scale * level
    return jnp.minimum(jnp.maximum(values, -reach), reach).astype(kind)


def setup_inputs(seed: int = 0) -> dict:
    seeds = jax.random.split(jax.random.key(seed), 16)
    return {
        "tokens": bell_draw(seeds[0], (TOKENS, D), 1.0, 6.0, ((0, 32),)),
        "lengths": draw_lengths(jax.random.fold_in(seeds[15], 71), 0),
        "deal": jax.vmap(lambda own: jax.random.permutation(own, GROUP))(jax.random.split(seeds[2], SETS)).reshape((SETS, GROUP)).astype(jnp.int32),
        "routes": different_ones(seeds[3], TOKENS, EXPERTS, 1, 512),
        "slot_order": draw_slot_order(jax.random.fold_in(seeds[15], 71), 0),
        "gain_attn": jnp.clip(1.0 + 0.15 * jax.random.normal(seeds[5], (D,), jnp.float32), 0.25, 1.75).astype(jnp.bfloat16),
        "gain_ffn": jnp.clip(1.0 + 0.15 * jax.random.normal(seeds[6], (D,), jnp.float32), 0.25, 1.75).astype(jnp.bfloat16),
        "w_qkv": bell_draw(seeds[7], (D, 3 * D), D ** -0.5, 0.1875, ((0, 32),)),
        "w_out": bell_draw(seeds[8], (D, D), (D // 128) ** -0.5, 2.0, ((0, 32),)),
        "centroids": bell_draw(seeds[9], (EXPERTS, D), (2 * D) ** -0.5, 0.125, ((0, 16),)),
        "expert_in": bell_draw(seeds[10], (EXPERTS, D, FF), D ** -0.5, 0.1875, ((0, 16), (2, 2))),
        "expert_out": bell_draw(seeds[11], (EXPERTS, FF, D), (FF // 4) ** -0.5, 0.1875, ((0, 16), (1, 2))),
        "second_in": bell_draw(seeds[12], (EXPERTS, D, FF), D ** -0.5, 0.1875, ((0, 16), (2, 2))),
        "second_out": bell_draw(seeds[13], (EXPERTS, FF, D), (FF // 4) ** -0.5, 0.1875, ((0, 16), (1, 2))),
        "cotangent": bell_draw(seeds[14], (TOKENS, D), 1.0, 6.0, ((0, 32),)),
    }


epsilon = 1e-05
highest = lax.Precision.HIGHEST

@jax.custom_vjp
def low(v):
    return lax.optimization_barrier(v.astype(jnp.bfloat16)).astype(jnp.float32)

@jax.custom_vjp
def low_back(v):
    return v

def low_keep(v):
    return (low(v), None)

def low_pass(kept, grad):
    return (grad,)

def back_keep(v):
    return (v, None)

def back_low(kept, grad):
    return (low(grad),)
low.defvjp(low_keep, low_pass)
low_back.defvjp(back_keep, back_low)

def layer_norm(row_block, gain_row):
    centre = lax.optimization_barrier(jnp.mean(row_block, axis=-1, keepdims=True))
    shifted = row_block - centre
    spread = lax.optimization_barrier(jnp.mean(shifted * shifted, axis=-1, keepdims=True))
    return shifted * lax.rsqrt(spread + epsilon) * gain_row

def real_rows(row_count, pack_lengths):
    positions = jnp.arange(row_count, dtype=jnp.int32)
    seat_index = positions // SEQ
    places = jnp.arange(PER, dtype=jnp.int32)
    limit = lax.optimization_barrier(jnp.sum(jnp.where(seat_index[:, None] == places[None, :], pack_lengths[None, :], 0), axis=1))
    return (seat_index, positions - seat_index * SEQ < limit)

def allowed_mask(row_count, pack_lengths):
    positions = jnp.arange(row_count, dtype=jnp.int32)
    seat_index, present = real_rows(row_count, pack_lengths)
    return (seat_index[:, None] == seat_index[None, :]) & (positions[None, :] <= positions[:, None]) & present[None, :]

def build_slots(route_row, order_row, pack_lengths, expert_count, capacity):
    row_count = route_row.shape[0]
    seat_index, present = real_rows(row_count, pack_lengths)
    priority = order_row * PER + seat_index
    same_expert = route_row[:, None] == route_row[None, :]
    earlier = priority[None, :] < priority[:, None]
    ahead_count = lax.optimization_barrier(jnp.sum((same_expert & earlier & present[None, :]).astype(jnp.int32), axis=1))
    accepted = present & (ahead_count < capacity)
    target = route_row * capacity + ahead_count
    slot_ids = jnp.arange(expert_count * capacity, dtype=jnp.int32)
    return ((slot_ids[:, None] == target[None, :]) & accepted[None, :]).astype(jnp.float32)

def seq_view(flat):
    last_dim = flat.shape[-1]
    blocks = flat.reshape(EXPERTS, SETS, GROUP, PIECE, last_dim)
    return blocks.transpose(1, 2, 0, 3, 4).reshape(SETS, GROUP, SEQ, last_dim)

def flat_view(sequences):
    last_dim = sequences.shape[-1]
    blocks = sequences.reshape(SETS, GROUP, EXPERTS, PIECE, last_dim)
    return blocks.transpose(2, 0, 1, 3, 4).reshape(TOKENS, last_dim)

def pack_forward(params, tokens_pack, route_row, order_row, pack_lengths):
    w_qkv, w_out, gain_attn, gain_ffn, centroids, expert_in, expert_out, second_in, second_out = params
    row_count = tokens_pack.shape[0]
    normed = low(layer_norm(tokens_pack, gain_attn))
    packed = low_back(low(jnp.dot(normed, w_qkv, precision=highest)))
    queries = packed[:, :D].reshape(row_count, HEADS, HEAD)
    keys_all = packed[:, D:2 * D].reshape(row_count, HEADS, HEAD)
    values_all = packed[:, 2 * D:].reshape(row_count, HEADS, HEAD)
    scores = low_back(jnp.einsum('qhd,khd->hqk', queries, keys_all, precision=highest) * 0.125)
    masked = jnp.where(allowed_mask(row_count, pack_lengths)[None], scores, -1e+30)
    row_peaks = lax.optimization_barrier(jnp.max(masked, axis=-1, keepdims=True))
    log_total = row_peaks + jnp.log(lax.optimization_barrier(jnp.sum(jnp.exp(masked - row_peaks), axis=-1, keepdims=True)))
    attn_probs = low(jnp.exp(masked - log_total))
    mixed_heads = jnp.einsum('hqk,khd->qhd', attn_probs, values_all, precision=highest).reshape(row_count, D)
    mixed_heads = low_back(low(mixed_heads))
    attended = low_back(jnp.dot(mixed_heads, w_out, precision=highest))
    residual = tokens_pack + attended
    shared = low_back(low(layer_norm(residual, gain_ffn)))
    dispatch = build_slots(route_row, order_row, pack_lengths, EXPERTS, CAP)
    slot_rows = jnp.dot(dispatch, shared, precision=highest).reshape(EXPERTS, CAP, D)
    pre_first = low_back(jnp.einsum('ecd,edf->ecf', slot_rows, expert_in, precision=highest))
    act_first = low(jax.nn.gelu(pre_first, approximate=True))
    middle = low_back(slot_rows + jnp.einsum('ecf,efd->ecd', act_first, expert_out, precision=highest))
    middle_lo = low(middle)
    pre_second = low_back(jnp.einsum('ecd,edf->ecf', middle_lo, second_in, precision=highest))
    act_second = low(jax.nn.gelu(pre_second, approximate=True))
    expert_sum = low_back(middle + jnp.einsum('ecf,efd->ecd', act_second, second_out, precision=highest))
    logits = jnp.einsum('ecd,ed->ec', slot_rows, centroids, precision=highest)
    gate_vals = jax.nn.sigmoid(logits)
    returned = low_back(low(gate_vals[:, :, None] * expert_sum)).reshape(EXPERTS * CAP, D)
    return residual + jnp.dot(dispatch.T, returned, precision=highest)

def reference(tokens, lengths, deal, routes, slot_order, gain_attn, gain_ffn, w_qkv, w_out, centroids, expert_in, expert_out, second_in, second_out, cotangent):
    pack_count = SETS * EXPERTS * MICRO
    pack_rows = PER * SEQ
    inverse = jnp.argsort(deal, axis=1).astype(jnp.int32)
    deal_index = deal.astype(jnp.int32)

    def to_packs(flat):
        sequences = seq_view(flat)
        dealt = jnp.take_along_axis(sequences, inverse[:, :, None, None], axis=1)
        return dealt.reshape(pack_count, pack_rows, flat.shape[-1])
    route_rows = to_packs(routes)[:, :, 0]
    order_rows = to_packs(slot_order)[:, :, 0]
    length_rows = jnp.take_along_axis(lengths, inverse, axis=1).reshape(pack_count, PER)
    params = tuple((weight.astype(jnp.float32) for weight in (w_qkv, w_out, gain_attn, gain_ffn, centroids, expert_in, expert_out, second_in, second_out)))
    checked = jax.checkpoint(pack_forward)

    def forward(weights, flat_inputs):
        packs = to_packs(flat_inputs)

        def scan_step(scan_carry, scan_item):
            return (scan_carry, checked(weights, scan_item[0], scan_item[1], scan_item[2], scan_item[3]))
        unused_carry, results = lax.scan(scan_step, jnp.zeros((), jnp.float32), (packs, route_rows, order_rows, length_rows))
        dealt = results.reshape(SETS, GROUP, SEQ, D)
        restored = jnp.take_along_axis(dealt, deal_index[:, :, None, None], axis=1)
        return flat_view(restored)
    result, pullback = jax.vjp(forward, params, tokens.astype(jnp.float32))
    weight_grads, grad_inputs = pullback(cotangent.astype(jnp.float32))
    grad_qkv, grad_attn_out, grad_gain_a, grad_gain_f, grad_cent, grad_in, grad_exp_out, grad_sec_in, grad_sec_out = weight_grads
    return (result.astype(jnp.bfloat16), grad_inputs, grad_gain_a, grad_gain_f, grad_qkv, grad_attn_out, grad_cent, grad_in, grad_exp_out, grad_sec_in, grad_sec_out)
```

```python
import jax
import jax.numpy as jnp
from jax import lax
from jax.sharding import PartitionSpec as P

HEADS = 16
HEAD = 64
MICRO = 4
PER = 2
SEQ = 64
PACK = PER * SEQ

epsilon = 1e-05
bf16 = jnp.bfloat16
f32 = jnp.float32


def mm(a, b, contract=(1, 0)):
    return lax.dot_general(
        a, b, (((contract[0],), (contract[1],)), ((), ())), preferred_element_type=f32
    )


def norm_parts(rows):
    centre = jnp.mean(rows, axis=-1, keepdims=True)
    shifted = rows - centre
    spread = jnp.mean(shifted * shifted, axis=-1, keepdims=True)
    inv = lax.rsqrt(spread + epsilon)
    return shifted * inv, inv


def norm_back(unit, inv, gain, grad):
    g = grad * gain
    m1 = jnp.mean(g, axis=-1, keepdims=True)
    m2 = jnp.mean(g * unit, axis=-1, keepdims=True)
    return inv * (g - m1 - unit * m2)


def gelu_act(pre_act):
    return jax.nn.gelu(pre_act, approximate=True)


def gather_hidden(rows):
    return lax.all_gather(rows, "hidden", axis=0, tiled=True)


def sum_hidden(terms):
    return lax.psum_scatter(terms, "hidden", scatter_dimension=0, tiled=True)


def swap(blocks):
    return lax.all_to_all(blocks, "expert", split_axis=0, concat_axis=0, tiled=True)


def shards(
    tokens,
    lengths,
    deal,
    routes,
    slot_order,
    gain_attn,
    gain_ffn,
    w_qkv,
    w_out,
    centroids,
    expert_in,
    expert_out,
    second_in,
    second_out,
    cotangent,
):
    width = tokens.shape[1]
    experts = lax.axis_size("expert")
    piece = SEQ // experts
    seats = MICRO * PER
    group = experts * seats
    rows = seats * SEQ
    capacity = (9 * PACK + 8 * experts - 1) // (8 * experts)
    per_dest = MICRO * capacity
    my_expert = lax.axis_index("expert")
    my_hidden = lax.axis_index("hidden")

    deal_row = lax.dynamic_index_in_dim(deal, my_hidden, 0, keepdims=False)
    length_row = lax.dynamic_index_in_dim(lengths, my_hidden, 0, keepdims=False)
    ids = jnp.arange(group, dtype=jnp.int32)
    inverse = jnp.sum(jnp.where(deal_row[None, :] == ids[:, None], ids[None, :], 0), axis=1)
    own = my_expert * seats + jnp.arange(seats, dtype=jnp.int32)
    own_lengths = jnp.sum(
        jnp.where(deal_row[None, :] == own[:, None], length_row[None, :], 0), axis=1
    )

    def to_dealt(flat):
        pieces = jnp.take(flat.reshape(group, piece, flat.shape[1]), inverse, axis=0)
        return lax.all_to_all(
            pieces.reshape(experts, seats, piece, flat.shape[1]),
            "expert",
            split_axis=0,
            concat_axis=2,
            tiled=True,
        ).reshape(rows, flat.shape[1])

    labels = jnp.concatenate([routes, slot_order], axis=1)
    lab = to_dealt(labels)
    tok = to_dealt(tokens)
    grad_output = to_dealt(cotangent)

    cat = jnp.concatenate(
        [w_qkv, w_out, gain_attn[:, None], gain_ffn[:, None], jnp.zeros((w_qkv.shape[0], 126), bf16)],
        axis=1,
    )
    cat = lax.all_gather(cat, ("expert", "hidden"), axis=0, tiled=True)
    qkv_w = cat[:, : 3 * width]
    out_w = cat[:, 3 * width : 4 * width]
    attn_gain = cat[:, 4 * width].astype(f32)[None, :]
    ffn_gain = cat[:, 4 * width + 1].astype(f32)[None, :]

    route = lab[:, 0].reshape(MICRO, PACK)
    order = lab[:, 1].reshape(MICRO, PACK)
    positions = jnp.arange(PACK, dtype=jnp.int32)
    seat = positions // SEQ
    pack_lengths = own_lengths.reshape(MICRO, PER)
    limit = jnp.repeat(pack_lengths, SEQ, axis=1)
    present = (positions % SEQ)[None, :] < limit
    priority = order * PER + seat[None, :]
    ahead = jnp.sum(
        (
            (route[:, :, None] == route[:, None, :])
            & (priority[:, None, :] < priority[:, :, None])
            & present[:, None, :]
        ).astype(jnp.int32),
        axis=2,
    )
    accepted = (present & (ahead < capacity)).reshape(rows)
    target = (
        route * per_dest + jnp.arange(MICRO, dtype=jnp.int32)[:, None] * capacity + ahead
    ).reshape(rows)
    target = jnp.where(accepted, target, -1)
    slot_ids = jnp.arange(experts * per_dest, dtype=jnp.int32)
    dispatch = (slot_ids[:, None] == target[None, :]).astype(bf16)

    def to_experts(values):
        out = mm(dispatch, values).astype(bf16)
        return swap(out.reshape(experts, per_dest, width)).reshape(experts * per_dest, width)

    cot_arrived = to_experts(grad_output)

    inputs = tok.astype(f32)
    unit_a, inv_a = norm_parts(inputs)
    normed = (unit_a * attn_gain).astype(bf16)
    packed = mm(normed, qkv_w).astype(bf16)
    allowed = (
        (seat[:, None] == seat[None, :]) & (positions[None, :] <= positions[:, None])
    )[None] & present[:, None, :]

    def heads(block):
        return block.reshape(MICRO, PACK, HEADS, HEAD)

    queries = heads(packed[:, :width])
    keys_all = heads(packed[:, width : 2 * width])
    values_all = heads(packed[:, 2 * width :])
    scores = jnp.einsum("pqhd,pkhd->phqk", queries, keys_all, preferred_element_type=f32) * 0.125
    masked = jnp.where(allowed[:, None], scores, -1e30)
    peaks = jnp.max(masked, axis=-1, keepdims=True)
    log_total = peaks + jnp.log(jnp.sum(jnp.exp(masked - peaks), axis=-1, keepdims=True))
    probs = jnp.exp(masked - log_total)
    probs_lo = probs.astype(bf16)
    mixed = (
        jnp.einsum("phqk,pkhd->pqhd", probs_lo, values_all, preferred_element_type=f32)
        .reshape(rows, width)
        .astype(bf16)
    )
    residual = inputs + mm(mixed, out_w)
    unit_f, inv_f = norm_parts(residual)
    shared = (unit_f * ffn_gain).astype(bf16)
    arrived = to_experts(shared)

    centroid_row = centroids[0]
    w_in, w_back = expert_in[0], expert_out[0]
    s_in, s_back = second_in[0], second_out[0]
    count = arrived.shape[0]
    arrived_f = arrived.astype(f32)
    gate_vals = jax.nn.sigmoid(
        jnp.sum(arrived_f * centroid_row.astype(f32)[None, :], axis=1, keepdims=True)
    )
    grad_result_own = (gate_vals * cot_arrived.astype(f32)).astype(bf16)
    gathered = gather_hidden(arrived)
    grad_result = gather_hidden(grad_result_own)
    pre_first = mm(gathered, w_in)
    act_first, pull_first = jax.vjp(gelu_act, pre_first)
    act_first = act_first.astype(bf16)
    middle = arrived_f + sum_hidden(mm(act_first, w_back).astype(bf16)).astype(f32)
    middle_lo = gather_hidden(middle.astype(bf16))
    pre_second = mm(middle_lo, s_in)
    act_second, pull_second = jax.vjp(gelu_act, pre_second)
    act_second = act_second.astype(bf16)
    expert_sum = middle + sum_hidden(mm(act_second, s_back).astype(bf16)).astype(f32)
    returned = (gate_vals * expert_sum).astype(bf16)
    came_back = swap(returned.reshape(experts, per_dest, width)).reshape(count, width)

    grad_logit = (
        jnp.sum(cot_arrived.astype(f32) * expert_sum, axis=1, keepdims=True)
        * gate_vals
        * (1.0 - gate_vals)
    )
    grad_pre_second = pull_second(mm(grad_result, s_back, (1, 1)))[0].astype(bf16)
    grad_middle_own = (
        grad_result_own.astype(f32)
        + sum_hidden(mm(grad_pre_second, s_in, (1, 1)).astype(bf16)).astype(f32)
    ).astype(bf16)
    grad_middle = gather_hidden(grad_middle_own)
    grad_pre = pull_first(mm(grad_middle, w_back, (1, 1)))[0].astype(bf16)
    grad_slots = (
        sum_hidden(mm(grad_pre, w_in, (1, 1)).astype(bf16)).astype(f32)
        + grad_middle_own.astype(f32)
        + grad_logit * centroid_row.astype(f32)[None, :]
    ).astype(bf16)
    grad_back = swap(grad_slots.reshape(experts, per_dest, width)).reshape(count, width)
    g_sec_out = mm(act_second, grad_result, (0, 0))
    g_sec_in = mm(middle_lo, grad_pre_second, (0, 0))
    g_exp_out = mm(act_first, grad_middle, (0, 0))
    g_exp_in = mm(gathered, grad_pre, (0, 0))
    g_cent = jnp.sum(grad_logit * arrived_f, axis=0, keepdims=True)

    combined = (residual + mm(dispatch, came_back, (0, 0))).astype(bf16)

    grad_shared = mm(dispatch, grad_back, (0, 0))
    g_gain_ffn = jnp.sum(grad_shared * unit_f, axis=0)
    grad_residual = grad_output.astype(f32) + norm_back(unit_f, inv_f, ffn_gain, grad_shared)
    grad_attended = grad_residual.astype(bf16)
    g_out_w = mm(mixed, grad_attended, (0, 0))
    grad_mixed = heads(mm(grad_attended, out_w, (1, 1)).astype(bf16))
    grad_probs = jnp.einsum("pqhd,pkhd->phqk", grad_mixed, values_all, preferred_element_type=f32)
    grad_values = jnp.einsum("phqk,pqhd->pkhd", probs_lo, grad_mixed, preferred_element_type=f32)
    inner = jnp.sum(probs * grad_probs, axis=-1, keepdims=True)
    grad_scores = (probs * (grad_probs - inner)).astype(bf16)
    grad_queries = (
        jnp.einsum("phqk,pkhd->pqhd", grad_scores, keys_all, preferred_element_type=f32) * 0.125
    )
    grad_keys = (
        jnp.einsum("phqk,pqhd->pkhd", grad_scores, queries, preferred_element_type=f32) * 0.125
    )
    grad_packed = jnp.concatenate(
        [g.reshape(rows, width) for g in (grad_queries, grad_keys, grad_values)], axis=1
    ).astype(bf16)
    g_qkv = mm(normed, grad_packed, (0, 0))
    grad_normed = mm(grad_packed, qkv_w, (1, 1))
    g_gain_attn = jnp.sum(grad_normed * unit_a, axis=0)
    input_grad = (grad_residual + norm_back(unit_a, inv_a, attn_gain, grad_normed)).astype(bf16)

    def scatter(partial):
        return lax.psum_scatter(
            partial, ("expert", "hidden"), scatter_dimension=0, tiled=True
        )

    g_cat = jnp.concatenate([g_qkv, g_out_w, g_gain_attn[:, None], g_gain_ffn[:, None], jnp.zeros((width, 126), f32)], axis=1)
    g_cat = scatter(g_cat)
    g_cent = lax.psum(g_cent, "hidden")

    def from_dealt(dealt):
        received = lax.all_to_all(
            dealt.reshape(1, seats, SEQ, width), "expert", split_axis=2, concat_axis=0, tiled=True
        ).reshape(group, piece, width)
        return jnp.take(received, deal_row, axis=0).reshape(group * piece, width)

    return (
        from_dealt(combined),
        from_dealt(input_grad).astype(f32),
        g_cat[:, 4 * width],
        g_cat[:, 4 * width + 1],
        g_cat[:, : 3 * width],
        g_cat[:, 3 * width : 4 * width],
        g_cent,
        g_exp_in[None],
        g_exp_out[None],
        g_sec_in[None],
        g_sec_out[None],
    )


def solution(mesh):
    both = ("expert", "hidden")
    return jax.shard_map(
        shards,
        mesh=mesh,
        in_specs=(
            P(both, None),
            P(),
            P(),
            P(both, None),
            P(both, None),
            P(both),
            P(both),
            P(both, None),
            P(both, None),
            P("expert", None),
            P("expert", None, "hidden"),
            P("expert", "hidden", None),
            P("expert", None, "hidden"),
            P("expert", "hidden", None),
            P(both, None),
        ),
        out_specs=(
            P(both, None),
            P(both, None),
            P(both),
            P(both),
            P(both, None),
            P(both, None),
            P("expert", None),
            P("expert", None, "hidden"),
            P("expert", "hidden", None),
            P("expert", None, "hidden"),
            P("expert", "hidden", None),
        ),
        check_vma=False,
    )
```

```python
import functools

import jax
import jax.numpy as jnp
from jax import lax
from jax.experimental import pallas as pl
from jax.experimental.pallas import tpu as pltpu
from jax.sharding import PartitionSpec as P

HEADS = 16
HEAD = 64
MICRO = 4
PER = 2
SEQ = 64
PACK = PER * SEQ

epsilon = 1e-05
bf16 = jnp.bfloat16
f32 = jnp.float32


def mm(a, b, contract=(1, 0)):
    return lax.dot_general(
        a, b, (((contract[0],), (contract[1],)), ((), ())), preferred_element_type=f32
    )


def norm_parts(rows):
    centre = jnp.mean(rows, axis=-1, keepdims=True)
    shifted = rows - centre
    spread = jnp.mean(shifted * shifted, axis=-1, keepdims=True)
    inv = lax.rsqrt(spread + epsilon)
    return shifted * inv, inv


def norm_back(unit, inv, gain, grad):
    g = grad * gain
    m1 = jnp.mean(g, axis=-1, keepdims=True)
    m2 = jnp.mean(g * unit, axis=-1, keepdims=True)
    return inv * (g - m1 - unit * m2)


def gelu_act(pre_act):
    return jax.nn.gelu(pre_act, approximate=True)


def gather_hidden(rows):
    return lax.all_gather(rows, "hidden", axis=0, tiled=True)


def sum_hidden(terms):
    return lax.psum_scatter(terms, "hidden", scatter_dimension=0, tiled=True)


def swap(blocks):
    return lax.all_to_all(blocks, "expert", split_axis=0, concat_axis=0, tiled=True)


MESH = pl.DeviceIdType.MESH
ANY = pl.BlockSpec(memory_space=pl.ANY)
VM = pl.BlockSpec(memory_space=pltpu.VMEM)
DMA = pltpu.SemaphoreType.DMA
VMEM_MAX = 63 << 20
PARTS = 4


def dims(experts, width):
    capacity = (9 * PACK + 8 * experts - 1) // (8 * experts)
    per_dest = MICRO * capacity
    main = per_dest // 16 * 16
    return per_dest, main, per_dest - main


def greet(experts, me, core, partner):
    barrier = pltpu.get_barrier_semaphore()

    def hello(k, carry):
        pl.semaphore_signal(
            barrier, inc=1, device_id=(lax.rem(me + k, experts), core), device_id_type=MESH
        )
        return carry

    lax.fori_loop(1, experts, hello, 0)
    if partner is not None:
        pl.semaphore_signal(barrier, inc=1, device_id=(me, partner), device_id_type=MESH)
    pl.semaphore_wait(barrier, experts - 1 + (partner is not None))


class Spread:
    def __init__(self, experts, me, core, src, dst, sends, recvs, local):
        self.experts, self.me, self.core = experts, me, core
        self.src, self.dst, self.sends, self.recvs, self.local = src, dst, sends, recvs, local
        self.rows = src.shape[0] // experts

    def block(self, ref, index):
        return ref.at[pl.ds(pl.multiple_of(index * self.rows, 16), self.rows)]

    def copy(self, k):
        to = lax.rem(self.me + k, self.experts)
        return pltpu.make_async_remote_copy(
            self.block(self.src, to),
            self.block(self.dst, self.me),
            self.sends.at[k],
            self.recvs.at[k],
            device_id=(to, self.core),
            device_id_type=MESH,
        )

    def own(self):
        return pltpu.make_async_copy(
            self.block(self.src, self.me), self.block(self.dst, self.me), self.local
        )

    def start(self):
        self.own().start()

        def go(k, carry):
            self.copy(k).start()
            return carry

        lax.fori_loop(1, self.experts, go, 0)

    def wait(self):
        self.own().wait()

        def stop(k, carry):
            self.copy(k).wait()
            return carry

        lax.fori_loop(1, self.experts, stop, 0)


def spread_kernel(experts, count, *refs):
    srcs, dsts = refs[:count], refs[count : 2 * count]
    sends, recvs, local = refs[2 * count :]
    me, core = lax.axis_index("expert"), lax.axis_index("hidden")
    greet(experts, me, core, None)
    moves = [
        Spread(experts, me, core, s, d, sends.at[i], recvs.at[i], local.at[i])
        for i, (s, d) in enumerate(zip(srcs, dsts))
    ]
    for move in moves:
        move.start()
    for move in moves:
        move.wait()


def spread(experts, call_id, name, *arrays):
    n = len(arrays)
    return pl.pallas_call(
        functools.partial(spread_kernel, experts, n),
        out_shape=[jax.ShapeDtypeStruct(a.shape, a.dtype) for a in arrays],
        in_specs=[ANY] * n,
        out_specs=[ANY] * n,
        scratch_shapes=[DMA((n, experts)), DMA((n, experts)), DMA((n,))],
        compiler_params=pltpu.CompilerParams(collective_id=call_id, has_side_effects=True),
        name=name,
    )(*arrays)


def tail_matrix(part, experts, tail, turned):
    size = PARTS * tail
    shape = (experts * tail, experts * size) if turned else (experts * size, experts * tail)
    there = lax.broadcasted_iota(jnp.int32, shape, 1 if turned else 0)
    here = lax.broadcasted_iota(jnp.int32, shape, 0 if turned else 1)
    want = here // tail * size + part * tail + here % tail
    return (there == want).astype(f32).astype(bf16)


def gelu_pair(v):
    u = v * v
    t = jnp.tanh(v * (0.7978845608 + 0.7978845608 * 0.044715 * u))
    h = 0.5 * t + 0.5
    slope = h + (h - h * h) * (v * (2 * 0.7978845608 + 6 * 0.7978845608 * 0.044715 * u))
    return v * h, slope


def experts_kernel(experts, tail, *refs):
    (a_in, b_in, ca_in, cb_in, cent, w1_h, w2_h, w3_h, w4_h) = refs[:9]
    (ra_out, rb_out, ga_out, gb_out, gcent, xg_o, mlo_o, grs_o, gm_o, act1_o, act2_o, gp1_o, gp2_o) = refs[9:22]
    (w1, w2, w3, w4, xg, mlo, grs, gm, act1, act2, d1, d2, mid, psend, precv, ca, cb, sa, sb) = refs[22:41]
    (wsem, osem, psems, prsems, xs, xr, asend, arecv, alocal) = refs[41:]
    me, core = lax.axis_index("expert"), lax.axis_index("hidden")
    other = 1 - core
    own, width = xg.shape[0] // 2, xg.shape[1]
    hid = w1.shape[1]
    main = a_in.shape[0]
    block = width // PARTS
    mine, theirs = pl.ds(0, own), pl.ds(own, own)

    loads = []
    for i, (h, v) in enumerate(((w1_h, w1), (w2_h, w2), (w3_h, w3), (w4_h, w4))):
        load = pltpu.make_async_copy(h, v, wsem.at[i])
        load.start()
        loads.append(load)
    greet(experts, me, core, other)

    def move(i, src, dst):
        return Spread(experts, me, core, src, dst, asend.at[i], arecv.at[i], alocal.at[i])

    cot_moves = (move(0, ca_in, ca), move(1, cb_in, cb))
    for m in cot_moves:
        m.start()

    def pair(src, dst, send, recv):
        return pltpu.make_async_remote_copy(
            src, dst, send, recv, device_id=(me, other), device_id_type=MESH
        )

    def mirror(i, ref):
        return pair(ref.at[mine], ref.at[theirs], xs.at[i], xr.at[i])

    def partial_send(i):
        return pair(psend, precv.at[i % 2], psems.at[i], prsems.at[i])

    def from_tail(ref, to, start):
        for q in range(PARTS):
            to[pl.ds(start, experts * tail), q * block : (q + 1) * block] = mm(
                tail_matrix(q, experts, tail, True), ref[...]
            ).astype(bf16)

    def to_tail(value, ref):
        total = None
        for q in range(PARTS):
            term = mm(tail_matrix(q, experts, tail, False), value[:, q * block : (q + 1) * block])
            total = term if total is None else total + term
        ref[...] = total.astype(bf16)

    outs = []

    def store(i, ref, out):
        copy = pltpu.make_async_copy(ref, out, osem.at[i])
        copy.start()
        outs.append(copy)

    TN = 256

    def over(size, body):
        def step(n, carry):
            body(pl.ds(pl.multiple_of(n * TN, TN), TN))
            return carry

        lax.fori_loop(0, size // TN, step, 0)

    def up(x, w, act, slope, rows):
        def body(cols):
            a, d = gelu_pair(mm(x[rows, :], w[:, cols]))
            act[rows, cols] = a.astype(bf16)
            slope[rows, cols] = d.astype(bf16)

        over(hid, body)

    def down(act, w, rows, put):
        over(width, lambda cols: put(cols, mm(act[rows, :], w[:, cols])))

    def up_back(g, w, slope, rows):
        def body(cols):
            t = mm(g[rows, :], w[cols, :], (1, 1)) * slope[rows, cols].astype(f32)
            slope[rows, cols] = t.astype(bf16)

        over(hid, body)

    def down_back(gp, w, rows, put):
        over(width, lambda cols: put(cols, mm(gp[rows, :], w[cols, :], (1, 1))))

    def to_send(cols, value):
        psend[:, cols] = value.astype(bf16)

    def to_mid(cols, value):
        mid[:, cols] = value

    def add_mid(cols, value):
        mid[:, cols] += value

    xg[pl.ds(0, main), :] = a_in[...]
    from_tail(b_in, xg, main)
    share_x = mirror(0, xg)
    share_x.start()
    slot = xg[mine, :].astype(f32)
    gate = jax.nn.sigmoid(jnp.sum(slot * cent[...], axis=1, keepdims=True))
    loads[0].wait()
    up(xg, w1, act1, d1, mine)
    share_x.wait()
    store(0, xg, xg_o)
    up(xg, w1, act1, d1, theirs)
    store(1, act1, act1_o)
    loads[1].wait()
    down(act1, w2, theirs, to_send)
    send0 = partial_send(0)
    send0.start()
    down(act1, w2, mine, to_mid)
    send0.wait()
    mid[...] = mid[...] + xg[mine, :].astype(f32) + precv[0].astype(f32)
    mlo[mine, :] = mid[...].astype(bf16)
    share_m = mirror(1, mlo)
    share_m.start()
    loads[2].wait()
    up(mlo, w3, act2, d2, mine)
    share_m.wait()
    store(2, mlo, mlo_o)
    up(mlo, w3, act2, d2, theirs)
    store(3, act2, act2_o)
    loads[3].wait()
    down(act2, w4, theirs, to_send)
    send1 = partial_send(1)
    send1.start()
    down(act2, w4, mine, add_mid)
    send1.wait()
    mid[...] = mid[...] + precv[1].astype(f32)
    returned = (gate * mid[...]).astype(bf16)
    sa[...] = returned[:main]
    to_tail(returned[main:], sb)
    ret_moves = (move(2, sa, ra_out), move(3, sb, rb_out))
    for m in ret_moves:
        m.start()
    for m in cot_moves:
        m.wait()
    grs[pl.ds(0, main), :] = ca[...]
    from_tail(cb, grs, main)
    cot = grs[mine, :].astype(f32)
    logit = jnp.sum(cot * mid[...], axis=1, keepdims=True) * gate * (1.0 - gate)
    grs[mine, :] = (gate * cot).astype(bf16)
    share_g = mirror(2, grs)
    share_g.start()
    up_back(grs, w4, d2, mine)
    share_g.wait()
    store(4, grs, grs_o)
    up_back(grs, w4, d2, theirs)
    store(5, d2, gp2_o)
    down_back(d2, w3, theirs, to_send)
    send2 = partial_send(2)
    send2.start()
    down_back(d2, w3, mine, to_mid)
    send2.wait()
    gm[mine, :] = (mid[...] + grs[mine, :].astype(f32) + precv[0].astype(f32)).astype(bf16)
    share_gm = mirror(3, gm)
    share_gm.start()
    up_back(gm, w2, d1, mine)
    share_gm.wait()
    store(6, gm, gm_o)
    up_back(gm, w2, d1, theirs)
    store(7, d1, gp1_o)
    down_back(d1, w1, theirs, to_send)
    send3 = partial_send(3)
    send3.start()
    down_back(d1, w1, mine, to_mid)
    gcent[...] = jnp.sum(logit * xg[mine, :].astype(f32), axis=0, keepdims=True)
    for m in ret_moves:
        m.wait()
    send3.wait()
    slots = (
        mid[...] + gm[mine, :].astype(f32) + precv[1].astype(f32) + logit * cent[...]
    ).astype(bf16)
    sa[...] = slots[:main]
    to_tail(slots[main:], sb)
    back_moves = (move(4, sa, ga_out), move(5, sb, gb_out))
    for m in back_moves:
        m.start()
    for copy in outs:
        copy.wait()
    for m in back_moves:
        m.wait()


def run_experts(experts, slots, tails, cots, cot_tails, centroid, weights):
    width, hid = weights[0].shape
    main = slots.shape[0]
    tail = tails.shape[0] // experts // PARTS
    own = main + experts * tail
    both = 2 * own

    def sds(*shape, dtype=bf16):
        return jax.ShapeDtypeStruct(shape, dtype)

    travel = [sds(*slots.shape), sds(*tails.shape)] * 2
    wide = [sds(both, width)] * 4 + [sds(both, hid)] * 4
    return pl.pallas_call(
        functools.partial(experts_kernel, experts, tail),
        out_shape=travel + [sds(1, width, dtype=f32)] + wide,
        in_specs=[VM, VM, ANY, ANY, VM, ANY, ANY, ANY, ANY],
        out_specs=[ANY] * 4 + [VM] + [ANY] * 8,
        scratch_shapes=[
            pltpu.VMEM((width, hid), bf16),
            pltpu.VMEM((hid, width), bf16),
            pltpu.VMEM((width, hid), bf16),
            pltpu.VMEM((hid, width), bf16),
            pltpu.VMEM((both, width), bf16),
            pltpu.VMEM((both, width), bf16),
            pltpu.VMEM((both, width), bf16),
            pltpu.VMEM((both, width), bf16),
            pltpu.VMEM((both, hid), bf16),
            pltpu.VMEM((both, hid), bf16),
            pltpu.VMEM((both, hid), bf16),
            pltpu.VMEM((both, hid), bf16),
            pltpu.VMEM((own, width), f32),
            pltpu.VMEM((own, width), bf16),
            pltpu.VMEM((2, own, width), bf16),
            pltpu.VMEM(slots.shape, bf16),
            pltpu.VMEM(tails.shape, bf16),
            pltpu.VMEM(slots.shape, bf16),
            pltpu.VMEM(tails.shape, bf16),
            DMA((4,)),
            DMA((8,)),
            DMA((4,)),
            DMA((4,)),
            DMA((4,)),
            DMA((4,)),
            DMA((6, experts)),
            DMA((6, experts)),
            DMA((6,)),
        ],
        compiler_params=pltpu.CompilerParams(
            collective_id=2, has_side_effects=True, vmem_limit_bytes=VMEM_MAX
        ),
        name="experts_pass",
    )(slots, tails, cots, cot_tails, centroid, *weights)


def shards(
    fast,
    tokens,
    lengths,
    deal,
    routes,
    slot_order,
    gain_attn,
    gain_ffn,
    w_qkv,
    w_out,
    centroids,
    expert_in,
    expert_out,
    second_in,
    second_out,
    cotangent,
):
    width = tokens.shape[1]
    experts = lax.axis_size("expert")
    piece = SEQ // experts
    seats = MICRO * PER
    group = experts * seats
    rows = seats * SEQ
    capacity = (9 * PACK + 8 * experts - 1) // (8 * experts)
    per_dest = MICRO * capacity
    my_expert = lax.axis_index("expert")
    my_hidden = lax.axis_index("hidden")

    deal_row = lax.dynamic_index_in_dim(deal, my_hidden, 0, keepdims=False)
    length_row = lax.dynamic_index_in_dim(lengths, my_hidden, 0, keepdims=False)
    ids = jnp.arange(group, dtype=jnp.int32)
    inverse = jnp.sum(jnp.where(deal_row[None, :] == ids[:, None], ids[None, :], 0), axis=1)
    own = my_expert * seats + jnp.arange(seats, dtype=jnp.int32)
    own_lengths = jnp.sum(
        jnp.where(deal_row[None, :] == own[:, None], length_row[None, :], 0), axis=1
    )

    def to_dealt(flat):
        pieces = jnp.take(flat.reshape(group, piece, flat.shape[1]), inverse, axis=0)
        return lax.all_to_all(
            pieces.reshape(experts, seats, piece, flat.shape[1]),
            "expert",
            split_axis=0,
            concat_axis=2,
            tiled=True,
        ).reshape(rows, flat.shape[1])

    labels = jnp.concatenate([routes, slot_order], axis=1)
    lab = to_dealt(labels)
    tok = to_dealt(tokens)
    grad_output = to_dealt(cotangent)

    cat = jnp.concatenate(
        [w_qkv, w_out, gain_attn[:, None], gain_ffn[:, None], jnp.zeros((w_qkv.shape[0], 126), bf16)],
        axis=1,
    )
    cat = lax.all_gather(cat, ("expert", "hidden"), axis=0, tiled=True)
    qkv_w = cat[:, : 3 * width]
    out_w = cat[:, 3 * width : 4 * width]
    attn_gain = cat[:, 4 * width].astype(f32)[None, :]
    ffn_gain = cat[:, 4 * width + 1].astype(f32)[None, :]

    route = lab[:, 0].reshape(MICRO, PACK)
    order = lab[:, 1].reshape(MICRO, PACK)
    positions = jnp.arange(PACK, dtype=jnp.int32)
    seat = positions // SEQ
    pack_lengths = own_lengths.reshape(MICRO, PER)
    limit = jnp.repeat(pack_lengths, SEQ, axis=1)
    present = (positions % SEQ)[None, :] < limit
    priority = order * PER + seat[None, :]
    ahead = jnp.sum(
        (
            (route[:, :, None] == route[:, None, :])
            & (priority[:, None, :] < priority[:, :, None])
            & present[:, None, :]
        ).astype(jnp.int32),
        axis=2,
    )
    accepted = (present & (ahead < capacity)).reshape(rows)
    target = (
        route * per_dest + jnp.arange(MICRO, dtype=jnp.int32)[:, None] * capacity + ahead
    ).reshape(rows)
    target = jnp.where(accepted, target, -1)
    slot_ids = jnp.arange(experts * per_dest, dtype=jnp.int32)
    dispatch = (slot_ids[:, None] == target[None, :]).astype(bf16)

    per_dest, main, tail = dims(experts, width)
    block = width // PARTS
    if fast:
        base = jnp.arange(MICRO, dtype=jnp.int32)[:, None] * capacity + ahead
        base = base.reshape(rows)
        route_flat = route.reshape(rows)
        head = jnp.where(accepted & (base < main), route_flat * main + base, -1)
        d_main = (jnp.arange(experts * main, dtype=jnp.int32)[:, None] == head[None, :]).astype(bf16)
        d_tail = []
        for q in range(PARTS):
            where = jnp.where(
                accepted & (base >= main), (route_flat * PARTS + q) * tail + base - main, -1
            )
            d_tail.append(
                (jnp.arange(experts * PARTS * tail, dtype=jnp.int32)[:, None] == where[None, :]).astype(bf16)
            )

    def split(values):
        total = sum(
            mm(d_tail[q], values[:, q * block : (q + 1) * block]) for q in range(PARTS)
        )
        return mm(d_main, values).astype(bf16), total.astype(bf16)

    def join(slots, tails):
        return mm(d_main, slots, (0, 0)) + jnp.concatenate(
            [mm(d_tail[q], tails, (0, 0)) for q in range(PARTS)], axis=1
        )

    def to_experts(values):
        out = mm(dispatch, values).astype(bf16)
        return swap(out.reshape(experts, per_dest, width)).reshape(experts * per_dest, width)

    inputs = tok.astype(f32)
    unit_a, inv_a = norm_parts(inputs)
    normed = (unit_a * attn_gain).astype(bf16)
    packed = mm(normed, qkv_w).astype(bf16)
    allowed = (
        (seat[:, None] == seat[None, :]) & (positions[None, :] <= positions[:, None])
    )[None] & present[:, None, :]

    def heads(block):
        return block.reshape(MICRO, PACK, HEADS, HEAD)

    queries = heads(packed[:, :width])
    keys_all = heads(packed[:, width : 2 * width])
    values_all = heads(packed[:, 2 * width :])
    scores = jnp.einsum("pqhd,pkhd->phqk", queries, keys_all, preferred_element_type=f32) * 0.125
    masked = jnp.where(allowed[:, None], scores, -1e30)
    peaks = jnp.max(masked, axis=-1, keepdims=True)
    log_total = peaks + jnp.log(jnp.sum(jnp.exp(masked - peaks), axis=-1, keepdims=True))
    probs = jnp.exp(masked - log_total)
    probs_lo = probs.astype(bf16)
    mixed = (
        jnp.einsum("phqk,pkhd->pqhd", probs_lo, values_all, preferred_element_type=f32)
        .reshape(rows, width)
        .astype(bf16)
    )
    residual = inputs + mm(mixed, out_w)
    unit_f, inv_f = norm_parts(residual)
    shared = (unit_f * ffn_gain).astype(bf16)
    centroid_row = centroids[0]
    w_in, w_back = expert_in[0], expert_out[0]
    s_in, s_back = second_in[0], second_out[0]
    if fast:
        slots, tails = spread(experts, 1, "slots_out", *split(shared))
        cots, cot_tails = split(grad_output)
        (ra, rb, ga, gb, g_cent, gathered, middle_lo, grad_result, grad_middle,
         act_first, act_second, grad_pre, grad_pre_second) = run_experts(
            experts, slots, tails, cots, cot_tails, centroids.astype(f32), (w_in, w_back, s_in, s_back)
        )
        g_sec_out = mm(act_second, grad_result, (0, 0))
        g_sec_in = mm(middle_lo, grad_pre_second, (0, 0))
        g_exp_out = mm(act_first, grad_middle, (0, 0))
        g_exp_in = mm(gathered, grad_pre, (0, 0))
        moe_out = join(ra, rb)
        grad_shared = join(ga, gb)
    else:
        cot_arrived = to_experts(grad_output)
        arrived = to_experts(shared)

        count = arrived.shape[0]
        arrived_f = arrived.astype(f32)
        gate_vals = jax.nn.sigmoid(
            jnp.sum(arrived_f * centroid_row.astype(f32)[None, :], axis=1, keepdims=True)
        )
        grad_result_own = (gate_vals * cot_arrived.astype(f32)).astype(bf16)
        gathered = gather_hidden(arrived)
        grad_result = gather_hidden(grad_result_own)
        pre_first = mm(gathered, w_in)
        act_first, pull_first = jax.vjp(gelu_act, pre_first)
        act_first = act_first.astype(bf16)
        middle = arrived_f + sum_hidden(mm(act_first, w_back).astype(bf16)).astype(f32)
        middle_lo = gather_hidden(middle.astype(bf16))
        pre_second = mm(middle_lo, s_in)
        act_second, pull_second = jax.vjp(gelu_act, pre_second)
        act_second = act_second.astype(bf16)
        expert_sum = middle + sum_hidden(mm(act_second, s_back).astype(bf16)).astype(f32)
        returned = (gate_vals * expert_sum).astype(bf16)
        came_back = swap(returned.reshape(experts, per_dest, width)).reshape(count, width)

        grad_logit = (
            jnp.sum(cot_arrived.astype(f32) * expert_sum, axis=1, keepdims=True)
            * gate_vals
            * (1.0 - gate_vals)
        )
        grad_pre_second = pull_second(mm(grad_result, s_back, (1, 1)))[0].astype(bf16)
        grad_middle_own = (
            grad_result_own.astype(f32)
            + sum_hidden(mm(grad_pre_second, s_in, (1, 1)).astype(bf16)).astype(f32)
        ).astype(bf16)
        grad_middle = gather_hidden(grad_middle_own)
        grad_pre = pull_first(mm(grad_middle, w_back, (1, 1)))[0].astype(bf16)
        grad_slots = (
            sum_hidden(mm(grad_pre, w_in, (1, 1)).astype(bf16)).astype(f32)
            + grad_middle_own.astype(f32)
            + grad_logit * centroid_row.astype(f32)[None, :]
        ).astype(bf16)
        grad_back = swap(grad_slots.reshape(experts, per_dest, width)).reshape(count, width)
        g_sec_out = mm(act_second, grad_result, (0, 0))
        g_sec_in = mm(middle_lo, grad_pre_second, (0, 0))
        g_exp_out = mm(act_first, grad_middle, (0, 0))
        g_exp_in = mm(gathered, grad_pre, (0, 0))
        g_cent = jnp.sum(grad_logit * arrived_f, axis=0, keepdims=True)
        moe_out = mm(dispatch, came_back, (0, 0))
        grad_shared = mm(dispatch, grad_back, (0, 0))

    combined = (residual + moe_out).astype(bf16)

    g_gain_ffn = jnp.sum(grad_shared * unit_f, axis=0)
    grad_residual = grad_output.astype(f32) + norm_back(unit_f, inv_f, ffn_gain, grad_shared)
    grad_attended = grad_residual.astype(bf16)
    g_out_w = mm(mixed, grad_attended, (0, 0))
    grad_mixed = heads(mm(grad_attended, out_w, (1, 1)).astype(bf16))
    grad_probs = jnp.einsum("pqhd,pkhd->phqk", grad_mixed, values_all, preferred_element_type=f32)
    grad_values = jnp.einsum("phqk,pqhd->pkhd", probs_lo, grad_mixed, preferred_element_type=f32)
    inner = jnp.sum(probs * grad_probs, axis=-1, keepdims=True)
    grad_scores = (probs * (grad_probs - inner)).astype(bf16)
    grad_queries = (
        jnp.einsum("phqk,pkhd->pqhd", grad_scores, keys_all, preferred_element_type=f32) * 0.125
    )
    grad_keys = (
        jnp.einsum("phqk,pqhd->pkhd", grad_scores, queries, preferred_element_type=f32) * 0.125
    )
    grad_packed = jnp.concatenate(
        [g.reshape(rows, width) for g in (grad_queries, grad_keys, grad_values)], axis=1
    ).astype(bf16)
    g_qkv = mm(normed, grad_packed, (0, 0))
    grad_normed = mm(grad_packed, qkv_w, (1, 1))
    g_gain_attn = jnp.sum(grad_normed * unit_a, axis=0)
    input_grad = (grad_residual + norm_back(unit_a, inv_a, attn_gain, grad_normed)).astype(bf16)

    def scatter(partial):
        return lax.psum_scatter(
            partial, ("expert", "hidden"), scatter_dimension=0, tiled=True
        )

    g_cat = jnp.concatenate([g_qkv, g_out_w, g_gain_attn[:, None], g_gain_ffn[:, None], jnp.zeros((width, 126), f32)], axis=1)
    g_cat = scatter(g_cat)
    g_cent = lax.psum(g_cent, "hidden")

    def from_dealt(dealt):
        received = lax.all_to_all(
            dealt.reshape(1, seats, SEQ, width), "expert", split_axis=2, concat_axis=0, tiled=True
        ).reshape(group, piece, width)
        return jnp.take(received, deal_row, axis=0).reshape(group * piece, width)

    return (
        from_dealt(combined),
        from_dealt(input_grad).astype(f32),
        g_cat[:, 4 * width],
        g_cat[:, 4 * width + 1],
        g_cat[:, : 3 * width],
        g_cat[:, 3 * width : 4 * width],
        g_cent,
        g_exp_in[None],
        g_exp_out[None],
        g_sec_in[None],
        g_sec_out[None],
    )


def solution(mesh):
    both = ("expert", "hidden")
    fast = mesh.shape["expert"] == 16 and mesh.shape["hidden"] == 2
    return jax.shard_map(
        functools.partial(shards, fast),
        mesh=mesh,
        in_specs=(
            P(both, None),
            P(),
            P(),
            P(both, None),
            P(both, None),
            P(both),
            P(both),
            P(both, None),
            P(both, None),
            P("expert", None),
            P("expert", None, "hidden"),
            P("expert", "hidden", None),
            P("expert", None, "hidden"),
            P("expert", "hidden", None),
            P(both, None),
        ),
        out_specs=(
            P(both, None),
            P(both, None),
            P(both),
            P(both),
            P(both, None),
            P(both, None),
            P("expert", None),
            P("expert", None, "hidden"),
            P("expert", "hidden", None),
            P("expert", None, "hidden"),
            P("expert", "hidden", None),
        ),
        check_vma=False,
    )
```

```python
import functools

import jax
import jax.numpy as jnp
from jax import lax
from jax.experimental import pallas as pl
from jax.experimental.pallas import tpu as pltpu
from jax.sharding import PartitionSpec as P

HEADS = 16
HEAD = 64
MICRO = 4
PER = 2
SEQ = 64
PACK = PER * SEQ

epsilon = 1e-05
bf16 = jnp.bfloat16
f32 = jnp.float32


def mm(a, b, contract=(1, 0)):
    return lax.dot_general(
        a, b, (((contract[0],), (contract[1],)), ((), ())), preferred_element_type=f32
    )


def norm_parts(rows):
    centre = jnp.mean(rows, axis=-1, keepdims=True)
    shifted = rows - centre
    spread = jnp.mean(shifted * shifted, axis=-1, keepdims=True)
    inv = lax.rsqrt(spread + epsilon)
    return shifted * inv, inv


def norm_back(unit, inv, gain, grad):
    g = grad * gain
    m1 = jnp.mean(g, axis=-1, keepdims=True)
    m2 = jnp.mean(g * unit, axis=-1, keepdims=True)
    return inv * (g - m1 - unit * m2)


def gelu_act(pre_act):
    return jax.nn.gelu(pre_act, approximate=True)


def gather_hidden(rows):
    return lax.all_gather(rows, "hidden", axis=0, tiled=True)


def sum_hidden(terms):
    return lax.psum_scatter(terms, "hidden", scatter_dimension=0, tiled=True)


def swap(blocks):
    return lax.all_to_all(blocks, "expert", split_axis=0, concat_axis=0, tiled=True)


MESH = pl.DeviceIdType.MESH
ANY = pl.BlockSpec(memory_space=pl.ANY)
VM = pl.BlockSpec(memory_space=pltpu.VMEM)
DMA = pltpu.SemaphoreType.DMA
VMEM_MAX = 63 << 20
PARTS = 4


def dims(experts, width):
    capacity = (9 * PACK + 8 * experts - 1) // (8 * experts)
    per_dest = MICRO * capacity
    main = per_dest // 16 * 16
    return per_dest, main, per_dest - main


def greet(experts, me, core, partner):
    barrier = pltpu.get_barrier_semaphore()

    def hello(k, carry):
        pl.semaphore_signal(
            barrier, inc=1, device_id=(lax.rem(me + k, experts), core), device_id_type=MESH
        )
        return carry

    lax.fori_loop(1, experts, hello, 0)
    if partner is not None:
        pl.semaphore_signal(barrier, inc=1, device_id=(me, partner), device_id_type=MESH)
    pl.semaphore_wait(barrier, experts - 1 + (partner is not None))


class Spread:
    def __init__(self, experts, me, core, src, dst, sends, recvs, local):
        self.experts, self.me, self.core = experts, me, core
        self.src, self.dst, self.sends, self.recvs, self.local = src, dst, sends, recvs, local
        self.rows = src.shape[0] // experts

    def block(self, ref, index):
        return ref.at[pl.ds(pl.multiple_of(index * self.rows, 16), self.rows)]

    def copy(self, k):
        to = lax.rem(self.me + k, self.experts)
        return pltpu.make_async_remote_copy(
            self.block(self.src, to),
            self.block(self.dst, self.me),
            self.sends.at[k],
            self.recvs.at[k],
            device_id=(to, self.core),
            device_id_type=MESH,
        )

    def own(self):
        return pltpu.make_async_copy(
            self.block(self.src, self.me), self.block(self.dst, self.me), self.local
        )

    def start(self):
        self.own().start()

        def go(k, carry):
            self.copy(k).start()
            return carry

        lax.fori_loop(1, self.experts, go, 0)

    def wait(self):
        self.own().wait()

        def stop(k, carry):
            self.copy(k).wait()
            return carry

        lax.fori_loop(1, self.experts, stop, 0)


def spread_kernel(experts, count, *refs):
    srcs, dsts = refs[:count], refs[count : 2 * count]
    sends, recvs, local = refs[2 * count :]
    me, core = lax.axis_index("expert"), lax.axis_index("hidden")
    greet(experts, me, core, None)
    moves = [
        Spread(experts, me, core, s, d, sends.at[i], recvs.at[i], local.at[i])
        for i, (s, d) in enumerate(zip(srcs, dsts))
    ]
    for move in moves:
        move.start()
    for move in moves:
        move.wait()


def spread(experts, call_id, name, *arrays):
    n = len(arrays)
    return pl.pallas_call(
        functools.partial(spread_kernel, experts, n),
        out_shape=[jax.ShapeDtypeStruct(a.shape, a.dtype) for a in arrays],
        in_specs=[ANY] * n,
        out_specs=[ANY] * n,
        scratch_shapes=[DMA((n, experts)), DMA((n, experts)), DMA((n,))],
        compiler_params=pltpu.CompilerParams(collective_id=call_id, has_side_effects=True),
        name=name,
    )(*arrays)


def tail_matrix(part, experts, tail, turned):
    size = PARTS * tail
    shape = (experts * tail, experts * size) if turned else (experts * size, experts * tail)
    there = lax.broadcasted_iota(jnp.int32, shape, 1 if turned else 0)
    here = lax.broadcasted_iota(jnp.int32, shape, 0 if turned else 1)
    want = here // tail * size + part * tail + here % tail
    return (there == want).astype(f32).astype(bf16)


def gelu_pair(v):
    u = v * v
    t = jnp.tanh(v * (0.7978845608 + 0.7978845608 * 0.044715 * u))
    h = 0.5 * t + 0.5
    slope = h + (h - h * h) * (v * (2 * 0.7978845608 + 6 * 0.7978845608 * 0.044715 * u))
    return v * h, slope


def experts_kernel(experts, tail, *refs):
    (a_in, b_in, ca_in, cb_in, cent, w1_h, w2_h, w3_h, w4_h) = refs[:9]
    (ra_out, rb_out, ga_out, gb_out, gcent, xg_o, mlo_o, grs_o, gm_o, act1_o, act2_o, gp1_o, gp2_o) = refs[9:22]
    (w1, w2, w3, w4, xg, mlo, grs, gm, act1, act2, d1, d2, mid, psend, precv, ca, cb, sa, sb) = refs[22:41]
    (wsem, osem, psems, prsems, xs, xr, asend, arecv, alocal) = refs[41:]
    me, core = lax.axis_index("expert"), lax.axis_index("hidden")
    other = 1 - core
    own, width = xg.shape[0] // 2, xg.shape[1]
    hid = w1.shape[1]
    main = a_in.shape[0]
    block = width // PARTS
    mine, theirs = pl.ds(0, own), pl.ds(own, own)

    loads = []
    for i, (h, v) in enumerate(((w1_h, w1), (w2_h, w2), (w3_h, w3), (w4_h, w4))):
        load = pltpu.make_async_copy(h, v, wsem.at[i])
        load.start()
        loads.append(load)
    greet(experts, me, core, other)

    def move(i, src, dst):
        return Spread(experts, me, core, src, dst, asend.at[i], arecv.at[i], alocal.at[i])

    cot_moves = (move(0, ca_in, ca), move(1, cb_in, cb))
    for m in cot_moves:
        m.start()

    def pair(src, dst, send, recv):
        return pltpu.make_async_remote_copy(
            src, dst, send, recv, device_id=(me, other), device_id_type=MESH
        )

    def mirror(i, ref):
        return pair(ref.at[mine], ref.at[theirs], xs.at[i], xr.at[i])

    def partial_send(i):
        return pair(psend, precv.at[i % 2], psems.at[i], prsems.at[i])

    def from_tail(ref, to, start):
        for q in range(PARTS):
            to[pl.ds(start, experts * tail), q * block : (q + 1) * block] = mm(
                tail_matrix(q, experts, tail, True), ref[...]
            ).astype(bf16)

    def to_tail(value, ref):
        total = None
        for q in range(PARTS):
            term = mm(tail_matrix(q, experts, tail, False), value[:, q * block : (q + 1) * block])
            total = term if total is None else total + term
        ref[...] = total.astype(bf16)

    outs = []

    def store(i, ref, out):
        copy = pltpu.make_async_copy(ref, out, osem.at[i])
        copy.start()
        outs.append(copy)

    TN = 256

    def over(size, body):
        def step(n, carry):
            body(pl.ds(pl.multiple_of(n * TN, TN), TN))
            return carry

        lax.fori_loop(0, size // TN, step, 0)

    def up(x, w, act, slope, rows):
        def body(cols):
            a, d = gelu_pair(mm(x[rows, :], w[:, cols]))
            act[rows, cols] = a.astype(bf16)
            slope[rows, cols] = d.astype(bf16)

        over(hid, body)

    def down(act, w, rows, put):
        over(width, lambda cols: put(cols, mm(act[rows, :], w[:, cols])))

    def up_back(g, w, slope, rows):
        def body(cols):
            t = mm(g[rows, :], w[cols, :], (1, 1)) * slope[rows, cols].astype(f32)
            slope[rows, cols] = t.astype(bf16)

        over(hid, body)

    def down_back(gp, w, rows, put):
        over(width, lambda cols: put(cols, mm(gp[rows, :], w[cols, :], (1, 1))))

    def to_send(cols, value):
        psend[:, cols] = value.astype(bf16)

    def to_mid(cols, value):
        mid[:, cols] = value

    def add_mid(cols, value):
        mid[:, cols] += value

    xg[pl.ds(0, main), :] = a_in[...]
    from_tail(b_in, xg, main)
    share_x = mirror(0, xg)
    share_x.start()
    slot = xg[mine, :].astype(f32)
    gate = jax.nn.sigmoid(jnp.sum(slot * cent[...], axis=1, keepdims=True))
    loads[0].wait()
    up(xg, w1, act1, d1, mine)
    share_x.wait()
    store(0, xg, xg_o)
    up(xg, w1, act1, d1, theirs)
    store(1, act1, act1_o)
    loads[1].wait()
    down(act1, w2, theirs, to_send)
    send0 = partial_send(0)
    send0.start()
    down(act1, w2, mine, to_mid)
    send0.wait()
    mid[...] = mid[...] + xg[mine, :].astype(f32) + precv[0].astype(f32)
    mlo[mine, :] = mid[...].astype(bf16)
    share_m = mirror(1, mlo)
    share_m.start()
    loads[2].wait()
    up(mlo, w3, act2, d2, mine)
    share_m.wait()
    store(2, mlo, mlo_o)
    up(mlo, w3, act2, d2, theirs)
    store(3, act2, act2_o)
    loads[3].wait()
    down(act2, w4, theirs, to_send)
    send1 = partial_send(1)
    send1.start()
    down(act2, w4, mine, add_mid)
    send1.wait()
    mid[...] = mid[...] + precv[1].astype(f32)
    returned = (gate * mid[...]).astype(bf16)
    sa[...] = returned[:main]
    to_tail(returned[main:], sb)
    ret_moves = (move(2, sa, ra_out), move(3, sb, rb_out))
    for m in ret_moves:
        m.start()
    for m in cot_moves:
        m.wait()
    grs[pl.ds(0, main), :] = ca[...]
    from_tail(cb, grs, main)
    cot = grs[mine, :].astype(f32)
    logit = jnp.sum(cot * mid[...], axis=1, keepdims=True) * gate * (1.0 - gate)
    grs[mine, :] = (gate * cot).astype(bf16)
    share_g = mirror(2, grs)
    share_g.start()
    up_back(grs, w4, d2, mine)
    share_g.wait()
    store(4, grs, grs_o)
    up_back(grs, w4, d2, theirs)
    store(5, d2, gp2_o)
    down_back(d2, w3, theirs, to_send)
    send2 = partial_send(2)
    send2.start()
    down_back(d2, w3, mine, to_mid)
    send2.wait()
    gm[mine, :] = (mid[...] + grs[mine, :].astype(f32) + precv[0].astype(f32)).astype(bf16)
    share_gm = mirror(3, gm)
    share_gm.start()
    up_back(gm, w2, d1, mine)
    share_gm.wait()
    store(6, gm, gm_o)
    up_back(gm, w2, d1, theirs)
    store(7, d1, gp1_o)
    down_back(d1, w1, theirs, to_send)
    send3 = partial_send(3)
    send3.start()
    down_back(d1, w1, mine, to_mid)
    gcent[...] = jnp.sum(logit * xg[mine, :].astype(f32), axis=0, keepdims=True)
    for m in ret_moves:
        m.wait()
    send3.wait()
    slots = (
        mid[...] + gm[mine, :].astype(f32) + precv[1].astype(f32) + logit * cent[...]
    ).astype(bf16)
    sa[...] = slots[:main]
    to_tail(slots[main:], sb)
    back_moves = (move(4, sa, ga_out), move(5, sb, gb_out))
    for m in back_moves:
        m.start()
    for copy in outs:
        copy.wait()
    for m in back_moves:
        m.wait()


def run_experts(experts, slots, tails, cots, cot_tails, centroid, weights):
    width, hid = weights[0].shape
    main = slots.shape[0]
    tail = tails.shape[0] // experts // PARTS
    own = main + experts * tail
    both = 2 * own

    def sds(*shape, dtype=bf16):
        return jax.ShapeDtypeStruct(shape, dtype)

    travel = [sds(*slots.shape), sds(*tails.shape)] * 2
    wide = [sds(both, width)] * 4 + [sds(both, hid)] * 4
    return pl.pallas_call(
        functools.partial(experts_kernel, experts, tail),
        out_shape=travel + [sds(1, width, dtype=f32)] + wide,
        in_specs=[VM, VM, ANY, ANY, VM, ANY, ANY, ANY, ANY],
        out_specs=[ANY] * 4 + [VM] + [ANY] * 8,
        scratch_shapes=[
            pltpu.VMEM((width, hid), bf16),
            pltpu.VMEM((hid, width), bf16),
            pltpu.VMEM((width, hid), bf16),
            pltpu.VMEM((hid, width), bf16),
            pltpu.VMEM((both, width), bf16),
            pltpu.VMEM((both, width), bf16),
            pltpu.VMEM((both, width), bf16),
            pltpu.VMEM((both, width), bf16),
            pltpu.VMEM((both, hid), bf16),
            pltpu.VMEM((both, hid), bf16),
            pltpu.VMEM((both, hid), bf16),
            pltpu.VMEM((both, hid), bf16),
            pltpu.VMEM((own, width), f32),
            pltpu.VMEM((own, width), bf16),
            pltpu.VMEM((2, own, width), bf16),
            pltpu.VMEM(slots.shape, bf16),
            pltpu.VMEM(tails.shape, bf16),
            pltpu.VMEM(slots.shape, bf16),
            pltpu.VMEM(tails.shape, bf16),
            DMA((4,)),
            DMA((8,)),
            DMA((4,)),
            DMA((4,)),
            DMA((4,)),
            DMA((4,)),
            DMA((6, experts)),
            DMA((6, experts)),
            DMA((6,)),
        ],
        compiler_params=pltpu.CompilerParams(
            collective_id=2, has_side_effects=True, vmem_limit_bytes=VMEM_MAX
        ),
        name="experts_pass",
    )(slots, tails, cots, cot_tails, centroid, *weights)

def back_kernel(experts, tail, *refs):
    (ra, rb, ga, gb, dm, dt, gains, cot_h, res_h, tok_h, packed_h, probs_h, mixed_h, wqkv_h, wout_h) = refs[:15]
    out_o, ig_o, grads_o, ggain_o = refs[15:19]
    (cot, res, tok, packed, probs, mixed, wqkv, wout, normed, gatt, gmix, gpk, so, si) = refs[19:33]
    keeps, psends, precvs, rv1s, rv2s, rv3s = (refs[33 + 5 * i : 38 + 5 * i] for i in range(6))
    lsem, sends, recvs, asend, arecv, alocal = refs[63:]
    me, core = lax.axis_index("expert"), lax.axis_index("hidden")
    other = 1 - core
    my_z, my_y, my_x = me // 4, lax.rem(me // 2, 2), lax.rem(me, 2)
    rows, width = tok.shape
    block = width // PARTS

    loads = {}
    for i, (name, h, v) in enumerate(
        (
            ("res", res_h, res),
            ("cot", cot_h, cot),
            ("mixed", mixed_h, mixed),
            ("wout", wout_h, wout),
            ("probs", probs_h, probs),
            ("packed", packed_h, packed),
            ("tok", tok_h, tok),
            ("wqkv", wqkv_h, wqkv),
        )
    ):
        loads[name] = pltpu.make_async_copy(h, v, lsem.at[i])
        loads[name].start()
    greet(experts, me, core, other)

    def join_slots(slots, tails):
        parts = []
        for q in range(PARTS):
            parts.append(
                mm(dm[...], slots[:, q * block : (q + 1) * block], (0, 0))
                + mm(dt[q], tails[...], (0, 0))
            )
        return jnp.concatenate(parts, axis=1)

    piece = SEQ // experts
    seats = MICRO * PER

    def to_blocks(value):
        shape = (rows, rows)
        to = lax.broadcasted_iota(jnp.int32, shape, 0)
        at = lax.broadcasted_iota(jnp.int32, shape, 1)
        b, s, q = to // (seats * piece), to // piece % seats, to % piece
        turn = (at == s * SEQ + b * piece + q).astype(f32).astype(bf16)
        return mm(turn, value).astype(bf16)

    def move(i, src, dst):
        return Spread(experts, me, core, src, dst, asend.at[i], arecv.at[i], alocal.at[i])

    my_a = jnp.where(core == 0, my_x, my_y)
    my_b = jnp.where(core == 0, my_y, my_x)

    def near(a_step, b_step):
        a, b = (1 - my_a if a_step else my_a), (1 - my_b if b_step else my_b)
        x, y = jnp.where(core == 0, a, b), jnp.where(core == 0, b, a)
        return my_z * 4 + y * 2 + x

    def remote(c, stage, src, dst, to, to_core):
        return pltpu.make_async_remote_copy(
            src, dst, sends.at[c, stage], recvs.at[c, stage],
            device_id=(to, to_core), device_id_type=MESH,
        )

    def pair_copy(c):
        return remote(c, 0, psends[c], precvs[c], me, other)

    def a_copy(c):
        return remote(c, 1, psends[c].at[pl.ds(0, 256)], rv1s[c], near(True, False), core)

    def b_copy(c):
        return remote(c, 2, psends[c].at[pl.ds(256, 128)], rv2s[c], near(False, True), core)

    def z_copy(c, dz):
        to_z = lax.rem(my_z + dz, 4)
        src = psends[c].at[pl.ds(pl.multiple_of(384 + to_z * 32, 32), 32)]
        return remote(c, 2 + dz, src, rv3s[c].at[dz - 1], to_z * 4 + my_y * 2 + my_x, core)

    def place(c, t, cols):
        for j in range(8):
            z, y = j // 2, j % 2
            for x in range(2):
                at = 128 * j + 64 * x
                even, odd = t[at : at + 32], t[at + 32 : at + 64]
                first, second = x * 8 + y * 4 + z, y * 8 + x * 4 + z
                mine = jnp.where(core == 0, first, second)
                theirs = jnp.where(core == 0, second, first)
                keeps[c][pl.ds(pl.multiple_of(mine * 32, 32), 32), cols] = jnp.where(
                    core == 0, even, odd
                )
                psends[c][pl.ds(pl.multiple_of(theirs * 32, 32), 32), cols] = jnp.where(
                    core == 0, odd, even
                ).astype(bf16)

    def compute(c, left, right, start):
        def body(n, carry):
            cols = pl.ds(pl.multiple_of(n * 512, 512), 512)
            from_cols = pl.ds(pl.multiple_of(start + n * 512, 512), 512)
            place(c, mm(left[...], right[:, from_cols], (0, 0)), cols)
            return carry

        lax.fori_loop(0, width // 512, body, 0)
        pair_copy(c).start()

    half_a = pl.ds(pl.multiple_of(my_a * 256, 256), 256)
    half_a_out = pl.ds(pl.multiple_of((1 - my_a) * 256, 256), 256)
    base_b = my_a * 256
    half_b = pl.ds(pl.multiple_of(base_b + my_b * 128, 128), 128)
    half_b_out = pl.ds(pl.multiple_of(base_b + (1 - my_b) * 128, 128), 128)

    def after_pair(c):
        pair_copy(c).wait()
        keep = keeps[c]
        keep[...] += precvs[c][...].astype(f32)
        psends[c][pl.ds(0, 256), :] = keep[half_a_out, :].astype(bf16)
        a_copy(c).start()

    def after_a(c):
        a_copy(c).wait()
        keep = keeps[c]
        keep[half_a, :] += rv1s[c][...].astype(f32)
        psends[c][pl.ds(256, 128), :] = keep[half_b_out, :].astype(bf16)
        b_copy(c).start()

    def after_b(c):
        b_copy(c).wait()
        keep = keeps[c]
        keep[half_b, :] += rv2s[c][...].astype(f32)
        psends[c][pl.ds(384, 128), :] = keep[half_b, :].astype(bf16)
        for dz in range(1, 4):
            z_copy(c, dz).start()

    def after_z(c, out, cols):
        for dz in range(1, 4):
            z_copy(c, dz).wait()
        at = pl.ds(pl.multiple_of(base_b + my_b * 128 + my_z * 32, 32), 32)
        total = keeps[c][at, :]
        for dz in range(3):
            total = total + rv3s[c][dz].astype(f32)
        out[:, cols] = total

    gain_a, gain_f = gains[0:1, :], gains[1:2, :]
    ones = jnp.ones((rows, 64), bf16)

    def column_sums(value):
        high = value.astype(bf16)
        low = (value - high.astype(f32)).astype(bf16)
        return mm(high, ones, (0, 0)) + mm(low, ones, (0, 0))

    loads["res"].wait()
    so[...] = to_blocks((res[...] + join_slots(ra, rb)).astype(bf16))
    out_move = move(0, so, out_o)
    out_move.start()
    unit, inv = norm_parts(res[...])
    grad_shared = join_slots(ga, gb)
    ffn_sums = column_sums(grad_shared * unit)
    loads["cot"].wait()
    grad = cot[...].astype(f32) + norm_back(unit, inv, gain_f, grad_shared)
    res[...] = grad
    gatt[...] = grad.astype(bf16)
    loads["mixed"].wait()
    compute(0, mixed, gatt, 0)
    loads["wout"].wait()
    gmix[...] = mm(gatt[...], wout[...], (1, 1)).astype(bf16)
    after_pair(0)
    loads["probs"].wait()
    loads["packed"].wait()
    lane = lax.broadcasted_iota(jnp.int32, (PACK, 2 * HEAD), 1)
    first = lane < HEAD

    def stacked(v):
        zero = jnp.zeros_like(v)
        return jnp.concatenate([jnp.where(first, v, zero), jnp.where(first, zero, v)], axis=0)

    def pack(p, carry):
        at = pl.ds(pl.multiple_of(p * PACK, PACK), PACK)
        for h in range(HEADS // 2):
            lo = h * 2 * HEAD
            q = packed[at, lo : lo + 2 * HEAD]
            k = packed[at, width + lo : width + lo + 2 * HEAD]
            v = packed[at, 2 * width + lo : 2 * width + lo + 2 * HEAD]
            gs = stacked(gmix[at, lo : lo + 2 * HEAD])
            pr_lo = probs[p * (HEADS // 2) + h]
            pr = pr_lo.astype(f32)
            gp = mm(gs, v, (1, 1))
            gv = mm(pr_lo, gs, (0, 0))
            inner = jnp.sum(pr * gp, axis=1, keepdims=True)
            ds_ = (pr * (gp - inner)).astype(bf16)
            t = mm(ds_, k)
            gq = jnp.where(first, t[:PACK], t[PACK:]) * 0.125
            gk = mm(ds_, stacked(q), (0, 0)) * 0.125
            gpk[at, lo : lo + 2 * HEAD] = gq.astype(bf16)
            gpk[at, width + lo : width + lo + 2 * HEAD] = gk.astype(bf16)
            gpk[at, 2 * width + lo : 2 * width + lo + 2 * HEAD] = gv.astype(bf16)
        return carry

    lax.fori_loop(0, MICRO, pack, 0)
    after_a(0)
    loads["tok"].wait()
    unit, inv = norm_parts(tok[...].astype(f32))
    normed[...] = (unit * gain_a).astype(bf16)
    compute(1, normed, gpk, 0)
    after_b(0)
    compute(2, normed, gpk, width)
    after_pair(1)
    compute(3, normed, gpk, 2 * width)
    after_pair(2)
    loads["wqkv"].wait()

    grad_normed = mm(gpk[...], wqkv[...], (1, 1))
    unit, inv = norm_parts(tok[...].astype(f32))
    sums = column_sums(grad_normed * unit)
    si[...] = to_blocks((res[...] + norm_back(unit, inv, gain_a, grad_normed)).astype(bf16))
    ig_move = move(1, si, ig_o)
    after_pair(3)
    ig_move.start()
    place(4, jnp.concatenate([sums, ffn_sums], axis=1), pl.ds(0, 128))
    pair_copy(4).start()
    after_z(0, grads_o, pl.ds(3 * width, width))
    after_pair(4)
    for c in (1, 2, 3, 4):
        after_a(c)
    for c in (1, 2, 3, 4):
        after_b(c)
    for c in (1, 2, 3):
        after_z(c, grads_o, pl.ds((c - 1) * width, width))
    after_z(4, ggain_o, pl.ds(0, 128))
    out_move.wait()
    ig_move.wait()


def run_back(experts, tail, slots, tails, grads, grad_tails, d_main, d_tail, gains, cot, residual, tok, packed, probs, mixed, wqkv, wout):
    rows, width = tok.shape

    def sds(*shape, dtype=bf16):
        return jax.ShapeDtypeStruct(shape, dtype)

    widths = (width,) * 4 + (128,)
    scratch = [
        pltpu.VMEM(cot.shape, bf16),
        pltpu.VMEM(residual.shape, f32),
        pltpu.VMEM(tok.shape, bf16),
        pltpu.VMEM(packed.shape, bf16),
        pltpu.VMEM(probs.shape, bf16),
        pltpu.VMEM(mixed.shape, bf16),
        pltpu.VMEM(wqkv.shape, bf16),
        pltpu.VMEM(wout.shape, bf16),
        pltpu.VMEM((rows, width), bf16),
        pltpu.VMEM((rows, width), bf16),
        pltpu.VMEM((rows, width), bf16),
        pltpu.VMEM((rows, 3 * width), bf16),
        pltpu.VMEM((rows, width), bf16),
        pltpu.VMEM((rows, width), bf16),
    ]
    scratch += [pltpu.VMEM((width // 2, w), f32) for w in widths]
    for part in (2, 2, 4, 8):
        scratch += [pltpu.VMEM((width // part, w), bf16) for w in widths]
    scratch += [pltpu.VMEM((3, 32, w), bf16) for w in widths]
    scratch += [
        DMA((8,)),
        DMA((5, 6)),
        DMA((5, 6)),
        DMA((2, experts)),
        DMA((2, experts)),
        DMA((2,)),
    ]
    return pl.pallas_call(
        functools.partial(back_kernel, experts, tail),
        out_shape=[sds(rows, width), sds(rows, width), sds(32, 4 * width, dtype=f32), sds(32, 128, dtype=f32)],
        in_specs=[VM] * 7 + [ANY] * 8,
        out_specs=[ANY, ANY, VM, VM],
        scratch_shapes=scratch,
        compiler_params=pltpu.CompilerParams(
            collective_id=3, has_side_effects=True, vmem_limit_bytes=VMEM_MAX
        ),
        name="attention_back",
    )(slots, tails, grads, grad_tails, d_main, d_tail, gains, cot, residual, tok, packed, probs, mixed, wqkv, wout)


def shards(
    fast,
    tokens,
    lengths,
    deal,
    routes,
    slot_order,
    gain_attn,
    gain_ffn,
    w_qkv,
    w_out,
    centroids,
    expert_in,
    expert_out,
    second_in,
    second_out,
    cotangent,
):
    width = tokens.shape[1]
    experts = lax.axis_size("expert")
    piece = SEQ // experts
    seats = MICRO * PER
    group = experts * seats
    rows = seats * SEQ
    capacity = (9 * PACK + 8 * experts - 1) // (8 * experts)
    per_dest = MICRO * capacity
    my_expert = lax.axis_index("expert")
    my_hidden = lax.axis_index("hidden")

    deal_row = lax.dynamic_index_in_dim(deal, my_hidden, 0, keepdims=False)
    length_row = lax.dynamic_index_in_dim(lengths, my_hidden, 0, keepdims=False)
    ids = jnp.arange(group, dtype=jnp.int32)
    inverse = jnp.sum(jnp.where(deal_row[None, :] == ids[:, None], ids[None, :], 0), axis=1)
    own = my_expert * seats + jnp.arange(seats, dtype=jnp.int32)
    own_lengths = jnp.sum(
        jnp.where(deal_row[None, :] == own[:, None], length_row[None, :], 0), axis=1
    )

    def to_dealt(flat):
        pieces = jnp.take(flat.reshape(group, piece, flat.shape[1]), inverse, axis=0)
        return lax.all_to_all(
            pieces.reshape(experts, seats, piece, flat.shape[1]),
            "expert",
            split_axis=0,
            concat_axis=2,
            tiled=True,
        ).reshape(rows, flat.shape[1])

    labels = jnp.concatenate([routes, slot_order], axis=1)
    lab = to_dealt(labels)
    tok = to_dealt(tokens)
    grad_output = to_dealt(cotangent)

    cat = jnp.concatenate(
        [w_qkv, w_out, gain_attn[:, None], gain_ffn[:, None], jnp.zeros((w_qkv.shape[0], 126), bf16)],
        axis=1,
    )
    cat = lax.all_gather(cat, ("expert", "hidden"), axis=0, tiled=True)
    qkv_w = cat[:, : 3 * width]
    out_w = cat[:, 3 * width : 4 * width]
    attn_gain = cat[:, 4 * width].astype(f32)[None, :]
    ffn_gain = cat[:, 4 * width + 1].astype(f32)[None, :]

    route = lab[:, 0].reshape(MICRO, PACK)
    order = lab[:, 1].reshape(MICRO, PACK)
    positions = jnp.arange(PACK, dtype=jnp.int32)
    seat = positions // SEQ
    pack_lengths = own_lengths.reshape(MICRO, PER)
    limit = jnp.repeat(pack_lengths, SEQ, axis=1)
    present = (positions % SEQ)[None, :] < limit
    priority = order * PER + seat[None, :]
    ahead = jnp.sum(
        (
            (route[:, :, None] == route[:, None, :])
            & (priority[:, None, :] < priority[:, :, None])
            & present[:, None, :]
        ).astype(jnp.int32),
        axis=2,
    )
    accepted = (present & (ahead < capacity)).reshape(rows)
    target = (
        route * per_dest + jnp.arange(MICRO, dtype=jnp.int32)[:, None] * capacity + ahead
    ).reshape(rows)
    target = jnp.where(accepted, target, -1)
    slot_ids = jnp.arange(experts * per_dest, dtype=jnp.int32)
    dispatch = (slot_ids[:, None] == target[None, :]).astype(bf16)

    per_dest, main, tail = dims(experts, width)
    block = width // PARTS
    if fast:
        base = jnp.arange(MICRO, dtype=jnp.int32)[:, None] * capacity + ahead
        base = base.reshape(rows)
        route_flat = route.reshape(rows)
        head = jnp.where(accepted & (base < main), route_flat * main + base, -1)
        d_main = (jnp.arange(experts * main, dtype=jnp.int32)[:, None] == head[None, :]).astype(bf16)
        d_tail = []
        for q in range(PARTS):
            where = jnp.where(
                accepted & (base >= main), (route_flat * PARTS + q) * tail + base - main, -1
            )
            d_tail.append(
                (jnp.arange(experts * PARTS * tail, dtype=jnp.int32)[:, None] == where[None, :]).astype(bf16)
            )

    def split(values):
        total = sum(
            mm(d_tail[q], values[:, q * block : (q + 1) * block]) for q in range(PARTS)
        )
        return mm(d_main, values).astype(bf16), total.astype(bf16)

    def to_experts(values):
        out = mm(dispatch, values).astype(bf16)
        return swap(out.reshape(experts, per_dest, width)).reshape(experts * per_dest, width)

    inputs = tok.astype(f32)
    unit_a, inv_a = norm_parts(inputs)
    normed = (unit_a * attn_gain).astype(bf16)
    packed = mm(normed, qkv_w).astype(bf16)
    allowed = (
        (seat[:, None] == seat[None, :]) & (positions[None, :] <= positions[:, None])
    )[None] & present[:, None, :]

    def heads(block):
        return block.reshape(MICRO, PACK, HEADS, HEAD)

    queries = heads(packed[:, :width])
    keys_all = heads(packed[:, width : 2 * width])
    values_all = heads(packed[:, 2 * width :])
    scores = jnp.einsum("pqhd,pkhd->phqk", queries, keys_all, preferred_element_type=f32) * 0.125
    masked = jnp.where(allowed[:, None], scores, -1e30)
    peaks = jnp.max(masked, axis=-1, keepdims=True)
    log_total = peaks + jnp.log(jnp.sum(jnp.exp(masked - peaks), axis=-1, keepdims=True))
    probs = jnp.exp(masked - log_total)
    probs_lo = probs.astype(bf16)
    mixed = (
        jnp.einsum("phqk,pkhd->pqhd", probs_lo, values_all, preferred_element_type=f32)
        .reshape(rows, width)
        .astype(bf16)
    )
    residual = inputs + mm(mixed, out_w)
    unit_f, inv_f = norm_parts(residual)
    shared = (unit_f * ffn_gain).astype(bf16)
    centroid_row = centroids[0]
    w_in, w_back = expert_in[0], expert_out[0]
    s_in, s_back = second_in[0], second_out[0]
    if fast:
        slots, tails = spread(experts, 1, "slots_out", *split(shared))
        cots, cot_tails = split(grad_output)
        (ra, rb, ga, gb, g_cent, gathered, middle_lo, grad_result, grad_middle,
         act_first, act_second, grad_pre, grad_pre_second) = run_experts(
            experts, slots, tails, cots, cot_tails, centroids.astype(f32), (w_in, w_back, s_in, s_back)
        )
        g_sec_out = mm(act_second, grad_result, (0, 0))
        g_sec_in = mm(middle_lo, grad_pre_second, (0, 0))
        g_exp_out = mm(act_first, grad_middle, (0, 0))
        g_exp_in = mm(gathered, grad_pre, (0, 0))
    else:
        cot_arrived = to_experts(grad_output)
        arrived = to_experts(shared)

        count = arrived.shape[0]
        arrived_f = arrived.astype(f32)
        gate_vals = jax.nn.sigmoid(
            jnp.sum(arrived_f * centroid_row.astype(f32)[None, :], axis=1, keepdims=True)
        )
        grad_result_own = (gate_vals * cot_arrived.astype(f32)).astype(bf16)
        gathered = gather_hidden(arrived)
        grad_result = gather_hidden(grad_result_own)
        pre_first = mm(gathered, w_in)
        act_first, pull_first = jax.vjp(gelu_act, pre_first)
        act_first = act_first.astype(bf16)
        middle = arrived_f + sum_hidden(mm(act_first, w_back).astype(bf16)).astype(f32)
        middle_lo = gather_hidden(middle.astype(bf16))
        pre_second = mm(middle_lo, s_in)
        act_second, pull_second = jax.vjp(gelu_act, pre_second)
        act_second = act_second.astype(bf16)
        expert_sum = middle + sum_hidden(mm(act_second, s_back).astype(bf16)).astype(f32)
        returned = (gate_vals * expert_sum).astype(bf16)
        came_back = swap(returned.reshape(experts, per_dest, width)).reshape(count, width)

        grad_logit = (
            jnp.sum(cot_arrived.astype(f32) * expert_sum, axis=1, keepdims=True)
            * gate_vals
            * (1.0 - gate_vals)
        )
        grad_pre_second = pull_second(mm(grad_result, s_back, (1, 1)))[0].astype(bf16)
        grad_middle_own = (
            grad_result_own.astype(f32)
            + sum_hidden(mm(grad_pre_second, s_in, (1, 1)).astype(bf16)).astype(f32)
        ).astype(bf16)
        grad_middle = gather_hidden(grad_middle_own)
        grad_pre = pull_first(mm(grad_middle, w_back, (1, 1)))[0].astype(bf16)
        grad_slots = (
            sum_hidden(mm(grad_pre, w_in, (1, 1)).astype(bf16)).astype(f32)
            + grad_middle_own.astype(f32)
            + grad_logit * centroid_row.astype(f32)[None, :]
        ).astype(bf16)
        grad_back = swap(grad_slots.reshape(experts, per_dest, width)).reshape(count, width)
        g_sec_out = mm(act_second, grad_result, (0, 0))
        g_sec_in = mm(middle_lo, grad_pre_second, (0, 0))
        g_exp_out = mm(act_first, grad_middle, (0, 0))
        g_exp_in = mm(gathered, grad_pre, (0, 0))
        g_cent = jnp.sum(grad_logit * arrived_f, axis=0, keepdims=True)
        moe_out = mm(dispatch, came_back, (0, 0))
        grad_shared = mm(dispatch, grad_back, (0, 0))

    if fast:
        probs_pairs = probs_lo.reshape(MICRO * HEADS // 2, 2 * PACK, PACK)
        out_r, ig_r, g_cat, g_gain = run_back(
            experts, tail, ra, rb, ga, gb, d_main, jnp.stack(d_tail),
            jnp.concatenate([attn_gain, ffn_gain], axis=0), grad_output, residual, tok,
            packed, probs_pairs, mixed, qkv_w, out_w,
        )
        flat = jnp.arange(rows, dtype=jnp.int32)
        goal = jnp.repeat(deal_row, piece) * piece + flat % piece
        undeal = (goal[:, None] == flat[None, :]).astype(bf16)
        return (
            mm(undeal, out_r).astype(bf16),
            mm(undeal, ig_r),
            g_gain[:, 0],
            g_gain[:, 64],
            g_cat[:, : 3 * width],
            g_cat[:, 3 * width :],
            lax.psum(g_cent, "hidden"),
            g_exp_in[None],
            g_exp_out[None],
            g_sec_in[None],
            g_sec_out[None],
        )

    combined = (residual + moe_out).astype(bf16)

    g_gain_ffn = jnp.sum(grad_shared * unit_f, axis=0)
    grad_residual = grad_output.astype(f32) + norm_back(unit_f, inv_f, ffn_gain, grad_shared)
    grad_attended = grad_residual.astype(bf16)
    g_out_w = mm(mixed, grad_attended, (0, 0))
    grad_mixed = heads(mm(grad_attended, out_w, (1, 1)).astype(bf16))
    grad_probs = jnp.einsum("pqhd,pkhd->phqk", grad_mixed, values_all, preferred_element_type=f32)
    grad_values = jnp.einsum("phqk,pqhd->pkhd", probs_lo, grad_mixed, preferred_element_type=f32)
    inner = jnp.sum(probs * grad_probs, axis=-1, keepdims=True)
    grad_scores = (probs * (grad_probs - inner)).astype(bf16)
    grad_queries = (
        jnp.einsum("phqk,pkhd->pqhd", grad_scores, keys_all, preferred_element_type=f32) * 0.125
    )
    grad_keys = (
        jnp.einsum("phqk,pqhd->pkhd", grad_scores, queries, preferred_element_type=f32) * 0.125
    )
    grad_packed = jnp.concatenate(
        [g.reshape(rows, width) for g in (grad_queries, grad_keys, grad_values)], axis=1
    ).astype(bf16)
    g_qkv = mm(normed, grad_packed, (0, 0))
    grad_normed = mm(grad_packed, qkv_w, (1, 1))
    g_gain_attn = jnp.sum(grad_normed * unit_a, axis=0)
    input_grad = (grad_residual + norm_back(unit_a, inv_a, attn_gain, grad_normed)).astype(bf16)

    def scatter(partial):
        return lax.psum_scatter(
            partial, ("expert", "hidden"), scatter_dimension=0, tiled=True
        )

    g_cat = jnp.concatenate([g_qkv, g_out_w, g_gain_attn[:, None], g_gain_ffn[:, None], jnp.zeros((width, 126), f32)], axis=1)
    g_cat = scatter(g_cat)
    g_cent = lax.psum(g_cent, "hidden")

    def from_dealt(dealt):
        received = lax.all_to_all(
            dealt.reshape(1, seats, SEQ, width), "expert", split_axis=2, concat_axis=0, tiled=True
        ).reshape(group, piece, width)
        return jnp.take(received, deal_row, axis=0).reshape(group * piece, width)

    return (
        from_dealt(combined),
        from_dealt(input_grad).astype(f32),
        g_cat[:, 4 * width],
        g_cat[:, 4 * width + 1],
        g_cat[:, : 3 * width],
        g_cat[:, 3 * width : 4 * width],
        g_cent,
        g_exp_in[None],
        g_exp_out[None],
        g_sec_in[None],
        g_sec_out[None],
    )


def solution(mesh):
    both = ("expert", "hidden")
    fast = mesh.shape["expert"] == 16 and mesh.shape["hidden"] == 2
    return jax.shard_map(
        functools.partial(shards, fast),
        mesh=mesh,
        in_specs=(
            P(both, None),
            P(),
            P(),
            P(both, None),
            P(both, None),
            P(both),
            P(both),
            P(both, None),
            P(both, None),
            P("expert", None),
            P("expert", None, "hidden"),
            P("expert", "hidden", None),
            P("expert", None, "hidden"),
            P("expert", "hidden", None),
            P(both, None),
        ),
        out_specs=(
            P(both, None),
            P(both, None),
            P(both),
            P(both),
            P(both, None),
            P(both, None),
            P("expert", None),
            P("expert", None, "hidden"),
            P("expert", "hidden", None),
            P("expert", None, "hidden"),
            P("expert", "hidden", None),
        ),
        check_vma=False,
    )
```

```python
import functools

import jax
import jax.numpy as jnp
from jax import lax
from jax.experimental import pallas as pl
from jax.experimental.pallas import tpu as pltpu
from jax.sharding import PartitionSpec as P

HEADS = 16
HEAD = 64
MICRO = 4
PER = 2
SEQ = 64
PACK = PER * SEQ

epsilon = 1e-05
bf16 = jnp.bfloat16
f32 = jnp.float32


def mm(a, b, contract=(1, 0)):
    return lax.dot_general(
        a, b, (((contract[0],), (contract[1],)), ((), ())), preferred_element_type=f32
    )


def norm_parts(rows):
    centre = jnp.mean(rows, axis=-1, keepdims=True)
    shifted = rows - centre
    spread = jnp.mean(shifted * shifted, axis=-1, keepdims=True)
    inv = lax.rsqrt(spread + epsilon)
    return shifted * inv, inv


def norm_back(unit, inv, gain, grad):
    g = grad * gain
    m1 = jnp.mean(g, axis=-1, keepdims=True)
    m2 = jnp.mean(g * unit, axis=-1, keepdims=True)
    return inv * (g - m1 - unit * m2)


def gelu_act(pre_act):
    return jax.nn.gelu(pre_act, approximate=True)


MESH = pl.DeviceIdType.MESH
ANY = pl.BlockSpec(memory_space=pl.ANY)
VM = pl.BlockSpec(memory_space=pltpu.VMEM)
DMA = pltpu.SemaphoreType.DMA
VMEM_MAX = 63 << 20
PARTS = 4


def dims(experts, width):
    capacity = (9 * PACK + 8 * experts - 1) // (8 * experts)
    per_dest = MICRO * capacity
    main = per_dest // 16 * 16
    return per_dest, main, per_dest - main


def greet(experts, me, core, partner):
    barrier = pltpu.get_barrier_semaphore()

    def hello(k, carry):
        pl.semaphore_signal(
            barrier, inc=1, device_id=(lax.rem(me + k, experts), core), device_id_type=MESH
        )
        return carry

    lax.fori_loop(1, experts, hello, 0)
    if partner is not None:
        pl.semaphore_signal(barrier, inc=1, device_id=(me, partner), device_id_type=MESH)
    pl.semaphore_wait(barrier, experts - 1 + (partner is not None))


class Spread:
    def __init__(self, experts, me, core, src, dst, sends, recvs, local):
        self.experts, self.me, self.core = experts, me, core
        self.src, self.dst, self.sends, self.recvs, self.local = src, dst, sends, recvs, local
        self.rows = src.shape[0] // experts

    def block(self, ref, index):
        return ref.at[pl.ds(pl.multiple_of(index * self.rows, 16), self.rows)]

    def copy(self, k):
        to = lax.rem(self.me + k, self.experts)
        return pltpu.make_async_remote_copy(
            self.block(self.src, to),
            self.block(self.dst, self.me),
            self.sends.at[k],
            self.recvs.at[k],
            device_id=(to, self.core),
            device_id_type=MESH,
        )

    def own(self):
        return pltpu.make_async_copy(
            self.block(self.src, self.me), self.block(self.dst, self.me), self.local
        )

    def start(self):
        self.own().start()

        def go(k, carry):
            self.copy(k).start()
            return carry

        lax.fori_loop(1, self.experts, go, 0)

    def wait(self):
        self.own().wait()

        def stop(k, carry):
            self.copy(k).wait()
            return carry

        lax.fori_loop(1, self.experts, stop, 0)


def tail_matrix(part, experts, tail, turned):
    size = PARTS * tail
    shape = (experts * tail, experts * size) if turned else (experts * size, experts * tail)
    there = lax.broadcasted_iota(jnp.int32, shape, 1 if turned else 0)
    here = lax.broadcasted_iota(jnp.int32, shape, 0 if turned else 1)
    want = here // tail * size + part * tail + here % tail
    return (there == want).astype(f32).astype(bf16)


def gelu_pair(v):
    u = v * v
    t = jnp.tanh(v * (0.7978845608 + 0.7978845608 * 0.044715 * u))
    h = 0.5 * t + 0.5
    slope = h + (h - h * h) * (v * (2 * 0.7978845608 + 6 * 0.7978845608 * 0.044715 * u))
    return v * h, slope


def experts_kernel(experts, tail, *refs):
    (a_in, b_in, ca_in, cb_in, cent, w1_h, w2_h, w3_h, w4_h) = refs[:9]
    (ra_out, rb_out, ga_out, gb_out, gcent, xg_o, mlo_o, grs_o, gm_o, act1_o, act2_o, gp1_o, gp2_o) = refs[9:22]
    (w1, w2, w3, w4, xg, mlo, grs, gm, act1, act2, d1, d2, mid, psend, precv, ca, cb, sa, sb, cent_s, cent_r) = refs[22:43]
    (wsem, osem, psems, prsems, xs, xr, asend, arecv, alocal) = refs[43:]
    me, core = lax.axis_index("expert"), lax.axis_index("hidden")
    other = 1 - core
    own, width = xg.shape[0] // 2, xg.shape[1]
    hid = w1.shape[1]
    main = a_in.shape[0]
    block = width // PARTS
    mine, theirs = pl.ds(0, own), pl.ds(own, own)

    loads = []
    for i, (h, v) in enumerate(((w1_h, w1), (w2_h, w2), (w3_h, w3), (w4_h, w4))):
        load = pltpu.make_async_copy(h, v, wsem.at[i])
        load.start()
        loads.append(load)
    greet(experts, me, core, other)

    def move(i, src, dst):
        return Spread(experts, me, core, src, dst, asend.at[i], arecv.at[i], alocal.at[i])

    cot_moves = (move(0, ca_in, ca), move(1, cb_in, cb))
    for m in cot_moves:
        m.start()

    def pair(src, dst, send, recv):
        return pltpu.make_async_remote_copy(
            src, dst, send, recv, device_id=(me, other), device_id_type=MESH
        )

    def mirror(i, ref):
        return pair(ref.at[mine], ref.at[theirs], xs.at[i], xr.at[i])

    def partial_send(i):
        return pair(psend, precv.at[i % 2], psems.at[i], prsems.at[i])

    def from_tail(ref, to, start):
        for q in range(PARTS):
            to[pl.ds(start, experts * tail), q * block : (q + 1) * block] = mm(
                tail_matrix(q, experts, tail, True), ref[...]
            ).astype(bf16)

    def to_tail(value, ref):
        total = None
        for q in range(PARTS):
            term = mm(tail_matrix(q, experts, tail, False), value[:, q * block : (q + 1) * block])
            total = term if total is None else total + term
        ref[...] = total.astype(bf16)

    outs = []

    def store(i, ref, out):
        copy = pltpu.make_async_copy(ref, out, osem.at[i])
        copy.start()
        outs.append(copy)

    TN = 256

    def over(size, body):
        def step(n, carry):
            body(pl.ds(pl.multiple_of(n * TN, TN), TN))
            return carry

        lax.fori_loop(0, size // TN, step, 0)

    def up(x, w, act, slope, rows):
        def body(cols):
            a, d = gelu_pair(mm(x[rows, :], w[:, cols]))
            act[rows, cols] = a.astype(bf16)
            slope[rows, cols] = d.astype(bf16)

        over(hid, body)

    def down(act, w, rows, put):
        over(width, lambda cols: put(cols, mm(act[rows, :], w[:, cols])))

    def up_back(g, w, slope, rows):
        def body(cols):
            t = mm(g[rows, :], w[cols, :], (1, 1)) * slope[rows, cols].astype(f32)
            slope[rows, cols] = t.astype(bf16)

        over(hid, body)

    def down_back(gp, w, rows, put):
        over(width, lambda cols: put(cols, mm(gp[rows, :], w[cols, :], (1, 1))))

    def to_send(cols, value):
        psend[:, cols] = value.astype(bf16)

    def to_mid(cols, value):
        mid[:, cols] = value

    def add_mid(cols, value):
        mid[:, cols] += value

    xg[pl.ds(0, main), :] = a_in[...]
    from_tail(b_in, xg, main)
    share_x = mirror(0, xg)
    share_x.start()
    slot = xg[mine, :].astype(f32)
    gate = jax.nn.sigmoid(jnp.sum(slot * cent[...].astype(f32), axis=1, keepdims=True))
    loads[0].wait()
    up(xg, w1, act1, d1, mine)
    share_x.wait()
    store(0, xg, xg_o)
    up(xg, w1, act1, d1, theirs)
    store(1, act1, act1_o)
    loads[1].wait()
    down(act1, w2, theirs, to_send)
    send0 = partial_send(0)
    send0.start()
    down(act1, w2, mine, to_mid)
    send0.wait()
    mid[...] = mid[...] + xg[mine, :].astype(f32) + precv[0].astype(f32)
    mlo[mine, :] = mid[...].astype(bf16)
    share_m = mirror(1, mlo)
    share_m.start()
    loads[2].wait()
    up(mlo, w3, act2, d2, mine)
    share_m.wait()
    store(2, mlo, mlo_o)
    up(mlo, w3, act2, d2, theirs)
    store(3, act2, act2_o)
    loads[3].wait()
    down(act2, w4, theirs, to_send)
    send1 = partial_send(1)
    send1.start()
    down(act2, w4, mine, add_mid)
    send1.wait()
    mid[...] = mid[...] + precv[1].astype(f32)
    returned = (gate * mid[...]).astype(bf16)
    sa[...] = returned[:main]
    to_tail(returned[main:], sb)
    ret_moves = (move(2, sa, ra_out), move(3, sb, rb_out))
    for m in ret_moves:
        m.start()
    for m in cot_moves:
        m.wait()
    grs[pl.ds(0, main), :] = ca[...]
    from_tail(cb, grs, main)
    cot = grs[mine, :].astype(f32)
    logit = jnp.sum(cot * mid[...], axis=1, keepdims=True) * gate * (1.0 - gate)
    grs[mine, :] = (gate * cot).astype(bf16)
    share_g = mirror(2, grs)
    share_g.start()
    up_back(grs, w4, d2, mine)
    share_g.wait()
    store(4, grs, grs_o)
    up_back(grs, w4, d2, theirs)
    store(5, d2, gp2_o)
    down_back(d2, w3, theirs, to_send)
    send2 = partial_send(2)
    send2.start()
    down_back(d2, w3, mine, to_mid)
    send2.wait()
    gm[mine, :] = (mid[...] + grs[mine, :].astype(f32) + precv[0].astype(f32)).astype(bf16)
    share_gm = mirror(3, gm)
    share_gm.start()
    up_back(gm, w2, d1, mine)
    share_gm.wait()
    store(6, gm, gm_o)
    up_back(gm, w2, d1, theirs)
    store(7, d1, gp1_o)
    down_back(d1, w1, theirs, to_send)
    send3 = partial_send(3)
    send3.start()
    down_back(d1, w1, mine, to_mid)
    cent_s[...] = jnp.sum(logit * xg[mine, :].astype(f32), axis=0, keepdims=True)
    share_c = pair(cent_s, cent_r, xs.at[4], xr.at[4])
    share_c.start()
    for m in ret_moves:
        m.wait()
    send3.wait()
    slots = (
        mid[...] + gm[mine, :].astype(f32) + precv[1].astype(f32) + logit * cent[...].astype(f32)
    ).astype(bf16)
    sa[...] = slots[:main]
    to_tail(slots[main:], sb)
    back_moves = (move(4, sa, ga_out), move(5, sb, gb_out))
    for m in back_moves:
        m.start()
    share_c.wait()
    gcent[...] = cent_s[...] + cent_r[...]
    for copy in outs:
        copy.wait()
    for m in back_moves:
        m.wait()


def run_experts(experts, slots, tails, cots, cot_tails, centroid, weights):
    width, hid = weights[0].shape
    main = slots.shape[0]
    tail = tails.shape[0] // experts // PARTS
    own = main + experts * tail
    both = 2 * own

    def sds(*shape, dtype=bf16):
        return jax.ShapeDtypeStruct(shape, dtype)

    travel = [sds(*slots.shape), sds(*tails.shape)] * 2
    wide = [sds(both, width)] * 4 + [sds(both, hid)] * 4
    return pl.pallas_call(
        functools.partial(experts_kernel, experts, tail),
        out_shape=travel + [sds(1, width, dtype=f32)] + wide,
        in_specs=[VM, VM, ANY, ANY, VM, ANY, ANY, ANY, ANY],
        out_specs=[ANY] * 4 + [VM] + [ANY] * 8,
        scratch_shapes=[
            pltpu.VMEM((width, hid), bf16),
            pltpu.VMEM((hid, width), bf16),
            pltpu.VMEM((width, hid), bf16),
            pltpu.VMEM((hid, width), bf16),
            pltpu.VMEM((both, width), bf16),
            pltpu.VMEM((both, width), bf16),
            pltpu.VMEM((both, width), bf16),
            pltpu.VMEM((both, width), bf16),
            pltpu.VMEM((both, hid), bf16),
            pltpu.VMEM((both, hid), bf16),
            pltpu.VMEM((both, hid), bf16),
            pltpu.VMEM((both, hid), bf16),
            pltpu.VMEM((own, width), f32),
            pltpu.VMEM((own, width), bf16),
            pltpu.VMEM((2, own, width), bf16),
            pltpu.VMEM(slots.shape, bf16),
            pltpu.VMEM(tails.shape, bf16),
            pltpu.VMEM(slots.shape, bf16),
            pltpu.VMEM(tails.shape, bf16),
            pltpu.VMEM((1, width), f32),
            pltpu.VMEM((1, width), f32),
            DMA((4,)),
            DMA((8,)),
            DMA((4,)),
            DMA((4,)),
            DMA((5,)),
            DMA((5,)),
            DMA((6, experts)),
            DMA((6, experts)),
            DMA((6,)),
        ],
        compiler_params=pltpu.CompilerParams(
            collective_id=2, has_side_effects=True, vmem_limit_bytes=VMEM_MAX
        ),
        name="experts_pass",
    )(slots, tails, cots, cot_tails, centroid, *weights)

def back_kernel(experts, tail, *refs):
    (ra, rb, ga, gb, dm, dt, gains, cot_h, res_h, tok_h, packed_h, probs_h, mixed_h, wall_h) = refs[:14]
    out_o, ig_o, gqkv_o, gout_o, ggain_o = refs[14:19]
    (cot, res, tok, packed, probs, mixed, wqkv, wout, normed, gatt, gmix, gpk, so, si) = refs[19:33]
    keeps, psends, precvs, rv1s, rv2s, rv3s = (refs[33 + 5 * i : 38 + 5 * i] for i in range(6))
    lsem, sends, recvs, asend, arecv, alocal = refs[63:]
    me, core = lax.axis_index("expert"), lax.axis_index("hidden")
    other = 1 - core
    my_z, my_y, my_x = me // 4, lax.rem(me // 2, 2), lax.rem(me, 2)
    rows, width = tok.shape
    block = width // PARTS

    loads = {}
    for i, (name, h, v) in enumerate(
        (
            ("res", res_h, res),
            ("cot", cot_h, cot),
            ("mixed", mixed_h, mixed),
            ("wout", wall_h.at[:, pl.ds(3 * width, width)], wout),
            ("probs", probs_h, probs),
            ("packed", packed_h, packed),
            ("tok", tok_h, tok),
            ("wqkv", wall_h.at[:, pl.ds(0, 3 * width)], wqkv),
        )
    ):
        loads[name] = pltpu.make_async_copy(h, v, lsem.at[i])
        loads[name].start()
    greet(experts, me, core, other)

    def join_slots(slots, tails):
        parts = []
        for q in range(PARTS):
            parts.append(
                mm(dm[...], slots[:, q * block : (q + 1) * block], (0, 0))
                + mm(dt[q], tails[...], (0, 0))
            )
        return jnp.concatenate(parts, axis=1)

    piece = SEQ // experts
    seats = MICRO * PER

    def to_blocks(value):
        shape = (rows, rows)
        to = lax.broadcasted_iota(jnp.int32, shape, 0)
        at = lax.broadcasted_iota(jnp.int32, shape, 1)
        b, s, q = to // (seats * piece), to // piece % seats, to % piece
        turn = (at == s * SEQ + b * piece + q).astype(f32).astype(bf16)
        return mm(turn, value).astype(bf16)

    def move(i, src, dst):
        return Spread(experts, me, core, src, dst, asend.at[i], arecv.at[i], alocal.at[i])

    my_a = jnp.where(core == 0, my_x, my_y)
    my_b = jnp.where(core == 0, my_y, my_x)

    def near(a_step, b_step):
        a, b = (1 - my_a if a_step else my_a), (1 - my_b if b_step else my_b)
        x, y = jnp.where(core == 0, a, b), jnp.where(core == 0, b, a)
        return my_z * 4 + y * 2 + x

    def remote(c, stage, src, dst, to, to_core):
        return pltpu.make_async_remote_copy(
            src, dst, sends.at[c, stage], recvs.at[c, stage],
            device_id=(to, to_core), device_id_type=MESH,
        )

    def pair_copy(c):
        return remote(c, 0, psends[c], precvs[c], me, other)

    def a_copy(c):
        return remote(c, 1, psends[c].at[pl.ds(0, 256)], rv1s[c], near(True, False), core)

    def b_copy(c):
        return remote(c, 2, psends[c].at[pl.ds(256, 128)], rv2s[c], near(False, True), core)

    def z_copy(c, dz):
        to_z = lax.rem(my_z + dz, 4)
        src = psends[c].at[pl.ds(pl.multiple_of(384 + to_z * 32, 32), 32)]
        return remote(c, 2 + dz, src, rv3s[c].at[dz - 1], to_z * 4 + my_y * 2 + my_x, core)

    def place(c, t, cols):
        for j in range(8):
            z, y = j // 2, j % 2
            for x in range(2):
                at = 128 * j + 64 * x
                even, odd = t[at : at + 32], t[at + 32 : at + 64]
                first, second = x * 8 + y * 4 + z, y * 8 + x * 4 + z
                mine = jnp.where(core == 0, first, second)
                theirs = jnp.where(core == 0, second, first)
                keeps[c][pl.ds(pl.multiple_of(mine * 32, 32), 32), cols] = jnp.where(
                    core == 0, even, odd
                )
                psends[c][pl.ds(pl.multiple_of(theirs * 32, 32), 32), cols] = jnp.where(
                    core == 0, odd, even
                ).astype(bf16)

    def compute(c, left, right, start):
        def body(n, carry):
            cols = pl.ds(pl.multiple_of(n * 512, 512), 512)
            from_cols = pl.ds(pl.multiple_of(start + n * 512, 512), 512)
            place(c, mm(left[...], right[:, from_cols], (0, 0)), cols)
            return carry

        lax.fori_loop(0, width // 512, body, 0)
        pair_copy(c).start()

    half_a = pl.ds(pl.multiple_of(my_a * 256, 256), 256)
    half_a_out = pl.ds(pl.multiple_of((1 - my_a) * 256, 256), 256)
    base_b = my_a * 256
    half_b = pl.ds(pl.multiple_of(base_b + my_b * 128, 128), 128)
    half_b_out = pl.ds(pl.multiple_of(base_b + (1 - my_b) * 128, 128), 128)

    def after_pair(c):
        pair_copy(c).wait()
        keep = keeps[c]
        keep[...] += precvs[c][...].astype(f32)
        psends[c][pl.ds(0, 256), :] = keep[half_a_out, :].astype(bf16)
        a_copy(c).start()

    def after_a(c):
        a_copy(c).wait()
        keep = keeps[c]
        keep[half_a, :] += rv1s[c][...].astype(f32)
        psends[c][pl.ds(256, 128), :] = keep[half_b_out, :].astype(bf16)
        b_copy(c).start()

    def after_b(c):
        b_copy(c).wait()
        keep = keeps[c]
        keep[half_b, :] += rv2s[c][...].astype(f32)
        psends[c][pl.ds(384, 128), :] = keep[half_b, :].astype(bf16)
        for dz in range(1, 4):
            z_copy(c, dz).start()

    def after_z(c, out, cols):
        for dz in range(1, 4):
            z_copy(c, dz).wait()
        at = pl.ds(pl.multiple_of(base_b + my_b * 128 + my_z * 32, 32), 32)
        total = keeps[c][at, :]
        for dz in range(3):
            total = total + rv3s[c][dz].astype(f32)
        out[:, cols] = total

    gain_a, gain_f = gains[0:1, :], gains[1:2, :]
    ones = jnp.ones((rows, 64), bf16)

    def column_sums(value):
        high = value.astype(bf16)
        low = (value - high.astype(f32)).astype(bf16)
        return mm(high, ones, (0, 0)) + mm(low, ones, (0, 0))

    loads["res"].wait()
    so[...] = to_blocks((res[...] + join_slots(ra, rb)).astype(bf16))
    out_move = move(0, so, out_o)
    out_move.start()
    unit, inv = norm_parts(res[...])
    grad_shared = join_slots(ga, gb)
    ffn_sums = column_sums(grad_shared * unit)
    loads["cot"].wait()
    grad = cot[...].astype(f32) + norm_back(unit, inv, gain_f, grad_shared)
    res[...] = grad
    gatt[...] = grad.astype(bf16)
    loads["mixed"].wait()
    compute(0, mixed, gatt, 0)
    loads["wout"].wait()
    gmix[...] = mm(gatt[...], wout[...], (1, 1)).astype(bf16)
    after_pair(0)
    loads["probs"].wait()
    loads["packed"].wait()
    lane = lax.broadcasted_iota(jnp.int32, (PACK, 2 * HEAD), 1)
    first = lane < HEAD

    def stacked(v):
        zero = jnp.zeros_like(v)
        return jnp.concatenate([jnp.where(first, v, zero), jnp.where(first, zero, v)], axis=0)

    def pack(p, carry):
        at = pl.ds(pl.multiple_of(p * PACK, PACK), PACK)
        for h in range(HEADS // 2):
            lo = h * 2 * HEAD
            q = packed[at, lo : lo + 2 * HEAD]
            k = packed[at, width + lo : width + lo + 2 * HEAD]
            v = packed[at, 2 * width + lo : 2 * width + lo + 2 * HEAD]
            gs = stacked(gmix[at, lo : lo + 2 * HEAD])
            pr_lo = probs[p * (HEADS // 2) + h]
            pr = pr_lo.astype(f32)
            gp = mm(gs, v, (1, 1))
            gv = mm(pr_lo, gs, (0, 0))
            inner = jnp.sum(pr * gp, axis=1, keepdims=True)
            ds_ = (pr * (gp - inner)).astype(bf16)
            t = mm(ds_, k)
            gq = jnp.where(first, t[:PACK], t[PACK:]) * 0.125
            gk = mm(ds_, stacked(q), (0, 0)) * 0.125
            gpk[at, lo : lo + 2 * HEAD] = gq.astype(bf16)
            gpk[at, width + lo : width + lo + 2 * HEAD] = gk.astype(bf16)
            gpk[at, 2 * width + lo : 2 * width + lo + 2 * HEAD] = gv.astype(bf16)
        return carry

    lax.fori_loop(0, MICRO, pack, 0)
    after_a(0)
    loads["tok"].wait()
    unit, inv = norm_parts(tok[...].astype(f32))
    normed[...] = (unit * gain_a).astype(bf16)
    compute(1, normed, gpk, 0)
    after_b(0)
    compute(2, normed, gpk, width)
    after_pair(1)
    compute(3, normed, gpk, 2 * width)
    after_pair(2)
    loads["wqkv"].wait()

    grad_normed = mm(gpk[...], wqkv[...], (1, 1))
    unit, inv = norm_parts(tok[...].astype(f32))
    sums = column_sums(grad_normed * unit)
    si[...] = to_blocks((res[...] + norm_back(unit, inv, gain_a, grad_normed)).astype(bf16))
    ig_move = move(1, si, ig_o)
    after_pair(3)
    ig_move.start()
    place(4, jnp.concatenate([sums, ffn_sums], axis=1), pl.ds(0, 128))
    pair_copy(4).start()
    after_z(0, gout_o, pl.ds(0, width))
    after_pair(4)
    for c in (1, 2, 3, 4):
        after_a(c)
    for c in (1, 2, 3, 4):
        after_b(c)
    for c in (1, 2, 3):
        after_z(c, gqkv_o, pl.ds((c - 1) * width, width))
    after_z(4, ggain_o, pl.ds(0, 128))
    out_move.wait()
    ig_move.wait()


def run_back(experts, tail, slots, tails, grads, grad_tails, d_main, d_tail, gains, cot, residual, tok, packed, probs, mixed, w_all):
    rows, width = tok.shape

    def sds(*shape, dtype=bf16):
        return jax.ShapeDtypeStruct(shape, dtype)

    widths = (width,) * 4 + (128,)
    scratch = [
        pltpu.VMEM(cot.shape, bf16),
        pltpu.VMEM(residual.shape, f32),
        pltpu.VMEM(tok.shape, bf16),
        pltpu.VMEM(packed.shape, bf16),
        pltpu.VMEM(probs.shape, bf16),
        pltpu.VMEM(mixed.shape, bf16),
        pltpu.VMEM((width, 3 * width), bf16),
        pltpu.VMEM((width, width), bf16),
        pltpu.VMEM((rows, width), bf16),
        pltpu.VMEM((rows, width), bf16),
        pltpu.VMEM((rows, width), bf16),
        pltpu.VMEM((rows, 3 * width), bf16),
        pltpu.VMEM((rows, width), bf16),
        pltpu.VMEM((rows, width), bf16),
    ]
    scratch += [pltpu.VMEM((width // 2, w), f32) for w in widths]
    for part in (2, 2, 4, 8):
        scratch += [pltpu.VMEM((width // part, w), bf16) for w in widths]
    scratch += [pltpu.VMEM((3, 32, w), bf16) for w in widths]
    scratch += [
        DMA((8,)),
        DMA((5, 6)),
        DMA((5, 6)),
        DMA((2, experts)),
        DMA((2, experts)),
        DMA((2,)),
    ]
    return pl.pallas_call(
        functools.partial(back_kernel, experts, tail),
        out_shape=[sds(rows, width), sds(rows, width), sds(32, 3 * width, dtype=f32), sds(32, width, dtype=f32), sds(32, 128, dtype=f32)],
        in_specs=[VM] * 7 + [ANY] * 7,
        out_specs=[ANY, ANY, VM, VM, VM],
        scratch_shapes=scratch,
        compiler_params=pltpu.CompilerParams(
            collective_id=3, has_side_effects=True, vmem_limit_bytes=VMEM_MAX
        ),
        name="attention_back",
    )(slots, tails, grads, grad_tails, d_main, d_tail, gains, cot, residual, tok, packed, probs, mixed, w_all)


def front_kernel(experts, tail, *refs):
    (tokens, cots, routes, orders, deal, lengths, g_attn, g_ffn, w_qkv, w_out) = refs[:10]
    (slots_o, tails_o, cslots_o, ctails_o, deal_o, dm_o, dt_o, gains_o, cot_o, res_o, tok_o, packed_o, probs_o, mixed_o, w_o) = refs[10:25]
    (st, sl, rt, rl, rc, tok, cot, w, packed, probs, mixed, res, shared, dm, dt, ftm, masks, ss, stl, cs, ctl) = refs[25:46]
    zs, zr, as_, ar, bs, br, ps, pr, asend, arecv, alocal, osem = refs[46:]
    me, core = lax.axis_index("expert"), lax.axis_index("hidden")
    other = 1 - core
    my_z, my_y, my_x = me // 4, lax.rem(me // 2, 2), lax.rem(me, 2)
    rows, width = tok.shape
    piece = SEQ // experts
    seats = MICRO * PER
    block = width // PARTS
    step = w_qkv.shape[0]
    per_dest = experts and dims(experts, width)[0]
    main = per_dest - tail
    capacity = per_dest // MICRO

    def iota(shape, axis):
        return lax.broadcasted_iota(jnp.int32, shape, axis)

    def one_hot(test):
        return test.astype(f32).astype(bf16)

    own_rows = pl.ds(pl.multiple_of((me * 2 + core) * step, step), step)
    w[own_rows, : 3 * width] = w_qkv[...]
    w[own_rows, 3 * width : 4 * width] = w_out[...]
    eye = iota((step, step), 0) == iota((step, step), 1)

    def as_column(row):
        return jnp.sum(jnp.where(eye, row[...].astype(f32), 0.0), axis=1, keepdims=True)

    gain_cols = jnp.where(iota((step, 128), 1) < 64, as_column(g_attn), as_column(g_ffn))
    w[own_rows, 4 * width :] = gain_cols.astype(bf16)

    def coords(z, y, x):
        return z * 4 + y * 2 + x

    def rows_of(e, c):
        return w.at[pl.ds(pl.multiple_of((e * 2 + c) * step, step), step)]

    def send(e, sem_s, sem_r, to, to_core):
        ref = rows_of(e, core)
        return pltpu.make_async_remote_copy(
            ref, ref, sem_s, sem_r, device_id=(to, to_core), device_id_type=MESH
        )

    a_to = jnp.where(core == 0, coords(my_z, my_y, 1 - my_x), coords(my_z, 1 - my_y, my_x))
    b_to = jnp.where(core == 0, coords(my_z, 1 - my_y, my_x), coords(my_z, my_y, 1 - my_x))
    shift_a = a_to - me

    def z_copy(dz):
        return send(me, zs.at[dz - 1], zr.at[dz - 1], lax.rem(my_z + dz, 4) * 4 + lax.rem(me, 4), core)

    def held(d):
        return lax.rem(my_z + 4 - d, 4) * 4 + lax.rem(me, 4)

    def a_copy(d):
        return send(held(d), as_.at[d], ar.at[d], a_to, core)

    def b_copy(d, from_a):
        return send(held(d) + (shift_a if from_a else 0), bs.at[4 * from_a + d], br.at[4 * from_a + d], b_to, core)

    def p_copy(i, e):
        return send(e, ps.at[i], pr.at[i], me, other)

    shift_b = b_to - me
    greet(experts, me, core, other)
    for dz in range(1, 4):
        z_copy(dz).start()

    def release(d):
        a_copy(d).start()
        b_copy(d, 0).start()
        p_copy(d, held(d)).start()

    release(0)

    def move(i, src, dst):
        return Spread(experts, me, core, src, dst, asend.at[i], arecv.at[i], alocal.at[i])

    group = deal.shape[1]
    deal_row = deal[pl.ds(core, 1), :]
    length_row = lengths[pl.ds(core, 1), :]
    spread_out = one_hot(iota((group, rows), 1) // piece == iota((group, rows), 0))
    wide = jnp.broadcast_to(deal_row.astype(f32), (8, group)).astype(bf16)
    goal = mm(wide, spread_out)[0:1].astype(jnp.int32) * piece + iota((1, rows), 1) % piece
    ftm[...] = one_hot(iota((rows, rows), 0) == goal)
    st[...] = mm(ftm[...], tokens[...]).astype(bf16)
    lab = jnp.where(iota((rows, 128), 1) < 64, routes[...], orders[...]).astype(f32).astype(bf16)
    sl[...] = mm(ftm[...], lab).astype(bf16)
    tok_moves = (move(0, st, rt), move(1, sl, rl))
    for m in tok_moves:
        m.start()
    cs[...] = mm(ftm[...], cots[...]).astype(bf16)
    for d in range(1, 4):
        z_copy(d).wait()
        release(d)
    for m in tok_moves:
        m.wait()
    cot_move = move(2, cs, rc)
    cot_move.start()

    outs = []

    def store(i, ref, out):
        copy = pltpu.make_async_copy(ref, out, osem.at[i])
        copy.start()
        outs.append(copy)

    store(0, ftm, deal_o)
    to, at = iota((rows, rows), 0), iota((rows, rows), 1)
    b, s, q = to // (seats * piece), to // piece % seats, to % piece
    turn = one_hot(at == s * SEQ + b * piece + q)
    tok[...] = mm(turn, rt[...], (0, 0)).astype(bf16)
    store(1, tok, tok_o)
    lab_col = mm(turn, rl[...], (0, 0))
    lab_row = mm(rl[...], turn, (0, 0))
    for d in range(4):
        a_copy(d).wait()
        b_copy(d, 1).start()
        p_copy(4 + d, held(d) + shift_a).start()
    ranks, heads_at, oks = [], [], []
    own = [
        jnp.sum(jnp.where(deal_row == me * seats + i, length_row, 0), axis=1, keepdims=True)
        for i in range(seats)
    ]
    posr, posc = iota((1, PACK), 1), iota((PACK, 1), 0)
    near_ = (iota((PACK, PACK), 0) // SEQ == iota((PACK, PACK), 1) // SEQ) & (
        iota((PACK, PACK), 1) <= iota((PACK, PACK), 0)
    )
    for p in range(MICRO):
        low, high = own[PER * p], own[PER * p + 1]
        here_r = posr % SEQ < jnp.where(posr < SEQ, low, high)
        here_c = posc % SEQ < jnp.where(posc < SEQ, low, high)
        masks[p] = (near_ & here_r).astype(f32)
        cols = slice(p * PACK, (p + 1) * PACK)
        route_r = lab_row[0:1, cols]
        key_r = lab_row[64:65, cols] * PER + (posr // SEQ).astype(f32)
        route_c = lab_col[cols, 0:1]
        key_c = lab_col[cols, 64:65] * PER + (posc // SEQ).astype(f32)
        ahead = jnp.sum(
            ((route_c == route_r) & (key_c < key_r) & here_c).astype(f32), axis=0, keepdims=True
        ).astype(jnp.int32)
        base = p * capacity + ahead
        good = here_r & (ahead < capacity)
        route_i = route_r.astype(jnp.int32)
        heads_at.append(jnp.where(good & (base < main), route_i * main + base, -1))
        oks.append(jnp.where(good & (base >= main), route_i * (PARTS * tail) + base - main, -PARTS * PARTS * tail))
    head_row = jnp.concatenate(heads_at, axis=1)
    tail_row = jnp.concatenate(oks, axis=1)
    dm[...] = one_hot(iota(dm.shape, 0) == head_row)
    for part in range(PARTS):
        dt[part] = one_hot(iota(dt.shape[1:], 0) == tail_row + part * tail)
    store(2, dm, dm_o)
    store(3, dt, dt_o)

    def split(ref, to_main, to_tails):
        to_main[...] = mm(dm[...], ref[...]).astype(bf16)
        total = None
        for part in range(PARTS):
            term = mm(dt[part], ref[:, part * block : (part + 1) * block])
            total = term if total is None else total + term
        to_tails[...] = total.astype(bf16)

    inputs = tok[...].astype(f32)
    unit, inv = norm_parts(inputs)
    res[...] = unit
    for d in range(4):
        b_copy(d, 0).wait()
        p_copy(8 + d, held(d) + shift_b).start()
    for d in range(4):
        b_copy(d, 1).wait()
        p_copy(12 + d, held(d) + shift_a + shift_b).start()
    for d in range(4):
        p_copy(d, held(d)).wait()
        p_copy(4 + d, held(d)).wait()
        p_copy(8 + d, held(d)).wait()
        p_copy(12 + d, held(d)).wait()
    store(4, w, w_o)
    big = iota((128, 128), 0) == iota((128, 128), 1)

    def gain_row(lane):
        parts = []
        for j in range(width // 128):
            col = w[128 * j : 128 * (j + 1), 4 * width :].astype(f32)[:, lane : lane + 1]
            parts.append(jnp.sum(jnp.where(big, col, 0.0), axis=0, keepdims=True))
        return jnp.concatenate(parts, axis=1)

    gain_a, gain_f = gain_row(0), gain_row(64)
    gains_o[0:1, :] = gain_a
    gains_o[1:2, :] = gain_f
    shared[...] = (res[...] * gain_a).astype(bf16)

    def project(n, carry):
        cols = pl.ds(pl.multiple_of(n * 256, 256), 256)
        packed[:, cols] = mm(shared[...], w[:, cols]).astype(bf16)
        return carry

    lax.fori_loop(0, 3 * width // 256, project, 0)
    store(5, packed, packed_o)
    first = iota((PACK, 2 * HEAD), 1) < HEAD

    def pack(p, carry):
        at = pl.ds(pl.multiple_of(p * PACK, PACK), PACK)
        mask = masks[p] > 0.5
        mask = jnp.concatenate([mask, mask], axis=0)
        for h in range(HEADS // 2):
            lo = h * 2 * HEAD
            q = packed[at, lo : lo + 2 * HEAD]
            k = packed[at, width + lo : width + lo + 2 * HEAD]
            v = packed[at, 2 * width + lo : 2 * width + lo + 2 * HEAD]
            zero = jnp.zeros_like(q)
            qs = jnp.concatenate([jnp.where(first, q, zero), jnp.where(first, zero, q)], axis=0)
            scores = jnp.where(mask, mm(qs, k, (1, 1)) * 0.125, -1e30)
            e = jnp.exp(scores - jnp.max(scores, axis=1, keepdims=True))
            prob = (e / jnp.sum(e, axis=1, keepdims=True)).astype(bf16)
            probs[p * (HEADS // 2) + h] = prob
            t = mm(prob, v)
            mixed[at, lo : lo + 2 * HEAD] = jnp.where(first, t[:PACK], t[PACK:]).astype(bf16)
        return carry

    lax.fori_loop(0, MICRO, pack, 0)
    store(6, probs, probs_o)
    store(7, mixed, mixed_o)
    residual = tok[...].astype(f32) + mm(mixed[...], w[:, 3 * width : 4 * width])
    res[...] = residual
    store(8, res, res_o)
    unit, inv = norm_parts(residual)
    shared[...] = (unit * gain_f).astype(bf16)
    split(shared, ss, stl)
    slot_moves = (move(3, ss, slots_o), move(4, stl, tails_o))
    cot_move.wait()
    for m in slot_moves:
        m.start()
    cot[...] = mm(turn, rc[...], (0, 0)).astype(bf16)
    store(9, cot, cot_o)
    split(cot, cs, ctl)
    store(10, cs, cslots_o)
    store(11, ctl, ctails_o)
    for copy in outs:
        copy.wait()
    for m in slot_moves:
        m.wait()


def run_front(experts, tail, tokens, cots, routes, orders, deal, lengths, g_attn, g_ffn, w_qkv, w_out):
    rows, width = tokens.shape
    per_dest = dims(experts, width)[0]
    main = (per_dest - tail) * experts
    side = experts * PARTS * tail

    def sds(*shape, dtype=bf16):
        return jax.ShapeDtypeStruct(shape, dtype)

    tails = (side, width // PARTS)
    out_shape = [
        sds(main, width),
        sds(*tails),
        sds(main, width),
        sds(*tails),
        sds(rows, rows),
        sds(main, rows),
        sds(PARTS, side, rows),
        sds(2, width, dtype=f32),
        sds(rows, width),
        sds(rows, width, dtype=f32),
        sds(rows, width),
        sds(rows, 3 * width),
        sds(MICRO * HEADS // 2, 2 * PACK, PACK),
        sds(rows, width),
        sds(width, 4 * width + 128),
    ]
    vm = pltpu.VMEM
    return pl.pallas_call(
        functools.partial(front_kernel, experts, tail),
        out_shape=out_shape,
        in_specs=[VM] * 10,
        out_specs=[ANY] * 7 + [VM] + [ANY] * 7,
        scratch_shapes=[
            vm((rows, width), bf16),
            vm((rows, 128), bf16),
            vm((rows, width), bf16),
            vm((rows, 128), bf16),
            vm((rows, width), bf16),
            vm((rows, width), bf16),
            vm((rows, width), bf16),
            vm((width, 4 * width + 128), bf16),
            vm((rows, 3 * width), bf16),
            vm((MICRO * HEADS // 2, 2 * PACK, PACK), bf16),
            vm((rows, width), bf16),
            vm((rows, width), f32),
            vm((rows, width), bf16),
            vm((main, rows), bf16),
            vm((PARTS, side, rows), bf16),
            vm((rows, rows), bf16),
            vm((MICRO, PACK, PACK), f32),
            vm((main, width), bf16),
            vm(tails, bf16),
            vm((main, width), bf16),
            vm(tails, bf16),
            DMA((3,)),
            DMA((3,)),
            DMA((4,)),
            DMA((4,)),
            DMA((8,)),
            DMA((8,)),
            DMA((16,)),
            DMA((16,)),
            DMA((5, experts)),
            DMA((5, experts)),
            DMA((5,)),
            DMA((12,)),
        ],
        compiler_params=pltpu.CompilerParams(
            collective_id=1, has_side_effects=True, vmem_limit_bytes=VMEM_MAX
        ),
        name="attention_front",
    )(tokens, cots, routes, orders, deal, lengths, g_attn, g_ffn, w_qkv, w_out)


def fast_shards(
    tokens,
    lengths,
    deal,
    routes,
    slot_order,
    gain_attn,
    gain_ffn,
    w_qkv,
    w_out,
    centroids,
    expert_in,
    expert_out,
    second_in,
    second_out,
    cotangent,
):
    width = tokens.shape[1]
    experts = lax.axis_size("expert")
    tail = dims(experts, width)[2]
    (slots, tails, cots, cot_tails, dealt, d_main, d_tail, gains, grad_output, residual, tok,
     packed, probs, mixed, w_all) = run_front(
        experts, tail, tokens, cotangent, routes, slot_order, deal, lengths,
        gain_attn[None], gain_ffn[None], w_qkv, w_out,
    )
    (ra, rb, ga, gb, g_cent, gathered, middle_lo, grad_result, grad_middle,
     act_first, act_second, grad_pre, grad_pre_second) = run_experts(
        experts, slots, tails, cots, cot_tails, centroids,
        (expert_in[0], expert_out[0], second_in[0], second_out[0]),
    )
    g_sec_out = mm(act_second, grad_result, (0, 0))
    g_sec_in = mm(middle_lo, grad_pre_second, (0, 0))
    g_exp_out = mm(act_first, grad_middle, (0, 0))
    g_exp_in = mm(gathered, grad_pre, (0, 0))
    out_r, ig_r, g_qkv, g_out, g_gain = run_back(
        experts, tail, ra, rb, ga, gb, d_main, d_tail, gains, grad_output, residual, tok,
        packed, probs, mixed, w_all,
    )
    return (
        mm(dealt, out_r, (0, 0)).astype(bf16),
        mm(dealt, ig_r, (0, 0)),
        g_gain[:, 0],
        g_gain[:, 64],
        g_qkv,
        g_out,
        g_cent,
        g_exp_in[None],
        g_exp_out[None],
        g_sec_in[None],
        g_sec_out[None],
    )


def gather_hidden(rows):
    return lax.all_gather(rows, "hidden", axis=0, tiled=True)


def sum_hidden(terms):
    return lax.psum_scatter(terms, "hidden", scatter_dimension=0, tiled=True)


def swap(blocks):
    return lax.all_to_all(blocks, "expert", split_axis=0, concat_axis=0, tiled=True)


def plain_shards(
    tokens,
    lengths,
    deal,
    routes,
    slot_order,
    gain_attn,
    gain_ffn,
    w_qkv,
    w_out,
    centroids,
    expert_in,
    expert_out,
    second_in,
    second_out,
    cotangent,
):
    width = tokens.shape[1]
    experts = lax.axis_size("expert")
    piece = SEQ // experts
    seats = MICRO * PER
    group = experts * seats
    rows = seats * SEQ
    capacity = (9 * PACK + 8 * experts - 1) // (8 * experts)
    per_dest = MICRO * capacity
    my_expert = lax.axis_index("expert")
    my_hidden = lax.axis_index("hidden")

    deal_row = lax.dynamic_index_in_dim(deal, my_hidden, 0, keepdims=False)
    length_row = lax.dynamic_index_in_dim(lengths, my_hidden, 0, keepdims=False)
    ids = jnp.arange(group, dtype=jnp.int32)
    inverse = jnp.sum(jnp.where(deal_row[None, :] == ids[:, None], ids[None, :], 0), axis=1)
    own = my_expert * seats + jnp.arange(seats, dtype=jnp.int32)
    own_lengths = jnp.sum(
        jnp.where(deal_row[None, :] == own[:, None], length_row[None, :], 0), axis=1
    )

    def to_dealt(flat):
        pieces = jnp.take(flat.reshape(group, piece, flat.shape[1]), inverse, axis=0)
        return lax.all_to_all(
            pieces.reshape(experts, seats, piece, flat.shape[1]),
            "expert",
            split_axis=0,
            concat_axis=2,
            tiled=True,
        ).reshape(rows, flat.shape[1])

    labels = jnp.concatenate([routes, slot_order], axis=1)
    lab = to_dealt(labels)
    tok = to_dealt(tokens)
    grad_output = to_dealt(cotangent)

    cat = jnp.concatenate(
        [w_qkv, w_out, gain_attn[:, None], gain_ffn[:, None], jnp.zeros((w_qkv.shape[0], 126), bf16)],
        axis=1,
    )
    cat = lax.all_gather(cat, ("expert", "hidden"), axis=0, tiled=True)
    qkv_w = cat[:, : 3 * width]
    out_w = cat[:, 3 * width : 4 * width]
    attn_gain = cat[:, 4 * width].astype(f32)[None, :]
    ffn_gain = cat[:, 4 * width + 1].astype(f32)[None, :]

    route = lab[:, 0].reshape(MICRO, PACK)
    order = lab[:, 1].reshape(MICRO, PACK)
    positions = jnp.arange(PACK, dtype=jnp.int32)
    seat = positions // SEQ
    pack_lengths = own_lengths.reshape(MICRO, PER)
    limit = jnp.repeat(pack_lengths, SEQ, axis=1)
    present = (positions % SEQ)[None, :] < limit
    priority = order * PER + seat[None, :]
    ahead = jnp.sum(
        (
            (route[:, :, None] == route[:, None, :])
            & (priority[:, None, :] < priority[:, :, None])
            & present[:, None, :]
        ).astype(jnp.int32),
        axis=2,
    )
    accepted = (present & (ahead < capacity)).reshape(rows)
    target = (
        route * per_dest + jnp.arange(MICRO, dtype=jnp.int32)[:, None] * capacity + ahead
    ).reshape(rows)
    target = jnp.where(accepted, target, -1)
    slot_ids = jnp.arange(experts * per_dest, dtype=jnp.int32)
    dispatch = (slot_ids[:, None] == target[None, :]).astype(bf16)

    def to_experts(values):
        out = mm(dispatch, values).astype(bf16)
        return swap(out.reshape(experts, per_dest, width)).reshape(experts * per_dest, width)

    cot_arrived = to_experts(grad_output)

    inputs = tok.astype(f32)
    unit_a, inv_a = norm_parts(inputs)
    normed = (unit_a * attn_gain).astype(bf16)
    packed = mm(normed, qkv_w).astype(bf16)
    allowed = (
        (seat[:, None] == seat[None, :]) & (positions[None, :] <= positions[:, None])
    )[None] & present[:, None, :]

    def heads(block):
        return block.reshape(MICRO, PACK, HEADS, HEAD)

    queries = heads(packed[:, :width])
    keys_all = heads(packed[:, width : 2 * width])
    values_all = heads(packed[:, 2 * width :])
    scores = jnp.einsum("pqhd,pkhd->phqk", queries, keys_all, preferred_element_type=f32) * 0.125
    masked = jnp.where(allowed[:, None], scores, -1e30)
    peaks = jnp.max(masked, axis=-1, keepdims=True)
    log_total = peaks + jnp.log(jnp.sum(jnp.exp(masked - peaks), axis=-1, keepdims=True))
    probs = jnp.exp(masked - log_total)
    probs_lo = probs.astype(bf16)
    mixed = (
        jnp.einsum("phqk,pkhd->pqhd", probs_lo, values_all, preferred_element_type=f32)
        .reshape(rows, width)
        .astype(bf16)
    )
    residual = inputs + mm(mixed, out_w)
    unit_f, inv_f = norm_parts(residual)
    shared = (unit_f * ffn_gain).astype(bf16)
    arrived = to_experts(shared)

    centroid_row = centroids[0]
    w_in, w_back = expert_in[0], expert_out[0]
    s_in, s_back = second_in[0], second_out[0]
    count = arrived.shape[0]
    arrived_f = arrived.astype(f32)
    gate_vals = jax.nn.sigmoid(
        jnp.sum(arrived_f * centroid_row.astype(f32)[None, :], axis=1, keepdims=True)
    )
    grad_result_own = (gate_vals * cot_arrived.astype(f32)).astype(bf16)
    gathered = gather_hidden(arrived)
    grad_result = gather_hidden(grad_result_own)
    pre_first = mm(gathered, w_in)
    act_first, pull_first = jax.vjp(gelu_act, pre_first)
    act_first = act_first.astype(bf16)
    middle = arrived_f + sum_hidden(mm(act_first, w_back).astype(bf16)).astype(f32)
    middle_lo = gather_hidden(middle.astype(bf16))
    pre_second = mm(middle_lo, s_in)
    act_second, pull_second = jax.vjp(gelu_act, pre_second)
    act_second = act_second.astype(bf16)
    expert_sum = middle + sum_hidden(mm(act_second, s_back).astype(bf16)).astype(f32)
    returned = (gate_vals * expert_sum).astype(bf16)
    came_back = swap(returned.reshape(experts, per_dest, width)).reshape(count, width)

    grad_logit = (
        jnp.sum(cot_arrived.astype(f32) * expert_sum, axis=1, keepdims=True)
        * gate_vals
        * (1.0 - gate_vals)
    )
    grad_pre_second = pull_second(mm(grad_result, s_back, (1, 1)))[0].astype(bf16)
    grad_middle_own = (
        grad_result_own.astype(f32)
        + sum_hidden(mm(grad_pre_second, s_in, (1, 1)).astype(bf16)).astype(f32)
    ).astype(bf16)
    grad_middle = gather_hidden(grad_middle_own)
    grad_pre = pull_first(mm(grad_middle, w_back, (1, 1)))[0].astype(bf16)
    grad_slots = (
        sum_hidden(mm(grad_pre, w_in, (1, 1)).astype(bf16)).astype(f32)
        + grad_middle_own.astype(f32)
        + grad_logit * centroid_row.astype(f32)[None, :]
    ).astype(bf16)
    grad_back = swap(grad_slots.reshape(experts, per_dest, width)).reshape(count, width)
    g_sec_out = mm(act_second, grad_result, (0, 0))
    g_sec_in = mm(middle_lo, grad_pre_second, (0, 0))
    g_exp_out = mm(act_first, grad_middle, (0, 0))
    g_exp_in = mm(gathered, grad_pre, (0, 0))
    g_cent = jnp.sum(grad_logit * arrived_f, axis=0, keepdims=True)

    combined = (residual + mm(dispatch, came_back, (0, 0))).astype(bf16)

    grad_shared = mm(dispatch, grad_back, (0, 0))
    g_gain_ffn = jnp.sum(grad_shared * unit_f, axis=0)
    grad_residual = grad_output.astype(f32) + norm_back(unit_f, inv_f, ffn_gain, grad_shared)
    grad_attended = grad_residual.astype(bf16)
    g_out_w = mm(mixed, grad_attended, (0, 0))
    grad_mixed = heads(mm(grad_attended, out_w, (1, 1)).astype(bf16))
    grad_probs = jnp.einsum("pqhd,pkhd->phqk", grad_mixed, values_all, preferred_element_type=f32)
    grad_values = jnp.einsum("phqk,pqhd->pkhd", probs_lo, grad_mixed, preferred_element_type=f32)
    inner = jnp.sum(probs * grad_probs, axis=-1, keepdims=True)
    grad_scores = (probs * (grad_probs - inner)).astype(bf16)
    grad_queries = (
        jnp.einsum("phqk,pkhd->pqhd", grad_scores, keys_all, preferred_element_type=f32) * 0.125
    )
    grad_keys = (
        jnp.einsum("phqk,pqhd->pkhd", grad_scores, queries, preferred_element_type=f32) * 0.125
    )
    grad_packed = jnp.concatenate(
        [g.reshape(rows, width) for g in (grad_queries, grad_keys, grad_values)], axis=1
    ).astype(bf16)
    g_qkv = mm(normed, grad_packed, (0, 0))
    grad_normed = mm(grad_packed, qkv_w, (1, 1))
    g_gain_attn = jnp.sum(grad_normed * unit_a, axis=0)
    input_grad = (grad_residual + norm_back(unit_a, inv_a, attn_gain, grad_normed)).astype(bf16)

    def scatter(partial):
        return lax.psum_scatter(
            partial, ("expert", "hidden"), scatter_dimension=0, tiled=True
        )

    g_cat = jnp.concatenate([g_qkv, g_out_w, g_gain_attn[:, None], g_gain_ffn[:, None], jnp.zeros((width, 126), f32)], axis=1)
    g_cat = scatter(g_cat)
    g_cent = lax.psum(g_cent, "hidden")

    def from_dealt(dealt):
        received = lax.all_to_all(
            dealt.reshape(1, seats, SEQ, width), "expert", split_axis=2, concat_axis=0, tiled=True
        ).reshape(group, piece, width)
        return jnp.take(received, deal_row, axis=0).reshape(group * piece, width)

    return (
        from_dealt(combined),
        from_dealt(input_grad).astype(f32),
        g_cat[:, 4 * width],
        g_cat[:, 4 * width + 1],
        g_cat[:, : 3 * width],
        g_cat[:, 3 * width : 4 * width],
        g_cent,
        g_exp_in[None],
        g_exp_out[None],
        g_sec_in[None],
        g_sec_out[None],
    )


def solution(mesh):
    both = ("expert", "hidden")
    fast = mesh.shape["expert"] == 16 and mesh.shape["hidden"] == 2
    return jax.shard_map(
        fast_shards if fast else plain_shards,
        mesh=mesh,
        in_specs=(
            P(both, None),
            P(),
            P(),
            P(both, None),
            P(both, None),
            P(both),
            P(both),
            P(both, None),
            P(both, None),
            P("expert", None),
            P("expert", None, "hidden"),
            P("expert", "hidden", None),
            P("expert", None, "hidden"),
            P("expert", "hidden", None),
            P(both, None),
        ),
        out_specs=(
            P(both, None),
            P(both, None),
            P(both),
            P(both),
            P(both, None),
            P(both, None),
            P("expert", None),
            P("expert", None, "hidden"),
            P("expert", "hidden", None),
            P("expert", None, "hidden"),
            P("expert", "hidden", None),
        ),
        check_vma=False,
    )
```

```python
import functools

import jax
import jax.numpy as jnp
from jax import lax
from jax.experimental import pallas as pl
from jax.experimental.pallas import tpu as pltpu
from jax.sharding import PartitionSpec as P

HEADS = 16
HEAD = 64
MICRO = 4
PER = 2
SEQ = 64
PACK = PER * SEQ

epsilon = 1e-05
bf16 = jnp.bfloat16
f32 = jnp.float32


def mm(a, b, contract=(1, 0)):
    return lax.dot_general(
        a, b, (((contract[0],), (contract[1],)), ((), ())), preferred_element_type=f32
    )


def norm_parts(rows):
    centre = jnp.mean(rows, axis=-1, keepdims=True)
    shifted = rows - centre
    spread = jnp.mean(shifted * shifted, axis=-1, keepdims=True)
    inv = lax.rsqrt(spread + epsilon)
    return shifted * inv, inv


def norm_back(unit, inv, gain, grad):
    g = grad * gain
    m1 = jnp.mean(g, axis=-1, keepdims=True)
    m2 = jnp.mean(g * unit, axis=-1, keepdims=True)
    return inv * (g - m1 - unit * m2)


def gelu_act(pre_act):
    return jax.nn.gelu(pre_act, approximate=True)


MESH = pl.DeviceIdType.MESH
ANY = pl.BlockSpec(memory_space=pl.ANY)
VM = pl.BlockSpec(memory_space=pltpu.VMEM)
DMA = pltpu.SemaphoreType.DMA
VMEM_MAX = 63 << 20
PARTS = 4


def dims(experts, width):
    capacity = (9 * PACK + 8 * experts - 1) // (8 * experts)
    per_dest = MICRO * capacity
    main = per_dest // 16 * 16
    return per_dest, main, per_dest - main


def greet(experts, me, core, partner):
    barrier = pltpu.get_barrier_semaphore()

    def hello(k, carry):
        pl.semaphore_signal(
            barrier, inc=1, device_id=(lax.rem(me + k, experts), core), device_id_type=MESH
        )
        return carry

    lax.fori_loop(1, experts, hello, 0)
    if partner is not None:
        pl.semaphore_signal(barrier, inc=1, device_id=(me, partner), device_id_type=MESH)
    pl.semaphore_wait(barrier, experts - 1 + (partner is not None))


class Spread:
    def __init__(self, experts, me, core, src, dst, sends, recvs, local):
        self.experts, self.me, self.core = experts, me, core
        self.src, self.dst, self.sends, self.recvs, self.local = src, dst, sends, recvs, local
        self.rows = src.shape[0] // experts

    def block(self, ref, index):
        return ref.at[pl.ds(pl.multiple_of(index * self.rows, 16), self.rows)]

    def copy(self, k):
        to = lax.rem(self.me + k, self.experts)
        return pltpu.make_async_remote_copy(
            self.block(self.src, to),
            self.block(self.dst, self.me),
            self.sends.at[k],
            self.recvs.at[k],
            device_id=(to, self.core),
            device_id_type=MESH,
        )

    def own(self):
        return pltpu.make_async_copy(
            self.block(self.src, self.me), self.block(self.dst, self.me), self.local
        )

    def start(self):
        self.own().start()

        def go(k, carry):
            self.copy(k).start()
            return carry

        lax.fori_loop(1, self.experts, go, 0)

    def wait(self):
        self.own().wait()

        def stop(k, carry):
            self.copy(k).wait()
            return carry

        lax.fori_loop(1, self.experts, stop, 0)


def tail_matrix(part, experts, tail, turned):
    size = PARTS * tail
    shape = (experts * tail, experts * size) if turned else (experts * size, experts * tail)
    there = lax.broadcasted_iota(jnp.int32, shape, 1 if turned else 0)
    here = lax.broadcasted_iota(jnp.int32, shape, 0 if turned else 1)
    want = here // tail * size + part * tail + here % tail
    return (there == want).astype(f32).astype(bf16)


def gelu_pair(v):
    u = v * v
    t = jnp.tanh(v * (0.7978845608 + 0.7978845608 * 0.044715 * u))
    h = 0.5 * t + 0.5
    slope = h + (h - h * h) * (v * (2 * 0.7978845608 + 6 * 0.7978845608 * 0.044715 * u))
    return v * h, slope


def experts_kernel(experts, tail, *refs):
    (a_in, b_in, ca_in, cb_in, cent, w1_h, w2_h, w3_h, w4_h) = refs[:9]
    (ra_out, rb_out, ga_out, gb_out, gcent, gw1_o, gw2_o, gw3_o, gw4_o) = refs[9:18]
    (w1, w2, w3, w4, xg, mlo, grs, gm, act1, act2, d1, d2, mid, psend, precv, ca, cb, sa, sb, cent_s, cent_r) = refs[18:39]
    (wsem, osem, psems, prsems, xs, xr, asend, arecv, alocal) = refs[39:]
    me, core = lax.axis_index("expert"), lax.axis_index("hidden")
    other = 1 - core
    own, width = xg.shape[0] // 2, xg.shape[1]
    hid = w1.shape[1]
    main = a_in.shape[0]
    block = width // PARTS
    mine, theirs = pl.ds(0, own), pl.ds(own, own)

    loads = []
    for i, (h, v) in enumerate(((w1_h, w1), (w2_h, w2), (w3_h, w3), (w4_h, w4))):
        load = pltpu.make_async_copy(h, v, wsem.at[i])
        load.start()
        loads.append(load)
    greet(experts, me, core, other)

    def move(i, src, dst):
        return Spread(experts, me, core, src, dst, asend.at[i], arecv.at[i], alocal.at[i])

    cot_moves = (move(0, ca_in, ca), move(1, cb_in, cb))
    for m in cot_moves:
        m.start()

    def pair(src, dst, send, recv):
        return pltpu.make_async_remote_copy(
            src, dst, send, recv, device_id=(me, other), device_id_type=MESH
        )

    def mirror(i, ref):
        return pair(ref.at[mine], ref.at[theirs], xs.at[i], xr.at[i])

    def partial_send(i):
        return pair(psend, precv.at[i % 2], psems.at[i], prsems.at[i])

    def from_tail(ref, to, start):
        for q in range(PARTS):
            to[pl.ds(start, experts * tail), q * block : (q + 1) * block] = mm(
                tail_matrix(q, experts, tail, True), ref[...]
            ).astype(bf16)

    def to_tail(value, ref):
        total = None
        for q in range(PARTS):
            term = mm(tail_matrix(q, experts, tail, False), value[:, q * block : (q + 1) * block])
            total = term if total is None else total + term
        ref[...] = total.astype(bf16)

    outs = []

    def store(i, ref, out):
        copy = pltpu.make_async_copy(ref, out, osem.at[i])
        copy.start()
        outs.append(copy)

    TN, WM, WN = 512, 512, 1024

    def over(size, body):
        def step(n, carry):
            body(pl.ds(pl.multiple_of(n * TN, TN), TN))
            return carry

        lax.fori_loop(0, size // TN, step, 0)

    def up(x, w, act, slope, rows):
        def body(cols):
            a, d = gelu_pair(mm(x[rows, :], w[:, cols]))
            act[rows, cols] = a.astype(bf16)
            slope[rows, cols] = d.astype(bf16)

        over(hid, body)

    def down(act, w, rows, put):
        over(width, lambda cols: put(cols, mm(act[rows, :], w[:, cols])))

    def up_back(g, w, slope, rows):
        def body(cols):
            t = mm(g[rows, :], w[cols, :], (1, 1)) * slope[rows, cols].astype(f32)
            slope[rows, cols] = t.astype(bf16)

        over(hid, body)

    def down_back(gp, w, rows, put):
        over(width, lambda cols: put(cols, mm(gp[rows, :], w[cols, :], (1, 1))))

    def to_send(cols, value):
        psend[:, cols] = value.astype(bf16)

    def to_mid(cols, value):
        mid[:, cols] = value

    def add_mid(cols, value):
        mid[:, cols] += value

    xg[pl.ds(0, main), :] = a_in[...]
    from_tail(b_in, xg, main)
    share_x = mirror(0, xg)
    share_x.start()
    slot = xg[mine, :].astype(f32)
    gate = jax.nn.sigmoid(jnp.sum(slot * cent[...].astype(f32), axis=1, keepdims=True))
    loads[0].wait()
    up(xg, w1, act1, d1, mine)
    share_x.wait()
    up(xg, w1, act1, d1, theirs)
    loads[1].wait()
    down(act1, w2, theirs, to_send)
    send0 = partial_send(0)
    send0.start()
    down(act1, w2, mine, to_mid)
    send0.wait()
    mid[...] = mid[...] + xg[mine, :].astype(f32) + precv[0].astype(f32)
    mlo[mine, :] = mid[...].astype(bf16)
    share_m = mirror(1, mlo)
    share_m.start()
    loads[2].wait()
    up(mlo, w3, act2, d2, mine)
    share_m.wait()
    up(mlo, w3, act2, d2, theirs)
    loads[3].wait()
    down(act2, w4, theirs, to_send)
    send1 = partial_send(1)
    send1.start()
    down(act2, w4, mine, add_mid)
    send1.wait()
    mid[...] = mid[...] + precv[1].astype(f32)
    returned = (gate * mid[...]).astype(bf16)
    sa[...] = returned[:main]
    to_tail(returned[main:], sb)
    ret_moves = (move(2, sa, ra_out), move(3, sb, rb_out))
    for m in ret_moves:
        m.start()
    for m in cot_moves:
        m.wait()
    grs[pl.ds(0, main), :] = ca[...]
    from_tail(cb, grs, main)
    cot = grs[mine, :].astype(f32)
    logit = jnp.sum(cot * mid[...], axis=1, keepdims=True) * gate * (1.0 - gate)
    grs[mine, :] = (gate * cot).astype(bf16)
    share_g = mirror(2, grs)
    share_g.start()
    up_back(grs, w4, d2, mine)
    share_g.wait()
    up_back(grs, w4, d2, theirs)
    down_back(d2, w3, theirs, to_send)
    send2 = partial_send(2)
    send2.start()
    down_back(d2, w3, mine, to_mid)
    send2.wait()
    gm[mine, :] = (mid[...] + grs[mine, :].astype(f32) + precv[0].astype(f32)).astype(bf16)
    share_gm = mirror(3, gm)
    share_gm.start()
    up_back(gm, w2, d1, mine)
    share_gm.wait()
    up_back(gm, w2, d1, theirs)
    down_back(d1, w1, theirs, to_send)
    send3 = partial_send(3)
    send3.start()
    down_back(d1, w1, mine, to_mid)
    cent_s[...] = jnp.sum(logit * xg[mine, :].astype(f32), axis=0, keepdims=True)
    share_c = pair(cent_s, cent_r, xs.at[4], xr.at[4])
    share_c.start()
    for m in ret_moves:
        m.wait()
    send3.wait()
    slots = (
        mid[...] + gm[mine, :].astype(f32) + precv[1].astype(f32) + logit * cent[...].astype(f32)
    ).astype(bf16)
    sa[...] = slots[:main]
    to_tail(slots[main:], sb)
    back_moves = (move(4, sa, ga_out), move(5, sb, gb_out))
    for m in back_moves:
        m.start()
    def weight_grad(i, left, right, to, out):
        wide_n = right.shape[1]

        def body(n, carry):
            m, c = n // (wide_n // WN), lax.rem(n, wide_n // WN)
            rows = pl.ds(pl.multiple_of(m * WM, WM), WM)
            cols = pl.ds(pl.multiple_of(c * WN, WN), WN)
            to[rows, cols] = mm(left[:, rows], right[:, cols], (0, 0)).astype(bf16)
            return carry

        lax.fori_loop(0, left.shape[1] // WM * (wide_n // WN), body, 0)
        store(i, to, out)

    weight_grad(0, act2, grs, w4, gw4_o)
    weight_grad(1, mlo, d2, w3, gw3_o)
    weight_grad(2, act1, gm, w2, gw2_o)
    weight_grad(3, xg, d1, w1, gw1_o)
    share_c.wait()
    gcent[...] = cent_s[...] + cent_r[...]
    for copy in outs:
        copy.wait()
    for m in back_moves:
        m.wait()


def run_experts(experts, slots, tails, cots, cot_tails, centroid, weights):
    width, hid = weights[0].shape
    main = slots.shape[0]
    tail = tails.shape[0] // experts // PARTS
    own = main + experts * tail
    both = 2 * own

    def sds(*shape, dtype=bf16):
        return jax.ShapeDtypeStruct(shape, dtype)

    travel = [sds(*slots.shape), sds(*tails.shape)] * 2
    wide = [sds(width, hid), sds(hid, width)] * 2
    return pl.pallas_call(
        functools.partial(experts_kernel, experts, tail),
        out_shape=travel + [sds(1, width, dtype=f32)] + wide,
        in_specs=[VM, VM, ANY, ANY, VM, ANY, ANY, ANY, ANY],
        out_specs=[ANY] * 4 + [VM] + [ANY] * 4,
        scratch_shapes=[
            pltpu.VMEM((width, hid), bf16),
            pltpu.VMEM((hid, width), bf16),
            pltpu.VMEM((width, hid), bf16),
            pltpu.VMEM((hid, width), bf16),
            pltpu.VMEM((both, width), bf16),
            pltpu.VMEM((both, width), bf16),
            pltpu.VMEM((both, width), bf16),
            pltpu.VMEM((both, width), bf16),
            pltpu.VMEM((both, hid), bf16),
            pltpu.VMEM((both, hid), bf16),
            pltpu.VMEM((both, hid), bf16),
            pltpu.VMEM((both, hid), bf16),
            pltpu.VMEM((own, width), f32),
            pltpu.VMEM((own, width), bf16),
            pltpu.VMEM((2, own, width), bf16),
            pltpu.VMEM(slots.shape, bf16),
            pltpu.VMEM(tails.shape, bf16),
            pltpu.VMEM(slots.shape, bf16),
            pltpu.VMEM(tails.shape, bf16),
            pltpu.VMEM((1, width), f32),
            pltpu.VMEM((1, width), f32),
            DMA((4,)),
            DMA((4,)),
            DMA((4,)),
            DMA((4,)),
            DMA((5,)),
            DMA((5,)),
            DMA((6, experts)),
            DMA((6, experts)),
            DMA((6,)),
        ],
        compiler_params=pltpu.CompilerParams(
            collective_id=2, has_side_effects=True, vmem_limit_bytes=VMEM_MAX
        ),
        name="experts_pass",
    )(slots, tails, cots, cot_tails, centroid, *weights)

def back_kernel(experts, tail, *refs):
    (ra, rb, ga, gb, dm, dt, gains, cot_h, res_h, tok_h, packed_h, probs_h, mixed_h, wall_h) = refs[:14]
    out_o, ig_o, gqkv_o, gout_o, ggain_o = refs[14:19]
    (cot, res, tok, packed, probs, mixed, wqkv, wout, normed, gatt, gmix, gpk, so, si, perm) = refs[19:34]
    keeps, psends, precvs, rv1s, rv2s, rv3s = (refs[34 + 6 * i : 40 + 6 * i] for i in range(6))
    lsem, sends, recvs, asend, arecv, alocal = refs[70:]
    me, core = lax.axis_index("expert"), lax.axis_index("hidden")
    other = 1 - core
    my_z, my_y, my_x = me // 4, lax.rem(me // 2, 2), lax.rem(me, 2)
    rows, width = tok.shape
    block = width // PARTS

    loads = {}
    for i, (name, h, v) in enumerate(
        (
            ("res", res_h, res),
            ("cot", cot_h, cot),
            ("mixed", mixed_h, mixed),
            ("wout", wall_h.at[:, pl.ds(3 * width + 128, width)], wout),
            ("probs", probs_h, probs),
            ("packed", packed_h, packed),
            ("tok", tok_h, tok),
            ("wqkv", wall_h.at[:, pl.ds(0, 3 * width)], wqkv),
        )
    ):
        loads[name] = pltpu.make_async_copy(h, v, lsem.at[i])
        loads[name].start()
    greet(experts, me, core, other)

    def join_slots(slots, tails):
        parts = []
        for q in range(PARTS):
            parts.append(
                mm(dm[...], slots[:, q * block : (q + 1) * block], (0, 0))
                + mm(dt[q], tails[...], (0, 0))
            )
        return jnp.concatenate(parts, axis=1)

    piece = SEQ // experts
    seats = MICRO * PER

    def to_blocks(value):
        shape = (rows, rows)
        to = lax.broadcasted_iota(jnp.int32, shape, 0)
        at = lax.broadcasted_iota(jnp.int32, shape, 1)
        b, s, q = to // (seats * piece), to // piece % seats, to % piece
        turn = (at == s * SEQ + b * piece + q).astype(f32).astype(bf16)
        return mm(turn, value).astype(bf16)

    def move(i, src, dst):
        return Spread(experts, me, core, src, dst, asend.at[i], arecv.at[i], alocal.at[i])

    my_a = jnp.where(core == 0, my_x, my_y)
    my_b = jnp.where(core == 0, my_y, my_x)

    def near(a_step, b_step):
        a, b = (1 - my_a if a_step else my_a), (1 - my_b if b_step else my_b)
        x, y = jnp.where(core == 0, a, b), jnp.where(core == 0, b, a)
        return my_z * 4 + y * 2 + x

    def remote(c, stage, src, dst, to, to_core):
        return pltpu.make_async_remote_copy(
            src, dst, sends.at[c, stage], recvs.at[c, stage],
            device_id=(to, to_core), device_id_type=MESH,
        )

    def pair_copy(c):
        return remote(c, 0, psends[c], precvs[c], me, other)

    def a_copy(c):
        return remote(c, 1, psends[c].at[pl.ds(0, 256)], rv1s[c], near(True, False), core)

    def b_copy(c):
        return remote(c, 2, psends[c].at[pl.ds(256, 128)], rv2s[c], near(False, True), core)

    def z_copy(c, dz):
        to_z = lax.rem(my_z + dz, 4)
        src = psends[c].at[pl.ds(pl.multiple_of(384 + to_z * 32, 32), 32)]
        return remote(c, 2 + dz, src, rv3s[c].at[dz - 1], to_z * 4 + my_y * 2 + my_x, core)

    def place(c, t, cols):
        keeps[c][:, cols] = t[: width // 2]
        psends[c][:, cols] = t[width // 2 :].astype(bf16)

    at = lax.broadcasted_iota(jnp.int32, (1, width), 1)
    goes = jnp.where(at < width // 2, core, other)
    high, mid_ = at // 256 % 2, at // 128 % 2
    to_x, to_y = jnp.where(goes == 0, high, mid_), jnp.where(goes == 0, mid_, high)
    source = (((at // 32 % 4) * 4 + to_y * 2 + to_x) * 2 + goes) * 32 + at % 32
    perm[...] = (lax.broadcasted_iota(jnp.int32, (width, width), 0) == source).astype(f32).astype(bf16)

    def compute(c, left, right, starts, size):
        for n, start in enumerate(starts):
            place(c, mm(left[...], right[:, start : start + size], (0, 0)), pl.ds(n * size, size))
        pair_copy(c).start()

    half_a = pl.ds(pl.multiple_of(my_a * 256, 256), 256)
    half_a_out = pl.ds(pl.multiple_of((1 - my_a) * 256, 256), 256)
    base_b = my_a * 256
    half_b = pl.ds(pl.multiple_of(base_b + my_b * 128, 128), 128)
    half_b_out = pl.ds(pl.multiple_of(base_b + (1 - my_b) * 128, 128), 128)

    def after_pair(c):
        pair_copy(c).wait()
        keep = keeps[c]
        keep[...] += precvs[c][...].astype(f32)
        psends[c][pl.ds(0, 256), :] = keep[half_a_out, :].astype(bf16)
        a_copy(c).start()

    def after_a(c):
        a_copy(c).wait()
        keep = keeps[c]
        keep[half_a, :] += rv1s[c][...].astype(f32)
        psends[c][pl.ds(256, 128), :] = keep[half_b_out, :].astype(bf16)
        b_copy(c).start()

    def after_b(c):
        b_copy(c).wait()
        keep = keeps[c]
        keep[half_b, :] += rv2s[c][...].astype(f32)
        psends[c][pl.ds(384, 128), :] = keep[half_b, :].astype(bf16)
        for dz in range(1, 4):
            z_copy(c, dz).start()

    def after_z(c, pieces):
        for dz in range(1, 4):
            z_copy(c, dz).wait()
        at = pl.ds(pl.multiple_of(base_b + my_b * 128 + my_z * 32, 32), 32)
        total = keeps[c][at, :]
        for dz in range(3):
            total = total + rv3s[c][dz].astype(f32)
        size = total.shape[1] // len(pieces)
        for n, (out, start) in enumerate(pieces):
            out[:, start : start + size] = total[:, n * size : (n + 1) * size]

    gain_a, gain_f = gains[0:1, :], gains[1:2, :]
    loads["res"].wait()
    so[...] = to_blocks((res[...] + join_slots(ra, rb)).astype(bf16))
    out_move = move(0, so, out_o)
    out_move.start()
    unit, inv = norm_parts(res[...])
    grad_shared = join_slots(ga, gb)
    ffn_sums = jnp.sum(grad_shared * unit, axis=0, keepdims=True)
    loads["cot"].wait()
    grad = cot[...].astype(f32) + norm_back(unit, inv, gain_f, grad_shared)
    res[...] = grad
    gatt[...] = grad.astype(bf16)
    loads["mixed"].wait()
    mixed[...] = mm(mixed[...], perm[...]).astype(bf16)
    compute(0, mixed, gatt, (0, width // 2), width // 2)
    loads["wout"].wait()
    gmix[...] = mm(gatt[...], wout[...], (1, 1)).astype(bf16)
    after_pair(0)
    loads["probs"].wait()
    loads["packed"].wait()
    lane = lax.broadcasted_iota(jnp.int32, (PACK, 2 * HEAD), 1)
    first = lane < HEAD

    def stacked(v):
        zero = jnp.zeros_like(v)
        return jnp.concatenate([jnp.where(first, v, zero), jnp.where(first, zero, v)], axis=0)

    def head_pair(p, h):
        at = pl.ds(pl.multiple_of(p * PACK, PACK), PACK)
        lo = h * 2 * HEAD
        q = packed[at, lo : lo + 2 * HEAD]
        k = packed[at, width + lo : width + lo + 2 * HEAD]
        v = packed[at, 2 * width + lo : 2 * width + lo + 2 * HEAD]
        gs = stacked(gmix[at, lo : lo + 2 * HEAD])
        pr_lo = probs[p * (HEADS // 2) + h]
        pr = pr_lo.astype(f32)
        gp = mm(gs, v, (1, 1))
        gv = mm(pr_lo, gs, (0, 0))
        inner = jnp.sum(pr * gp, axis=1, keepdims=True)
        ds_ = (pr * (gp - inner)).astype(bf16)
        t = mm(ds_, k)
        gq = jnp.where(first, t[:PACK], t[PACK:]) * 0.125
        gk = mm(ds_, stacked(q), (0, 0)) * 0.125
        gpk[at, lo : lo + 2 * HEAD] = gq.astype(bf16)
        gpk[at, width + lo : width + lo + 2 * HEAD] = gk.astype(bf16)
        gpk[at, 2 * width + lo : 2 * width + lo + 2 * HEAD] = gv.astype(bf16)

    part = width // 4

    def group_pieces(g):
        return tuple(part * g + width * i for i in range(3))

    def group(g):
        def packs(p, carry):
            for i in range(2):
                for h in range(HEADS // 8):
                    head_pair(p * 2 + i, g * (HEADS // 8) + h)
            return carry

        lax.fori_loop(0, MICRO // 2, packs, 0)
        compute(1 + g, normed, gpk, group_pieces(g), part)

    def finish(g):
        after_z(1 + g, [(gqkv_o, start) for start in group_pieces(g)])

    loads["tok"].wait()
    unit, inv = norm_parts(tok[...].astype(f32))
    normed[...] = mm((unit * gain_a).astype(bf16), perm[...]).astype(bf16)
    group(0)
    after_a(0)
    group(1)
    after_pair(1)
    after_b(0)
    group(2)
    after_pair(2)
    after_a(1)
    group(3)
    after_pair(3)
    after_a(2)
    after_b(1)
    loads["wqkv"].wait()
    grad_normed = mm(gpk[...], wqkv[...], (1, 1))
    unit, inv = norm_parts(tok[...].astype(f32))
    attn_sums = jnp.sum(grad_normed * unit, axis=0, keepdims=True)
    si[...] = to_blocks((res[...] + norm_back(unit, inv, gain_a, grad_normed)).astype(bf16))
    ig_move = move(1, si, ig_o)
    after_pair(4)
    ig_move.start()
    sums = jnp.where(lax.broadcasted_iota(jnp.int32, (128, width), 0) < 64, attn_sums, ffn_sums)
    sums_hi = sums.astype(bf16)
    sums_lo = (sums - sums_hi.astype(f32)).astype(bf16)
    place(5, mm(perm[...], sums_hi, (0, 1)) + mm(perm[...], sums_lo, (0, 1)), pl.ds(0, 128))
    pair_copy(5).start()
    after_a(3)
    after_b(2)
    after_z(0, [(gout_o, 0)])
    after_pair(5)
    finish(0)
    after_a(4)
    after_b(3)
    finish(1)
    after_a(5)
    after_b(4)
    finish(2)
    after_b(5)
    finish(3)
    after_z(5, [(ggain_o, 0)])
    out_move.wait()
    ig_move.wait()


def run_back(experts, tail, slots, tails, grads, grad_tails, d_main, d_tail, gains, cot, residual, tok, packed, probs, mixed, w_all):
    rows, width = tok.shape

    def sds(*shape, dtype=bf16):
        return jax.ShapeDtypeStruct(shape, dtype)

    widths = (width,) + (3 * width // 4,) * 4 + (128,)
    scratch = [
        pltpu.VMEM(cot.shape, bf16),
        pltpu.VMEM(residual.shape, f32),
        pltpu.VMEM(tok.shape, bf16),
        pltpu.VMEM(packed.shape, bf16),
        pltpu.VMEM(probs.shape, bf16),
        pltpu.VMEM(mixed.shape, bf16),
        pltpu.VMEM((width, 3 * width), bf16),
        pltpu.VMEM((width, width), bf16),
        pltpu.VMEM((rows, width), bf16),
        pltpu.VMEM((rows, width), bf16),
        pltpu.VMEM((rows, width), bf16),
        pltpu.VMEM((rows, 3 * width), bf16),
        pltpu.VMEM((rows, width), bf16),
        pltpu.VMEM((rows, width), bf16),
        pltpu.VMEM((width, width), bf16),
    ]
    scratch += [pltpu.VMEM((width // 2, w), f32) for w in widths]
    for part in (2, 2, 4, 8):
        scratch += [pltpu.VMEM((width // part, w), bf16) for w in widths]
    scratch += [pltpu.VMEM((3, 32, w), bf16) for w in widths]
    scratch += [
        DMA((8,)),
        DMA((6, 6)),
        DMA((6, 6)),
        DMA((2, experts)),
        DMA((2, experts)),
        DMA((2,)),
    ]
    return pl.pallas_call(
        functools.partial(back_kernel, experts, tail),
        out_shape=[sds(rows, width), sds(rows, width), sds(32, 3 * width, dtype=f32), sds(32, width, dtype=f32), sds(32, 128, dtype=f32)],
        in_specs=[VM] * 7 + [ANY] * 7,
        out_specs=[ANY, ANY, VM, VM, VM],
        scratch_shapes=scratch,
        compiler_params=pltpu.CompilerParams(
            collective_id=3, has_side_effects=True, vmem_limit_bytes=VMEM_MAX
        ),
        name="attention_back",
    )(slots, tails, grads, grad_tails, d_main, d_tail, gains, cot, residual, tok, packed, probs, mixed, w_all)


def front_kernel(experts, tail, *refs):
    (tokens, cots, routes, orders, deal, lengths, g_attn, g_ffn, w_qkv, w_out) = refs[:10]
    (slots_o, tails_o, cslots_o, ctails_o, deal_o, dm_o, dt_o, gains_o, cot_o, res_o, tok_o, packed_o, probs_o, mixed_o, w_o) = refs[10:25]
    (st, sl, rt, rl, rc, tok, cot, w, packed, probs, mixed, res, shared, dm, dt, ftm, masks, ss, stl, cs, ctl) = refs[25:46]
    zs, zr, as_, ar, bs, br, ps, pr, asend, arecv, alocal, osem = refs[46:]
    me, core = lax.axis_index("expert"), lax.axis_index("hidden")
    other = 1 - core
    my_z, my_y, my_x = me // 4, lax.rem(me // 2, 2), lax.rem(me, 2)
    rows, width = tok.shape
    piece = SEQ // experts
    seats = MICRO * PER
    block = width // PARTS
    step = w_qkv.shape[0]
    per_dest = experts and dims(experts, width)[0]
    main = per_dest - tail
    capacity = per_dest // MICRO

    def iota(shape, axis):
        return lax.broadcasted_iota(jnp.int32, shape, axis)

    def one_hot(test):
        return test.astype(f32).astype(bf16)

    own_rows = pl.ds(pl.multiple_of((me * 2 + core) * step, step), step)
    gain_at, out_at = 3 * width, 3 * width + 128
    w[own_rows, :gain_at] = w_qkv[...]
    w[own_rows, out_at:] = w_out[...]
    eye = iota((step, step), 0) == iota((step, step), 1)

    def as_column(row):
        return jnp.sum(jnp.where(eye, row[...].astype(f32), 0.0), axis=1, keepdims=True)

    gain_cols = jnp.where(iota((step, 128), 1) < 64, as_column(g_attn), as_column(g_ffn))
    w[own_rows, gain_at:out_at] = gain_cols.astype(bf16)
    cuts = ((0, out_at), (out_at, width))

    line = lax.rem(me, 4)
    a_to = jnp.where(core == 0, my_z * 4 + my_y * 2 + 1 - my_x, my_z * 4 + 2 - 2 * my_y + my_x)
    b_to = jnp.where(core == 0, my_z * 4 + 2 - 2 * my_y + my_x, my_z * 4 + my_y * 2 + 1 - my_x)
    shift_a, shift_b = a_to - me, b_to - me

    def send(j, e, sem_s, sem_r, to, to_core):
        start, size = cuts[j]
        ref = w.at[pl.ds(pl.multiple_of((e * 2 + core) * step, step), step), pl.ds(start, size)]
        return pltpu.make_async_remote_copy(
            ref, ref, sem_s, sem_r, device_id=(to, to_core), device_id_type=MESH
        )

    def up(j, d):
        s = my_z - d
        return send(j, s * 4 + line, zs.at[j, d], zr.at[j, s], me + 4, core)

    def down(j, d):
        s = my_z + d
        return send(j, s * 4 + line, zs.at[j, 4 + d], zr.at[j, s], me - 4, core)

    def a_copy(j, s):
        return send(j, s * 4 + line, as_.at[j, s], ar.at[j, s], a_to, core)

    def b_copy(j, f, s):
        return send(j, s * 4 + line + f * shift_a, bs.at[j, 4 * f + s], br.at[j, 4 * f + s], b_to, core)

    def p_copy(j, f, s):
        e = s * 4 + line + (f % 2) * shift_a + (f // 2) * shift_b
        return send(j, e, ps.at[j, 4 * f + s], pr.at[j, 4 * f + s], me, other)

    def release(j, s):
        b_copy(j, 0, s).start()
        a_copy(j, s).start()
        p_copy(j, 0, s).start()

    def chain(j, d):
        @pl.when(my_z >= d)
        def _():
            if d:
                up(j, d).wait_recv()

            @pl.when(my_z < 3)
            def _():
                up(j, d).start()

            if d:
                release(j, my_z - d)

        @pl.when(my_z + d <= 3)
        def _():
            if d:
                down(j, d).wait_recv()

            @pl.when(my_z > 0)
            def _():
                down(j, d).start()

            if d:
                release(j, my_z + d)

        if not d:
            release(j, my_z)

    def places():
        return [lax.rem(my_z + k, 4) for k in (0, 1, 3, 2)]

    def fan_a(j):
        for s in places():
            a_copy(j, s).wait_recv()
            b_copy(j, 1, s).start()
            p_copy(j, 1, s).start()

    def fan_b(j):
        for f in range(2):
            for s in places():
                b_copy(j, f, s).wait_recv()
                p_copy(j, 2 + f, s).start()

    def fan_p(j):
        for f in range(4):
            for s in range(4):
                p_copy(j, f, s).wait_recv()

    def all_sent(j):
        for d in range(4):

            @pl.when((my_z >= d) & (my_z < 3))
            def _():
                up(j, d).wait_send()

            @pl.when((my_z + d <= 3) & (my_z > 0))
            def _():
                down(j, d).wait_send()

        for s in range(4):
            a_copy(j, s).wait_send()
            for f in range(2):
                b_copy(j, f, s).wait_send()
            for f in range(4):
                p_copy(j, f, s).wait_send()

    greet(experts, me, core, other)
    chain(0, 0)

    def move(i, src, dst):
        return Spread(experts, me, core, src, dst, asend.at[i], arecv.at[i], alocal.at[i])

    group = deal.shape[1]
    deal_row = deal[pl.ds(core, 1), :]
    length_row = lengths[pl.ds(core, 1), :]
    spread_out = one_hot(iota((group, rows), 1) // piece == iota((group, rows), 0))
    wide = jnp.broadcast_to(deal_row.astype(f32), (8, group)).astype(bf16)
    goal = mm(wide, spread_out)[0:1].astype(jnp.int32) * piece + iota((1, rows), 1) % piece
    ftm[...] = one_hot(iota((rows, rows), 0) == goal)
    st[...] = mm(ftm[...], tokens[...]).astype(bf16)
    lab = jnp.where(iota((128, rows), 0) < 64, routes[...], orders[...]).astype(f32).astype(bf16)
    sl[...] = mm(ftm[...], lab, (1, 1)).astype(bf16)
    tok_moves = (move(0, st, rt), move(1, sl, rl))
    for m in tok_moves:
        m.start()
    chain(0, 1)
    cs[...] = mm(ftm[...], cots[...]).astype(bf16)
    chain(0, 2)
    chain(0, 3)
    chain(1, 0)
    fan_a(0)
    chain(1, 1)
    chain(1, 2)
    chain(1, 3)
    for m in tok_moves:
        m.wait()
    cot_move = move(2, cs, rc)
    cot_move.start()

    outs = []

    def store(i, ref, out):
        copy = pltpu.make_async_copy(ref, out, osem.at[i])
        copy.start()
        outs.append(copy)

    store(0, ftm, deal_o)
    to, at = iota((rows, rows), 0), iota((rows, rows), 1)
    b, s, q = to // (seats * piece), to // piece % seats, to % piece
    turn = one_hot(at == s * SEQ + b * piece + q)
    tok[...] = mm(turn, rt[...], (0, 0)).astype(bf16)
    store(1, tok, tok_o)
    lab_col = mm(turn, rl[...], (0, 0))
    lab_row = mm(rl[...], turn, (0, 0))
    fan_a(1)
    ranks, heads_at, oks = [], [], []
    own = [
        jnp.sum(jnp.where(deal_row == me * seats + i, length_row, 0), axis=1, keepdims=True)
        for i in range(seats)
    ]
    posr, posc = iota((1, PACK), 1), iota((PACK, 1), 0)
    near_ = (iota((PACK, PACK), 0) // SEQ == iota((PACK, PACK), 1) // SEQ) & (
        iota((PACK, PACK), 1) <= iota((PACK, PACK), 0)
    )
    for p in range(MICRO):
        low, high = own[PER * p], own[PER * p + 1]
        here_r = posr % SEQ < jnp.where(posr < SEQ, low, high)
        here_c = posc % SEQ < jnp.where(posc < SEQ, low, high)
        masks[p] = (near_ & here_r).astype(f32)
        cols = slice(p * PACK, (p + 1) * PACK)
        route_r = lab_row[0:1, cols]
        key_r = lab_row[64:65, cols] * PER + (posr // SEQ).astype(f32)
        route_c = lab_col[cols, 0:1]
        key_c = lab_col[cols, 64:65] * PER + (posc // SEQ).astype(f32)
        ahead = jnp.sum(
            ((route_c == route_r) & (key_c < key_r) & here_c).astype(f32), axis=0, keepdims=True
        ).astype(jnp.int32)
        base = p * capacity + ahead
        good = here_r & (ahead < capacity)
        route_i = route_r.astype(jnp.int32)
        heads_at.append(jnp.where(good & (base < main), route_i * main + base, -1))
        oks.append(jnp.where(good & (base >= main), route_i * (PARTS * tail) + base - main, -PARTS * PARTS * tail))
    head_row = jnp.concatenate(heads_at, axis=1)
    tail_row = jnp.concatenate(oks, axis=1)
    dm[...] = one_hot(iota(dm.shape, 0) == head_row)
    for part in range(PARTS):
        dt[part] = one_hot(iota(dt.shape[1:], 0) == tail_row + part * tail)
    store(2, dm, dm_o)
    store(3, dt, dt_o)

    def split(ref, to_main, to_tails):
        to_main[...] = mm(dm[...], ref[...]).astype(bf16)
        total = None
        for part in range(PARTS):
            term = mm(dt[part], ref[:, part * block : (part + 1) * block])
            total = term if total is None else total + term
        to_tails[...] = total.astype(bf16)

    inputs = tok[...].astype(f32)
    unit, inv = norm_parts(inputs)
    res[...] = unit
    fan_b(0)
    fan_p(0)
    big = iota((128, 128), 0) == iota((128, 128), 1)

    def gain_row(lane):
        parts = []
        for j in range(width // 128):
            col = w[128 * j : 128 * (j + 1), gain_at:out_at].astype(f32)[:, lane : lane + 1]
            parts.append(jnp.sum(jnp.where(big, col, 0.0), axis=0, keepdims=True))
        return jnp.concatenate(parts, axis=1)

    gain_a, gain_f = gain_row(0), gain_row(64)
    gains_o[0:1, :] = gain_a
    gains_o[1:2, :] = gain_f
    shared[...] = (res[...] * gain_a).astype(bf16)

    def project(n, carry):
        cols = pl.ds(pl.multiple_of(n * 256, 256), 256)
        packed[:, cols] = mm(shared[...], w[:, cols]).astype(bf16)
        return carry

    lax.fori_loop(0, 3 * width // 256, project, 0)
    store(5, packed, packed_o)
    fan_b(1)
    first = iota((PACK, 2 * HEAD), 1) < HEAD

    def pack(p, carry):
        at = pl.ds(pl.multiple_of(p * PACK, PACK), PACK)
        mask = masks[p] > 0.5
        mask = jnp.concatenate([mask, mask], axis=0)
        for h in range(HEADS // 2):
            lo = h * 2 * HEAD
            q = packed[at, lo : lo + 2 * HEAD]
            k = packed[at, width + lo : width + lo + 2 * HEAD]
            v = packed[at, 2 * width + lo : 2 * width + lo + 2 * HEAD]
            zero = jnp.zeros_like(q)
            qs = jnp.concatenate([jnp.where(first, q, zero), jnp.where(first, zero, q)], axis=0)
            scores = jnp.where(mask, mm(qs, k, (1, 1)) * 0.125, -1e30)
            e = jnp.exp(scores - jnp.max(scores, axis=1, keepdims=True))
            prob = (e / jnp.sum(e, axis=1, keepdims=True)).astype(bf16)
            probs[p * (HEADS // 2) + h] = prob
            t = mm(prob, v)
            mixed[at, lo : lo + 2 * HEAD] = jnp.where(first, t[:PACK], t[PACK:]).astype(bf16)
        return carry

    lax.fori_loop(0, MICRO, pack, 0)
    store(6, probs, probs_o)
    fan_p(1)
    store(4, w, w_o)
    store(7, mixed, mixed_o)
    residual = tok[...].astype(f32) + mm(mixed[...], w[:, out_at:])
    res[...] = residual
    store(8, res, res_o)
    unit, inv = norm_parts(residual)
    shared[...] = (unit * gain_f).astype(bf16)
    split(shared, ss, stl)
    slot_moves = (move(3, ss, slots_o), move(4, stl, tails_o))
    cot_move.wait()
    for m in slot_moves:
        m.start()
    cot[...] = mm(turn, rc[...], (0, 0)).astype(bf16)
    store(9, cot, cot_o)
    split(cot, cs, ctl)
    store(10, cs, cslots_o)
    store(11, ctl, ctails_o)
    all_sent(0)
    all_sent(1)
    for copy in outs:
        copy.wait()
    for m in slot_moves:
        m.wait()


def run_front(experts, tail, tokens, cots, routes, orders, deal, lengths, g_attn, g_ffn, w_qkv, w_out):
    rows, width = tokens.shape
    per_dest = dims(experts, width)[0]
    main = (per_dest - tail) * experts
    side = experts * PARTS * tail

    def sds(*shape, dtype=bf16):
        return jax.ShapeDtypeStruct(shape, dtype)

    tails = (side, width // PARTS)
    out_shape = [
        sds(main, width),
        sds(*tails),
        sds(main, width),
        sds(*tails),
        sds(rows, rows),
        sds(main, rows),
        sds(PARTS, side, rows),
        sds(2, width, dtype=f32),
        sds(rows, width),
        sds(rows, width, dtype=f32),
        sds(rows, width),
        sds(rows, 3 * width),
        sds(MICRO * HEADS // 2, 2 * PACK, PACK),
        sds(rows, width),
        sds(width, 4 * width + 128),
    ]
    vm = pltpu.VMEM
    return pl.pallas_call(
        functools.partial(front_kernel, experts, tail),
        out_shape=out_shape,
        in_specs=[VM] * 10,
        out_specs=[ANY] * 7 + [VM] + [ANY] * 7,
        scratch_shapes=[
            vm((rows, width), bf16),
            vm((rows, 128), bf16),
            vm((rows, width), bf16),
            vm((rows, 128), bf16),
            vm((rows, width), bf16),
            vm((rows, width), bf16),
            vm((rows, width), bf16),
            vm((width, 4 * width + 128), bf16),
            vm((rows, 3 * width), bf16),
            vm((MICRO * HEADS // 2, 2 * PACK, PACK), bf16),
            vm((rows, width), bf16),
            vm((rows, width), f32),
            vm((rows, width), bf16),
            vm((main, rows), bf16),
            vm((PARTS, side, rows), bf16),
            vm((rows, rows), bf16),
            vm((MICRO, PACK, PACK), f32),
            vm((main, width), bf16),
            vm(tails, bf16),
            vm((main, width), bf16),
            vm(tails, bf16),
            DMA((2, 8)),
            DMA((2, 4)),
            DMA((2, 4)),
            DMA((2, 4)),
            DMA((2, 8)),
            DMA((2, 8)),
            DMA((2, 16)),
            DMA((2, 16)),
            DMA((5, experts)),
            DMA((5, experts)),
            DMA((5,)),
            DMA((12,)),
        ],
        compiler_params=pltpu.CompilerParams(
            collective_id=1, has_side_effects=True, vmem_limit_bytes=VMEM_MAX
        ),
        name="attention_front",
    )(tokens, cots, routes, orders, deal, lengths, g_attn, g_ffn, w_qkv, w_out)


def fast_shards(
    tokens,
    lengths,
    deal,
    routes,
    slot_order,
    gain_attn,
    gain_ffn,
    w_qkv,
    w_out,
    centroids,
    expert_in,
    expert_out,
    second_in,
    second_out,
    cotangent,
):
    width = tokens.shape[1]
    experts = lax.axis_size("expert")
    tail = dims(experts, width)[2]
    (slots, tails, cots, cot_tails, dealt, d_main, d_tail, gains, grad_output, residual, tok,
     packed, probs, mixed, w_all) = run_front(
        experts, tail, tokens, cotangent, routes.reshape(1, -1), slot_order.reshape(1, -1), deal, lengths,
        gain_attn[None], gain_ffn[None], w_qkv, w_out,
    )
    ra, rb, ga, gb, g_cent, *g_experts = run_experts(
        experts, slots, tails, cots, cot_tails, centroids,
        (expert_in[0], expert_out[0], second_in[0], second_out[0]),
    )
    out_r, ig_r, g_qkv, g_out, g_gain = run_back(
        experts, tail, ra, rb, ga, gb, d_main, d_tail, gains, grad_output, residual, tok,
        packed, probs, mixed, w_all,
    )
    return (
        mm(dealt, out_r, (0, 0)).astype(bf16),
        mm(dealt, ig_r, (0, 0)),
        g_gain[:, 0],
        g_gain[:, 64],
        g_qkv,
        g_out,
        g_cent,
        *(g.astype(f32)[None] for g in g_experts),
    )


def gather_hidden(rows):
    return lax.all_gather(rows, "hidden", axis=0, tiled=True)


def sum_hidden(terms):
    return lax.psum_scatter(terms, "hidden", scatter_dimension=0, tiled=True)


def swap(blocks):
    return lax.all_to_all(blocks, "expert", split_axis=0, concat_axis=0, tiled=True)


def plain_shards(
    tokens,
    lengths,
    deal,
    routes,
    slot_order,
    gain_attn,
    gain_ffn,
    w_qkv,
    w_out,
    centroids,
    expert_in,
    expert_out,
    second_in,
    second_out,
    cotangent,
):
    width = tokens.shape[1]
    experts = lax.axis_size("expert")
    piece = SEQ // experts
    seats = MICRO * PER
    group = experts * seats
    rows = seats * SEQ
    capacity = (9 * PACK + 8 * experts - 1) // (8 * experts)
    per_dest = MICRO * capacity
    my_expert = lax.axis_index("expert")
    my_hidden = lax.axis_index("hidden")

    deal_row = lax.dynamic_index_in_dim(deal, my_hidden, 0, keepdims=False)
    length_row = lax.dynamic_index_in_dim(lengths, my_hidden, 0, keepdims=False)
    ids = jnp.arange(group, dtype=jnp.int32)
    inverse = jnp.sum(jnp.where(deal_row[None, :] == ids[:, None], ids[None, :], 0), axis=1)
    own = my_expert * seats + jnp.arange(seats, dtype=jnp.int32)
    own_lengths = jnp.sum(
        jnp.where(deal_row[None, :] == own[:, None], length_row[None, :], 0), axis=1
    )

    def to_dealt(flat):
        pieces = jnp.take(flat.reshape(group, piece, flat.shape[1]), inverse, axis=0)
        return lax.all_to_all(
            pieces.reshape(experts, seats, piece, flat.shape[1]),
            "expert",
            split_axis=0,
            concat_axis=2,
            tiled=True,
        ).reshape(rows, flat.shape[1])

    labels = jnp.concatenate([routes, slot_order], axis=1)
    lab = to_dealt(labels)
    tok = to_dealt(tokens)
    grad_output = to_dealt(cotangent)

    cat = jnp.concatenate(
        [w_qkv, w_out, gain_attn[:, None], gain_ffn[:, None], jnp.zeros((w_qkv.shape[0], 126), bf16)],
        axis=1,
    )
    cat = lax.all_gather(cat, ("expert", "hidden"), axis=0, tiled=True)
    qkv_w = cat[:, : 3 * width]
    out_w = cat[:, 3 * width : 4 * width]
    attn_gain = cat[:, 4 * width].astype(f32)[None, :]
    ffn_gain = cat[:, 4 * width + 1].astype(f32)[None, :]

    route = lab[:, 0].reshape(MICRO, PACK)
    order = lab[:, 1].reshape(MICRO, PACK)
    positions = jnp.arange(PACK, dtype=jnp.int32)
    seat = positions // SEQ
    pack_lengths = own_lengths.reshape(MICRO, PER)
    limit = jnp.repeat(pack_lengths, SEQ, axis=1)
    present = (positions % SEQ)[None, :] < limit
    priority = order * PER + seat[None, :]
    ahead = jnp.sum(
        (
            (route[:, :, None] == route[:, None, :])
            & (priority[:, None, :] < priority[:, :, None])
            & present[:, None, :]
        ).astype(jnp.int32),
        axis=2,
    )
    accepted = (present & (ahead < capacity)).reshape(rows)
    target = (
        route * per_dest + jnp.arange(MICRO, dtype=jnp.int32)[:, None] * capacity + ahead
    ).reshape(rows)
    target = jnp.where(accepted, target, -1)
    slot_ids = jnp.arange(experts * per_dest, dtype=jnp.int32)
    dispatch = (slot_ids[:, None] == target[None, :]).astype(bf16)

    def to_experts(values):
        out = mm(dispatch, values).astype(bf16)
        return swap(out.reshape(experts, per_dest, width)).reshape(experts * per_dest, width)

    cot_arrived = to_experts(grad_output)

    inputs = tok.astype(f32)
    unit_a, inv_a = norm_parts(inputs)
    normed = (unit_a * attn_gain).astype(bf16)
    packed = mm(normed, qkv_w).astype(bf16)
    allowed = (
        (seat[:, None] == seat[None, :]) & (positions[None, :] <= positions[:, None])
    )[None] & present[:, None, :]

    def heads(block):
        return block.reshape(MICRO, PACK, HEADS, HEAD)

    queries = heads(packed[:, :width])
    keys_all = heads(packed[:, width : 2 * width])
    values_all = heads(packed[:, 2 * width :])
    scores = jnp.einsum("pqhd,pkhd->phqk", queries, keys_all, preferred_element_type=f32) * 0.125
    masked = jnp.where(allowed[:, None], scores, -1e30)
    peaks = jnp.max(masked, axis=-1, keepdims=True)
    log_total = peaks + jnp.log(jnp.sum(jnp.exp(masked - peaks), axis=-1, keepdims=True))
    probs = jnp.exp(masked - log_total)
    probs_lo = probs.astype(bf16)
    mixed = (
        jnp.einsum("phqk,pkhd->pqhd", probs_lo, values_all, preferred_element_type=f32)
        .reshape(rows, width)
        .astype(bf16)
    )
    residual = inputs + mm(mixed, out_w)
    unit_f, inv_f = norm_parts(residual)
    shared = (unit_f * ffn_gain).astype(bf16)
    arrived = to_experts(shared)

    centroid_row = centroids[0]
    w_in, w_back = expert_in[0], expert_out[0]
    s_in, s_back = second_in[0], second_out[0]
    count = arrived.shape[0]
    arrived_f = arrived.astype(f32)
    gate_vals = jax.nn.sigmoid(
        jnp.sum(arrived_f * centroid_row.astype(f32)[None, :], axis=1, keepdims=True)
    )
    grad_result_own = (gate_vals * cot_arrived.astype(f32)).astype(bf16)
    gathered = gather_hidden(arrived)
    grad_result = gather_hidden(grad_result_own)
    pre_first = mm(gathered, w_in)
    act_first, pull_first = jax.vjp(gelu_act, pre_first)
    act_first = act_first.astype(bf16)
    middle = arrived_f + sum_hidden(mm(act_first, w_back).astype(bf16)).astype(f32)
    middle_lo = gather_hidden(middle.astype(bf16))
    pre_second = mm(middle_lo, s_in)
    act_second, pull_second = jax.vjp(gelu_act, pre_second)
    act_second = act_second.astype(bf16)
    expert_sum = middle + sum_hidden(mm(act_second, s_back).astype(bf16)).astype(f32)
    returned = (gate_vals * expert_sum).astype(bf16)
    came_back = swap(returned.reshape(experts, per_dest, width)).reshape(count, width)

    grad_logit = (
        jnp.sum(cot_arrived.astype(f32) * expert_sum, axis=1, keepdims=True)
        * gate_vals
        * (1.0 - gate_vals)
    )
    grad_pre_second = pull_second(mm(grad_result, s_back, (1, 1)))[0].astype(bf16)
    grad_middle_own = (
        grad_result_own.astype(f32)
        + sum_hidden(mm(grad_pre_second, s_in, (1, 1)).astype(bf16)).astype(f32)
    ).astype(bf16)
    grad_middle = gather_hidden(grad_middle_own)
    grad_pre = pull_first(mm(grad_middle, w_back, (1, 1)))[0].astype(bf16)
    grad_slots = (
        sum_hidden(mm(grad_pre, w_in, (1, 1)).astype(bf16)).astype(f32)
        + grad_middle_own.astype(f32)
        + grad_logit * centroid_row.astype(f32)[None, :]
    ).astype(bf16)
    grad_back = swap(grad_slots.reshape(experts, per_dest, width)).reshape(count, width)
    g_sec_out = mm(act_second, grad_result, (0, 0))
    g_sec_in = mm(middle_lo, grad_pre_second, (0, 0))
    g_exp_out = mm(act_first, grad_middle, (0, 0))
    g_exp_in = mm(gathered, grad_pre, (0, 0))
    g_cent = jnp.sum(grad_logit * arrived_f, axis=0, keepdims=True)

    combined = (residual + mm(dispatch, came_back, (0, 0))).astype(bf16)

    grad_shared = mm(dispatch, grad_back, (0, 0))
    g_gain_ffn = jnp.sum(grad_shared * unit_f, axis=0)
    grad_residual = grad_output.astype(f32) + norm_back(unit_f, inv_f, ffn_gain, grad_shared)
    grad_attended = grad_residual.astype(bf16)
    g_out_w = mm(mixed, grad_attended, (0, 0))
    grad_mixed = heads(mm(grad_attended, out_w, (1, 1)).astype(bf16))
    grad_probs = jnp.einsum("pqhd,pkhd->phqk", grad_mixed, values_all, preferred_element_type=f32)
    grad_values = jnp.einsum("phqk,pqhd->pkhd", probs_lo, grad_mixed, preferred_element_type=f32)
    inner = jnp.sum(probs * grad_probs, axis=-1, keepdims=True)
    grad_scores = (probs * (grad_probs - inner)).astype(bf16)
    grad_queries = (
        jnp.einsum("phqk,pkhd->pqhd", grad_scores, keys_all, preferred_element_type=f32) * 0.125
    )
    grad_keys = (
        jnp.einsum("phqk,pqhd->pkhd", grad_scores, queries, preferred_element_type=f32) * 0.125
    )
    grad_packed = jnp.concatenate(
        [g.reshape(rows, width) for g in (grad_queries, grad_keys, grad_values)], axis=1
    ).astype(bf16)
    g_qkv = mm(normed, grad_packed, (0, 0))
    grad_normed = mm(grad_packed, qkv_w, (1, 1))
    g_gain_attn = jnp.sum(grad_normed * unit_a, axis=0)
    input_grad = (grad_residual + norm_back(unit_a, inv_a, attn_gain, grad_normed)).astype(bf16)

    def scatter(partial):
        return lax.psum_scatter(
            partial, ("expert", "hidden"), scatter_dimension=0, tiled=True
        )

    g_cat = jnp.concatenate([g_qkv, g_out_w, g_gain_attn[:, None], g_gain_ffn[:, None], jnp.zeros((width, 126), f32)], axis=1)
    g_cat = scatter(g_cat)
    g_cent = lax.psum(g_cent, "hidden")

    def from_dealt(dealt):
        received = lax.all_to_all(
            dealt.reshape(1, seats, SEQ, width), "expert", split_axis=2, concat_axis=0, tiled=True
        ).reshape(group, piece, width)
        return jnp.take(received, deal_row, axis=0).reshape(group * piece, width)

    return (
        from_dealt(combined),
        from_dealt(input_grad).astype(f32),
        g_cat[:, 4 * width],
        g_cat[:, 4 * width + 1],
        g_cat[:, : 3 * width],
        g_cat[:, 3 * width : 4 * width],
        g_cent,
        g_exp_in[None],
        g_exp_out[None],
        g_sec_in[None],
        g_sec_out[None],
    )


def solution(mesh):
    both = ("expert", "hidden")
    fast = mesh.shape["expert"] == 16 and mesh.shape["hidden"] == 2
    return jax.shard_map(
        fast_shards if fast else plain_shards,
        mesh=mesh,
        in_specs=(
            P(both, None),
            P(),
            P(),
            P(both, None),
            P(both, None),
            P(both),
            P(both),
            P(both, None),
            P(both, None),
            P("expert", None),
            P("expert", None, "hidden"),
            P("expert", "hidden", None),
            P("expert", None, "hidden"),
            P("expert", "hidden", None),
            P(both, None),
        ),
        out_specs=(
            P(both, None),
            P(both, None),
            P(both),
            P(both),
            P(both, None),
            P(both, None),
            P("expert", None),
            P("expert", None, "hidden"),
            P("expert", "hidden", None),
            P("expert", None, "hidden"),
            P("expert", "hidden", None),
        ),
        check_vma=False,
    )
```

```python
import functools

import jax
import jax.numpy as jnp
from jax import lax
from jax.experimental import pallas as pl
from jax.experimental.pallas import tpu as pltpu
from jax.sharding import PartitionSpec as P

HEADS = 16
HEAD = 64
MICRO = 4
PER = 2
SEQ = 64
PACK = PER * SEQ

epsilon = 1e-05
bf16 = jnp.bfloat16
f32 = jnp.float32


def mm(a, b, contract=(1, 0)):
    return lax.dot_general(
        a, b, (((contract[0],), (contract[1],)), ((), ())), preferred_element_type=f32
    )


def norm_parts(rows):
    centre = jnp.mean(rows, axis=-1, keepdims=True)
    shifted = rows - centre
    spread = jnp.mean(shifted * shifted, axis=-1, keepdims=True)
    inv = lax.rsqrt(spread + epsilon)
    return shifted * inv, inv


def norm_back(unit, inv, gain, grad):
    g = grad * gain
    m1 = jnp.mean(g, axis=-1, keepdims=True)
    m2 = jnp.mean(g * unit, axis=-1, keepdims=True)
    return inv * (g - m1 - unit * m2)


def gelu_act(pre_act):
    return jax.nn.gelu(pre_act, approximate=True)


MESH = pl.DeviceIdType.MESH
ANY = pl.BlockSpec(memory_space=pl.ANY)
VM = pl.BlockSpec(memory_space=pltpu.VMEM)
DMA = pltpu.SemaphoreType.DMA
VMEM_MAX = 63 << 20
PARTS = 4


def dims(experts, width):
    capacity = (9 * PACK + 8 * experts - 1) // (8 * experts)
    per_dest = MICRO * capacity
    main = per_dest // 16 * 16
    return per_dest, main, per_dest - main


def by_columns(width, size, body):
    def step(n, carry):
        body(pl.ds(pl.multiple_of(n * size, size), size), n)
        return carry

    lax.fori_loop(0, width // size, step, 0)


def apply_rows(matrix, src, dst, contract=(1, 0)):
    def body(cols, n):
        dst[:, cols] = mm(matrix[...], src[:, cols], contract).astype(dst.dtype)

    by_columns(src.shape[1], 256, body)


def greet(experts, me, core, partner):
    barrier = pltpu.get_barrier_semaphore()

    def hello(k, carry):
        pl.semaphore_signal(
            barrier, inc=1, device_id=(lax.rem(me + k, experts), core), device_id_type=MESH
        )
        return carry

    lax.fori_loop(1, experts, hello, 0)
    if partner is not None:
        pl.semaphore_signal(barrier, inc=1, device_id=(me, partner), device_id_type=MESH)
    pl.semaphore_wait(barrier, experts - 1 + (partner is not None))


class Spread:
    def __init__(self, experts, me, core, src, dst, sends, recvs, local):
        self.experts, self.me, self.core = experts, me, core
        self.src, self.dst, self.sends, self.recvs, self.local = src, dst, sends, recvs, local
        self.rows = src.shape[0] // experts

    def block(self, ref, index):
        return ref.at[pl.ds(pl.multiple_of(index * self.rows, 16), self.rows)]

    def copy(self, k):
        to = lax.rem(self.me + k, self.experts)
        return pltpu.make_async_remote_copy(
            self.block(self.src, to),
            self.block(self.dst, self.me),
            self.sends.at[k],
            self.recvs.at[k],
            device_id=(to, self.core),
            device_id_type=MESH,
        )

    def own(self):
        return pltpu.make_async_copy(
            self.block(self.src, self.me), self.block(self.dst, self.me), self.local
        )

    def start(self):
        self.own().start()

        def go(k, carry):
            self.copy(k).start()
            return carry

        lax.fori_loop(1, self.experts, go, 0)

    def wait(self):
        self.own().wait()

        def stop(k, carry):
            self.copy(k).wait()
            return carry

        lax.fori_loop(1, self.experts, stop, 0)


def tail_matrix(part, experts, tail, turned):
    size = PARTS * tail
    shape = (experts * tail, experts * size) if turned else (experts * size, experts * tail)
    there = lax.broadcasted_iota(jnp.int32, shape, 1 if turned else 0)
    here = lax.broadcasted_iota(jnp.int32, shape, 0 if turned else 1)
    want = here // tail * size + part * tail + here % tail
    return (there == want).astype(f32).astype(bf16)


def gelu_pair(v):
    u = v * v
    t = jnp.tanh(v * (0.7978845608 + 0.7978845608 * 0.044715 * u))
    h = 0.5 * t + 0.5
    slope = h + (h - h * h) * (v * (2 * 0.7978845608 + 6 * 0.7978845608 * 0.044715 * u))
    return v * h, slope


def experts_kernel(experts, tail, *refs):
    (a_in, b_in, ca_in, cb_in, cent, w1_h, w2_h, w3_h, w4_h) = refs[:9]
    (ra_out, rb_out, ga_out, gb_out, gcent, gw1_o, gw2_o, gw3_o, gw4_o) = refs[9:18]
    (wu, wd, xs_, gs_, act, slope, mid, psend, precv, ca, cb, sa, sb, cent_s, cent_r) = refs[18:33]
    (wsem, osem, psems, prsems, xs, xr, asend, arecv, alocal) = refs[33:]
    me, core = lax.axis_index("expert"), lax.axis_index("hidden")
    other = 1 - core
    both, width = xs_.shape[1], xs_.shape[2]
    own = both // 2
    hid = wu.shape[2]
    main = a_in.shape[0]
    block = width // PARTS
    mine, theirs = pl.ds(0, own), pl.ds(own, own)

    loads = []
    for i, (h, v) in enumerate(((w1_h, wu.at[0]), (w2_h, wd.at[0]), (w3_h, wu.at[1]), (w4_h, wd.at[1]))):
        load = pltpu.make_async_copy(h, v, wsem.at[i])
        load.start()
        loads.append(load)
    greet(experts, me, core, other)

    def move(i, src, dst):
        return Spread(experts, me, core, src, dst, asend.at[i], arecv.at[i], alocal.at[i])

    cot_moves = (move(0, ca_in, ca), move(1, cb_in, cb))
    for m in cot_moves:
        m.start()

    def pair(src, dst, send, recv):
        return pltpu.make_async_remote_copy(
            src, dst, send, recv, device_id=(me, other), device_id_type=MESH
        )

    def share_x(i):
        return pair(xs_.at[i, mine], xs_.at[i, theirs], xs.at[i], xr.at[i])

    def share_g(i):
        return pair(gs_.at[i, mine], gs_.at[i, theirs], xs.at[2 + i], xr.at[2 + i])

    def partial_send(step):
        return pair(psend, precv.at[lax.rem(step, 2)], psems.at[step], prsems.at[step])

    def from_tail(ref, to, start):
        for q in range(PARTS):
            to[0, pl.ds(start, experts * tail), q * block : (q + 1) * block] = mm(
                tail_matrix(q, experts, tail, True), ref[...]
            ).astype(bf16)

    def to_tail(value, ref):
        total = None
        for q in range(PARTS):
            term = mm(tail_matrix(q, experts, tail, False), value[:, q * block : (q + 1) * block])
            total = term if total is None else total + term
        ref[...] = total.astype(bf16)

    TN, WM, WN = 512, 512, 512

    def over(size, body):
        def step(n, carry):
            body(pl.ds(pl.multiple_of(n * TN, TN), TN))
            return carry

        lax.fori_loop(0, size // TN, step, 0)

    def halves(body):
        def step(r, carry):
            body(r, pl.ds(pl.multiple_of(r * own, own), own))
            return carry

        lax.fori_loop(0, 2, step, 0)

    def exchange(step, source, weights, turned):
        def rows_of(r, unused):
            rows = pl.ds(pl.multiple_of((1 - r) * own, own), own)

            def body(cols):
                if turned:
                    value = mm(source[rows, :], weights[cols, :], (1, 1))
                else:
                    value = mm(source[rows, :], weights[:, cols])

                @pl.when(r == 0)
                def _():
                    psend[:, cols] = value.astype(bf16)

                @pl.when(r == 1)
                def _():
                    mid[:, cols] += value

            over(width, body)

            @pl.when(r == 0)
            def _():
                partial_send(step).start()

        halves(rows_of)
        partial_send(step).wait()
        mid[...] += precv[lax.rem(step, 2)].astype(f32)

    xs_[0, pl.ds(0, main), :] = a_in[...]
    from_tail(b_in, xs_, main)
    share_x(0).start()
    slot = xs_[0, mine, :].astype(f32)
    mid[...] = slot
    gate = jax.nn.sigmoid(jnp.sum(slot * cent[...].astype(f32), axis=1, keepdims=True))

    def forward(i, carry):
        def up(r, rows):
            @pl.when(r == 1)
            def _():
                share_x(i).wait()

            def body(cols):
                a, d = gelu_pair(mm(xs_[i, rows, :], wu[i, :, cols]))
                act[i, rows, cols] = a.astype(bf16)
                slope[i, rows, cols] = d.astype(bf16)

            over(hid, body)

        for k in range(2):

            @pl.when(i == k)
            def _():
                loads[2 * k].wait()

        halves(up)
        for k in range(2):

            @pl.when(i == k)
            def _():
                loads[2 * k + 1].wait()

        exchange(i, act.at[i], wd.at[i], False)

        @pl.when(i == 0)
        def _():
            xs_[1, mine, :] = mid[...].astype(bf16)
            share_x(1).start()

        return carry

    lax.fori_loop(0, 2, forward, 0)
    returned = (gate * mid[...]).astype(bf16)
    sa[...] = returned[:main]
    to_tail(returned[main:], sb)
    ret_moves = (move(2, sa, ra_out), move(3, sb, rb_out))
    for m in ret_moves:
        m.start()
    for m in cot_moves:
        m.wait()
    gs_[0, pl.ds(0, main), :] = ca[...]
    from_tail(cb, gs_, main)
    cot = gs_[0, mine, :].astype(f32)
    logit = jnp.sum(cot * mid[...], axis=1, keepdims=True) * gate * (1.0 - gate)
    cent_s[...] = jnp.sum(logit * xs_[0, mine, :].astype(f32), axis=0, keepdims=True)
    share_c = pair(cent_s, cent_r, xs.at[4], xr.at[4])
    share_c.start()
    start_grad = (gate * cot).astype(bf16)
    gs_[1, mine, :] = start_grad
    mid[...] = start_grad.astype(f32)
    share_g(1).start()

    def backward(k, carry):
        i = 1 - k

        def up_back(r, rows):
            @pl.when(r == 1)
            def _():
                share_g(i).wait()

            def body(cols):
                t = mm(gs_[i, rows, :], wd[i, cols, :], (1, 1)) * slope[i, rows, cols].astype(f32)
                slope[i, rows, cols] = t.astype(bf16)

            over(hid, body)

        halves(up_back)
        exchange(2 + k, slope.at[i], wu.at[i], True)

        @pl.when(k == 0)
        def _():
            gm = mid[...].astype(bf16)
            gs_[0, mine, :] = gm
            mid[...] = gm.astype(f32) + logit * cent[...].astype(f32)
            share_g(0).start()

        return carry

    lax.fori_loop(0, 2, backward, 0)
    for m in ret_moves:
        m.wait()
    slots = mid[...].astype(bf16)
    sa[...] = slots[:main]
    to_tail(slots[main:], sb)
    back_moves = (move(4, sa, ga_out), move(5, sb, gb_out))
    for m in back_moves:
        m.start()

    def weight_grad(left, right, to):
        wide_n = right.shape[1]

        def body(n, carry):
            m, c = n // (wide_n // WN), lax.rem(n, wide_n // WN)
            rows = pl.ds(pl.multiple_of(m * WM, WM), WM)
            cols = pl.ds(pl.multiple_of(c * WN, WN), WN)
            to[rows, cols] = mm(left[:, rows], right[:, cols], (0, 0)).astype(bf16)
            return carry

        lax.fori_loop(0, left.shape[1] // WM * (wide_n // WN), body, 0)

    def weight_grads(i, carry):
        weight_grad(act.at[i], gs_.at[i], wd.at[i])
        weight_grad(xs_.at[i], slope.at[i], wu.at[i])
        for k, (up_out, down_out) in enumerate(((gw1_o, gw2_o), (gw3_o, gw4_o))):

            @pl.when(i == k)
            def _():
                pltpu.make_async_copy(wd.at[k], down_out, osem.at[2 * k]).start()
                pltpu.make_async_copy(wu.at[k], up_out, osem.at[2 * k + 1]).start()

        return carry

    lax.fori_loop(0, 2, weight_grads, 0)
    for k, (up_out, down_out) in enumerate(((gw1_o, gw2_o), (gw3_o, gw4_o))):
        pltpu.make_async_copy(wd.at[k], down_out, osem.at[2 * k]).wait()
        pltpu.make_async_copy(wu.at[k], up_out, osem.at[2 * k + 1]).wait()
    share_c.wait()
    gcent[...] = cent_s[...] + cent_r[...]
    for m in back_moves:
        m.wait()


def run_experts(experts, slots, tails, cots, cot_tails, centroid, weights):
    width, hid = weights[0].shape
    main = slots.shape[0]
    tail = tails.shape[0] // experts // PARTS
    own = main + experts * tail
    both = 2 * own

    def sds(*shape, dtype=bf16):
        return jax.ShapeDtypeStruct(shape, dtype)

    travel = [sds(*slots.shape), sds(*tails.shape)] * 2
    wide = [sds(width, hid), sds(hid, width)] * 2
    return pl.pallas_call(
        functools.partial(experts_kernel, experts, tail),
        out_shape=travel + [sds(1, width, dtype=f32)] + wide,
        in_specs=[VM, VM, ANY, ANY, VM, ANY, ANY, ANY, ANY],
        out_specs=[ANY] * 4 + [VM] + [ANY] * 4,
        scratch_shapes=[
            pltpu.VMEM((2, width, hid), bf16),
            pltpu.VMEM((2, hid, width), bf16),
            pltpu.VMEM((2, both, width), bf16),
            pltpu.VMEM((2, both, width), bf16),
            pltpu.VMEM((2, both, hid), bf16),
            pltpu.VMEM((2, both, hid), bf16),
            pltpu.VMEM((own, width), f32),
            pltpu.VMEM((own, width), bf16),
            pltpu.VMEM((2, own, width), bf16),
            pltpu.VMEM(slots.shape, bf16),
            pltpu.VMEM(tails.shape, bf16),
            pltpu.VMEM(slots.shape, bf16),
            pltpu.VMEM(tails.shape, bf16),
            pltpu.VMEM((1, width), f32),
            pltpu.VMEM((1, width), f32),
            DMA((4,)),
            DMA((4,)),
            DMA((4,)),
            DMA((4,)),
            DMA((5,)),
            DMA((5,)),
            DMA((6, experts)),
            DMA((6, experts)),
            DMA((6,)),
        ],
        compiler_params=pltpu.CompilerParams(
            collective_id=2, has_side_effects=True, vmem_limit_bytes=VMEM_MAX
        ),
        name="experts_pass",
    )(slots, tails, cots, cot_tails, centroid, *weights)

def back_kernel(experts, tail, *refs):
    (ra, rb, ga, gb, dm, dt, gains, cot_h, res_h, tok_h, packed_h, probs_h, mixed_h, wall_h) = refs[:14]
    out_o, ig_o, gqkv_o, gout_o, ggain_o = refs[14:19]
    (cot, res, tok, packed, probs, mixed, wqkv, wout, normed, gatt, gmix, gpk, so, si, perm, wide, turn) = refs[19:36]
    keeps, psends, precvs, rv1s, rv2s, rv3s = (refs[36 + 6 * i : 42 + 6 * i] for i in range(6))
    lsem, sends, recvs, asend, arecv, alocal = refs[72:]
    me, core = lax.axis_index("expert"), lax.axis_index("hidden")
    other = 1 - core
    my_z, my_y, my_x = me // 4, lax.rem(me // 2, 2), lax.rem(me, 2)
    rows, width = tok.shape
    block = width // PARTS

    loads = {}
    for i, (name, h, v) in enumerate(
        (
            ("res", res_h, res),
            ("cot", cot_h, cot),
            ("mixed", mixed_h, mixed),
            ("wout", wall_h.at[:, pl.ds(3 * width + 128, width)], wout),
            ("probs", probs_h, probs),
            ("packed", packed_h, packed),
            ("tok", tok_h, tok),
            ("wqkv", wall_h.at[:, pl.ds(0, 3 * width)], wqkv),
        )
    ):
        loads[name] = pltpu.make_async_copy(h, v, lsem.at[i])
        loads[name].start()
    greet(experts, me, core, other)

    def join_slots(slots, tails):
        def body(cols, q):
            wide[:, cols] = mm(dm[...], slots[:, cols], (0, 0)) + mm(dt[q], tails[...], (0, 0))

        by_columns(width, block, body)

    piece = SEQ // experts
    seats = MICRO * PER

    shape = (rows, rows)
    to, at = lax.broadcasted_iota(jnp.int32, shape, 0), lax.broadcasted_iota(jnp.int32, shape, 1)
    b, s, q = to // (seats * piece), to // piece % seats, to % piece
    turn[...] = (at == s * SEQ + b * piece + q).astype(f32).astype(bf16)

    def move(i, src, dst):
        return Spread(experts, me, core, src, dst, asend.at[i], arecv.at[i], alocal.at[i])

    my_a = jnp.where(core == 0, my_x, my_y)
    my_b = jnp.where(core == 0, my_y, my_x)

    def near(a_step, b_step):
        a, b = (1 - my_a if a_step else my_a), (1 - my_b if b_step else my_b)
        x, y = jnp.where(core == 0, a, b), jnp.where(core == 0, b, a)
        return my_z * 4 + y * 2 + x

    def remote(c, stage, src, dst, to, to_core):
        return pltpu.make_async_remote_copy(
            src, dst, sends.at[c, stage], recvs.at[c, stage],
            device_id=(to, to_core), device_id_type=MESH,
        )

    def pair_copy(c):
        return remote(c, 0, psends[c], precvs[c], me, other)

    def a_copy(c):
        return remote(c, 1, psends[c].at[pl.ds(0, 256)], rv1s[c], near(True, False), core)

    def b_copy(c):
        return remote(c, 2, psends[c].at[pl.ds(256, 128)], rv2s[c], near(False, True), core)

    def z_copy(c, dz):
        to_z = lax.rem(my_z + dz, 4)
        src = psends[c].at[pl.ds(pl.multiple_of(384 + to_z * 32, 32), 32)]
        return remote(c, 2 + dz, src, rv3s[c].at[dz - 1], to_z * 4 + my_y * 2 + my_x, core)

    def place(c, t, cols):
        keeps[c][:, cols] = t[: width // 2]
        psends[c][:, cols] = t[width // 2 :].astype(bf16)

    at = lax.broadcasted_iota(jnp.int32, (1, width), 1)
    goes = jnp.where(at < width // 2, core, other)
    high, mid_ = at // 256 % 2, at // 128 % 2
    to_x, to_y = jnp.where(goes == 0, high, mid_), jnp.where(goes == 0, mid_, high)
    source = (((at // 32 % 4) * 4 + to_y * 2 + to_x) * 2 + goes) * 32 + at % 32
    perm[...] = (lax.broadcasted_iota(jnp.int32, (width, width), 0) == source).astype(f32).astype(bf16)

    def compute(c, left, right, start, stride, count, size):
        def body(n, carry):
            cols = pl.ds(pl.multiple_of(start + n * stride, size), size)
            place(c, mm(left[...], right[:, cols], (0, 0)), pl.ds(pl.multiple_of(n * size, size), size))
            return carry

        lax.fori_loop(0, count, body, 0)
        pair_copy(c).start()

    half_a = pl.ds(pl.multiple_of(my_a * 256, 256), 256)
    half_a_out = pl.ds(pl.multiple_of((1 - my_a) * 256, 256), 256)
    base_b = my_a * 256
    half_b = pl.ds(pl.multiple_of(base_b + my_b * 128, 128), 128)
    half_b_out = pl.ds(pl.multiple_of(base_b + (1 - my_b) * 128, 128), 128)

    def after_pair(c):
        pair_copy(c).wait()
        keep = keeps[c]
        keep[...] += precvs[c][...].astype(f32)
        psends[c][pl.ds(0, 256), :] = keep[half_a_out, :].astype(bf16)
        a_copy(c).start()

    def after_a(c):
        a_copy(c).wait()
        keep = keeps[c]
        keep[half_a, :] += rv1s[c][...].astype(f32)
        psends[c][pl.ds(256, 128), :] = keep[half_b_out, :].astype(bf16)
        b_copy(c).start()

    def after_b(c):
        b_copy(c).wait()
        keep = keeps[c]
        keep[half_b, :] += rv2s[c][...].astype(f32)
        psends[c][pl.ds(384, 128), :] = keep[half_b, :].astype(bf16)
        for dz in range(1, 4):
            z_copy(c, dz).start()

    def after_z(c, pieces):
        for dz in range(1, 4):
            z_copy(c, dz).wait()
        at = pl.ds(pl.multiple_of(base_b + my_b * 128 + my_z * 32, 32), 32)
        total = keeps[c][at, :]
        for dz in range(3):
            total = total + rv3s[c][dz].astype(f32)
        size = total.shape[1] // len(pieces)
        for n, (out, start) in enumerate(pieces):
            out[:, start : start + size] = total[:, n * size : (n + 1) * size]

    gain_a, gain_f = gains[0:1, :], gains[1:2, :]
    loads["res"].wait()
    join_slots(ra, rb)
    gmix[...] = (res[...] + wide[...]).astype(bf16)
    apply_rows(turn, gmix, so)
    out_move = move(0, so, out_o)
    out_move.start()
    unit, inv = norm_parts(res[...])
    join_slots(ga, gb)
    grad_shared = wide[...]
    ffn_sums = jnp.sum(grad_shared * unit, axis=0, keepdims=True)
    loads["cot"].wait()
    grad = cot[...].astype(f32) + norm_back(unit, inv, gain_f, grad_shared)
    res[...] = grad
    gatt[...] = grad.astype(bf16)
    loads["mixed"].wait()
    gpk_view = gpk.at[:, pl.ds(0, width)]
    apply_rows(mixed, perm, gpk_view)
    compute(0, gpk_view, gatt, 0, width // 4, 4, width // 4)
    loads["wout"].wait()

    def mix(cols, n):
        gmix[:, cols] = mm(gatt[...], wout[cols, :], (1, 1)).astype(bf16)

    by_columns(width, 256, mix)
    after_pair(0)
    loads["probs"].wait()
    loads["packed"].wait()
    lane = lax.broadcasted_iota(jnp.int32, (PACK, 2 * HEAD), 1)
    first = lane < HEAD

    def stacked(v):
        zero = jnp.zeros_like(v)
        return jnp.concatenate([jnp.where(first, v, zero), jnp.where(first, zero, v)], axis=0)

    def head_pair(p, h):
        at = pl.ds(pl.multiple_of(p * PACK, PACK), PACK)
        lo = h * 2 * HEAD
        q = packed[at, lo : lo + 2 * HEAD]
        k = packed[at, width + lo : width + lo + 2 * HEAD]
        v = packed[at, 2 * width + lo : 2 * width + lo + 2 * HEAD]
        gs = stacked(gmix[at, lo : lo + 2 * HEAD])
        pr_lo = probs[p * (HEADS // 2) + h]
        pr = pr_lo.astype(f32)
        gp = mm(gs, v, (1, 1))
        gv = mm(pr_lo, gs, (0, 0))
        inner = jnp.sum(pr * gp, axis=1, keepdims=True)
        ds_ = (pr * (gp - inner)).astype(bf16)
        t = mm(ds_, k)
        gq = jnp.where(first, t[:PACK], t[PACK:]) * 0.125
        gk = mm(ds_, stacked(q), (0, 0)) * 0.125
        gpk[at, lo : lo + 2 * HEAD] = gq.astype(bf16)
        gpk[at, width + lo : width + lo + 2 * HEAD] = gk.astype(bf16)
        gpk[at, 2 * width + lo : 2 * width + lo + 2 * HEAD] = gv.astype(bf16)

    part = width // 4

    def group_pieces(g):
        return tuple(part * g + width * i for i in range(3))

    def group(g):
        def packs(p, carry):
            for h in range(HEADS // 8):
                head_pair(p, g * (HEADS // 8) + h)
            return carry

        lax.fori_loop(0, MICRO, packs, 0)

    def set_off(g):
        compute(1 + g, normed, gpk, part * g, width, 3, part)

    def finish(g):
        after_z(1 + g, [(gqkv_o, start) for start in group_pieces(g)])

    loads["tok"].wait()
    unit, inv = norm_parts(tok[...].astype(f32))
    so2 = gpk.at[:, pl.ds(2 * width, width)]
    so2[...] = (unit * gain_a).astype(bf16)
    apply_rows(so2, perm, normed)
    group(0)
    set_off(0)
    group(1)
    set_off(1)
    after_pair(1)
    after_a(0)
    group(2)
    set_off(2)
    after_pair(2)
    group(3)
    after_pair(3)
    after_a(1)
    after_b(0)
    loads["wqkv"].wait()

    def pull(cols, n):
        wide[:, cols] = mm(gpk[...], wqkv[cols, :], (1, 1))

    by_columns(width, 256, pull)
    grad_normed = wide[...]
    unit, inv = norm_parts(tok[...].astype(f32))
    attn_sums = jnp.sum(grad_normed * unit, axis=0, keepdims=True)
    gmix[...] = (res[...] + norm_back(unit, inv, gain_a, grad_normed)).astype(bf16)
    apply_rows(turn, gmix, si)
    ig_move = move(1, si, ig_o)
    ig_move.start()
    set_off(3)
    after_a(2)
    after_b(1)
    sums = jnp.where(lax.broadcasted_iota(jnp.int32, (128, width), 0) < 64, attn_sums, ffn_sums)
    sums_hi = sums.astype(bf16)
    sums_lo = (sums - sums_hi.astype(f32)).astype(bf16)
    place(5, mm(perm[...], sums_hi, (0, 1)) + mm(perm[...], sums_lo, (0, 1)), pl.ds(0, 128))
    pair_copy(5).start()
    after_pair(4)
    after_pair(5)
    after_z(0, [(gout_o, 0)])
    after_a(3)
    after_b(2)
    finish(0)
    after_a(4)
    after_a(5)
    after_b(3)
    finish(1)
    after_b(4)
    after_b(5)
    finish(2)
    finish(3)
    after_z(5, [(ggain_o, 0)])
    out_move.wait()
    ig_move.wait()


def run_back(experts, tail, slots, tails, grads, grad_tails, d_main, d_tail, gains, cot, residual, tok, packed, probs, mixed, w_all):
    rows, width = tok.shape

    def sds(*shape, dtype=bf16):
        return jax.ShapeDtypeStruct(shape, dtype)

    widths = (width,) + (3 * width // 4,) * 4 + (128,)
    scratch = [
        pltpu.VMEM(cot.shape, bf16),
        pltpu.VMEM(residual.shape, f32),
        pltpu.VMEM(tok.shape, bf16),
        pltpu.VMEM(packed.shape, bf16),
        pltpu.VMEM(probs.shape, bf16),
        pltpu.VMEM(mixed.shape, bf16),
        pltpu.VMEM((width, 3 * width), bf16),
        pltpu.VMEM((width, width), bf16),
        pltpu.VMEM((rows, width), bf16),
        pltpu.VMEM((rows, width), bf16),
        pltpu.VMEM((rows, width), bf16),
        pltpu.VMEM((rows, 3 * width), bf16),
        pltpu.VMEM((rows, width), bf16),
        pltpu.VMEM((rows, width), bf16),
        pltpu.VMEM((width, width), bf16),
        pltpu.VMEM((rows, width), f32),
        pltpu.VMEM((rows, rows), bf16),
    ]
    scratch += [pltpu.VMEM((width // 2, w), f32) for w in widths]
    for part in (2, 2, 4, 8):
        scratch += [pltpu.VMEM((width // part, w), bf16) for w in widths]
    scratch += [pltpu.VMEM((3, 32, w), bf16) for w in widths]
    scratch += [
        DMA((8,)),
        DMA((6, 6)),
        DMA((6, 6)),
        DMA((2, experts)),
        DMA((2, experts)),
        DMA((2,)),
    ]
    return pl.pallas_call(
        functools.partial(back_kernel, experts, tail),
        out_shape=[sds(rows, width), sds(rows, width), sds(32, 3 * width, dtype=f32), sds(32, width, dtype=f32), sds(32, 128, dtype=f32)],
        in_specs=[VM] * 7 + [ANY] * 7,
        out_specs=[ANY, ANY, VM, VM, VM],
        scratch_shapes=scratch,
        compiler_params=pltpu.CompilerParams(
            collective_id=3, has_side_effects=True, vmem_limit_bytes=VMEM_MAX
        ),
        name="attention_back",
    )(slots, tails, grads, grad_tails, d_main, d_tail, gains, cot, residual, tok, packed, probs, mixed, w_all)


def front_kernel(experts, tail, *refs):
    (tokens, cots, routes, orders, deal, lengths, g_attn, g_ffn, w_qkv, w_out) = refs[:10]
    (slots_o, tails_o, cslots_o, ctails_o, deal_o, dm_o, dt_o, gains_o, cot_o, res_o, tok_o, packed_o, probs_o, mixed_o, w_o) = refs[10:25]
    (st, sl, rt, rl, rc, tok, cot, w, packed, probs, mixed, res, shared, dm, dt, ftm, masks, ss, stl, cs, ctl, turn) = refs[25:47]
    zs, zr, as_, ar, bs, br, ps, pr, asend, arecv, alocal, osem = refs[47:]
    me, core = lax.axis_index("expert"), lax.axis_index("hidden")
    other = 1 - core
    my_z, my_y, my_x = me // 4, lax.rem(me // 2, 2), lax.rem(me, 2)
    rows, width = tok.shape
    piece = SEQ // experts
    seats = MICRO * PER
    block = width // PARTS
    step = w_qkv.shape[0]
    per_dest = experts and dims(experts, width)[0]
    main = per_dest - tail
    capacity = per_dest // MICRO

    def iota(shape, axis):
        return lax.broadcasted_iota(jnp.int32, shape, axis)

    def one_hot(test):
        return test.astype(f32).astype(bf16)

    own_rows = pl.ds(pl.multiple_of((me * 2 + core) * step, step), step)
    gain_at, out_at = 3 * width, 3 * width + 128
    w[own_rows, :gain_at] = w_qkv[...]
    w[own_rows, out_at:] = w_out[...]
    eye = iota((step, step), 0) == iota((step, step), 1)

    def as_column(row):
        return jnp.sum(jnp.where(eye, row[...].astype(f32), 0.0), axis=1, keepdims=True)

    gain_cols = jnp.where(iota((step, 128), 1) < 64, as_column(g_attn), as_column(g_ffn))
    w[own_rows, gain_at:out_at] = gain_cols.astype(bf16)
    cuts = ((0, out_at), (out_at, width))

    line = lax.rem(me, 4)
    a_to = jnp.where(core == 0, my_z * 4 + my_y * 2 + 1 - my_x, my_z * 4 + 2 - 2 * my_y + my_x)
    b_to = jnp.where(core == 0, my_z * 4 + 2 - 2 * my_y + my_x, my_z * 4 + my_y * 2 + 1 - my_x)
    shift_a, shift_b = a_to - me, b_to - me

    def send(j, e, sem_s, sem_r, to, to_core):
        start, size = cuts[j]
        ref = w.at[pl.ds(pl.multiple_of((e * 2 + core) * step, step), step), pl.ds(start, size)]
        return pltpu.make_async_remote_copy(
            ref, ref, sem_s, sem_r, device_id=(to, to_core), device_id_type=MESH
        )

    def up(j, d):
        s = my_z - d
        return send(j, s * 4 + line, zs.at[j, d], zr.at[j, s], me + 4, core)

    def down(j, d):
        s = my_z + d
        return send(j, s * 4 + line, zs.at[j, 4 + d], zr.at[j, s], me - 4, core)

    def a_copy(j, s):
        return send(j, s * 4 + line, as_.at[j, s], ar.at[j, s], a_to, core)

    def b_copy(j, f, s):
        return send(j, s * 4 + line + f * shift_a, bs.at[j, 4 * f + s], br.at[j, 4 * f + s], b_to, core)

    def p_copy(j, f, s):
        e = s * 4 + line + (f % 2) * shift_a + (f // 2) * shift_b
        return send(j, e, ps.at[j, 4 * f + s], pr.at[j, 4 * f + s], me, other)

    def release(j, s):
        b_copy(j, 0, s).start()
        a_copy(j, s).start()
        p_copy(j, 0, s).start()

    def chain(j, d):
        @pl.when(my_z >= d)
        def _():
            if d:
                up(j, d).wait_recv()

            @pl.when(my_z < 3)
            def _():
                up(j, d).start()

            if d:
                release(j, my_z - d)

        @pl.when(my_z + d <= 3)
        def _():
            if d:
                down(j, d).wait_recv()

            @pl.when(my_z > 0)
            def _():
                down(j, d).start()

            if d:
                release(j, my_z + d)

        if not d:
            release(j, my_z)

    def places():
        return [lax.rem(my_z + k, 4) for k in (0, 1, 3, 2)]

    def fan_a(j):
        for s in places():
            a_copy(j, s).wait_recv()
            b_copy(j, 1, s).start()
            p_copy(j, 1, s).start()

    def fan_b(j):
        for f in range(2):
            for s in places():
                b_copy(j, f, s).wait_recv()
                p_copy(j, 2 + f, s).start()

    def fan_p(j):
        for f in range(4):
            for s in range(4):
                p_copy(j, f, s).wait_recv()

    def all_sent(j):
        for d in range(4):

            @pl.when((my_z >= d) & (my_z < 3))
            def _():
                up(j, d).wait_send()

            @pl.when((my_z + d <= 3) & (my_z > 0))
            def _():
                down(j, d).wait_send()

        for s in range(4):
            a_copy(j, s).wait_send()
            for f in range(2):
                b_copy(j, f, s).wait_send()
            for f in range(4):
                p_copy(j, f, s).wait_send()

    greet(experts, me, core, other)
    chain(0, 0)
    chain(1, 0)

    def move(i, src, dst):
        return Spread(experts, me, core, src, dst, asend.at[i], arecv.at[i], alocal.at[i])

    group = deal.shape[1]
    deal_row = deal[pl.ds(core, 1), :]
    length_row = lengths[pl.ds(core, 1), :]
    spread_out = one_hot(iota((group, rows), 1) // piece == iota((group, rows), 0))
    wide = jnp.broadcast_to(deal_row.astype(f32), (8, group)).astype(bf16)
    goal = mm(wide, spread_out)[0:1].astype(jnp.int32) * piece + iota((1, rows), 1) % piece
    ftm[...] = one_hot(iota((rows, rows), 0) == goal)
    apply_rows(ftm, tokens, st)
    lab = jnp.where(iota((128, rows), 0) < 64, routes[...], orders[...]).astype(f32).astype(bf16)
    sl[...] = mm(ftm[...], lab, (1, 1)).astype(bf16)
    tok_moves = (move(0, st, rt), move(1, sl, rl))
    for m in tok_moves:
        m.start()
    chain(0, 1)
    apply_rows(ftm, cots, cs)
    chain(0, 2)
    goal_col = mm(spread_out, wide, (0, 1))[:, 0:1].astype(jnp.int32) * piece + iota((rows, 1), 0) % piece
    ftm[...] = one_hot(iota((rows, rows), 1) == goal_col)
    chain(0, 3)
    fan_a(0)
    chain(1, 1)
    chain(1, 2)
    chain(1, 3)
    for m in tok_moves:
        m.wait()

    outs = []

    def store(i, ref, out):
        copy = pltpu.make_async_copy(ref, out, osem.at[i])
        copy.start()
        outs.append(copy)

    cot_move = move(2, cs, rc)
    cot_move.start()
    store(0, ftm, deal_o)
    to, at = iota((rows, rows), 0), iota((rows, rows), 1)
    b, s, q = to // (seats * piece), to // piece % seats, to % piece
    turn[...] = one_hot(at == s * SEQ + b * piece + q)
    apply_rows(turn, rt, tok, (0, 0))
    store(1, tok, tok_o)
    lab_col = mm(turn[...], rl[...], (0, 0))
    lab_row = mm(rl[...], turn[...], (0, 0))
    fan_a(1)
    ranks, heads_at, oks = [], [], []
    own = [
        jnp.sum(jnp.where(deal_row == me * seats + i, length_row, 0), axis=1, keepdims=True)
        for i in range(seats)
    ]
    posr, posc = iota((1, PACK), 1), iota((PACK, 1), 0)
    near_ = (iota((PACK, PACK), 0) // SEQ == iota((PACK, PACK), 1) // SEQ) & (
        iota((PACK, PACK), 1) <= iota((PACK, PACK), 0)
    )
    for p in range(MICRO):
        low, high = own[PER * p], own[PER * p + 1]
        here_r = posr % SEQ < jnp.where(posr < SEQ, low, high)
        here_c = posc % SEQ < jnp.where(posc < SEQ, low, high)
        masks[p] = (near_ & here_r).astype(f32)
        cols = slice(p * PACK, (p + 1) * PACK)
        route_r = lab_row[0:1, cols]
        key_r = lab_row[64:65, cols] * PER + (posr // SEQ).astype(f32)
        route_c = lab_col[cols, 0:1]
        key_c = lab_col[cols, 64:65] * PER + (posc // SEQ).astype(f32)
        ahead = jnp.sum(
            ((route_c == route_r) & (key_c < key_r) & here_c).astype(f32), axis=0, keepdims=True
        ).astype(jnp.int32)
        base = p * capacity + ahead
        good = here_r & (ahead < capacity)
        route_i = route_r.astype(jnp.int32)
        heads_at.append(jnp.where(good & (base < main), route_i * main + base, -1))
        oks.append(jnp.where(good & (base >= main), route_i * (PARTS * tail) + base - main, -PARTS * PARTS * tail))
    head_row = jnp.concatenate(heads_at, axis=1)
    tail_row = jnp.concatenate(oks, axis=1)
    dm[...] = one_hot(iota(dm.shape, 0) == head_row)
    for part in range(PARTS):
        dt[part] = one_hot(iota(dt.shape[1:], 0) == tail_row + part * tail)
    store(2, dm, dm_o)
    store(3, dt, dt_o)

    def split(ref, to_main, to_tails):
        apply_rows(dm, ref, to_main)
        total = None
        for part in range(PARTS):
            term = mm(dt[part], ref[:, part * block : (part + 1) * block])
            total = term if total is None else total + term
        to_tails[...] = total.astype(bf16)

    inputs = tok[...].astype(f32)
    unit, inv = norm_parts(inputs)
    res[...] = unit
    fan_b(0)
    fan_p(0)
    big = iota((128, 128), 0) == iota((128, 128), 1)

    def gain_row(lane):
        parts = []
        for j in range(width // 128):
            col = w[128 * j : 128 * (j + 1), gain_at:out_at].astype(f32)[:, lane : lane + 1]
            parts.append(jnp.sum(jnp.where(big, col, 0.0), axis=0, keepdims=True))
        return jnp.concatenate(parts, axis=1)

    gain_a, gain_f = gain_row(0), gain_row(64)
    gains_o[0:1, :] = gain_a
    gains_o[1:2, :] = gain_f
    shared[...] = (res[...] * gain_a).astype(bf16)

    def project(n, carry):
        cols = pl.ds(pl.multiple_of(n * 256, 256), 256)
        packed[:, cols] = mm(shared[...], w[:, cols]).astype(bf16)
        return carry

    lax.fori_loop(0, 3 * width // 256, project, 0)
    store(5, packed, packed_o)
    first = iota((PACK, 2 * HEAD), 1) < HEAD

    def pack(p, carry):
        at = pl.ds(pl.multiple_of(p * PACK, PACK), PACK)
        mask = masks[p] > 0.5
        mask = jnp.concatenate([mask, mask], axis=0)
        for h in range(HEADS // 2):
            lo = h * 2 * HEAD
            q = packed[at, lo : lo + 2 * HEAD]
            k = packed[at, width + lo : width + lo + 2 * HEAD]
            v = packed[at, 2 * width + lo : 2 * width + lo + 2 * HEAD]
            zero = jnp.zeros_like(q)
            qs = jnp.concatenate([jnp.where(first, q, zero), jnp.where(first, zero, q)], axis=0)
            scores = jnp.where(mask, mm(qs, k, (1, 1)) * 0.125, -1e30)
            e = jnp.exp(scores - jnp.max(scores, axis=1, keepdims=True))
            prob = (e / jnp.sum(e, axis=1, keepdims=True)).astype(bf16)
            probs[p * (HEADS // 2) + h] = prob
            t = mm(prob, v)
            mixed[at, lo : lo + 2 * HEAD] = jnp.where(first, t[:PACK], t[PACK:]).astype(bf16)
        return carry

    fan_b(1)
    lax.fori_loop(0, MICRO, pack, 0)
    store(6, probs, probs_o)
    fan_p(1)
    store(4, w, w_o)
    store(7, mixed, mixed_o)
    apply_rows(mixed, w.at[:, pl.ds(out_at, width)], res)
    residual = tok[...].astype(f32) + res[...]
    res[...] = residual
    store(8, res, res_o)
    unit, inv = norm_parts(residual)
    shared[...] = (unit * gain_f).astype(bf16)
    split(shared, ss, stl)
    slot_moves = (move(3, ss, slots_o), move(4, stl, tails_o))
    cot_move.wait()
    for m in slot_moves:
        m.start()
    apply_rows(turn, rc, cot, (0, 0))
    store(9, cot, cot_o)
    split(cot, cs, ctl)
    store(10, cs, cslots_o)
    store(11, ctl, ctails_o)
    all_sent(0)
    all_sent(1)
    for copy in outs:
        copy.wait()
    for m in slot_moves:
        m.wait()


def run_front(experts, tail, tokens, cots, routes, orders, deal, lengths, g_attn, g_ffn, w_qkv, w_out):
    rows, width = tokens.shape
    per_dest = dims(experts, width)[0]
    main = (per_dest - tail) * experts
    side = experts * PARTS * tail

    def sds(*shape, dtype=bf16):
        return jax.ShapeDtypeStruct(shape, dtype)

    tails = (side, width // PARTS)
    out_shape = [
        sds(main, width),
        sds(*tails),
        sds(main, width),
        sds(*tails),
        sds(rows, rows),
        sds(main, rows),
        sds(PARTS, side, rows),
        sds(2, width, dtype=f32),
        sds(rows, width),
        sds(rows, width, dtype=f32),
        sds(rows, width),
        sds(rows, 3 * width),
        sds(MICRO * HEADS // 2, 2 * PACK, PACK),
        sds(rows, width),
        sds(width, 4 * width + 128),
    ]
    vm = pltpu.VMEM
    return pl.pallas_call(
        functools.partial(front_kernel, experts, tail),
        out_shape=out_shape,
        in_specs=[VM] * 10,
        out_specs=[ANY] * 7 + [VM] + [ANY] * 7,
        scratch_shapes=[
            vm((rows, width), bf16),
            vm((rows, 128), bf16),
            vm((rows, width), bf16),
            vm((rows, 128), bf16),
            vm((rows, width), bf16),
            vm((rows, width), bf16),
            vm((rows, width), bf16),
            vm((width, 4 * width + 128), bf16),
            vm((rows, 3 * width), bf16),
            vm((MICRO * HEADS // 2, 2 * PACK, PACK), bf16),
            vm((rows, width), bf16),
            vm((rows, width), f32),
            vm((rows, width), bf16),
            vm((main, rows), bf16),
            vm((PARTS, side, rows), bf16),
            vm((rows, rows), bf16),
            vm((MICRO, PACK, PACK), f32),
            vm((main, width), bf16),
            vm(tails, bf16),
            vm((main, width), bf16),
            vm(tails, bf16),
            vm((rows, rows), bf16),
            DMA((2, 8)),
            DMA((2, 4)),
            DMA((2, 4)),
            DMA((2, 4)),
            DMA((2, 8)),
            DMA((2, 8)),
            DMA((2, 16)),
            DMA((2, 16)),
            DMA((5, experts)),
            DMA((5, experts)),
            DMA((5,)),
            DMA((12,)),
        ],
        compiler_params=pltpu.CompilerParams(
            collective_id=1, has_side_effects=True, vmem_limit_bytes=VMEM_MAX
        ),
        name="attention_front",
    )(tokens, cots, routes, orders, deal, lengths, g_attn, g_ffn, w_qkv, w_out)


def finish_kernel(f, out_r, ig_r, *refs):
    out_o, ig_o = refs[4:6]
    out_o[...] = mm(f[...], out_r[...]).astype(bf16)
    ig_o[...] = mm(f[...], ig_r[...])
    for narrow, full in zip(refs[:4], refs[6:]):
        full[...] = narrow[...].astype(f32)


def run_finish(f, out_r, ig_r, grads):
    steps = 16
    rows, width = out_r.shape

    def cut(shape):
        return pl.BlockSpec((shape[0] // steps, shape[1]), lambda i: (i, 0))

    def whole(shape):
        return pl.BlockSpec(shape, lambda i: (0, 0))

    outs = [
        jax.ShapeDtypeStruct((rows, width), bf16),
        jax.ShapeDtypeStruct((rows, width), f32),
    ] + [jax.ShapeDtypeStruct(g.shape, f32) for g in grads]
    return pl.pallas_call(
        finish_kernel,
        grid=(steps,),
        out_shape=outs,
        in_specs=[cut(f.shape), whole(out_r.shape), whole(ig_r.shape)] + [cut(g.shape) for g in grads],
        out_specs=[cut(o.shape) for o in outs],
        compiler_params=pltpu.CompilerParams(vmem_limit_bytes=VMEM_MAX),
        name="finish",
    )(f, out_r, ig_r, *grads)


def fast_shards(
    tokens,
    lengths,
    deal,
    routes,
    slot_order,
    gain_attn,
    gain_ffn,
    w_qkv,
    w_out,
    centroids,
    expert_in,
    expert_out,
    second_in,
    second_out,
    cotangent,
):
    width = tokens.shape[1]
    experts = lax.axis_size("expert")
    tail = dims(experts, width)[2]
    (slots, tails, cots, cot_tails, dealt, d_main, d_tail, gains, grad_output, residual, tok,
     packed, probs, mixed, w_all) = run_front(
        experts, tail, tokens, cotangent, routes.reshape(1, -1), slot_order.reshape(1, -1), deal, lengths,
        gain_attn[None], gain_ffn[None], w_qkv, w_out,
    )
    ra, rb, ga, gb, g_cent, *g_experts = run_experts(
        experts, slots, tails, cots, cot_tails, centroids,
        (expert_in[0], expert_out[0], second_in[0], second_out[0]),
    )
    out_r, ig_r, g_qkv, g_out, g_gain = run_back(
        experts, tail, ra, rb, ga, gb, d_main, d_tail, gains, grad_output, residual, tok,
        packed, probs, mixed, w_all,
    )
    output, input_grad, *g_experts = run_finish(dealt, out_r, ig_r, g_experts)
    return (
        output,
        input_grad,
        g_gain[:, 0],
        g_gain[:, 64],
        g_qkv,
        g_out,
        g_cent,
        *(g[None] for g in g_experts),
    )


def gather_hidden(rows):
    return lax.all_gather(rows, "hidden", axis=0, tiled=True)


def sum_hidden(terms):
    return lax.psum_scatter(terms, "hidden", scatter_dimension=0, tiled=True)


def swap(blocks):
    return lax.all_to_all(blocks, "expert", split_axis=0, concat_axis=0, tiled=True)


def plain_shards(
    tokens,
    lengths,
    deal,
    routes,
    slot_order,
    gain_attn,
    gain_ffn,
    w_qkv,
    w_out,
    centroids,
    expert_in,
    expert_out,
    second_in,
    second_out,
    cotangent,
):
    width = tokens.shape[1]
    experts = lax.axis_size("expert")
    piece = SEQ // experts
    seats = MICRO * PER
    group = experts * seats
    rows = seats * SEQ
    capacity = (9 * PACK + 8 * experts - 1) // (8 * experts)
    per_dest = MICRO * capacity
    my_expert = lax.axis_index("expert")
    my_hidden = lax.axis_index("hidden")

    deal_row = lax.dynamic_index_in_dim(deal, my_hidden, 0, keepdims=False)
    length_row = lax.dynamic_index_in_dim(lengths, my_hidden, 0, keepdims=False)
    ids = jnp.arange(group, dtype=jnp.int32)
    inverse = jnp.sum(jnp.where(deal_row[None, :] == ids[:, None], ids[None, :], 0), axis=1)
    own = my_expert * seats + jnp.arange(seats, dtype=jnp.int32)
    own_lengths = jnp.sum(
        jnp.where(deal_row[None, :] == own[:, None], length_row[None, :], 0), axis=1
    )

    def to_dealt(flat):
        pieces = jnp.take(flat.reshape(group, piece, flat.shape[1]), inverse, axis=0)
        return lax.all_to_all(
            pieces.reshape(experts, seats, piece, flat.shape[1]),
            "expert",
            split_axis=0,
            concat_axis=2,
            tiled=True,
        ).reshape(rows, flat.shape[1])

    labels = jnp.concatenate([routes, slot_order], axis=1)
    lab = to_dealt(labels)
    tok = to_dealt(tokens)
    grad_output = to_dealt(cotangent)

    cat = jnp.concatenate(
        [w_qkv, w_out, gain_attn[:, None], gain_ffn[:, None], jnp.zeros((w_qkv.shape[0], 126), bf16)],
        axis=1,
    )
    cat = lax.all_gather(cat, ("expert", "hidden"), axis=0, tiled=True)
    qkv_w = cat[:, : 3 * width]
    out_w = cat[:, 3 * width : 4 * width]
    attn_gain = cat[:, 4 * width].astype(f32)[None, :]
    ffn_gain = cat[:, 4 * width + 1].astype(f32)[None, :]

    route = lab[:, 0].reshape(MICRO, PACK)
    order = lab[:, 1].reshape(MICRO, PACK)
    positions = jnp.arange(PACK, dtype=jnp.int32)
    seat = positions // SEQ
    pack_lengths = own_lengths.reshape(MICRO, PER)
    limit = jnp.repeat(pack_lengths, SEQ, axis=1)
    present = (positions % SEQ)[None, :] < limit
    priority = order * PER + seat[None, :]
    ahead = jnp.sum(
        (
            (route[:, :, None] == route[:, None, :])
            & (priority[:, None, :] < priority[:, :, None])
            & present[:, None, :]
        ).astype(jnp.int32),
        axis=2,
    )
    accepted = (present & (ahead < capacity)).reshape(rows)
    target = (
        route * per_dest + jnp.arange(MICRO, dtype=jnp.int32)[:, None] * capacity + ahead
    ).reshape(rows)
    target = jnp.where(accepted, target, -1)
    slot_ids = jnp.arange(experts * per_dest, dtype=jnp.int32)
    dispatch = (slot_ids[:, None] == target[None, :]).astype(bf16)

    def to_experts(values):
        out = mm(dispatch, values).astype(bf16)
        return swap(out.reshape(experts, per_dest, width)).reshape(experts * per_dest, width)

    cot_arrived = to_experts(grad_output)

    inputs = tok.astype(f32)
    unit_a, inv_a = norm_parts(inputs)
    normed = (unit_a * attn_gain).astype(bf16)
    packed = mm(normed, qkv_w).astype(bf16)
    allowed = (
        (seat[:, None] == seat[None, :]) & (positions[None, :] <= positions[:, None])
    )[None] & present[:, None, :]

    def heads(block):
        return block.reshape(MICRO, PACK, HEADS, HEAD)

    queries = heads(packed[:, :width])
    keys_all = heads(packed[:, width : 2 * width])
    values_all = heads(packed[:, 2 * width :])
    scores = jnp.einsum("pqhd,pkhd->phqk", queries, keys_all, preferred_element_type=f32) * 0.125
    masked = jnp.where(allowed[:, None], scores, -1e30)
    peaks = jnp.max(masked, axis=-1, keepdims=True)
    log_total = peaks + jnp.log(jnp.sum(jnp.exp(masked - peaks), axis=-1, keepdims=True))
    probs = jnp.exp(masked - log_total)
    probs_lo = probs.astype(bf16)
    mixed = (
        jnp.einsum("phqk,pkhd->pqhd", probs_lo, values_all, preferred_element_type=f32)
        .reshape(rows, width)
        .astype(bf16)
    )
    residual = inputs + mm(mixed, out_w)
    unit_f, inv_f = norm_parts(residual)
    shared = (unit_f * ffn_gain).astype(bf16)
    arrived = to_experts(shared)

    centroid_row = centroids[0]
    w_in, w_back = expert_in[0], expert_out[0]
    s_in, s_back = second_in[0], second_out[0]
    count = arrived.shape[0]
    arrived_f = arrived.astype(f32)
    gate_vals = jax.nn.sigmoid(
        jnp.sum(arrived_f * centroid_row.astype(f32)[None, :], axis=1, keepdims=True)
    )
    grad_result_own = (gate_vals * cot_arrived.astype(f32)).astype(bf16)
    gathered = gather_hidden(arrived)
    grad_result = gather_hidden(grad_result_own)
    pre_first = mm(gathered, w_in)
    act_first, pull_first = jax.vjp(gelu_act, pre_first)
    act_first = act_first.astype(bf16)
    middle = arrived_f + sum_hidden(mm(act_first, w_back).astype(bf16)).astype(f32)
    middle_lo = gather_hidden(middle.astype(bf16))
    pre_second = mm(middle_lo, s_in)
    act_second, pull_second = jax.vjp(gelu_act, pre_second)
    act_second = act_second.astype(bf16)
    expert_sum = middle + sum_hidden(mm(act_second, s_back).astype(bf16)).astype(f32)
    returned = (gate_vals * expert_sum).astype(bf16)
    came_back = swap(returned.reshape(experts, per_dest, width)).reshape(count, width)

    grad_logit = (
        jnp.sum(cot_arrived.astype(f32) * expert_sum, axis=1, keepdims=True)
        * gate_vals
        * (1.0 - gate_vals)
    )
    grad_pre_second = pull_second(mm(grad_result, s_back, (1, 1)))[0].astype(bf16)
    grad_middle_own = (
        grad_result_own.astype(f32)
        + sum_hidden(mm(grad_pre_second, s_in, (1, 1)).astype(bf16)).astype(f32)
    ).astype(bf16)
    grad_middle = gather_hidden(grad_middle_own)
    grad_pre = pull_first(mm(grad_middle, w_back, (1, 1)))[0].astype(bf16)
    grad_slots = (
        sum_hidden(mm(grad_pre, w_in, (1, 1)).astype(bf16)).astype(f32)
        + grad_middle_own.astype(f32)
        + grad_logit * centroid_row.astype(f32)[None, :]
    ).astype(bf16)
    grad_back = swap(grad_slots.reshape(experts, per_dest, width)).reshape(count, width)
    g_sec_out = mm(act_second, grad_result, (0, 0))
    g_sec_in = mm(middle_lo, grad_pre_second, (0, 0))
    g_exp_out = mm(act_first, grad_middle, (0, 0))
    g_exp_in = mm(gathered, grad_pre, (0, 0))
    g_cent = jnp.sum(grad_logit * arrived_f, axis=0, keepdims=True)

    combined = (residual + mm(dispatch, came_back, (0, 0))).astype(bf16)

    grad_shared = mm(dispatch, grad_back, (0, 0))
    g_gain_ffn = jnp.sum(grad_shared * unit_f, axis=0)
    grad_residual = grad_output.astype(f32) + norm_back(unit_f, inv_f, ffn_gain, grad_shared)
    grad_attended = grad_residual.astype(bf16)
    g_out_w = mm(mixed, grad_attended, (0, 0))
    grad_mixed = heads(mm(grad_attended, out_w, (1, 1)).astype(bf16))
    grad_probs = jnp.einsum("pqhd,pkhd->phqk", grad_mixed, values_all, preferred_element_type=f32)
    grad_values = jnp.einsum("phqk,pqhd->pkhd", probs_lo, grad_mixed, preferred_element_type=f32)
    inner = jnp.sum(probs * grad_probs, axis=-1, keepdims=True)
    grad_scores = (probs * (grad_probs - inner)).astype(bf16)
    grad_queries = (
        jnp.einsum("phqk,pkhd->pqhd", grad_scores, keys_all, preferred_element_type=f32) * 0.125
    )
    grad_keys = (
        jnp.einsum("phqk,pqhd->pkhd", grad_scores, queries, preferred_element_type=f32) * 0.125
    )
    grad_packed = jnp.concatenate(
        [g.reshape(rows, width) for g in (grad_queries, grad_keys, grad_values)], axis=1
    ).astype(bf16)
    g_qkv = mm(normed, grad_packed, (0, 0))
    grad_normed = mm(grad_packed, qkv_w, (1, 1))
    g_gain_attn = jnp.sum(grad_normed * unit_a, axis=0)
    input_grad = (grad_residual + norm_back(unit_a, inv_a, attn_gain, grad_normed)).astype(bf16)

    def scatter(partial):
        return lax.psum_scatter(
            partial, ("expert", "hidden"), scatter_dimension=0, tiled=True
        )

    g_cat = jnp.concatenate([g_qkv, g_out_w, g_gain_attn[:, None], g_gain_ffn[:, None], jnp.zeros((width, 126), f32)], axis=1)
    g_cat = scatter(g_cat)
    g_cent = lax.psum(g_cent, "hidden")

    def from_dealt(dealt):
        received = lax.all_to_all(
            dealt.reshape(1, seats, SEQ, width), "expert", split_axis=2, concat_axis=0, tiled=True
        ).reshape(group, piece, width)
        return jnp.take(received, deal_row, axis=0).reshape(group * piece, width)

    return (
        from_dealt(combined),
        from_dealt(input_grad).astype(f32),
        g_cat[:, 4 * width],
        g_cat[:, 4 * width + 1],
        g_cat[:, : 3 * width],
        g_cat[:, 3 * width : 4 * width],
        g_cent,
        g_exp_in[None],
        g_exp_out[None],
        g_sec_in[None],
        g_sec_out[None],
    )


def solution(mesh):
    both = ("expert", "hidden")
    fast = mesh.shape["expert"] == 16 and mesh.shape["hidden"] == 2
    return jax.shard_map(
        fast_shards if fast else plain_shards,
        mesh=mesh,
        in_specs=(
            P(both, None),
            P(),
            P(),
            P(both, None),
            P(both, None),
            P(both),
            P(both),
            P(both, None),
            P(both, None),
            P("expert", None),
            P("expert", None, "hidden"),
            P("expert", "hidden", None),
            P("expert", None, "hidden"),
            P("expert", "hidden", None),
            P(both, None),
        ),
        out_specs=(
            P(both, None),
            P(both, None),
            P(both),
            P(both),
            P(both, None),
            P(both, None),
            P("expert", None),
            P("expert", None, "hidden"),
            P("expert", "hidden", None),
            P("expert", None, "hidden"),
            P("expert", "hidden", None),
        ),
        check_vma=False,
    )
```

```python
import functools

import jax
import jax.numpy as jnp
from jax import lax
from jax.experimental import pallas as pl
from jax.experimental.pallas import tpu as pltpu
from jax.sharding import PartitionSpec as P

HEADS = 16
HEAD = 64
MICRO = 4
PER = 2
SEQ = 64
PACK = PER * SEQ

epsilon = 1e-05
bf16 = jnp.bfloat16
f32 = jnp.float32


def mm(a, b, contract=(1, 0)):
    return lax.dot_general(
        a, b, (((contract[0],), (contract[1],)), ((), ())), preferred_element_type=f32
    )


def norm_parts(rows):
    centre = jnp.mean(rows, axis=-1, keepdims=True)
    shifted = rows - centre
    spread = jnp.mean(shifted * shifted, axis=-1, keepdims=True)
    inv = lax.rsqrt(spread + epsilon)
    return shifted * inv, inv


def norm_back(unit, inv, gain, grad):
    g = grad * gain
    m1 = jnp.mean(g, axis=-1, keepdims=True)
    m2 = jnp.mean(g * unit, axis=-1, keepdims=True)
    return inv * (g - m1 - unit * m2)


def gelu_act(pre_act):
    return jax.nn.gelu(pre_act, approximate=True)


MESH = pl.DeviceIdType.MESH
ANY = pl.BlockSpec(memory_space=pl.ANY)
VM = pl.BlockSpec(memory_space=pltpu.VMEM)
DMA = pltpu.SemaphoreType.DMA
VMEM_MAX = 63 << 20
PARTS = 4


def dims(experts, width):
    capacity = (9 * PACK + 8 * experts - 1) // (8 * experts)
    per_dest = MICRO * capacity
    main = per_dest // 16 * 16
    return per_dest, main, per_dest - main


def by_columns(width, size, body):
    def step(n, carry):
        body(pl.ds(pl.multiple_of(n * size, size), size), n)
        return carry

    lax.fori_loop(0, width // size, step, 0)


def apply_rows(matrix, src, dst, contract=(1, 0)):
    def body(cols, n):
        dst[:, cols] = mm(matrix[...], src[:, cols], contract).astype(dst.dtype)

    by_columns(src.shape[1], 256, body)


def greet(experts, me, core, partner):
    barrier = pltpu.get_barrier_semaphore()

    def hello(k, carry):
        pl.semaphore_signal(
            barrier, inc=1, device_id=(lax.rem(me + k, experts), core), device_id_type=MESH
        )
        return carry

    lax.fori_loop(1, experts, hello, 0)
    if partner is not None:
        pl.semaphore_signal(barrier, inc=1, device_id=(me, partner), device_id_type=MESH)
    pl.semaphore_wait(barrier, experts - 1 + (partner is not None))


class Spread:
    def __init__(self, experts, me, core, src, dst, sends, recvs, local):
        self.experts, self.me, self.core = experts, me, core
        self.src, self.dst, self.sends, self.recvs, self.local = src, dst, sends, recvs, local
        self.rows = src.shape[0] // experts

    def block(self, ref, index):
        return ref.at[pl.ds(pl.multiple_of(index * self.rows, 16), self.rows)]

    def copy(self, k):
        to = lax.rem(self.me + k, self.experts)
        return pltpu.make_async_remote_copy(
            self.block(self.src, to),
            self.block(self.dst, self.me),
            self.sends.at[k],
            self.recvs.at[k],
            device_id=(to, self.core),
            device_id_type=MESH,
        )

    def own(self):
        return pltpu.make_async_copy(
            self.block(self.src, self.me), self.block(self.dst, self.me), self.local
        )

    def start(self):
        self.own().start()

        def go(k, carry):
            self.copy(k).start()
            return carry

        lax.fori_loop(1, self.experts, go, 0)

    def wait(self):
        self.own().wait()

        def stop(k, carry):
            self.copy(k).wait()
            return carry

        lax.fori_loop(1, self.experts, stop, 0)


def tail_matrix(part, experts, tail, turned):
    size = PARTS * tail
    shape = (experts * tail, experts * size) if turned else (experts * size, experts * tail)
    there = lax.broadcasted_iota(jnp.int32, shape, 1 if turned else 0)
    here = lax.broadcasted_iota(jnp.int32, shape, 0 if turned else 1)
    want = here // tail * size + part * tail + here % tail
    return (there == want).astype(f32).astype(bf16)


def gelu_pair(v):
    u = v * v
    t = jnp.tanh(v * (0.7978845608 + 0.7978845608 * 0.044715 * u))
    h = 0.5 * t + 0.5
    slope = h + (h - h * h) * (v * (2 * 0.7978845608 + 6 * 0.7978845608 * 0.044715 * u))
    return v * h, slope


def experts_kernel(experts, tail, *refs):
    (a_in, b_in, ca_in, cb_in, cent, w1_h, w2_h, w3_h, w4_h) = refs[:9]
    (ra_out, rb_out, ga_out, gb_out, gcent, wu, wd) = refs[9:16]
    (xs_, gs_, act, slope, mid, psend, precv, ca, cb, sa, sb, cent_s, cent_r) = refs[16:29]
    (wsem, psems, prsems, xs, xr, asend, arecv, alocal) = refs[29:]
    me, core = lax.axis_index("expert"), lax.axis_index("hidden")
    other = 1 - core
    both, width = xs_.shape[1], xs_.shape[2]
    own = both // 2
    hid = wu.shape[2]
    main = a_in.shape[0]
    block = width // PARTS
    mine, theirs = pl.ds(0, own), pl.ds(own, own)

    loads = []
    for i, (h, v) in enumerate(((w1_h, wu.at[0]), (w2_h, wd.at[0]), (w3_h, wu.at[1]), (w4_h, wd.at[1]))):
        load = pltpu.make_async_copy(h, v, wsem.at[i])
        load.start()
        loads.append(load)
    greet(experts, me, core, other)

    def move(i, src, dst):
        return Spread(experts, me, core, src, dst, asend.at[i], arecv.at[i], alocal.at[i])

    cot_moves = (move(0, ca_in, ca), move(1, cb_in, cb))
    for m in cot_moves:
        m.start()

    def pair(src, dst, send, recv):
        return pltpu.make_async_remote_copy(
            src, dst, send, recv, device_id=(me, other), device_id_type=MESH
        )

    def share_x(i):
        return pair(xs_.at[i, mine], xs_.at[i, theirs], xs.at[i], xr.at[i])

    def share_g(i):
        return pair(gs_.at[i, mine], gs_.at[i, theirs], xs.at[2 + i], xr.at[2 + i])

    def partial_send(step):
        return pair(psend, precv.at[lax.rem(step, 2)], psems.at[step], prsems.at[step])

    def from_tail(ref, to, start):
        for q in range(PARTS):
            to[0, pl.ds(start, experts * tail), q * block : (q + 1) * block] = mm(
                tail_matrix(q, experts, tail, True), ref[...]
            ).astype(bf16)

    def to_tail(value, ref):
        total = None
        for q in range(PARTS):
            term = mm(tail_matrix(q, experts, tail, False), value[:, q * block : (q + 1) * block])
            total = term if total is None else total + term
        ref[...] = total.astype(bf16)

    TN, WM, WN = 512, 512, 1024

    def over(size, body):
        def step(n, carry):
            body(pl.ds(pl.multiple_of(n * TN, TN), TN))
            return carry

        lax.fori_loop(0, size // TN, step, 0)

    def halves(body):
        def step(r, carry):
            body(r, pl.ds(pl.multiple_of(r * own, own), own))
            return carry

        lax.fori_loop(0, 2, step, 0)

    def exchange(step, source, weights, turned):
        def rows_of(r, unused):
            rows = pl.ds(pl.multiple_of((1 - r) * own, own), own)

            def body(cols):
                if turned:
                    value = mm(source[rows, :], weights[cols, :], (1, 1))
                else:
                    value = mm(source[rows, :], weights[:, cols])

                @pl.when(r == 0)
                def _():
                    psend[:, cols] = value.astype(bf16)

                @pl.when(r == 1)
                def _():
                    mid[:, cols] += value

            over(width, body)

            @pl.when(r == 0)
            def _():
                partial_send(step).start()

        halves(rows_of)
        partial_send(step).wait()
        mid[...] += precv[lax.rem(step, 2)].astype(f32)

    xs_[0, pl.ds(0, main), :] = a_in[...]
    from_tail(b_in, xs_, main)
    share_x(0).start()
    slot = xs_[0, mine, :].astype(f32)
    mid[...] = slot
    gate = jax.nn.sigmoid(jnp.sum(slot * cent[...].astype(f32), axis=1, keepdims=True))

    def forward(i, carry):
        def up(r, rows):
            @pl.when(r == 1)
            def _():
                share_x(i).wait()

            def body(cols):
                a, d = gelu_pair(mm(xs_[i, rows, :], wu[i, :, cols]))
                act[i, rows, cols] = a.astype(bf16)
                slope[i, rows, cols] = d.astype(bf16)

            over(hid, body)

        for k in range(2):

            @pl.when(i == k)
            def _():
                loads[2 * k].wait()

        halves(up)
        for k in range(2):

            @pl.when(i == k)
            def _():
                loads[2 * k + 1].wait()

        exchange(i, act.at[i], wd.at[i], False)

        @pl.when(i == 0)
        def _():
            xs_[1, mine, :] = mid[...].astype(bf16)
            share_x(1).start()

        return carry

    lax.fori_loop(0, 2, forward, 0)
    returned = (gate * mid[...]).astype(bf16)
    sa[...] = returned[:main]
    to_tail(returned[main:], sb)
    ret_moves = (move(2, sa, ra_out), move(3, sb, rb_out))
    for m in ret_moves:
        m.start()
    for m in cot_moves:
        m.wait()
    gs_[0, pl.ds(0, main), :] = ca[...]
    from_tail(cb, gs_, main)
    cot = gs_[0, mine, :].astype(f32)
    logit = jnp.sum(cot * mid[...], axis=1, keepdims=True) * gate * (1.0 - gate)
    cent_s[...] = jnp.sum(logit * xs_[0, mine, :].astype(f32), axis=0, keepdims=True)
    share_c = pair(cent_s, cent_r, xs.at[4], xr.at[4])
    share_c.start()
    start_grad = (gate * cot).astype(bf16)
    gs_[1, mine, :] = start_grad
    mid[...] = start_grad.astype(f32)
    share_g(1).start()

    def backward(k, carry):
        i = 1 - k

        def up_back(r, rows):
            @pl.when(r == 1)
            def _():
                share_g(i).wait()

            def body(cols):
                t = mm(gs_[i, rows, :], wd[i, cols, :], (1, 1)) * slope[i, rows, cols].astype(f32)
                slope[i, rows, cols] = t.astype(bf16)

            over(hid, body)

        halves(up_back)
        exchange(2 + k, slope.at[i], wu.at[i], True)

        @pl.when(k == 0)
        def _():
            gm = mid[...].astype(bf16)
            gs_[0, mine, :] = gm
            mid[...] = gm.astype(f32) + logit * cent[...].astype(f32)
            share_g(0).start()

        return carry

    lax.fori_loop(0, 2, backward, 0)
    for m in ret_moves:
        m.wait()
    slots = mid[...].astype(bf16)
    sa[...] = slots[:main]
    to_tail(slots[main:], sb)
    back_moves = (move(4, sa, ga_out), move(5, sb, gb_out))
    for m in back_moves:
        m.start()

    def weight_grad(left, right, to):
        wide_n = right.shape[1]

        def body(n, carry):
            m, c = n // (wide_n // WN), lax.rem(n, wide_n // WN)
            rows = pl.ds(pl.multiple_of(m * WM, WM), WM)
            cols = pl.ds(pl.multiple_of(c * WN, WN), WN)
            to[rows, cols] = mm(left[:, rows], right[:, cols], (0, 0)).astype(bf16)
            return carry

        lax.fori_loop(0, left.shape[1] // WM * (wide_n // WN), body, 0)

    def weight_grads(i, carry):
        weight_grad(act.at[i], gs_.at[i], wd.at[i])
        weight_grad(xs_.at[i], slope.at[i], wu.at[i])
        return carry

    lax.fori_loop(0, 2, weight_grads, 0)
    share_c.wait()
    gcent[...] = cent_s[...] + cent_r[...]
    for m in back_moves:
        m.wait()


def run_experts(experts, slots, tails, cots, cot_tails, centroid, weights):
    width, hid = weights[0].shape
    main = slots.shape[0]
    tail = tails.shape[0] // experts // PARTS
    own = main + experts * tail
    both = 2 * own

    def sds(*shape, dtype=bf16):
        return jax.ShapeDtypeStruct(shape, dtype)

    travel = [sds(*slots.shape), sds(*tails.shape)] * 2
    wide = [pltpu.VMEM((2, width, hid), bf16), pltpu.VMEM((2, hid, width), bf16)]
    return pl.pallas_call(
        functools.partial(experts_kernel, experts, tail),
        out_shape=travel + [sds(1, width, dtype=f32)] + wide,
        in_specs=[VM, VM, ANY, ANY, VM, ANY, ANY, ANY, ANY],
        out_specs=[ANY] * 4 + [VM] * 3,
        scratch_shapes=[
            pltpu.VMEM((2, both, width), bf16),
            pltpu.VMEM((2, both, width), bf16),
            pltpu.VMEM((2, both, hid), bf16),
            pltpu.VMEM((2, both, hid), bf16),
            pltpu.VMEM((own, width), f32),
            pltpu.VMEM((own, width), bf16),
            pltpu.VMEM((2, own, width), bf16),
            pltpu.VMEM(slots.shape, bf16),
            pltpu.VMEM(tails.shape, bf16),
            pltpu.VMEM(slots.shape, bf16),
            pltpu.VMEM(tails.shape, bf16),
            pltpu.VMEM((1, width), f32),
            pltpu.VMEM((1, width), f32),
            DMA((4,)),
            DMA((4,)),
            DMA((4,)),
            DMA((5,)),
            DMA((5,)),
            DMA((6, experts)),
            DMA((6, experts)),
            DMA((6,)),
        ],
        compiler_params=pltpu.CompilerParams(
            collective_id=2, has_side_effects=True, vmem_limit_bytes=45 << 20
        ),
        name="experts_pass",
    )(slots, tails, cots, cot_tails, centroid, *weights)

def back_kernel(experts, tail, *refs):
    (ra, rb, ga, gb, dm, dt, gains, cot_h, res_h, tok_h, packed_h, probs_h, mixed_h, wall_h) = refs[:14]
    refs = refs[:14] + refs[15:]
    out_o, ig_o, gqkv_o, gout_o, ggain_o = refs[14:19]
    (cot, res, tok, packed, probs, mixed, wqkv, wout, normed, gatt, gmix, gpk, so, si, perm, wide, turn) = refs[19:36]
    keeps, psends, precvs, rv1s, rv2s, rv3s = (refs[36 + 6 * i : 42 + 6 * i] for i in range(6))
    lsem, sends, recvs, asend, arecv, alocal = refs[72:]
    me, core = lax.axis_index("expert"), lax.axis_index("hidden")
    other = 1 - core
    my_z, my_y, my_x = me // 4, lax.rem(me // 2, 2), lax.rem(me, 2)
    rows, width = tok.shape
    block = width // PARTS

    loads = {}
    for i, (name, h, v) in enumerate(
        (
            ("res", res_h, res),
            ("cot", cot_h, cot),
            ("mixed", mixed_h, mixed),
            ("wout", wall_h.at[:, pl.ds(3 * width + 128, width)], wout),
            ("probs", probs_h, probs),
            ("packed", packed_h, packed),
            ("tok", tok_h, tok),
            ("wqkv", wall_h.at[:, pl.ds(0, 3 * width)], wqkv),
        )
    ):
        loads[name] = pltpu.make_async_copy(h, v, lsem.at[i])
        loads[name].start()
    greet(experts, me, core, other)

    def join_slots(slots, tails):
        def body(cols, q):
            wide[:, cols] = mm(dm[...], slots[:, cols], (0, 0)) + mm(dt[q], tails[...], (0, 0))

        by_columns(width, block, body)

    piece = SEQ // experts
    seats = MICRO * PER

    shape = (rows, rows)
    to, at = lax.broadcasted_iota(jnp.int32, shape, 0), lax.broadcasted_iota(jnp.int32, shape, 1)
    b, s, q = to // (seats * piece), to // piece % seats, to % piece
    turn[...] = (at == s * SEQ + b * piece + q).astype(f32).astype(bf16)

    def move(i, src, dst):
        return Spread(experts, me, core, src, dst, asend.at[i], arecv.at[i], alocal.at[i])

    my_a = jnp.where(core == 0, my_x, my_y)
    my_b = jnp.where(core == 0, my_y, my_x)

    def near(a_step, b_step):
        a, b = (1 - my_a if a_step else my_a), (1 - my_b if b_step else my_b)
        x, y = jnp.where(core == 0, a, b), jnp.where(core == 0, b, a)
        return my_z * 4 + y * 2 + x

    def remote(c, stage, src, dst, to, to_core):
        return pltpu.make_async_remote_copy(
            src, dst, sends.at[c, stage], recvs.at[c, stage],
            device_id=(to, to_core), device_id_type=MESH,
        )

    def pair_copy(c):
        return remote(c, 0, psends[c], precvs[c], me, other)

    def a_copy(c):
        return remote(c, 1, psends[c].at[pl.ds(0, 256)], rv1s[c], near(True, False), core)

    def b_copy(c):
        return remote(c, 2, psends[c].at[pl.ds(256, 128)], rv2s[c], near(False, True), core)

    def z_copy(c, dz):
        to_z = lax.rem(my_z + dz, 4)
        src = psends[c].at[pl.ds(pl.multiple_of(384 + to_z * 32, 32), 32)]
        return remote(c, 2 + dz, src, rv3s[c].at[dz - 1], to_z * 4 + my_y * 2 + my_x, core)

    def place(c, t, cols):
        keeps[c][:, cols] = t[: width // 2]
        psends[c][:, cols] = t[width // 2 :].astype(bf16)

    at = lax.broadcasted_iota(jnp.int32, (1, width), 1)
    goes = jnp.where(at < width // 2, core, other)
    high, mid_ = at // 256 % 2, at // 128 % 2
    to_x, to_y = jnp.where(goes == 0, high, mid_), jnp.where(goes == 0, mid_, high)
    source = (((at // 32 % 4) * 4 + to_y * 2 + to_x) * 2 + goes) * 32 + at % 32
    perm[...] = (lax.broadcasted_iota(jnp.int32, (width, width), 0) == source).astype(f32).astype(bf16)

    def compute(c, left, right, start, stride, count, size):
        def body(n, carry):
            cols = pl.ds(pl.multiple_of(start + n * stride, size), size)
            place(c, mm(left[...], right[:, cols], (0, 0)), pl.ds(pl.multiple_of(n * size, size), size))
            return carry

        lax.fori_loop(0, count, body, 0)
        pair_copy(c).start()

    half_a = pl.ds(pl.multiple_of(my_a * 256, 256), 256)
    half_a_out = pl.ds(pl.multiple_of((1 - my_a) * 256, 256), 256)
    base_b = my_a * 256
    half_b = pl.ds(pl.multiple_of(base_b + my_b * 128, 128), 128)
    half_b_out = pl.ds(pl.multiple_of(base_b + (1 - my_b) * 128, 128), 128)

    def after_pair(c):
        pair_copy(c).wait()
        keep = keeps[c]
        keep[...] += precvs[c][...].astype(f32)
        psends[c][pl.ds(0, 256), :] = keep[half_a_out, :].astype(bf16)
        a_copy(c).start()

    def after_a(c):
        a_copy(c).wait()
        keep = keeps[c]
        keep[half_a, :] += rv1s[c][...].astype(f32)
        psends[c][pl.ds(256, 128), :] = keep[half_b_out, :].astype(bf16)
        b_copy(c).start()

    def after_b(c):
        b_copy(c).wait()
        keep = keeps[c]
        keep[half_b, :] += rv2s[c][...].astype(f32)
        psends[c][pl.ds(384, 128), :] = keep[half_b, :].astype(bf16)
        for dz in range(1, 4):
            z_copy(c, dz).start()

    def after_z(c, pieces):
        for dz in range(1, 4):
            z_copy(c, dz).wait()
        at = pl.ds(pl.multiple_of(base_b + my_b * 128 + my_z * 32, 32), 32)
        total = keeps[c][at, :]
        for dz in range(3):
            total = total + rv3s[c][dz].astype(f32)
        size = total.shape[1] // len(pieces)
        for n, (out, start) in enumerate(pieces):
            out[:, start : start + size] = total[:, n * size : (n + 1) * size]

    gain_a, gain_f = gains[0:1, :], gains[1:2, :]
    loads["res"].wait()
    join_slots(ra, rb)
    gmix[...] = (res[...] + wide[...]).astype(bf16)
    apply_rows(turn, gmix, so)
    out_move = move(0, so, out_o)
    out_move.start()
    unit, inv = norm_parts(res[...])
    join_slots(ga, gb)
    grad_shared = wide[...]
    ffn_sums = jnp.sum(grad_shared * unit, axis=0, keepdims=True)
    loads["cot"].wait()
    grad = cot[...].astype(f32) + norm_back(unit, inv, gain_f, grad_shared)
    res[...] = grad
    gatt[...] = grad.astype(bf16)
    loads["mixed"].wait()
    gpk_view = gpk.at[:, pl.ds(0, width)]
    apply_rows(mixed, perm, gpk_view)
    compute(0, gpk_view, gatt, 0, width // 4, 4, width // 4)
    loads["wout"].wait()

    def mix(cols, n):
        gmix[:, cols] = mm(gatt[...], wout[cols, :], (1, 1)).astype(bf16)

    by_columns(width, 256, mix)
    after_pair(0)
    loads["probs"].wait()
    loads["packed"].wait()
    lane = lax.broadcasted_iota(jnp.int32, (PACK, 2 * HEAD), 1)
    first = lane < HEAD

    def stacked(v):
        zero = jnp.zeros_like(v)
        return jnp.concatenate([jnp.where(first, v, zero), jnp.where(first, zero, v)], axis=0)

    def head_pair(p, h):
        at = pl.ds(pl.multiple_of(p * PACK, PACK), PACK)
        lo = h * 2 * HEAD
        q = packed[at, lo : lo + 2 * HEAD]
        k = packed[at, width + lo : width + lo + 2 * HEAD]
        v = packed[at, 2 * width + lo : 2 * width + lo + 2 * HEAD]
        gs = stacked(gmix[at, lo : lo + 2 * HEAD])
        pr_lo = probs[p * (HEADS // 2) + h]
        pr = pr_lo.astype(f32)
        gp = mm(gs, v, (1, 1))
        gv = mm(pr_lo, gs, (0, 0))
        inner = jnp.sum(pr * gp, axis=1, keepdims=True)
        ds_ = (pr * (gp - inner)).astype(bf16)
        t = mm(ds_, k)
        gq = jnp.where(first, t[:PACK], t[PACK:]) * 0.125
        gk = mm(ds_, stacked(q), (0, 0)) * 0.125
        gpk[at, lo : lo + 2 * HEAD] = gq.astype(bf16)
        gpk[at, width + lo : width + lo + 2 * HEAD] = gk.astype(bf16)
        gpk[at, 2 * width + lo : 2 * width + lo + 2 * HEAD] = gv.astype(bf16)

    part = width // 4

    def group_pieces(g):
        return tuple(part * g + width * i for i in range(3))

    def group(g):
        def packs(p, carry):
            for h in range(HEADS // 8):
                head_pair(p, g * (HEADS // 8) + h)
            return carry

        lax.fori_loop(0, MICRO, packs, 0)

    def set_off(g):
        compute(1 + g, normed, gpk, part * g, width, 3, part)

    def finish(g):
        after_z(1 + g, [(gqkv_o, start) for start in group_pieces(g)])

    loads["tok"].wait()
    unit, inv = norm_parts(tok[...].astype(f32))
    so2 = gpk.at[:, pl.ds(2 * width, width)]
    so2[...] = (unit * gain_a).astype(bf16)
    apply_rows(so2, perm, normed)
    group(0)
    set_off(0)
    group(1)
    set_off(1)
    after_pair(1)
    after_a(0)
    group(2)
    set_off(2)
    after_pair(2)
    group(3)
    after_pair(3)
    after_a(1)
    after_b(0)
    loads["wqkv"].wait()

    def pull(cols, n):
        wide[:, cols] = mm(gpk[...], wqkv[cols, :], (1, 1))

    by_columns(width, 256, pull)
    grad_normed = wide[...]
    unit, inv = norm_parts(tok[...].astype(f32))
    attn_sums = jnp.sum(grad_normed * unit, axis=0, keepdims=True)
    gmix[...] = (res[...] + norm_back(unit, inv, gain_a, grad_normed)).astype(bf16)
    apply_rows(turn, gmix, si)
    ig_move = move(1, si, ig_o)
    ig_move.start()
    set_off(3)
    after_a(2)
    after_b(1)
    sums = jnp.where(lax.broadcasted_iota(jnp.int32, (128, width), 0) < 64, attn_sums, ffn_sums)
    sums_hi = sums.astype(bf16)
    sums_lo = (sums - sums_hi.astype(f32)).astype(bf16)
    place(5, mm(perm[...], sums_hi, (0, 1)) + mm(perm[...], sums_lo, (0, 1)), pl.ds(0, 128))
    pair_copy(5).start()
    after_pair(4)
    after_pair(5)
    after_z(0, [(gout_o, 0)])
    after_a(3)
    after_b(2)
    finish(0)
    after_a(4)
    after_a(5)
    after_b(3)
    finish(1)
    after_b(4)
    after_b(5)
    finish(2)
    finish(3)
    after_z(5, [(ggain_o, 0)])
    out_move.wait()
    ig_move.wait()


def run_back(experts, tail, slots, tails, grads, grad_tails, d_main, d_tail, gains, cot, residual, tok, packed, probs, mixed, w_all, done):
    rows, width = tok.shape

    def sds(*shape, dtype=bf16):
        return jax.ShapeDtypeStruct(shape, dtype)

    widths = (width,) + (3 * width // 4,) * 4 + (128,)
    scratch = [
        pltpu.VMEM(cot.shape, bf16),
        pltpu.VMEM(residual.shape, f32),
        pltpu.VMEM(tok.shape, bf16),
        pltpu.VMEM(packed.shape, bf16),
        pltpu.VMEM(probs.shape, bf16),
        pltpu.VMEM(mixed.shape, bf16),
        pltpu.VMEM((width, 3 * width), bf16),
        pltpu.VMEM((width, width), bf16),
        pltpu.VMEM((rows, width), bf16),
        pltpu.VMEM((rows, width), bf16),
        pltpu.VMEM((rows, width), bf16),
        pltpu.VMEM((rows, 3 * width), bf16),
        pltpu.VMEM((rows, width), bf16),
        pltpu.VMEM((rows, width), bf16),
        pltpu.VMEM((width, width), bf16),
        pltpu.VMEM((rows, width), f32),
        pltpu.VMEM((rows, rows), bf16),
    ]
    scratch += [pltpu.VMEM((width // 2, w), f32) for w in widths]
    for part in (2, 2, 4, 8):
        scratch += [pltpu.VMEM((width // part, w), bf16) for w in widths]
    scratch += [pltpu.VMEM((3, 32, w), bf16) for w in widths]
    scratch += [
        DMA((8,)),
        DMA((6, 6)),
        DMA((6, 6)),
        DMA((2, experts)),
        DMA((2, experts)),
        DMA((2,)),
    ]
    return pl.pallas_call(
        functools.partial(back_kernel, experts, tail),
        out_shape=[sds(rows, width), sds(rows, width), sds(32, 3 * width, dtype=f32), sds(32, width, dtype=f32), sds(32, 128, dtype=f32)],
        in_specs=[VM] * 7 + [ANY] * 8,
        out_specs=[ANY, ANY, VM, VM, VM],
        scratch_shapes=scratch,
        compiler_params=pltpu.CompilerParams(
            collective_id=3, has_side_effects=True, vmem_limit_bytes=VMEM_MAX
        ),
        name="attention_back",
    )(slots, tails, grads, grad_tails, d_main, d_tail, gains, cot, residual, tok, packed, probs, mixed, w_all, done)


def front_kernel(experts, tail, *refs):
    (tokens, cots, routes, orders, deal, lengths, g_attn, g_ffn, w_qkv, w_out) = refs[:10]
    (slots_o, tails_o, cslots_o, ctails_o, deal_o, dm_o, dt_o, gains_o, cot_o, res_o, tok_o, packed_o, probs_o, mixed_o, w_o) = refs[10:25]
    (st, sl, rt, rl, rc, tok, cot, w, packed, probs, mixed, res, shared, dm, dt, ftm, masks, ss, stl, cs, ctl, turn) = refs[25:47]
    zs, zr, as_, ar, bs, br, ps, pr, asend, arecv, alocal, osem = refs[47:]
    me, core = lax.axis_index("expert"), lax.axis_index("hidden")
    other = 1 - core
    my_z, my_y, my_x = me // 4, lax.rem(me // 2, 2), lax.rem(me, 2)
    rows, width = tok.shape
    piece = SEQ // experts
    seats = MICRO * PER
    block = width // PARTS
    step = w_qkv.shape[0]
    per_dest = experts and dims(experts, width)[0]
    main = per_dest - tail
    capacity = per_dest // MICRO

    def iota(shape, axis):
        return lax.broadcasted_iota(jnp.int32, shape, axis)

    def one_hot(test):
        return test.astype(f32).astype(bf16)

    own_rows = pl.ds(pl.multiple_of((me * 2 + core) * step, step), step)
    gain_at, out_at = 3 * width, 3 * width + 128
    w[own_rows, :gain_at] = w_qkv[...]
    w[own_rows, out_at:] = w_out[...]
    eye = iota((step, step), 0) == iota((step, step), 1)

    def as_column(row):
        return jnp.sum(jnp.where(eye, row[...].astype(f32), 0.0), axis=1, keepdims=True)

    gain_cols = jnp.where(iota((step, 128), 1) < 64, as_column(g_attn), as_column(g_ffn))
    w[own_rows, gain_at:out_at] = gain_cols.astype(bf16)
    cuts = ((0, out_at), (out_at, width))

    line = lax.rem(me, 4)
    a_to = jnp.where(core == 0, my_z * 4 + my_y * 2 + 1 - my_x, my_z * 4 + 2 - 2 * my_y + my_x)
    b_to = jnp.where(core == 0, my_z * 4 + 2 - 2 * my_y + my_x, my_z * 4 + my_y * 2 + 1 - my_x)
    shift_a, shift_b = a_to - me, b_to - me

    def send(j, e, sem_s, sem_r, to, to_core):
        start, size = cuts[j]
        ref = w.at[pl.ds(pl.multiple_of((e * 2 + core) * step, step), step), pl.ds(start, size)]
        return pltpu.make_async_remote_copy(
            ref, ref, sem_s, sem_r, device_id=(to, to_core), device_id_type=MESH
        )

    def up(j, d):
        s = my_z - d
        return send(j, s * 4 + line, zs.at[j, d], zr.at[j, s], me + 4, core)

    def down(j, d):
        s = my_z + d
        return send(j, s * 4 + line, zs.at[j, 4 + d], zr.at[j, s], me - 4, core)

    def a_copy(j, s):
        return send(j, s * 4 + line, as_.at[j, s], ar.at[j, s], a_to, core)

    def b_copy(j, f, s):
        return send(j, s * 4 + line + f * shift_a, bs.at[j, 4 * f + s], br.at[j, 4 * f + s], b_to, core)

    def p_copy(j, f, s):
        e = s * 4 + line + (f % 2) * shift_a + (f // 2) * shift_b
        return send(j, e, ps.at[j, 4 * f + s], pr.at[j, 4 * f + s], me, other)

    def release(j, s):
        b_copy(j, 0, s).start()
        a_copy(j, s).start()
        p_copy(j, 0, s).start()

    def chain(j, d):
        @pl.when(my_z >= d)
        def _():
            if d:
                up(j, d).wait_recv()

            @pl.when(my_z < 3)
            def _():
                up(j, d).start()

            if d:
                release(j, my_z - d)

        @pl.when(my_z + d <= 3)
        def _():
            if d:
                down(j, d).wait_recv()

            @pl.when(my_z > 0)
            def _():
                down(j, d).start()

            if d:
                release(j, my_z + d)

        if not d:
            release(j, my_z)

    def places():
        return [lax.rem(my_z + k, 4) for k in (0, 1, 3, 2)]

    def fan_a(j):
        for s in places():
            a_copy(j, s).wait_recv()
            b_copy(j, 1, s).start()
            p_copy(j, 1, s).start()

    def fan_b(j):
        for f in range(2):
            for s in places():
                b_copy(j, f, s).wait_recv()
                p_copy(j, 2 + f, s).start()

    def fan_p(j):
        for f in range(4):
            for s in range(4):
                p_copy(j, f, s).wait_recv()

    def all_sent(j):
        for d in range(4):

            @pl.when((my_z >= d) & (my_z < 3))
            def _():
                up(j, d).wait_send()

            @pl.when((my_z + d <= 3) & (my_z > 0))
            def _():
                down(j, d).wait_send()

        for s in range(4):
            a_copy(j, s).wait_send()
            for f in range(2):
                b_copy(j, f, s).wait_send()
            for f in range(4):
                p_copy(j, f, s).wait_send()

    greet(experts, me, core, other)
    chain(0, 0)
    chain(1, 0)

    def move(i, src, dst):
        return Spread(experts, me, core, src, dst, asend.at[i], arecv.at[i], alocal.at[i])

    group = deal.shape[1]
    deal_row = deal[pl.ds(core, 1), :]
    length_row = lengths[pl.ds(core, 1), :]
    spread_out = one_hot(iota((group, rows), 1) // piece == iota((group, rows), 0))
    wide = jnp.broadcast_to(deal_row.astype(f32), (8, group)).astype(bf16)
    goal = mm(wide, spread_out)[0:1].astype(jnp.int32) * piece + iota((1, rows), 1) % piece
    ftm[...] = one_hot(iota((rows, rows), 0) == goal)
    apply_rows(ftm, tokens, st)
    lab = jnp.where(iota((128, rows), 0) < 64, routes[...], orders[...]).astype(f32).astype(bf16)
    sl[...] = mm(ftm[...], lab, (1, 1)).astype(bf16)
    tok_moves = (move(0, st, rt), move(1, sl, rl))
    for m in tok_moves:
        m.start()
    chain(0, 1)
    apply_rows(ftm, cots, cs)
    chain(0, 2)
    goal_col = mm(spread_out, wide, (0, 1))[:, 0:1].astype(jnp.int32) * piece + iota((rows, 1), 0) % piece
    ftm[...] = one_hot(iota((rows, rows), 1) == goal_col)
    chain(0, 3)
    fan_a(0)
    chain(1, 1)
    chain(1, 2)
    chain(1, 3)
    for m in tok_moves:
        m.wait()

    outs = []

    def store(i, ref, out):
        copy = pltpu.make_async_copy(ref, out, osem.at[i])
        copy.start()
        outs.append(copy)

    cot_move = move(2, cs, rc)
    cot_move.start()
    store(0, ftm, deal_o)
    to, at = iota((rows, rows), 0), iota((rows, rows), 1)
    b, s, q = to // (seats * piece), to // piece % seats, to % piece
    turn[...] = one_hot(at == s * SEQ + b * piece + q)
    apply_rows(turn, rt, tok, (0, 0))
    store(1, tok, tok_o)
    lab_col = mm(turn[...], rl[...], (0, 0))
    lab_row = mm(rl[...], turn[...], (0, 0))
    fan_a(1)
    ranks, heads_at, oks = [], [], []
    own = [
        jnp.sum(jnp.where(deal_row == me * seats + i, length_row, 0), axis=1, keepdims=True)
        for i in range(seats)
    ]
    posr, posc = iota((1, PACK), 1), iota((PACK, 1), 0)
    near_ = (iota((PACK, PACK), 0) // SEQ == iota((PACK, PACK), 1) // SEQ) & (
        iota((PACK, PACK), 1) <= iota((PACK, PACK), 0)
    )
    for p in range(MICRO):
        low, high = own[PER * p], own[PER * p + 1]
        here_r = posr % SEQ < jnp.where(posr < SEQ, low, high)
        here_c = posc % SEQ < jnp.where(posc < SEQ, low, high)
        masks[p] = (near_ & here_r).astype(f32)
        cols = slice(p * PACK, (p + 1) * PACK)
        route_r = lab_row[0:1, cols]
        key_r = lab_row[64:65, cols] * PER + (posr // SEQ).astype(f32)
        route_c = lab_col[cols, 0:1]
        key_c = lab_col[cols, 64:65] * PER + (posc // SEQ).astype(f32)
        ahead = jnp.sum(
            ((route_c == route_r) & (key_c < key_r) & here_c).astype(f32), axis=0, keepdims=True
        ).astype(jnp.int32)
        base = p * capacity + ahead
        good = here_r & (ahead < capacity)
        route_i = route_r.astype(jnp.int32)
        heads_at.append(jnp.where(good & (base < main), route_i * main + base, -1))
        oks.append(jnp.where(good & (base >= main), route_i * (PARTS * tail) + base - main, -PARTS * PARTS * tail))
    head_row = jnp.concatenate(heads_at, axis=1)
    tail_row = jnp.concatenate(oks, axis=1)
    dm[...] = one_hot(iota(dm.shape, 0) == head_row)
    for part in range(PARTS):
        dt[part] = one_hot(iota(dt.shape[1:], 0) == tail_row + part * tail)
    store(2, dm, dm_o)
    store(3, dt, dt_o)

    def split(ref, to_main, to_tails):
        apply_rows(dm, ref, to_main)
        total = None
        for part in range(PARTS):
            term = mm(dt[part], ref[:, part * block : (part + 1) * block])
            total = term if total is None else total + term
        to_tails[...] = total.astype(bf16)

    inputs = tok[...].astype(f32)
    unit, inv = norm_parts(inputs)
    res[...] = unit
    fan_b(0)
    fan_p(0)
    big = iota((128, 128), 0) == iota((128, 128), 1)

    def gain_row(lane):
        parts = []
        for j in range(width // 128):
            col = w[128 * j : 128 * (j + 1), gain_at:out_at].astype(f32)[:, lane : lane + 1]
            parts.append(jnp.sum(jnp.where(big, col, 0.0), axis=0, keepdims=True))
        return jnp.concatenate(parts, axis=1)

    gain_a, gain_f = gain_row(0), gain_row(64)
    gains_o[0:1, :] = gain_a
    gains_o[1:2, :] = gain_f
    shared[...] = (res[...] * gain_a).astype(bf16)

    def project(n, carry):
        cols = pl.ds(pl.multiple_of(n * 256, 256), 256)
        packed[:, cols] = mm(shared[...], w[:, cols]).astype(bf16)
        return carry

    lax.fori_loop(0, 3 * width // 256, project, 0)
    store(5, packed, packed_o)
    first = iota((PACK, 2 * HEAD), 1) < HEAD

    def pack(n, carry):
        p, half = n // 2, lax.rem(n, 2)
        at = pl.ds(pl.multiple_of(p * PACK, PACK), PACK)
        mask = masks[p] > 0.5
        mask = jnp.concatenate([mask, mask], axis=0)
        for j in range(HEADS // 4):
            h = half * (HEADS // 4) + j
            own_lanes, key_lanes, value_lanes = (
                pl.ds(pl.multiple_of(h * 2 * HEAD + n * width, 2 * HEAD), 2 * HEAD) for n in range(3)
            )
            q, k, v = packed[at, own_lanes], packed[at, key_lanes], packed[at, value_lanes]
            zero = jnp.zeros_like(q)
            qs = jnp.concatenate([jnp.where(first, q, zero), jnp.where(first, zero, q)], axis=0)
            scores = jnp.where(mask, mm(qs, k, (1, 1)) * 0.125, -1e30)
            e = jnp.exp(scores - jnp.max(scores, axis=1, keepdims=True))
            prob = (e / jnp.sum(e, axis=1, keepdims=True)).astype(bf16)
            probs[p * (HEADS // 2) + h] = prob
            t = mm(prob, v)
            mixed[at, own_lanes] = jnp.where(first, t[:PACK], t[PACK:]).astype(bf16)
        return carry

    fan_b(1)
    lax.fori_loop(0, 2 * MICRO, pack, 0)
    store(6, probs, probs_o)
    fan_p(1)
    store(4, w, w_o)
    store(7, mixed, mixed_o)
    apply_rows(mixed, w.at[:, pl.ds(out_at, width)], res)
    residual = tok[...].astype(f32) + res[...]
    res[...] = residual
    store(8, res, res_o)
    unit, inv = norm_parts(residual)
    shared[...] = (unit * gain_f).astype(bf16)
    split(shared, ss, stl)
    slot_moves = (move(3, ss, slots_o), move(4, stl, tails_o))
    cot_move.wait()
    for m in slot_moves:
        m.start()
    apply_rows(turn, rc, cot, (0, 0))
    store(9, cot, cot_o)
    split(cot, cs, ctl)
    store(10, cs, cslots_o)
    store(11, ctl, ctails_o)
    all_sent(0)
    all_sent(1)
    for copy in outs:
        copy.wait()
    for m in slot_moves:
        m.wait()


def run_front(experts, tail, tokens, cots, routes, orders, deal, lengths, g_attn, g_ffn, w_qkv, w_out):
    rows, width = tokens.shape
    per_dest = dims(experts, width)[0]
    main = (per_dest - tail) * experts
    side = experts * PARTS * tail

    def sds(*shape, dtype=bf16):
        return jax.ShapeDtypeStruct(shape, dtype)

    tails = (side, width // PARTS)
    out_shape = [
        sds(main, width),
        sds(*tails),
        sds(main, width),
        sds(*tails),
        sds(rows, rows),
        sds(main, rows),
        sds(PARTS, side, rows),
        sds(2, width, dtype=f32),
        sds(rows, width),
        sds(rows, width, dtype=f32),
        sds(rows, width),
        sds(rows, 3 * width),
        sds(MICRO * HEADS // 2, 2 * PACK, PACK),
        sds(rows, width),
        sds(width, 4 * width + 128),
    ]
    vm = pltpu.VMEM
    return pl.pallas_call(
        functools.partial(front_kernel, experts, tail),
        out_shape=out_shape,
        in_specs=[VM] * 10,
        out_specs=[ANY] * 7 + [VM] + [ANY] * 7,
        scratch_shapes=[
            vm((rows, width), bf16),
            vm((rows, 128), bf16),
            vm((rows, width), bf16),
            vm((rows, 128), bf16),
            vm((rows, width), bf16),
            vm((rows, width), bf16),
            vm((rows, width), bf16),
            vm((width, 4 * width + 128), bf16),
            vm((rows, 3 * width), bf16),
            vm((MICRO * HEADS // 2, 2 * PACK, PACK), bf16),
            vm((rows, width), bf16),
            vm((rows, width), f32),
            vm((rows, width), bf16),
            vm((main, rows), bf16),
            vm((PARTS, side, rows), bf16),
            vm((rows, rows), bf16),
            vm((MICRO, PACK, PACK), f32),
            vm((main, width), bf16),
            vm(tails, bf16),
            vm((main, width), bf16),
            vm(tails, bf16),
            vm((rows, rows), bf16),
            DMA((2, 8)),
            DMA((2, 4)),
            DMA((2, 4)),
            DMA((2, 4)),
            DMA((2, 8)),
            DMA((2, 8)),
            DMA((2, 16)),
            DMA((2, 16)),
            DMA((5, experts)),
            DMA((5, experts)),
            DMA((5,)),
            DMA((12,)),
        ],
        compiler_params=pltpu.CompilerParams(
            collective_id=1, has_side_effects=True, vmem_limit_bytes=VMEM_MAX
        ),
        name="attention_front",
    )(tokens, cots, routes, orders, deal, lengths, g_attn, g_ffn, w_qkv, w_out)


def finish_kernel(f, out_r, ig_r, out_o, ig_o):
    out_o[...] = mm(f[...], out_r[...]).astype(bf16)
    ig_o[...] = mm(f[...], ig_r[...])


def run_finish(f, out_r, ig_r):
    steps = 2
    rows, width = out_r.shape

    def cut(shape):
        return pl.BlockSpec((shape[0] // steps, shape[1]), lambda i: (i, 0))

    def whole(shape):
        return pl.BlockSpec(shape, lambda i: (0, 0))

    outs = [
        jax.ShapeDtypeStruct((rows, width), bf16),
        jax.ShapeDtypeStruct((rows, width), f32),
    ]
    return pl.pallas_call(
        finish_kernel,
        grid=(steps,),
        out_shape=outs,
        in_specs=[cut(f.shape), whole(out_r.shape), whole(ig_r.shape)],
        out_specs=[cut(o.shape) for o in outs],
        name="finish",
    )(f, out_r, ig_r)


def widen_kernel(ups, downs, up_first, down_first, up_second, down_second, done):
    i = pl.program_id(0)
    for k, (up, down) in enumerate(((up_first, down_first), (up_second, down_second))):
        for narrow, full in ((ups, up), (downs, down)):
            size = full.shape[0]
            full[...] = narrow[k, pl.ds(pl.multiple_of(i * size, size), size), :].astype(f32)
    done[...] = jnp.zeros_like(done)


def run_widen(ups, downs):
    steps = 16

    def cut(shape):
        return pl.BlockSpec((shape[0] // steps, shape[1]), lambda i: (i, 0))

    outs = [jax.ShapeDtypeStruct(g.shape[1:], f32) for g in (ups, downs)] * 2
    return pl.pallas_call(
        widen_kernel,
        grid=(steps,),
        out_shape=outs + [jax.ShapeDtypeStruct((8, 128), f32)],
        in_specs=[VM, VM],
        out_specs=[cut(o.shape) for o in outs] + [pl.BlockSpec((8, 128), lambda i: (0, 0))],
        compiler_params=pltpu.CompilerParams(vmem_limit_bytes=24 << 20),
        name="widen",
    )(ups, downs)


def fast_shards(
    tokens,
    lengths,
    deal,
    routes,
    slot_order,
    gain_attn,
    gain_ffn,
    w_qkv,
    w_out,
    centroids,
    expert_in,
    expert_out,
    second_in,
    second_out,
    cotangent,
):
    width = tokens.shape[1]
    experts = lax.axis_size("expert")
    tail = dims(experts, width)[2]
    (slots, tails, cots, cot_tails, dealt, d_main, d_tail, gains, grad_output, residual, tok,
     packed, probs, mixed, w_all) = run_front(
        experts, tail, tokens, cotangent, routes.reshape(1, -1), slot_order.reshape(1, -1), deal, lengths,
        gain_attn[None], gain_ffn[None], w_qkv, w_out,
    )
    ra, rb, ga, gb, g_cent, ups, downs = run_experts(
        experts, slots, tails, cots, cot_tails, centroids,
        (expert_in[0], expert_out[0], second_in[0], second_out[0]),
    )
    *g_experts, done = run_widen(ups, downs)
    out_r, ig_r, g_qkv, g_out, g_gain = run_back(
        experts, tail, ra, rb, ga, gb, d_main, d_tail, gains, grad_output, residual, tok,
        packed, probs, mixed, w_all, done,
    )
    output, input_grad = run_finish(dealt, out_r, ig_r)
    return (
        output,
        input_grad,
        g_gain[:, 0],
        g_gain[:, 64],
        g_qkv,
        g_out,
        g_cent,
        *(g[None] for g in g_experts),
    )


def gather_hidden(rows):
    return lax.all_gather(rows, "hidden", axis=0, tiled=True)


def sum_hidden(terms):
    return lax.psum_scatter(terms, "hidden", scatter_dimension=0, tiled=True)


def swap(blocks):
    return lax.all_to_all(blocks, "expert", split_axis=0, concat_axis=0, tiled=True)


def plain_shards(
    tokens,
    lengths,
    deal,
    routes,
    slot_order,
    gain_attn,
    gain_ffn,
    w_qkv,
    w_out,
    centroids,
    expert_in,
    expert_out,
    second_in,
    second_out,
    cotangent,
):
    width = tokens.shape[1]
    experts = lax.axis_size("expert")
    piece = SEQ // experts
    seats = MICRO * PER
    group = experts * seats
    rows = seats * SEQ
    capacity = (9 * PACK + 8 * experts - 1) // (8 * experts)
    per_dest = MICRO * capacity
    my_expert = lax.axis_index("expert")
    my_hidden = lax.axis_index("hidden")

    deal_row = lax.dynamic_index_in_dim(deal, my_hidden, 0, keepdims=False)
    length_row = lax.dynamic_index_in_dim(lengths, my_hidden, 0, keepdims=False)
    ids = jnp.arange(group, dtype=jnp.int32)
    inverse = jnp.sum(jnp.where(deal_row[None, :] == ids[:, None], ids[None, :], 0), axis=1)
    own = my_expert * seats + jnp.arange(seats, dtype=jnp.int32)
    own_lengths = jnp.sum(
        jnp.where(deal_row[None, :] == own[:, None], length_row[None, :], 0), axis=1
    )

    def to_dealt(flat):
        pieces = jnp.take(flat.reshape(group, piece, flat.shape[1]), inverse, axis=0)
        return lax.all_to_all(
            pieces.reshape(experts, seats, piece, flat.shape[1]),
            "expert",
            split_axis=0,
            concat_axis=2,
            tiled=True,
        ).reshape(rows, flat.shape[1])

    labels = jnp.concatenate([routes, slot_order], axis=1)
    lab = to_dealt(labels)
    tok = to_dealt(tokens)
    grad_output = to_dealt(cotangent)

    cat = jnp.concatenate(
        [w_qkv, w_out, gain_attn[:, None], gain_ffn[:, None], jnp.zeros((w_qkv.shape[0], 126), bf16)],
        axis=1,
    )
    cat = lax.all_gather(cat, ("expert", "hidden"), axis=0, tiled=True)
    qkv_w = cat[:, : 3 * width]
    out_w = cat[:, 3 * width : 4 * width]
    attn_gain = cat[:, 4 * width].astype(f32)[None, :]
    ffn_gain = cat[:, 4 * width + 1].astype(f32)[None, :]

    route = lab[:, 0].reshape(MICRO, PACK)
    order = lab[:, 1].reshape(MICRO, PACK)
    positions = jnp.arange(PACK, dtype=jnp.int32)
    seat = positions // SEQ
    pack_lengths = own_lengths.reshape(MICRO, PER)
    limit = jnp.repeat(pack_lengths, SEQ, axis=1)
    present = (positions % SEQ)[None, :] < limit
    priority = order * PER + seat[None, :]
    ahead = jnp.sum(
        (
            (route[:, :, None] == route[:, None, :])
            & (priority[:, None, :] < priority[:, :, None])
            & present[:, None, :]
        ).astype(jnp.int32),
        axis=2,
    )
    accepted = (present & (ahead < capacity)).reshape(rows)
    target = (
        route * per_dest + jnp.arange(MICRO, dtype=jnp.int32)[:, None] * capacity + ahead
    ).reshape(rows)
    target = jnp.where(accepted, target, -1)
    slot_ids = jnp.arange(experts * per_dest, dtype=jnp.int32)
    dispatch = (slot_ids[:, None] == target[None, :]).astype(bf16)

    def to_experts(values):
        out = mm(dispatch, values).astype(bf16)
        return swap(out.reshape(experts, per_dest, width)).reshape(experts * per_dest, width)

    cot_arrived = to_experts(grad_output)

    inputs = tok.astype(f32)
    unit_a, inv_a = norm_parts(inputs)
    normed = (unit_a * attn_gain).astype(bf16)
    packed = mm(normed, qkv_w).astype(bf16)
    allowed = (
        (seat[:, None] == seat[None, :]) & (positions[None, :] <= positions[:, None])
    )[None] & present[:, None, :]

    def heads(block):
        return block.reshape(MICRO, PACK, HEADS, HEAD)

    queries = heads(packed[:, :width])
    keys_all = heads(packed[:, width : 2 * width])
    values_all = heads(packed[:, 2 * width :])
    scores = jnp.einsum("pqhd,pkhd->phqk", queries, keys_all, preferred_element_type=f32) * 0.125
    masked = jnp.where(allowed[:, None], scores, -1e30)
    peaks = jnp.max(masked, axis=-1, keepdims=True)
    log_total = peaks + jnp.log(jnp.sum(jnp.exp(masked - peaks), axis=-1, keepdims=True))
    probs = jnp.exp(masked - log_total)
    probs_lo = probs.astype(bf16)
    mixed = (
        jnp.einsum("phqk,pkhd->pqhd", probs_lo, values_all, preferred_element_type=f32)
        .reshape(rows, width)
        .astype(bf16)
    )
    residual = inputs + mm(mixed, out_w)
    unit_f, inv_f = norm_parts(residual)
    shared = (unit_f * ffn_gain).astype(bf16)
    arrived = to_experts(shared)

    centroid_row = centroids[0]
    w_in, w_back = expert_in[0], expert_out[0]
    s_in, s_back = second_in[0], second_out[0]
    count = arrived.shape[0]
    arrived_f = arrived.astype(f32)
    gate_vals = jax.nn.sigmoid(
        jnp.sum(arrived_f * centroid_row.astype(f32)[None, :], axis=1, keepdims=True)
    )
    grad_result_own = (gate_vals * cot_arrived.astype(f32)).astype(bf16)
    gathered = gather_hidden(arrived)
    grad_result = gather_hidden(grad_result_own)
    pre_first = mm(gathered, w_in)
    act_first, pull_first = jax.vjp(gelu_act, pre_first)
    act_first = act_first.astype(bf16)
    middle = arrived_f + sum_hidden(mm(act_first, w_back).astype(bf16)).astype(f32)
    middle_lo = gather_hidden(middle.astype(bf16))
    pre_second = mm(middle_lo, s_in)
    act_second, pull_second = jax.vjp(gelu_act, pre_second)
    act_second = act_second.astype(bf16)
    expert_sum = middle + sum_hidden(mm(act_second, s_back).astype(bf16)).astype(f32)
    returned = (gate_vals * expert_sum).astype(bf16)
    came_back = swap(returned.reshape(experts, per_dest, width)).reshape(count, width)

    grad_logit = (
        jnp.sum(cot_arrived.astype(f32) * expert_sum, axis=1, keepdims=True)
        * gate_vals
        * (1.0 - gate_vals)
    )
    grad_pre_second = pull_second(mm(grad_result, s_back, (1, 1)))[0].astype(bf16)
    grad_middle_own = (
        grad_result_own.astype(f32)
        + sum_hidden(mm(grad_pre_second, s_in, (1, 1)).astype(bf16)).astype(f32)
    ).astype(bf16)
    grad_middle = gather_hidden(grad_middle_own)
    grad_pre = pull_first(mm(grad_middle, w_back, (1, 1)))[0].astype(bf16)
    grad_slots = (
        sum_hidden(mm(grad_pre, w_in, (1, 1)).astype(bf16)).astype(f32)
        + grad_middle_own.astype(f32)
        + grad_logit * centroid_row.astype(f32)[None, :]
    ).astype(bf16)
    grad_back = swap(grad_slots.reshape(experts, per_dest, width)).reshape(count, width)
    g_sec_out = mm(act_second, grad_result, (0, 0))
    g_sec_in = mm(middle_lo, grad_pre_second, (0, 0))
    g_exp_out = mm(act_first, grad_middle, (0, 0))
    g_exp_in = mm(gathered, grad_pre, (0, 0))
    g_cent = jnp.sum(grad_logit * arrived_f, axis=0, keepdims=True)

    combined = (residual + mm(dispatch, came_back, (0, 0))).astype(bf16)

    grad_shared = mm(dispatch, grad_back, (0, 0))
    g_gain_ffn = jnp.sum(grad_shared * unit_f, axis=0)
    grad_residual = grad_output.astype(f32) + norm_back(unit_f, inv_f, ffn_gain, grad_shared)
    grad_attended = grad_residual.astype(bf16)
    g_out_w = mm(mixed, grad_attended, (0, 0))
    grad_mixed = heads(mm(grad_attended, out_w, (1, 1)).astype(bf16))
    grad_probs = jnp.einsum("pqhd,pkhd->phqk", grad_mixed, values_all, preferred_element_type=f32)
    grad_values = jnp.einsum("phqk,pqhd->pkhd", probs_lo, grad_mixed, preferred_element_type=f32)
    inner = jnp.sum(probs * grad_probs, axis=-1, keepdims=True)
    grad_scores = (probs * (grad_probs - inner)).astype(bf16)
    grad_queries = (
        jnp.einsum("phqk,pkhd->pqhd", grad_scores, keys_all, preferred_element_type=f32) * 0.125
    )
    grad_keys = (
        jnp.einsum("phqk,pqhd->pkhd", grad_scores, queries, preferred_element_type=f32) * 0.125
    )
    grad_packed = jnp.concatenate(
        [g.reshape(rows, width) for g in (grad_queries, grad_keys, grad_values)], axis=1
    ).astype(bf16)
    g_qkv = mm(normed, grad_packed, (0, 0))
    grad_normed = mm(grad_packed, qkv_w, (1, 1))
    g_gain_attn = jnp.sum(grad_normed * unit_a, axis=0)
    input_grad = (grad_residual + norm_back(unit_a, inv_a, attn_gain, grad_normed)).astype(bf16)

    def scatter(partial):
        return lax.psum_scatter(
            partial, ("expert", "hidden"), scatter_dimension=0, tiled=True
        )

    g_cat = jnp.concatenate([g_qkv, g_out_w, g_gain_attn[:, None], g_gain_ffn[:, None], jnp.zeros((width, 126), f32)], axis=1)
    g_cat = scatter(g_cat)
    g_cent = lax.psum(g_cent, "hidden")

    def from_dealt(dealt):
        received = lax.all_to_all(
            dealt.reshape(1, seats, SEQ, width), "expert", split_axis=2, concat_axis=0, tiled=True
        ).reshape(group, piece, width)
        return jnp.take(received, deal_row, axis=0).reshape(group * piece, width)

    return (
        from_dealt(combined),
        from_dealt(input_grad).astype(f32),
        g_cat[:, 4 * width],
        g_cat[:, 4 * width + 1],
        g_cat[:, : 3 * width],
        g_cat[:, 3 * width : 4 * width],
        g_cent,
        g_exp_in[None],
        g_exp_out[None],
        g_sec_in[None],
        g_sec_out[None],
    )


def solution(mesh):
    both = ("expert", "hidden")
    fast = mesh.shape["expert"] == 16 and mesh.shape["hidden"] == 2
    return jax.shard_map(
        fast_shards if fast else plain_shards,
        mesh=mesh,
        in_specs=(
            P(both, None),
            P(),
            P(),
            P(both, None),
            P(both, None),
            P(both),
            P(both),
            P(both, None),
            P(both, None),
            P("expert", None),
            P("expert", None, "hidden"),
            P("expert", "hidden", None),
            P("expert", None, "hidden"),
            P("expert", "hidden", None),
            P(both, None),
        ),
        out_specs=(
            P(both, None),
            P(both, None),
            P(both),
            P(both),
            P(both, None),
            P(both, None),
            P("expert", None),
            P("expert", None, "hidden"),
            P("expert", "hidden", None),
            P("expert", None, "hidden"),
            P("expert", "hidden", None),
        ),
        check_vma=False,
    )
```

```python
import functools

import jax
import jax.numpy as jnp
from jax import lax
from jax.experimental import pallas as pl
from jax.experimental.pallas import tpu as pltpu
from jax.sharding import PartitionSpec as P

HEADS = 16
HEAD = 64
MICRO = 4
PER = 2
SEQ = 64
PACK = PER * SEQ

epsilon = 1e-05
bf16 = jnp.bfloat16
f32 = jnp.float32


def mm(a, b, contract=(1, 0)):
    return lax.dot_general(
        a, b, (((contract[0],), (contract[1],)), ((), ())), preferred_element_type=f32
    )


def norm_parts(rows):
    centre = jnp.mean(rows, axis=-1, keepdims=True)
    shifted = rows - centre
    spread = jnp.mean(shifted * shifted, axis=-1, keepdims=True)
    inv = lax.rsqrt(spread + epsilon)
    return shifted * inv, inv


def norm_back(unit, inv, gain, grad):
    g = grad * gain
    m1 = jnp.mean(g, axis=-1, keepdims=True)
    m2 = jnp.mean(g * unit, axis=-1, keepdims=True)
    return inv * (g - m1 - unit * m2)


def gelu_act(pre_act):
    return jax.nn.gelu(pre_act, approximate=True)


MESH = pl.DeviceIdType.MESH
ANY = pl.BlockSpec(memory_space=pl.ANY)
VM = pl.BlockSpec(memory_space=pltpu.VMEM)
DMA = pltpu.SemaphoreType.DMA
VMEM_MAX = 63 << 20
PARTS = 4


def dims(experts, width):
    capacity = (9 * PACK + 8 * experts - 1) // (8 * experts)
    per_dest = MICRO * capacity
    main = per_dest // 16 * 16
    return per_dest, main, per_dest - main


def by_columns(width, size, body):
    def step(n, carry):
        body(pl.ds(pl.multiple_of(n * size, size), size), n)
        return carry

    lax.fori_loop(0, width // size, step, 0)


def apply_rows(matrix, src, dst, contract=(1, 0)):
    def body(cols, n):
        dst[:, cols] = mm(matrix[...], src[:, cols], contract).astype(dst.dtype)

    by_columns(src.shape[1], 256, body)


def greet(experts, me, core, partner):
    barrier = pltpu.get_barrier_semaphore()

    def hello(k, carry):
        pl.semaphore_signal(
            barrier, inc=1, device_id=(lax.rem(me + k, experts), core), device_id_type=MESH
        )
        return carry

    lax.fori_loop(1, experts, hello, 0)
    if partner is not None:
        pl.semaphore_signal(barrier, inc=1, device_id=(me, partner), device_id_type=MESH)
    pl.semaphore_wait(barrier, experts - 1 + (partner is not None))


class Spread:
    def __init__(self, experts, me, core, src, dst, sends, recvs, local):
        self.experts, self.me, self.core = experts, me, core
        self.src, self.dst, self.sends, self.recvs, self.local = src, dst, sends, recvs, local
        self.rows = src.shape[0] // experts

    def block(self, ref, index):
        return ref.at[pl.ds(pl.multiple_of(index * self.rows, 16), self.rows)]

    def copy(self, k):
        to = lax.rem(self.me + k, self.experts)
        return pltpu.make_async_remote_copy(
            self.block(self.src, to),
            self.block(self.dst, self.me),
            self.sends.at[k],
            self.recvs.at[k],
            device_id=(to, self.core),
            device_id_type=MESH,
        )

    def own(self):
        return pltpu.make_async_copy(
            self.block(self.src, self.me), self.block(self.dst, self.me), self.local
        )

    def start(self):
        self.own().start()

        def go(k, carry):
            self.copy(k).start()
            return carry

        lax.fori_loop(1, self.experts, go, 0)

    def wait(self):
        self.own().wait()

        def stop(k, carry):
            self.copy(k).wait()
            return carry

        lax.fori_loop(1, self.experts, stop, 0)


def tail_matrix(part, experts, tail, turned):
    size = PARTS * tail
    shape = (experts * tail, experts * size) if turned else (experts * size, experts * tail)
    there = lax.broadcasted_iota(jnp.int32, shape, 1 if turned else 0)
    here = lax.broadcasted_iota(jnp.int32, shape, 0 if turned else 1)
    want = here // tail * size + part * tail + here % tail
    return (there == want).astype(f32).astype(bf16)


def gelu_pair(v):
    u = v * v
    t = jnp.tanh(v * (0.7978845608 + 0.7978845608 * 0.044715 * u))
    h = 0.5 * t + 0.5
    slope = h + (h - h * h) * (v * (2 * 0.7978845608 + 6 * 0.7978845608 * 0.044715 * u))
    return v * h, slope


def experts_kernel(experts, tail, *refs):
    (a_in, b_in, ca_in, cb_in, cent, w1_h, w2_h, w3_h, w4_h) = refs[:9]
    (ra_out, rb_out, ga_out, gb_out, gcent, wu, wd) = refs[9:16]
    (xs_, gs_, act, slope, mid, psend, precv, ca, cb, sa, sb, cent_s, cent_r) = refs[16:29]
    (wsem, psems, prsems, xs, xr, asend, arecv, alocal) = refs[29:]
    me, core = lax.axis_index("expert"), lax.axis_index("hidden")
    other = 1 - core
    both, width = xs_.shape[1], xs_.shape[2]
    own = both // 2
    hid = wu.shape[2]
    main = a_in.shape[0]
    block = width // PARTS
    mine, theirs = pl.ds(0, own), pl.ds(own, own)

    loads = []
    for i, (h, v) in enumerate(((w1_h, wu.at[0]), (w2_h, wd.at[0]), (w3_h, wu.at[1]), (w4_h, wd.at[1]))):
        load = pltpu.make_async_copy(h, v, wsem.at[i])
        load.start()
        loads.append(load)
    greet(experts, me, core, other)

    def move(i, src, dst):
        return Spread(experts, me, core, src, dst, asend.at[i], arecv.at[i], alocal.at[i])

    cot_moves = (move(0, ca_in, ca), move(1, cb_in, cb))
    for m in cot_moves:
        m.start()

    def pair(src, dst, send, recv):
        return pltpu.make_async_remote_copy(
            src, dst, send, recv, device_id=(me, other), device_id_type=MESH
        )

    def share_x(i):
        return pair(xs_.at[i, mine], xs_.at[i, theirs], xs.at[i], xr.at[i])

    def share_g(i):
        return pair(gs_.at[i, mine], gs_.at[i, theirs], xs.at[2 + i], xr.at[2 + i])

    def partial_send(step):
        return pair(psend, precv.at[lax.rem(step, 2)], psems.at[step], prsems.at[step])

    def from_tail(ref, to, start):
        for q in range(PARTS):
            to[0, pl.ds(start, experts * tail), q * block : (q + 1) * block] = mm(
                tail_matrix(q, experts, tail, True), ref[...]
            ).astype(bf16)

    def to_tail(value, ref):
        total = None
        for q in range(PARTS):
            term = mm(tail_matrix(q, experts, tail, False), value[:, q * block : (q + 1) * block])
            total = term if total is None else total + term
        ref[...] = total.astype(bf16)

    TN, WM, WN = 512, 512, 1024

    def over(size, body):
        def step(n, carry):
            body(pl.ds(pl.multiple_of(n * TN, TN), TN))
            return carry

        lax.fori_loop(0, size // TN, step, 0)

    def halves(body):
        def step(r, carry):
            body(r, pl.ds(pl.multiple_of(r * own, own), own))
            return carry

        lax.fori_loop(0, 2, step, 0)

    def exchange(step, source, weights, turned):
        def rows_of(r, unused):
            rows = pl.ds(pl.multiple_of((1 - r) * own, own), own)

            def body(cols):
                if turned:
                    value = mm(source[rows, :], weights[cols, :], (1, 1))
                else:
                    value = mm(source[rows, :], weights[:, cols])

                @pl.when(r == 0)
                def _():
                    psend[:, cols] = value.astype(bf16)

                @pl.when(r == 1)
                def _():
                    mid[:, cols] += value

            over(width, body)

            @pl.when(r == 0)
            def _():
                partial_send(step).start()

        halves(rows_of)
        partial_send(step).wait()
        mid[...] += precv[lax.rem(step, 2)].astype(f32)

    xs_[0, pl.ds(0, main), :] = a_in[...]
    from_tail(b_in, xs_, main)
    share_x(0).start()
    slot = xs_[0, mine, :].astype(f32)
    mid[...] = slot
    gate = jax.nn.sigmoid(jnp.sum(slot * cent[...].astype(f32), axis=1, keepdims=True))

    def forward(i, carry):
        def up(r, rows):
            @pl.when(r == 1)
            def _():
                share_x(i).wait()

            def body(cols):
                a, d = gelu_pair(mm(xs_[i, rows, :], wu[i, :, cols]))
                act[i, rows, cols] = a.astype(bf16)
                slope[i, rows, cols] = d.astype(bf16)

            over(hid, body)

        for k in range(2):

            @pl.when(i == k)
            def _():
                loads[2 * k].wait()

        halves(up)
        for k in range(2):

            @pl.when(i == k)
            def _():
                loads[2 * k + 1].wait()

        exchange(i, act.at[i], wd.at[i], False)

        @pl.when(i == 0)
        def _():
            xs_[1, mine, :] = mid[...].astype(bf16)
            share_x(1).start()

        return carry

    lax.fori_loop(0, 2, forward, 0)
    returned = (gate * mid[...]).astype(bf16)
    sa[...] = returned[:main]
    to_tail(returned[main:], sb)
    ret_moves = (move(2, sa, ra_out), move(3, sb, rb_out))
    for m in ret_moves:
        m.start()
    for m in cot_moves:
        m.wait()
    gs_[0, pl.ds(0, main), :] = ca[...]
    from_tail(cb, gs_, main)
    cot = gs_[0, mine, :].astype(f32)
    logit = jnp.sum(cot * mid[...], axis=1, keepdims=True) * gate * (1.0 - gate)
    cent_s[...] = jnp.sum(logit * xs_[0, mine, :].astype(f32), axis=0, keepdims=True)
    share_c = pair(cent_s, cent_r, xs.at[4], xr.at[4])
    share_c.start()
    start_grad = (gate * cot).astype(bf16)
    gs_[1, mine, :] = start_grad
    mid[...] = start_grad.astype(f32)
    share_g(1).start()

    def backward(k, carry):
        i = 1 - k

        def up_back(r, rows):
            @pl.when(r == 1)
            def _():
                share_g(i).wait()

            def body(cols):
                t = mm(gs_[i, rows, :], wd[i, cols, :], (1, 1)) * slope[i, rows, cols].astype(f32)
                slope[i, rows, cols] = t.astype(bf16)

            over(hid, body)

        halves(up_back)
        exchange(2 + k, slope.at[i], wu.at[i], True)

        @pl.when(k == 0)
        def _():
            gm = mid[...].astype(bf16)
            gs_[0, mine, :] = gm
            mid[...] = gm.astype(f32) + logit * cent[...].astype(f32)
            share_g(0).start()

        return carry

    lax.fori_loop(0, 2, backward, 0)
    for m in ret_moves:
        m.wait()
    slots = mid[...].astype(bf16)
    sa[...] = slots[:main]
    to_tail(slots[main:], sb)
    back_moves = (move(4, sa, ga_out), move(5, sb, gb_out))
    for m in back_moves:
        m.start()

    def weight_grad(left, right, to):
        wide_n = right.shape[1]

        def body(n, carry):
            m, c = n // (wide_n // WN), lax.rem(n, wide_n // WN)
            rows = pl.ds(pl.multiple_of(m * WM, WM), WM)
            cols = pl.ds(pl.multiple_of(c * WN, WN), WN)
            to[rows, cols] = mm(left[:, rows], right[:, cols], (0, 0)).astype(bf16)
            return carry

        lax.fori_loop(0, left.shape[1] // WM * (wide_n // WN), body, 0)

    def weight_grads(i, carry):
        weight_grad(act.at[i], gs_.at[i], wd.at[i])
        weight_grad(xs_.at[i], slope.at[i], wu.at[i])
        return carry

    lax.fori_loop(0, 2, weight_grads, 0)
    share_c.wait()
    gcent[...] = cent_s[...] + cent_r[...]
    for m in back_moves:
        m.wait()


def run_experts(experts, slots, tails, cots, cot_tails, centroid, weights):
    width, hid = weights[0].shape
    main = slots.shape[0]
    tail = tails.shape[0] // experts // PARTS
    own = main + experts * tail
    both = 2 * own

    def sds(*shape, dtype=bf16):
        return jax.ShapeDtypeStruct(shape, dtype)

    travel = [sds(*slots.shape), sds(*tails.shape)] * 2
    wide = [pltpu.VMEM((2, width, hid), bf16), pltpu.VMEM((2, hid, width), bf16)]
    return pl.pallas_call(
        functools.partial(experts_kernel, experts, tail),
        out_shape=travel + [sds(1, width, dtype=f32)] + wide,
        in_specs=[VM, VM, ANY, ANY, VM, ANY, ANY, ANY, ANY],
        out_specs=[ANY] * 4 + [VM] * 3,
        scratch_shapes=[
            pltpu.VMEM((2, both, width), bf16),
            pltpu.VMEM((2, both, width), bf16),
            pltpu.VMEM((2, both, hid), bf16),
            pltpu.VMEM((2, both, hid), bf16),
            pltpu.VMEM((own, width), f32),
            pltpu.VMEM((own, width), bf16),
            pltpu.VMEM((2, own, width), bf16),
            pltpu.VMEM(slots.shape, bf16),
            pltpu.VMEM(tails.shape, bf16),
            pltpu.VMEM(slots.shape, bf16),
            pltpu.VMEM(tails.shape, bf16),
            pltpu.VMEM((1, width), f32),
            pltpu.VMEM((1, width), f32),
            DMA((4,)),
            DMA((4,)),
            DMA((4,)),
            DMA((5,)),
            DMA((5,)),
            DMA((6, experts)),
            DMA((6, experts)),
            DMA((6,)),
        ],
        compiler_params=pltpu.CompilerParams(
            collective_id=2, has_side_effects=True, vmem_limit_bytes=45 << 20
        ),
        name="experts_pass",
    )(slots, tails, cots, cot_tails, centroid, *weights)

def back_kernel(experts, tail, *refs):
    (ra, rb, ga, gb, dm, dt, gains, cot_h, res_h, tok_h, packed_h, probs_h, mixed_h, wall_h) = refs[:14]
    refs = refs[:14] + refs[15:]
    out_o, ig_o, gqkv_o, gout_o, ggain_o = refs[14:19]
    (cot, res, tok, packed, probs, mixed, wqkv, wout, normed, gatt, gmix, gpk, so, si, perm, wide, turn) = refs[19:36]
    keeps, psends, precvs, rv1s, rv2s, rv3s = (refs[36 + 6 * i : 42 + 6 * i] for i in range(6))
    lsem, sends, recvs, asend, arecv, alocal = refs[72:]
    me, core = lax.axis_index("expert"), lax.axis_index("hidden")
    other = 1 - core
    my_z, my_y, my_x = me // 4, lax.rem(me // 2, 2), lax.rem(me, 2)
    rows, width = tok.shape
    block = width // PARTS

    loads = {}
    for i, (name, h, v) in enumerate(
        (
            ("res", res_h, res),
            ("cot", cot_h, cot),
            ("mixed", mixed_h, mixed),
            ("wout", wall_h.at[:, pl.ds(3 * width + 128, width)], wout),
            ("probs", probs_h, probs),
            ("packed", packed_h, packed),
            ("tok", tok_h, tok),
            ("wqkv", wall_h.at[:, pl.ds(0, 3 * width)], wqkv),
        )
    ):
        loads[name] = pltpu.make_async_copy(h, v, lsem.at[i])
        loads[name].start()
    greet(experts, me, core, other)

    def join_slots(slots, tails):
        def body(cols, q):
            wide[:, cols] = mm(dm[...], slots[:, cols], (0, 0)) + mm(dt[q], tails[...], (0, 0))

        by_columns(width, block, body)

    piece = SEQ // experts
    seats = MICRO * PER

    shape = (rows, rows)
    to, at = lax.broadcasted_iota(jnp.int32, shape, 0), lax.broadcasted_iota(jnp.int32, shape, 1)
    b, s, q = to // (seats * piece), to // piece % seats, to % piece
    turn[...] = (at == s * SEQ + b * piece + q).astype(f32).astype(bf16)

    def move(i, src, dst):
        return Spread(experts, me, core, src, dst, asend.at[i], arecv.at[i], alocal.at[i])

    my_a = jnp.where(core == 0, my_x, my_y)
    my_b = jnp.where(core == 0, my_y, my_x)

    def near(a_step, b_step):
        a, b = (1 - my_a if a_step else my_a), (1 - my_b if b_step else my_b)
        x, y = jnp.where(core == 0, a, b), jnp.where(core == 0, b, a)
        return my_z * 4 + y * 2 + x

    def remote(c, stage, src, dst, to, to_core):
        return pltpu.make_async_remote_copy(
            src, dst, sends.at[c, stage], recvs.at[c, stage],
            device_id=(to, to_core), device_id_type=MESH,
        )

    def pair_copy(c):
        return remote(c, 0, psends[c], precvs[c], me, other)

    def a_copy(c):
        return remote(c, 1, psends[c].at[pl.ds(0, 256)], rv1s[c], near(True, False), core)

    def b_copy(c):
        return remote(c, 2, psends[c].at[pl.ds(256, 128)], rv2s[c], near(False, True), core)

    line = lax.rem(me, 4)
    my_set = jnp.where((my_z == 0) | (my_z == 3), 0, 1)
    my_place = my_z // 2

    def c_copy(c):
        to_z = my_z + 1 - 2 * lax.rem(my_z, 2)
        return remote(c, 3, psends[c].at[pl.ds(384, 64)], rv3s[c].at[pl.ds(0, 64)], to_z * 4 + line, core)

    def z_copy(c):
        return remote(c, 4, psends[c].at[pl.ds(448, 32)], rv3s[c].at[pl.ds(64, 32)], (3 - my_z) * 4 + line, core)

    def place(c, t, cols):
        keeps[c][:, cols] = t[: width // 2]
        psends[c][:, cols] = t[width // 2 :].astype(bf16)

    at = lax.broadcasted_iota(jnp.int32, (1, width), 1)
    goes = jnp.where(at < width // 2, core, other)
    high, mid_ = at // 256 % 2, at // 128 % 2
    to_x, to_y = jnp.where(goes == 0, high, mid_), jnp.where(goes == 0, mid_, high)
    level = at // 32 % 4
    to_z = jnp.where(level == 0, 0, jnp.where(level == 1, 3, level - 1))
    source = ((to_z * 4 + to_y * 2 + to_x) * 2 + goes) * 32 + at % 32
    perm[...] = (lax.broadcasted_iota(jnp.int32, (width, width), 0) == source).astype(f32).astype(bf16)

    def compute(c, left, right, start, stride, count, size):
        def body(n, carry):
            cols = pl.ds(pl.multiple_of(start + n * stride, size), size)
            place(c, mm(left[...], right[:, cols], (0, 0)), pl.ds(pl.multiple_of(n * size, size), size))
            return carry

        lax.fori_loop(0, count, body, 0)
        pair_copy(c).start()

    half_a = pl.ds(pl.multiple_of(my_a * 256, 256), 256)
    half_a_out = pl.ds(pl.multiple_of((1 - my_a) * 256, 256), 256)
    base_b = my_a * 256
    half_b = pl.ds(pl.multiple_of(base_b + my_b * 128, 128), 128)
    half_b_out = pl.ds(pl.multiple_of(base_b + (1 - my_b) * 128, 128), 128)
    base_c = base_b + my_b * 128
    half_c = pl.ds(pl.multiple_of(base_c + my_set * 64, 64), 64)
    half_c_out = pl.ds(pl.multiple_of(base_c + (1 - my_set) * 64, 64), 64)
    base_z = base_c + my_set * 64
    place_in = pl.ds(pl.multiple_of(base_z + my_place * 32, 32), 32)
    place_out = pl.ds(pl.multiple_of(base_z + (1 - my_place) * 32, 32), 32)

    def after_pair(c):
        pair_copy(c).wait()
        keep = keeps[c]
        keep[...] += precvs[c][...].astype(f32)
        psends[c][pl.ds(0, 256), :] = keep[half_a_out, :].astype(bf16)
        a_copy(c).start()

    def after_a(c):
        a_copy(c).wait()
        keep = keeps[c]
        keep[half_a, :] += rv1s[c][...].astype(f32)
        psends[c][pl.ds(256, 128), :] = keep[half_b_out, :].astype(bf16)
        b_copy(c).start()

    def after_b(c):
        b_copy(c).wait()
        keep = keeps[c]
        keep[half_b, :] += rv2s[c][...].astype(f32)
        psends[c][pl.ds(384, 64), :] = keep[half_c_out, :].astype(bf16)
        c_copy(c).start()

    def after_c(c):
        c_copy(c).wait()
        keep = keeps[c]
        keep[half_c, :] += rv3s[c][pl.ds(0, 64), :].astype(f32)
        psends[c][pl.ds(448, 32), :] = keep[place_out, :].astype(bf16)
        z_copy(c).start()

    def after_z(c, pieces):
        z_copy(c).wait()
        total = keeps[c][place_in, :] + rv3s[c][pl.ds(64, 32), :].astype(f32)
        size = total.shape[1] // len(pieces)
        for n, (out, start) in enumerate(pieces):
            out[:, start : start + size] = total[:, n * size : (n + 1) * size]

    gain_a, gain_f = gains[0:1, :], gains[1:2, :]
    loads["res"].wait()
    join_slots(ra, rb)
    gmix[...] = (res[...] + wide[...]).astype(bf16)
    apply_rows(turn, gmix, so)
    out_move = move(0, so, out_o)
    out_move.start()
    unit, inv = norm_parts(res[...])
    join_slots(ga, gb)
    grad_shared = wide[...]
    ffn_sums = jnp.sum(grad_shared * unit, axis=0, keepdims=True)
    loads["cot"].wait()
    grad = cot[...].astype(f32) + norm_back(unit, inv, gain_f, grad_shared)
    res[...] = grad
    gatt[...] = grad.astype(bf16)
    loads["mixed"].wait()
    gpk_view = gpk.at[:, pl.ds(0, width)]
    apply_rows(mixed, perm, gpk_view)
    compute(0, gpk_view, gatt, 0, width // 4, 4, width // 4)
    loads["wout"].wait()

    def mix(cols, n):
        gmix[:, cols] = mm(gatt[...], wout[cols, :], (1, 1)).astype(bf16)

    by_columns(width, 256, mix)
    after_pair(0)
    loads["probs"].wait()
    loads["packed"].wait()
    lane = lax.broadcasted_iota(jnp.int32, (PACK, 2 * HEAD), 1)
    first = lane < HEAD

    def stacked(v):
        zero = jnp.zeros_like(v)
        return jnp.concatenate([jnp.where(first, v, zero), jnp.where(first, zero, v)], axis=0)

    def head_pair(p, h):
        at = pl.ds(pl.multiple_of(p * PACK, PACK), PACK)
        lo = h * 2 * HEAD
        q = packed[at, lo : lo + 2 * HEAD]
        k = packed[at, width + lo : width + lo + 2 * HEAD]
        v = packed[at, 2 * width + lo : 2 * width + lo + 2 * HEAD]
        gs = stacked(gmix[at, lo : lo + 2 * HEAD])
        pr_lo = probs[p * (HEADS // 2) + h]
        pr = pr_lo.astype(f32)
        gp = mm(gs, v, (1, 1))
        gv = mm(pr_lo, gs, (0, 0))
        inner = jnp.sum(pr * gp, axis=1, keepdims=True)
        ds_ = (pr * (gp - inner)).astype(bf16)
        t = mm(ds_, k)
        gq = jnp.where(first, t[:PACK], t[PACK:]) * 0.125
        gk = mm(ds_, stacked(q), (0, 0)) * 0.125
        gpk[at, lo : lo + 2 * HEAD] = gq.astype(bf16)
        gpk[at, width + lo : width + lo + 2 * HEAD] = gk.astype(bf16)
        gpk[at, 2 * width + lo : 2 * width + lo + 2 * HEAD] = gv.astype(bf16)

    part = width // 4

    def group_pieces(g):
        return tuple(part * g + width * i for i in range(3))

    def group(g):
        def packs(p, carry):
            for h in range(HEADS // 8):
                head_pair(p, g * (HEADS // 8) + h)
            return carry

        lax.fori_loop(0, MICRO, packs, 0)

    def set_off(g):
        compute(1 + g, normed, gpk, part * g, width, 3, part)

    def finish(g):
        after_z(1 + g, [(gqkv_o, start) for start in group_pieces(g)])

    loads["tok"].wait()
    unit, inv = norm_parts(tok[...].astype(f32))
    so2 = gpk.at[:, pl.ds(2 * width, width)]
    so2[...] = (unit * gain_a).astype(bf16)
    apply_rows(so2, perm, normed)
    group(0)
    set_off(0)
    group(1)
    set_off(1)
    after_pair(1)
    after_a(0)
    group(2)
    set_off(2)
    after_pair(2)
    after_b(0)
    group(3)
    after_pair(3)
    after_a(1)
    after_c(0)
    loads["wqkv"].wait()

    def pull(cols, n):
        wide[:, cols] = mm(gpk[...], wqkv[cols, :], (1, 1))

    by_columns(width, 256, pull)
    grad_normed = wide[...]
    unit, inv = norm_parts(tok[...].astype(f32))
    attn_sums = jnp.sum(grad_normed * unit, axis=0, keepdims=True)
    gmix[...] = (res[...] + norm_back(unit, inv, gain_a, grad_normed)).astype(bf16)
    apply_rows(turn, gmix, si)
    ig_move = move(1, si, ig_o)
    ig_move.start()
    set_off(3)
    after_a(2)
    after_b(1)
    sums = jnp.where(lax.broadcasted_iota(jnp.int32, (128, width), 0) < 64, attn_sums, ffn_sums)
    sums_hi = sums.astype(bf16)
    sums_lo = (sums - sums_hi.astype(f32)).astype(bf16)
    place(5, mm(perm[...], sums_hi, (0, 1)) + mm(perm[...], sums_lo, (0, 1)), pl.ds(0, 128))
    pair_copy(5).start()
    after_pair(4)
    after_pair(5)
    after_z(0, [(gout_o, 0)])
    after_a(3)
    after_b(2)
    after_c(1)
    after_a(4)
    after_a(5)
    after_b(3)
    after_c(2)
    finish(0)
    after_b(4)
    after_b(5)
    after_c(3)
    finish(1)
    after_c(4)
    after_c(5)
    finish(2)
    finish(3)
    after_z(5, [(ggain_o, 0)])
    out_move.wait()
    ig_move.wait()


def run_back(experts, tail, slots, tails, grads, grad_tails, d_main, d_tail, gains, cot, residual, tok, packed, probs, mixed, w_all, done):
    rows, width = tok.shape

    def sds(*shape, dtype=bf16):
        return jax.ShapeDtypeStruct(shape, dtype)

    widths = (width,) + (3 * width // 4,) * 4 + (128,)
    scratch = [
        pltpu.VMEM(cot.shape, bf16),
        pltpu.VMEM(residual.shape, f32),
        pltpu.VMEM(tok.shape, bf16),
        pltpu.VMEM(packed.shape, bf16),
        pltpu.VMEM(probs.shape, bf16),
        pltpu.VMEM(mixed.shape, bf16),
        pltpu.VMEM((width, 3 * width), bf16),
        pltpu.VMEM((width, width), bf16),
        pltpu.VMEM((rows, width), bf16),
        pltpu.VMEM((rows, width), bf16),
        pltpu.VMEM((rows, width), bf16),
        pltpu.VMEM((rows, 3 * width), bf16),
        pltpu.VMEM((rows, width), bf16),
        pltpu.VMEM((rows, width), bf16),
        pltpu.VMEM((width, width), bf16),
        pltpu.VMEM((rows, width), f32),
        pltpu.VMEM((rows, rows), bf16),
    ]
    scratch += [pltpu.VMEM((width // 2, w), f32) for w in widths]
    for part in (2, 2, 4, 8):
        scratch += [pltpu.VMEM((width // part, w), bf16) for w in widths]
    scratch += [pltpu.VMEM((96, w), bf16) for w in widths]
    scratch += [
        DMA((8,)),
        DMA((6, 6)),
        DMA((6, 6)),
        DMA((2, experts)),
        DMA((2, experts)),
        DMA((2,)),
    ]
    return pl.pallas_call(
        functools.partial(back_kernel, experts, tail),
        out_shape=[sds(rows, width), sds(rows, width), sds(32, 3 * width, dtype=f32), sds(32, width, dtype=f32), sds(32, 128, dtype=f32)],
        in_specs=[VM] * 7 + [ANY] * 8,
        out_specs=[ANY, ANY, VM, VM, VM],
        scratch_shapes=scratch,
        compiler_params=pltpu.CompilerParams(
            collective_id=3, has_side_effects=True, vmem_limit_bytes=VMEM_MAX
        ),
        name="attention_back",
    )(slots, tails, grads, grad_tails, d_main, d_tail, gains, cot, residual, tok, packed, probs, mixed, w_all, done)


def front_kernel(experts, tail, *refs):
    (tokens, cots, routes, orders, deal, lengths, g_attn, g_ffn, w_qkv, w_out) = refs[:10]
    (slots_o, tails_o, cslots_o, ctails_o, deal_o, dm_o, dt_o, gains_o, cot_o, res_o, tok_o, packed_o, probs_o, mixed_o, w_o) = refs[10:25]
    (st, sl, rt, rl, rc, tok, cot, w, packed, probs, mixed, res, shared, dm, dt, ftm, masks, ss, stl, cs, ctl, turn) = refs[25:47]
    zs, zr, as_, ar, bs, br, ps, pr, asend, arecv, alocal, osem = refs[47:]
    me, core = lax.axis_index("expert"), lax.axis_index("hidden")
    other = 1 - core
    my_z, my_y, my_x = me // 4, lax.rem(me // 2, 2), lax.rem(me, 2)
    rows, width = tok.shape
    piece = SEQ // experts
    seats = MICRO * PER
    block = width // PARTS
    step = w_qkv.shape[0]
    per_dest = experts and dims(experts, width)[0]
    main = per_dest - tail
    capacity = per_dest // MICRO

    def iota(shape, axis):
        return lax.broadcasted_iota(jnp.int32, shape, axis)

    def one_hot(test):
        return test.astype(f32).astype(bf16)

    own_rows = pl.ds(pl.multiple_of((me * 2 + core) * step, step), step)
    gain_at, out_at = 3 * width, 3 * width + 128
    w[own_rows, :gain_at] = w_qkv[...]
    w[own_rows, out_at:] = w_out[...]
    eye = iota((step, step), 0) == iota((step, step), 1)

    def as_column(row):
        return jnp.sum(jnp.where(eye, row[...].astype(f32), 0.0), axis=1, keepdims=True)

    gain_cols = jnp.where(iota((step, 128), 1) < 64, as_column(g_attn), as_column(g_ffn))
    w[own_rows, gain_at:out_at] = gain_cols.astype(bf16)
    cuts = ((0, out_at), (out_at, width))

    line = lax.rem(me, 4)
    a_to = jnp.where(core == 0, my_z * 4 + my_y * 2 + 1 - my_x, my_z * 4 + 2 - 2 * my_y + my_x)
    b_to = jnp.where(core == 0, my_z * 4 + 2 - 2 * my_y + my_x, my_z * 4 + my_y * 2 + 1 - my_x)
    shift_a, shift_b = a_to - me, b_to - me

    def send(j, e, sem_s, sem_r, to, to_core):
        start, size = cuts[j]
        ref = w.at[pl.ds(pl.multiple_of((e * 2 + core) * step, step), step), pl.ds(start, size)]
        return pltpu.make_async_remote_copy(
            ref, ref, sem_s, sem_r, device_id=(to, to_core), device_id_type=MESH
        )

    def up(j, d):
        s = my_z - d
        return send(j, s * 4 + line, zs.at[j, d], zr.at[j, s], me + 4, core)

    def down(j, d):
        s = my_z + d
        return send(j, s * 4 + line, zs.at[j, 4 + d], zr.at[j, s], me - 4, core)

    def a_copy(j, s):
        return send(j, s * 4 + line, as_.at[j, s], ar.at[j, s], a_to, core)

    def b_copy(j, f, s):
        return send(j, s * 4 + line + f * shift_a, bs.at[j, 4 * f + s], br.at[j, 4 * f + s], b_to, core)

    def p_copy(j, f, s):
        e = s * 4 + line + (f % 2) * shift_a + (f // 2) * shift_b
        return send(j, e, ps.at[j, 4 * f + s], pr.at[j, 4 * f + s], me, other)

    def release(j, s):
        b_copy(j, 0, s).start()
        a_copy(j, s).start()
        p_copy(j, 0, s).start()

    def chain(j, d):
        @pl.when(my_z >= d)
        def _():
            if d:
                up(j, d).wait_recv()

            @pl.when(my_z < 3)
            def _():
                up(j, d).start()

            if d:
                release(j, my_z - d)

        @pl.when(my_z + d <= 3)
        def _():
            if d:
                down(j, d).wait_recv()

            @pl.when(my_z > 0)
            def _():
                down(j, d).start()

            if d:
                release(j, my_z + d)

        if not d:
            release(j, my_z)

    def places():
        return [lax.rem(my_z + k, 4) for k in (0, 1, 3, 2)]

    def fan_a(j):
        for s in places():
            a_copy(j, s).wait_recv()
            b_copy(j, 1, s).start()
            p_copy(j, 1, s).start()

    def fan_b(j):
        for f in range(2):
            for s in places():
                b_copy(j, f, s).wait_recv()
                p_copy(j, 2 + f, s).start()

    def fan_p(j):
        for f in range(4):
            for s in range(4):
                p_copy(j, f, s).wait_recv()

    def all_sent(j):
        for d in range(4):

            @pl.when((my_z >= d) & (my_z < 3))
            def _():
                up(j, d).wait_send()

            @pl.when((my_z + d <= 3) & (my_z > 0))
            def _():
                down(j, d).wait_send()

        for s in range(4):
            a_copy(j, s).wait_send()
            for f in range(2):
                b_copy(j, f, s).wait_send()
            for f in range(4):
                p_copy(j, f, s).wait_send()

    greet(experts, me, core, other)
    chain(0, 0)
    chain(1, 0)

    def move(i, src, dst):
        return Spread(experts, me, core, src, dst, asend.at[i], arecv.at[i], alocal.at[i])

    group = deal.shape[1]
    deal_row = deal[pl.ds(core, 1), :]
    length_row = lengths[pl.ds(core, 1), :]
    spread_out = one_hot(iota((group, rows), 1) // piece == iota((group, rows), 0))
    wide = jnp.broadcast_to(deal_row.astype(f32), (8, group)).astype(bf16)
    goal = mm(wide, spread_out)[0:1].astype(jnp.int32) * piece + iota((1, rows), 1) % piece
    ftm[...] = one_hot(iota((rows, rows), 0) == goal)
    apply_rows(ftm, tokens, st)
    lab = jnp.where(iota((128, rows), 0) < 64, routes[...], orders[...]).astype(f32).astype(bf16)
    sl[...] = mm(ftm[...], lab, (1, 1)).astype(bf16)
    tok_moves = (move(0, st, rt), move(1, sl, rl))
    for m in tok_moves:
        m.start()
    chain(0, 1)
    chain(1, 1)
    chain(0, 2)
    chain(1, 2)
    apply_rows(ftm, cots, cs)
    goal_col = mm(spread_out, wide, (0, 1))[:, 0:1].astype(jnp.int32) * piece + iota((rows, 1), 0) % piece
    ftm[...] = one_hot(iota((rows, rows), 1) == goal_col)
    chain(0, 3)
    chain(1, 3)
    fan_a(0)
    fan_a(1)
    for m in tok_moves:
        m.wait()

    outs = []

    def store(i, ref, out):
        copy = pltpu.make_async_copy(ref, out, osem.at[i])
        copy.start()
        outs.append(copy)

    cot_move = move(2, cs, rc)
    cot_move.start()
    store(0, ftm, deal_o)
    to, at = iota((rows, rows), 0), iota((rows, rows), 1)
    b, s, q = to // (seats * piece), to // piece % seats, to % piece
    turn[...] = one_hot(at == s * SEQ + b * piece + q)
    apply_rows(turn, rt, tok, (0, 0))
    store(1, tok, tok_o)
    lab_col = mm(turn[...], rl[...], (0, 0))
    lab_row = mm(rl[...], turn[...], (0, 0))
    ranks, heads_at, oks = [], [], []
    own = [
        jnp.sum(jnp.where(deal_row == me * seats + i, length_row, 0), axis=1, keepdims=True)
        for i in range(seats)
    ]
    posr, posc = iota((1, PACK), 1), iota((PACK, 1), 0)
    near_ = (iota((PACK, PACK), 0) // SEQ == iota((PACK, PACK), 1) // SEQ) & (
        iota((PACK, PACK), 1) <= iota((PACK, PACK), 0)
    )
    for p in range(MICRO):
        low, high = own[PER * p], own[PER * p + 1]
        here_r = posr % SEQ < jnp.where(posr < SEQ, low, high)
        here_c = posc % SEQ < jnp.where(posc < SEQ, low, high)
        masks[p] = (near_ & here_r).astype(f32)
        cols = slice(p * PACK, (p + 1) * PACK)
        route_r = lab_row[0:1, cols]
        key_r = lab_row[64:65, cols] * PER + (posr // SEQ).astype(f32)
        route_c = lab_col[cols, 0:1]
        key_c = lab_col[cols, 64:65] * PER + (posc // SEQ).astype(f32)
        ahead = jnp.sum(
            ((route_c == route_r) & (key_c < key_r) & here_c).astype(f32), axis=0, keepdims=True
        ).astype(jnp.int32)
        base = p * capacity + ahead
        good = here_r & (ahead < capacity)
        route_i = route_r.astype(jnp.int32)
        heads_at.append(jnp.where(good & (base < main), route_i * main + base, -1))
        oks.append(jnp.where(good & (base >= main), route_i * (PARTS * tail) + base - main, -PARTS * PARTS * tail))
    head_row = jnp.concatenate(heads_at, axis=1)
    tail_row = jnp.concatenate(oks, axis=1)
    dm[...] = one_hot(iota(dm.shape, 0) == head_row)
    for part in range(PARTS):
        dt[part] = one_hot(iota(dt.shape[1:], 0) == tail_row + part * tail)
    store(2, dm, dm_o)
    store(3, dt, dt_o)

    def split(ref, to_main, to_tails):
        apply_rows(dm, ref, to_main)
        total = None
        for part in range(PARTS):
            term = mm(dt[part], ref[:, part * block : (part + 1) * block])
            total = term if total is None else total + term
        to_tails[...] = total.astype(bf16)

    inputs = tok[...].astype(f32)
    unit, inv = norm_parts(inputs)
    res[...] = unit
    fan_b(0)
    fan_p(0)
    big = iota((128, 128), 0) == iota((128, 128), 1)

    def gain_row(lane):
        parts = []
        for j in range(width // 128):
            col = w[128 * j : 128 * (j + 1), gain_at:out_at].astype(f32)[:, lane : lane + 1]
            parts.append(jnp.sum(jnp.where(big, col, 0.0), axis=0, keepdims=True))
        return jnp.concatenate(parts, axis=1)

    gain_a, gain_f = gain_row(0), gain_row(64)
    gains_o[0:1, :] = gain_a
    gains_o[1:2, :] = gain_f
    shared[...] = (res[...] * gain_a).astype(bf16)

    def project(n, carry):
        cols = pl.ds(pl.multiple_of(n * 256, 256), 256)
        packed[:, cols] = mm(shared[...], w[:, cols]).astype(bf16)
        return carry

    lax.fori_loop(0, 3 * width // 256, project, 0)
    store(5, packed, packed_o)
    first = iota((PACK, 2 * HEAD), 1) < HEAD

    def pack(n, carry):
        p, half = n // 2, lax.rem(n, 2)
        at = pl.ds(pl.multiple_of(p * PACK, PACK), PACK)
        mask = masks[p] > 0.5
        mask = jnp.concatenate([mask, mask], axis=0)
        for j in range(HEADS // 4):
            h = half * (HEADS // 4) + j
            own_lanes, key_lanes, value_lanes = (
                pl.ds(pl.multiple_of(h * 2 * HEAD + n * width, 2 * HEAD), 2 * HEAD) for n in range(3)
            )
            q, k, v = packed[at, own_lanes], packed[at, key_lanes], packed[at, value_lanes]
            zero = jnp.zeros_like(q)
            qs = jnp.concatenate([jnp.where(first, q, zero), jnp.where(first, zero, q)], axis=0)
            scores = jnp.where(mask, mm(qs, k, (1, 1)) * 0.125, -1e30)
            e = jnp.exp(scores - jnp.max(scores, axis=1, keepdims=True))
            prob = (e / jnp.sum(e, axis=1, keepdims=True)).astype(bf16)
            probs[p * (HEADS // 2) + h] = prob
            t = mm(prob, v)
            mixed[at, own_lanes] = jnp.where(first, t[:PACK], t[PACK:]).astype(bf16)
        return carry

    fan_b(1)
    lax.fori_loop(0, 2 * MICRO, pack, 0)
    store(6, probs, probs_o)
    fan_p(1)
    store(4, w, w_o)
    store(7, mixed, mixed_o)
    apply_rows(mixed, w.at[:, pl.ds(out_at, width)], res)
    residual = tok[...].astype(f32) + res[...]
    res[...] = residual
    store(8, res, res_o)
    unit, inv = norm_parts(residual)
    shared[...] = (unit * gain_f).astype(bf16)
    split(shared, ss, stl)
    slot_moves = (move(3, ss, slots_o), move(4, stl, tails_o))
    cot_move.wait()
    for m in slot_moves:
        m.start()
    apply_rows(turn, rc, cot, (0, 0))
    store(9, cot, cot_o)
    split(cot, cs, ctl)
    store(10, cs, cslots_o)
    store(11, ctl, ctails_o)
    all_sent(0)
    all_sent(1)
    for copy in outs:
        copy.wait()
    for m in slot_moves:
        m.wait()


def run_front(experts, tail, tokens, cots, routes, orders, deal, lengths, g_attn, g_ffn, w_qkv, w_out):
    rows, width = tokens.shape
    per_dest = dims(experts, width)[0]
    main = (per_dest - tail) * experts
    side = experts * PARTS * tail

    def sds(*shape, dtype=bf16):
        return jax.ShapeDtypeStruct(shape, dtype)

    tails = (side, width // PARTS)
    out_shape = [
        sds(main, width),
        sds(*tails),
        sds(main, width),
        sds(*tails),
        sds(rows, rows),
        sds(main, rows),
        sds(PARTS, side, rows),
        sds(2, width, dtype=f32),
        sds(rows, width),
        sds(rows, width, dtype=f32),
        sds(rows, width),
        sds(rows, 3 * width),
        sds(MICRO * HEADS // 2, 2 * PACK, PACK),
        sds(rows, width),
        sds(width, 4 * width + 128),
    ]
    vm = pltpu.VMEM
    return pl.pallas_call(
        functools.partial(front_kernel, experts, tail),
        out_shape=out_shape,
        in_specs=[VM] * 10,
        out_specs=[ANY] * 7 + [VM] + [ANY] * 7,
        scratch_shapes=[
            vm((rows, width), bf16),
            vm((rows, 128), bf16),
            vm((rows, width), bf16),
            vm((rows, 128), bf16),
            vm((rows, width), bf16),
            vm((rows, width), bf16),
            vm((rows, width), bf16),
            vm((width, 4 * width + 128), bf16),
            vm((rows, 3 * width), bf16),
            vm((MICRO * HEADS // 2, 2 * PACK, PACK), bf16),
            vm((rows, width), bf16),
            vm((rows, width), f32),
            vm((rows, width), bf16),
            vm((main, rows), bf16),
            vm((PARTS, side, rows), bf16),
            vm((rows, rows), bf16),
            vm((MICRO, PACK, PACK), f32),
            vm((main, width), bf16),
            vm(tails, bf16),
            vm((main, width), bf16),
            vm(tails, bf16),
            vm((rows, rows), bf16),
            DMA((2, 8)),
            DMA((2, 4)),
            DMA((2, 4)),
            DMA((2, 4)),
            DMA((2, 8)),
            DMA((2, 8)),
            DMA((2, 16)),
            DMA((2, 16)),
            DMA((5, experts)),
            DMA((5, experts)),
            DMA((5,)),
            DMA((12,)),
        ],
        compiler_params=pltpu.CompilerParams(
            collective_id=1, has_side_effects=True, vmem_limit_bytes=VMEM_MAX
        ),
        name="attention_front",
    )(tokens, cots, routes, orders, deal, lengths, g_attn, g_ffn, w_qkv, w_out)


def finish_kernel(f, out_r, ig_r, out_o, ig_o):
    out_o[...] = mm(f[...], out_r[...]).astype(bf16)
    ig_o[...] = mm(f[...], ig_r[...])


def run_finish(f, out_r, ig_r):
    steps = 2
    rows, width = out_r.shape

    def cut(shape):
        return pl.BlockSpec((shape[0] // steps, shape[1]), lambda i: (i, 0))

    def whole(shape):
        return pl.BlockSpec(shape, lambda i: (0, 0))

    outs = [
        jax.ShapeDtypeStruct((rows, width), bf16),
        jax.ShapeDtypeStruct((rows, width), f32),
    ]
    return pl.pallas_call(
        finish_kernel,
        grid=(steps,),
        out_shape=outs,
        in_specs=[cut(f.shape), whole(out_r.shape), whole(ig_r.shape)],
        out_specs=[cut(o.shape) for o in outs],
        name="finish",
    )(f, out_r, ig_r)


def widen_kernel(ups, downs, up_first, down_first, up_second, down_second, done):
    i = pl.program_id(0)
    for k, (up, down) in enumerate(((up_first, down_first), (up_second, down_second))):
        for narrow, full in ((ups, up), (downs, down)):
            size = full.shape[0]
            full[...] = narrow[k, pl.ds(pl.multiple_of(i * size, size), size), :].astype(f32)
    done[...] = jnp.zeros_like(done)


def run_widen(ups, downs):
    steps = 16

    def cut(shape):
        return pl.BlockSpec((shape[0] // steps, shape[1]), lambda i: (i, 0))

    outs = [jax.ShapeDtypeStruct(g.shape[1:], f32) for g in (ups, downs)] * 2
    return pl.pallas_call(
        widen_kernel,
        grid=(steps,),
        out_shape=outs + [jax.ShapeDtypeStruct((8, 128), f32)],
        in_specs=[VM, VM],
        out_specs=[cut(o.shape) for o in outs] + [pl.BlockSpec((8, 128), lambda i: (0, 0))],
        compiler_params=pltpu.CompilerParams(vmem_limit_bytes=24 << 20),
        name="widen",
    )(ups, downs)


def fast_shards(
    tokens,
    lengths,
    deal,
    routes,
    slot_order,
    gain_attn,
    gain_ffn,
    w_qkv,
    w_out,
    centroids,
    expert_in,
    expert_out,
    second_in,
    second_out,
    cotangent,
):
    width = tokens.shape[1]
    experts = lax.axis_size("expert")
    tail = dims(experts, width)[2]
    (slots, tails, cots, cot_tails, dealt, d_main, d_tail, gains, grad_output, residual, tok,
     packed, probs, mixed, w_all) = run_front(
        experts, tail, tokens, cotangent, routes.reshape(1, -1), slot_order.reshape(1, -1), deal, lengths,
        gain_attn[None], gain_ffn[None], w_qkv, w_out,
    )
    ra, rb, ga, gb, g_cent, ups, downs = run_experts(
        experts, slots, tails, cots, cot_tails, centroids,
        (expert_in[0], expert_out[0], second_in[0], second_out[0]),
    )
    *g_experts, done = run_widen(ups, downs)
    out_r, ig_r, g_qkv, g_out, g_gain = run_back(
        experts, tail, ra, rb, ga, gb, d_main, d_tail, gains, grad_output, residual, tok,
        packed, probs, mixed, w_all, done,
    )
    output, input_grad = run_finish(dealt, out_r, ig_r)
    return (
        output,
        input_grad,
        g_gain[:, 0],
        g_gain[:, 64],
        g_qkv,
        g_out,
        g_cent,
        *(g[None] for g in g_experts),
    )


def gather_hidden(rows):
    return lax.all_gather(rows, "hidden", axis=0, tiled=True)


def sum_hidden(terms):
    return lax.psum_scatter(terms, "hidden", scatter_dimension=0, tiled=True)


def swap(blocks):
    return lax.all_to_all(blocks, "expert", split_axis=0, concat_axis=0, tiled=True)


def plain_shards(
    tokens,
    lengths,
    deal,
    routes,
    slot_order,
    gain_attn,
    gain_ffn,
    w_qkv,
    w_out,
    centroids,
    expert_in,
    expert_out,
    second_in,
    second_out,
    cotangent,
):
    width = tokens.shape[1]
    experts = lax.axis_size("expert")
    piece = SEQ // experts
    seats = MICRO * PER
    group = experts * seats
    rows = seats * SEQ
    capacity = (9 * PACK + 8 * experts - 1) // (8 * experts)
    per_dest = MICRO * capacity
    my_expert = lax.axis_index("expert")
    my_hidden = lax.axis_index("hidden")

    deal_row = lax.dynamic_index_in_dim(deal, my_hidden, 0, keepdims=False)
    length_row = lax.dynamic_index_in_dim(lengths, my_hidden, 0, keepdims=False)
    ids = jnp.arange(group, dtype=jnp.int32)
    inverse = jnp.sum(jnp.where(deal_row[None, :] == ids[:, None], ids[None, :], 0), axis=1)
    own = my_expert * seats + jnp.arange(seats, dtype=jnp.int32)
    own_lengths = jnp.sum(
        jnp.where(deal_row[None, :] == own[:, None], length_row[None, :], 0), axis=1
    )

    def to_dealt(flat):
        pieces = jnp.take(flat.reshape(group, piece, flat.shape[1]), inverse, axis=0)
        return lax.all_to_all(
            pieces.reshape(experts, seats, piece, flat.shape[1]),
            "expert",
            split_axis=0,
            concat_axis=2,
            tiled=True,
        ).reshape(rows, flat.shape[1])

    labels = jnp.concatenate([routes, slot_order], axis=1)
    lab = to_dealt(labels)
    tok = to_dealt(tokens)
    grad_output = to_dealt(cotangent)

    cat = jnp.concatenate(
        [w_qkv, w_out, gain_attn[:, None], gain_ffn[:, None], jnp.zeros((w_qkv.shape[0], 126), bf16)],
        axis=1,
    )
    cat = lax.all_gather(cat, ("expert", "hidden"), axis=0, tiled=True)
    qkv_w = cat[:, : 3 * width]
    out_w = cat[:, 3 * width : 4 * width]
    attn_gain = cat[:, 4 * width].astype(f32)[None, :]
    ffn_gain = cat[:, 4 * width + 1].astype(f32)[None, :]

    route = lab[:, 0].reshape(MICRO, PACK)
    order = lab[:, 1].reshape(MICRO, PACK)
    positions = jnp.arange(PACK, dtype=jnp.int32)
    seat = positions // SEQ
    pack_lengths = own_lengths.reshape(MICRO, PER)
    limit = jnp.repeat(pack_lengths, SEQ, axis=1)
    present = (positions % SEQ)[None, :] < limit
    priority = order * PER + seat[None, :]
    ahead = jnp.sum(
        (
            (route[:, :, None] == route[:, None, :])
            & (priority[:, None, :] < priority[:, :, None])
            & present[:, None, :]
        ).astype(jnp.int32),
        axis=2,
    )
    accepted = (present & (ahead < capacity)).reshape(rows)
    target = (
        route * per_dest + jnp.arange(MICRO, dtype=jnp.int32)[:, None] * capacity + ahead
    ).reshape(rows)
    target = jnp.where(accepted, target, -1)
    slot_ids = jnp.arange(experts * per_dest, dtype=jnp.int32)
    dispatch = (slot_ids[:, None] == target[None, :]).astype(bf16)

    def to_experts(values):
        out = mm(dispatch, values).astype(bf16)
        return swap(out.reshape(experts, per_dest, width)).reshape(experts * per_dest, width)

    cot_arrived = to_experts(grad_output)

    inputs = tok.astype(f32)
    unit_a, inv_a = norm_parts(inputs)
    normed = (unit_a * attn_gain).astype(bf16)
    packed = mm(normed, qkv_w).astype(bf16)
    allowed = (
        (seat[:, None] == seat[None, :]) & (positions[None, :] <= positions[:, None])
    )[None] & present[:, None, :]

    def heads(block):
        return block.reshape(MICRO, PACK, HEADS, HEAD)

    queries = heads(packed[:, :width])
    keys_all = heads(packed[:, width : 2 * width])
    values_all = heads(packed[:, 2 * width :])
    scores = jnp.einsum("pqhd,pkhd->phqk", queries, keys_all, preferred_element_type=f32) * 0.125
    masked = jnp.where(allowed[:, None], scores, -1e30)
    peaks = jnp.max(masked, axis=-1, keepdims=True)
    log_total = peaks + jnp.log(jnp.sum(jnp.exp(masked - peaks), axis=-1, keepdims=True))
    probs = jnp.exp(masked - log_total)
    probs_lo = probs.astype(bf16)
    mixed = (
        jnp.einsum("phqk,pkhd->pqhd", probs_lo, values_all, preferred_element_type=f32)
        .reshape(rows, width)
        .astype(bf16)
    )
    residual = inputs + mm(mixed, out_w)
    unit_f, inv_f = norm_parts(residual)
    shared = (unit_f * ffn_gain).astype(bf16)
    arrived = to_experts(shared)

    centroid_row = centroids[0]
    w_in, w_back = expert_in[0], expert_out[0]
    s_in, s_back = second_in[0], second_out[0]
    count = arrived.shape[0]
    arrived_f = arrived.astype(f32)
    gate_vals = jax.nn.sigmoid(
        jnp.sum(arrived_f * centroid_row.astype(f32)[None, :], axis=1, keepdims=True)
    )
    grad_result_own = (gate_vals * cot_arrived.astype(f32)).astype(bf16)
    gathered = gather_hidden(arrived)
    grad_result = gather_hidden(grad_result_own)
    pre_first = mm(gathered, w_in)
    act_first, pull_first = jax.vjp(gelu_act, pre_first)
    act_first = act_first.astype(bf16)
    middle = arrived_f + sum_hidden(mm(act_first, w_back).astype(bf16)).astype(f32)
    middle_lo = gather_hidden(middle.astype(bf16))
    pre_second = mm(middle_lo, s_in)
    act_second, pull_second = jax.vjp(gelu_act, pre_second)
    act_second = act_second.astype(bf16)
    expert_sum = middle + sum_hidden(mm(act_second, s_back).astype(bf16)).astype(f32)
    returned = (gate_vals * expert_sum).astype(bf16)
    came_back = swap(returned.reshape(experts, per_dest, width)).reshape(count, width)

    grad_logit = (
        jnp.sum(cot_arrived.astype(f32) * expert_sum, axis=1, keepdims=True)
        * gate_vals
        * (1.0 - gate_vals)
    )
    grad_pre_second = pull_second(mm(grad_result, s_back, (1, 1)))[0].astype(bf16)
    grad_middle_own = (
        grad_result_own.astype(f32)
        + sum_hidden(mm(grad_pre_second, s_in, (1, 1)).astype(bf16)).astype(f32)
    ).astype(bf16)
    grad_middle = gather_hidden(grad_middle_own)
    grad_pre = pull_first(mm(grad_middle, w_back, (1, 1)))[0].astype(bf16)
    grad_slots = (
        sum_hidden(mm(grad_pre, w_in, (1, 1)).astype(bf16)).astype(f32)
        + grad_middle_own.astype(f32)
        + grad_logit * centroid_row.astype(f32)[None, :]
    ).astype(bf16)
    grad_back = swap(grad_slots.reshape(experts, per_dest, width)).reshape(count, width)
    g_sec_out = mm(act_second, grad_result, (0, 0))
    g_sec_in = mm(middle_lo, grad_pre_second, (0, 0))
    g_exp_out = mm(act_first, grad_middle, (0, 0))
    g_exp_in = mm(gathered, grad_pre, (0, 0))
    g_cent = jnp.sum(grad_logit * arrived_f, axis=0, keepdims=True)

    combined = (residual + mm(dispatch, came_back, (0, 0))).astype(bf16)

    grad_shared = mm(dispatch, grad_back, (0, 0))
    g_gain_ffn = jnp.sum(grad_shared * unit_f, axis=0)
    grad_residual = grad_output.astype(f32) + norm_back(unit_f, inv_f, ffn_gain, grad_shared)
    grad_attended = grad_residual.astype(bf16)
    g_out_w = mm(mixed, grad_attended, (0, 0))
    grad_mixed = heads(mm(grad_attended, out_w, (1, 1)).astype(bf16))
    grad_probs = jnp.einsum("pqhd,pkhd->phqk", grad_mixed, values_all, preferred_element_type=f32)
    grad_values = jnp.einsum("phqk,pqhd->pkhd", probs_lo, grad_mixed, preferred_element_type=f32)
    inner = jnp.sum(probs * grad_probs, axis=-1, keepdims=True)
    grad_scores = (probs * (grad_probs - inner)).astype(bf16)
    grad_queries = (
        jnp.einsum("phqk,pkhd->pqhd", grad_scores, keys_all, preferred_element_type=f32) * 0.125
    )
    grad_keys = (
        jnp.einsum("phqk,pqhd->pkhd", grad_scores, queries, preferred_element_type=f32) * 0.125
    )
    grad_packed = jnp.concatenate(
        [g.reshape(rows, width) for g in (grad_queries, grad_keys, grad_values)], axis=1
    ).astype(bf16)
    g_qkv = mm(normed, grad_packed, (0, 0))
    grad_normed = mm(grad_packed, qkv_w, (1, 1))
    g_gain_attn = jnp.sum(grad_normed * unit_a, axis=0)
    input_grad = (grad_residual + norm_back(unit_a, inv_a, attn_gain, grad_normed)).astype(bf16)

    def scatter(partial):
        return lax.psum_scatter(
            partial, ("expert", "hidden"), scatter_dimension=0, tiled=True
        )

    g_cat = jnp.concatenate([g_qkv, g_out_w, g_gain_attn[:, None], g_gain_ffn[:, None], jnp.zeros((width, 126), f32)], axis=1)
    g_cat = scatter(g_cat)
    g_cent = lax.psum(g_cent, "hidden")

    def from_dealt(dealt):
        received = lax.all_to_all(
            dealt.reshape(1, seats, SEQ, width), "expert", split_axis=2, concat_axis=0, tiled=True
        ).reshape(group, piece, width)
        return jnp.take(received, deal_row, axis=0).reshape(group * piece, width)

    return (
        from_dealt(combined),
        from_dealt(input_grad).astype(f32),
        g_cat[:, 4 * width],
        g_cat[:, 4 * width + 1],
        g_cat[:, : 3 * width],
        g_cat[:, 3 * width : 4 * width],
        g_cent,
        g_exp_in[None],
        g_exp_out[None],
        g_sec_in[None],
        g_sec_out[None],
    )


def solution(mesh):
    both = ("expert", "hidden")
    fast = mesh.shape["expert"] == 16 and mesh.shape["hidden"] == 2
    return jax.shard_map(
        fast_shards if fast else plain_shards,
        mesh=mesh,
        in_specs=(
            P(both, None),
            P(),
            P(),
            P(both, None),
            P(both, None),
            P(both),
            P(both),
            P(both, None),
            P(both, None),
            P("expert", None),
            P("expert", None, "hidden"),
            P("expert", "hidden", None),
            P("expert", None, "hidden"),
            P("expert", "hidden", None),
            P(both, None),
        ),
        out_specs=(
            P(both, None),
            P(both, None),
            P(both),
            P(both),
            P(both, None),
            P(both, None),
            P("expert", None),
            P("expert", None, "hidden"),
            P("expert", "hidden", None),
            P("expert", None, "hidden"),
            P("expert", "hidden", None),
        ),
        check_vma=False,
    )
```

```python
import functools

import jax
import jax.numpy as jnp
from jax import lax
from jax.experimental import pallas as pl
from jax.experimental.pallas import tpu as pltpu
from jax.sharding import PartitionSpec as P

HEADS = 16
HEAD = 64
MICRO = 4
PER = 2
SEQ = 64
PACK = PER * SEQ

epsilon = 1e-05
bf16 = jnp.bfloat16
f32 = jnp.float32


def mm(a, b, contract=(1, 0)):
    return lax.dot_general(
        a, b, (((contract[0],), (contract[1],)), ((), ())), preferred_element_type=f32
    )


def norm_parts(rows):
    centre = jnp.mean(rows, axis=-1, keepdims=True)
    shifted = rows - centre
    spread = jnp.mean(shifted * shifted, axis=-1, keepdims=True)
    inv = lax.rsqrt(spread + epsilon)
    return shifted * inv, inv


def norm_back(unit, inv, gain, grad):
    g = grad * gain
    m1 = jnp.mean(g, axis=-1, keepdims=True)
    m2 = jnp.mean(g * unit, axis=-1, keepdims=True)
    return inv * (g - m1 - unit * m2)


def gelu_act(pre_act):
    return jax.nn.gelu(pre_act, approximate=True)


MESH = pl.DeviceIdType.MESH
ANY = pl.BlockSpec(memory_space=pl.ANY)
VM = pl.BlockSpec(memory_space=pltpu.VMEM)
DMA = pltpu.SemaphoreType.DMA
VMEM_MAX = 63 << 20
PARTS = 4


def dims(experts, width):
    capacity = (9 * PACK + 8 * experts - 1) // (8 * experts)
    per_dest = MICRO * capacity
    main = per_dest // 16 * 16
    return per_dest, main, per_dest - main


def by_columns(width, size, body):
    def step(n, carry):
        body(pl.ds(pl.multiple_of(n * size, size), size), n)
        return carry

    lax.fori_loop(0, width // size, step, 0)


def apply_rows(matrix, src, dst, contract=(1, 0)):
    def body(cols, n):
        dst[:, cols] = mm(matrix[...], src[:, cols], contract).astype(dst.dtype)

    by_columns(src.shape[1], 256, body)


def greet(experts, me, core, partner):
    barrier = pltpu.get_barrier_semaphore()

    def hello(k, carry):
        pl.semaphore_signal(
            barrier, inc=1, device_id=(lax.rem(me + k, experts), core), device_id_type=MESH
        )
        return carry

    lax.fori_loop(1, experts, hello, 0)
    if partner is not None:
        pl.semaphore_signal(barrier, inc=1, device_id=(me, partner), device_id_type=MESH)
    pl.semaphore_wait(barrier, experts - 1 + (partner is not None))


class Spread:
    def __init__(self, experts, me, core, src, dst, sends, recvs, local):
        self.experts, self.me, self.core = experts, me, core
        self.src, self.dst, self.sends, self.recvs, self.local = src, dst, sends, recvs, local
        self.rows = src.shape[0] // experts

    def block(self, ref, index):
        return ref.at[pl.ds(pl.multiple_of(index * self.rows, 16), self.rows)]

    def copy(self, k):
        to = lax.rem(self.me + k, self.experts)
        return pltpu.make_async_remote_copy(
            self.block(self.src, to),
            self.block(self.dst, self.me),
            self.sends.at[k],
            self.recvs.at[k],
            device_id=(to, self.core),
            device_id_type=MESH,
        )

    def own(self):
        return pltpu.make_async_copy(
            self.block(self.src, self.me), self.block(self.dst, self.me), self.local
        )

    def start(self):
        self.own().start()

        def go(k, carry):
            self.copy(k).start()
            return carry

        lax.fori_loop(1, self.experts, go, 0)

    def wait(self):
        self.own().wait()

        def stop(k, carry):
            self.copy(k).wait()
            return carry

        lax.fori_loop(1, self.experts, stop, 0)


def tail_matrix(part, experts, tail, turned):
    size = PARTS * tail
    shape = (experts * tail, experts * size) if turned else (experts * size, experts * tail)
    there = lax.broadcasted_iota(jnp.int32, shape, 1 if turned else 0)
    here = lax.broadcasted_iota(jnp.int32, shape, 0 if turned else 1)
    want = here // tail * size + part * tail + here % tail
    return (there == want).astype(f32).astype(bf16)


def gelu_pair(v):
    u = v * v
    t = jnp.tanh(v * (0.7978845608 + 0.7978845608 * 0.044715 * u))
    h = 0.5 * t + 0.5
    slope = h + (h - h * h) * (v * (2 * 0.7978845608 + 6 * 0.7978845608 * 0.044715 * u))
    return v * h, slope


def experts_kernel(experts, tail, *refs):
    (a_in, b_in, ca_in, cb_in, cent, w1_h, w2_h, w3_h, w4_h) = refs[:9]
    (ra_out, rb_out, ga_out, gb_out, gcent, wu, wd) = refs[9:16]
    (xs_, gs_, act, slope, mid, psend, precv, ca, cb, sa, sb, cent_s, cent_r) = refs[16:29]
    (wsem, psems, prsems, xs, xr, asend, arecv, alocal) = refs[29:]
    me, core = lax.axis_index("expert"), lax.axis_index("hidden")
    other = 1 - core
    both, width = xs_.shape[1], xs_.shape[2]
    own = both // 2
    hid = wu.shape[2]
    main = a_in.shape[0]
    block = width // PARTS
    mine, theirs = pl.ds(0, own), pl.ds(own, own)

    loads = []
    for i, (h, v) in enumerate(((w1_h, wu.at[0]), (w2_h, wd.at[0]), (w3_h, wu.at[1]), (w4_h, wd.at[1]))):
        load = pltpu.make_async_copy(h, v, wsem.at[i])
        load.start()
        loads.append(load)
    greet(experts, me, core, other)

    def move(i, src, dst):
        return Spread(experts, me, core, src, dst, asend.at[i], arecv.at[i], alocal.at[i])

    cot_moves = (move(0, ca_in, ca), move(1, cb_in, cb))
    for m in cot_moves:
        m.start()

    def pair(src, dst, send, recv):
        return pltpu.make_async_remote_copy(
            src, dst, send, recv, device_id=(me, other), device_id_type=MESH
        )

    def share_x(i):
        return pair(xs_.at[i, mine], xs_.at[i, theirs], xs.at[i], xr.at[i])

    def share_g(i):
        return pair(gs_.at[i, mine], gs_.at[i, theirs], xs.at[2 + i], xr.at[2 + i])

    def partial_send(step):
        return pair(psend, precv.at[lax.rem(step, 2)], psems.at[step], prsems.at[step])

    def from_tail(ref, to, start):
        for q in range(PARTS):
            to[0, pl.ds(start, experts * tail), q * block : (q + 1) * block] = mm(
                tail_matrix(q, experts, tail, True), ref[...]
            ).astype(bf16)

    def to_tail(value, ref):
        total = None
        for q in range(PARTS):
            term = mm(tail_matrix(q, experts, tail, False), value[:, q * block : (q + 1) * block])
            total = term if total is None else total + term
        ref[...] = total.astype(bf16)

    TN, WM, WN = 512, 512, 1024

    def over(size, body):
        def step(n, carry):
            body(pl.ds(pl.multiple_of(n * TN, TN), TN))
            return carry

        lax.fori_loop(0, size // TN, step, 0)

    def halves(body):
        def step(r, carry):
            body(r, pl.ds(pl.multiple_of(r * own, own), own))
            return carry

        lax.fori_loop(0, 2, step, 0)

    def exchange(step, source, weights, turned):
        def rows_of(r, unused):
            rows = pl.ds(pl.multiple_of((1 - r) * own, own), own)

            def body(cols):
                if turned:
                    value = mm(source[rows, :], weights[cols, :], (1, 1))
                else:
                    value = mm(source[rows, :], weights[:, cols])

                @pl.when(r == 0)
                def _():
                    psend[:, cols] = value.astype(bf16)

                @pl.when(r == 1)
                def _():
                    mid[:, cols] += value

            over(width, body)

            @pl.when(r == 0)
            def _():
                partial_send(step).start()

        halves(rows_of)
        partial_send(step).wait()
        mid[...] += precv[lax.rem(step, 2)].astype(f32)

    xs_[0, pl.ds(0, main), :] = a_in[...]
    from_tail(b_in, xs_, main)
    share_x(0).start()
    slot = xs_[0, mine, :].astype(f32)
    mid[...] = slot
    gate = jax.nn.sigmoid(jnp.sum(slot * cent[...].astype(f32), axis=1, keepdims=True))

    def forward(i, carry):
        def up(r, rows):
            @pl.when(r == 1)
            def _():
                share_x(i).wait()

            def body(cols):
                a, d = gelu_pair(mm(xs_[i, rows, :], wu[i, :, cols]))
                act[i, rows, cols] = a.astype(bf16)
                slope[i, rows, cols] = d.astype(bf16)

            over(hid, body)

        for k in range(2):

            @pl.when(i == k)
            def _():
                loads[2 * k].wait()

        halves(up)
        for k in range(2):

            @pl.when(i == k)
            def _():
                loads[2 * k + 1].wait()

        exchange(i, act.at[i], wd.at[i], False)

        @pl.when(i == 0)
        def _():
            xs_[1, mine, :] = mid[...].astype(bf16)
            share_x(1).start()

        return carry

    lax.fori_loop(0, 2, forward, 0)
    returned = (gate * mid[...]).astype(bf16)
    sa[...] = returned[:main]
    to_tail(returned[main:], sb)
    ret_moves = (move(2, sa, ra_out), move(3, sb, rb_out))
    for m in ret_moves:
        m.start()
    for m in cot_moves:
        m.wait()
    gs_[0, pl.ds(0, main), :] = ca[...]
    from_tail(cb, gs_, main)
    cot = gs_[0, mine, :].astype(f32)
    logit = jnp.sum(cot * mid[...], axis=1, keepdims=True) * gate * (1.0 - gate)
    cent_s[...] = jnp.sum(logit * xs_[0, mine, :].astype(f32), axis=0, keepdims=True)
    share_c = pair(cent_s, cent_r, xs.at[4], xr.at[4])
    share_c.start()
    start_grad = (gate * cot).astype(bf16)
    gs_[1, mine, :] = start_grad
    mid[...] = start_grad.astype(f32)
    share_g(1).start()

    def backward(k, carry):
        i = 1 - k

        def up_back(r, rows):
            @pl.when(r == 1)
            def _():
                share_g(i).wait()

            def body(cols):
                t = mm(gs_[i, rows, :], wd[i, cols, :], (1, 1)) * slope[i, rows, cols].astype(f32)
                slope[i, rows, cols] = t.astype(bf16)

            over(hid, body)

        halves(up_back)
        exchange(2 + k, slope.at[i], wu.at[i], True)

        @pl.when(k == 0)
        def _():
            gm = mid[...].astype(bf16)
            gs_[0, mine, :] = gm
            mid[...] = gm.astype(f32) + logit * cent[...].astype(f32)
            share_g(0).start()

        return carry

    lax.fori_loop(0, 2, backward, 0)
    for m in ret_moves:
        m.wait()
    slots = mid[...].astype(bf16)
    sa[...] = slots[:main]
    to_tail(slots[main:], sb)
    back_moves = (move(4, sa, ga_out), move(5, sb, gb_out))
    for m in back_moves:
        m.start()

    def weight_grad(left, right, to):
        wide_n = right.shape[1]

        def body(n, carry):
            m, c = n // (wide_n // WN), lax.rem(n, wide_n // WN)
            rows = pl.ds(pl.multiple_of(m * WM, WM), WM)
            cols = pl.ds(pl.multiple_of(c * WN, WN), WN)
            to[rows, cols] = mm(left[:, rows], right[:, cols], (0, 0)).astype(bf16)
            return carry

        lax.fori_loop(0, left.shape[1] // WM * (wide_n // WN), body, 0)

    def weight_grads(i, carry):
        weight_grad(act.at[i], gs_.at[i], wd.at[i])
        weight_grad(xs_.at[i], slope.at[i], wu.at[i])
        return carry

    lax.fori_loop(0, 2, weight_grads, 0)
    share_c.wait()
    gcent[...] = cent_s[...] + cent_r[...]
    for m in back_moves:
        m.wait()


def run_experts(experts, slots, tails, cots, cot_tails, centroid, weights):
    width, hid = weights[0].shape
    main = slots.shape[0]
    tail = tails.shape[0] // experts // PARTS
    own = main + experts * tail
    both = 2 * own

    def sds(*shape, dtype=bf16):
        return jax.ShapeDtypeStruct(shape, dtype)

    travel = [sds(*slots.shape), sds(*tails.shape)] * 2
    wide = [pltpu.VMEM((2, width, hid), bf16), pltpu.VMEM((2, hid, width), bf16)]
    return pl.pallas_call(
        functools.partial(experts_kernel, experts, tail),
        out_shape=travel + [sds(1, width, dtype=f32)] + wide,
        in_specs=[VM, VM, ANY, ANY, VM, ANY, ANY, ANY, ANY],
        out_specs=[ANY] * 4 + [VM] * 3,
        scratch_shapes=[
            pltpu.VMEM((2, both, width), bf16),
            pltpu.VMEM((2, both, width), bf16),
            pltpu.VMEM((2, both, hid), bf16),
            pltpu.VMEM((2, both, hid), bf16),
            pltpu.VMEM((own, width), f32),
            pltpu.VMEM((own, width), bf16),
            pltpu.VMEM((2, own, width), bf16),
            pltpu.VMEM(slots.shape, bf16),
            pltpu.VMEM(tails.shape, bf16),
            pltpu.VMEM(slots.shape, bf16),
            pltpu.VMEM(tails.shape, bf16),
            pltpu.VMEM((1, width), f32),
            pltpu.VMEM((1, width), f32),
            DMA((4,)),
            DMA((4,)),
            DMA((4,)),
            DMA((5,)),
            DMA((5,)),
            DMA((6, experts)),
            DMA((6, experts)),
            DMA((6,)),
        ],
        compiler_params=pltpu.CompilerParams(
            collective_id=2, has_side_effects=True, vmem_limit_bytes=45 << 20
        ),
        name="experts_pass",
    )(slots, tails, cots, cot_tails, centroid, *weights)

def back_kernel(experts, tail, *refs):
    (ra, rb, ga, gb, dm, dt, gains, cot_h, res_h, tok_h, packed_h, probs_h, mixed_h, wall_h) = refs[:14]
    refs = refs[:14] + refs[15:]
    out_o, ig_o, gqkv_o, gout_o, ggain_o = refs[14:19]
    (cot, res, tok, packed, probs, mixed, wqkv, wout, normed, gatt, gmix, gpk, so, si, perm, wide, turn) = refs[19:36]
    keeps, psends, precvs, rv1s, rv2s, rv3s = (refs[36 + 6 * i : 42 + 6 * i] for i in range(6))
    lsem, sends, recvs, asend, arecv, alocal = refs[72:]
    me, core = lax.axis_index("expert"), lax.axis_index("hidden")
    other = 1 - core
    my_z, my_y, my_x = me // 4, lax.rem(me // 2, 2), lax.rem(me, 2)
    rows, width = tok.shape
    block = width // PARTS

    loads = {}
    for i, (name, h, v) in enumerate(
        (
            ("res", res_h, res),
            ("cot", cot_h, cot),
            ("mixed", mixed_h, mixed),
            ("wout", wall_h.at[:, pl.ds(3 * width + 128, width)], wout),
            ("probs", probs_h, probs),
            ("packed", packed_h, packed),
            ("tok", tok_h, tok),
            ("wqkv", wall_h.at[:, pl.ds(0, 3 * width)], wqkv),
        )
    ):
        loads[name] = pltpu.make_async_copy(h, v, lsem.at[i])
        loads[name].start()
    greet(experts, me, core, other)

    def join_slots(slots, tails):
        def body(cols, q):
            wide[:, cols] = mm(dm[...], slots[:, cols], (0, 0)) + mm(dt[q], tails[...], (0, 0))

        by_columns(width, block, body)

    piece = SEQ // experts
    seats = MICRO * PER

    shape = (rows, rows)
    to, at = lax.broadcasted_iota(jnp.int32, shape, 0), lax.broadcasted_iota(jnp.int32, shape, 1)
    b, s, q = to // (seats * piece), to // piece % seats, to % piece
    turn[...] = (at == s * SEQ + b * piece + q).astype(f32).astype(bf16)

    def move(i, src, dst):
        return Spread(experts, me, core, src, dst, asend.at[i], arecv.at[i], alocal.at[i])

    my_a = jnp.where(core == 0, my_x, my_y)
    my_b = jnp.where(core == 0, my_y, my_x)

    def near(a_step, b_step):
        a, b = (1 - my_a if a_step else my_a), (1 - my_b if b_step else my_b)
        x, y = jnp.where(core == 0, a, b), jnp.where(core == 0, b, a)
        return my_z * 4 + y * 2 + x

    def remote(c, stage, src, dst, to, to_core):
        return pltpu.make_async_remote_copy(
            src, dst, sends.at[c, stage], recvs.at[c, stage],
            device_id=(to, to_core), device_id_type=MESH,
        )

    def pair_copy(c):
        return remote(c, 0, psends[c], precvs[c], me, other)

    def a_copy(c):
        return remote(c, 1, psends[c].at[pl.ds(0, 256)], rv1s[c], near(True, False), core)

    def b_copy(c):
        return remote(c, 2, psends[c].at[pl.ds(256, 128)], rv2s[c], near(False, True), core)

    line = lax.rem(me, 4)
    my_set = jnp.where((my_z == 0) | (my_z == 3), 0, 1)
    my_place = my_z // 2

    def c_copy(c):
        to_z = my_z + 1 - 2 * lax.rem(my_z, 2)
        return remote(c, 3, psends[c].at[pl.ds(384, 64)], rv3s[c].at[pl.ds(0, 64)], to_z * 4 + line, core)

    def z_copy(c):
        return remote(c, 4, psends[c].at[pl.ds(448, 32)], rv3s[c].at[pl.ds(64, 32)], (3 - my_z) * 4 + line, core)

    def place(c, t, cols):
        keeps[c][:, cols] = t[: width // 2]
        psends[c][:, cols] = t[width // 2 :].astype(bf16)

    at = lax.broadcasted_iota(jnp.int32, (1, width), 1)
    goes = jnp.where(at < width // 2, core, other)
    high, mid_ = at // 256 % 2, at // 128 % 2
    to_x, to_y = jnp.where(goes == 0, high, mid_), jnp.where(goes == 0, mid_, high)
    level = at // 32 % 4
    to_z = jnp.where(level == 0, 0, jnp.where(level == 1, 3, level - 1))
    source = ((to_z * 4 + to_y * 2 + to_x) * 2 + goes) * 32 + at % 32
    perm[...] = (lax.broadcasted_iota(jnp.int32, (width, width), 0) == source).astype(f32).astype(bf16)

    def compute(c, left, right, start, stride, count, size):
        def body(n, carry):
            cols = pl.ds(pl.multiple_of(start + n * stride, size), size)
            place(c, mm(left[...], right[:, cols], (0, 0)), pl.ds(pl.multiple_of(n * size, size), size))
            return carry

        lax.fori_loop(0, count, body, 0)
        pair_copy(c).start()

    half_a = pl.ds(pl.multiple_of(my_a * 256, 256), 256)
    half_a_out = pl.ds(pl.multiple_of((1 - my_a) * 256, 256), 256)
    base_b = my_a * 256
    half_b = pl.ds(pl.multiple_of(base_b + my_b * 128, 128), 128)
    half_b_out = pl.ds(pl.multiple_of(base_b + (1 - my_b) * 128, 128), 128)
    base_c = base_b + my_b * 128
    half_c = pl.ds(pl.multiple_of(base_c + my_set * 64, 64), 64)
    half_c_out = pl.ds(pl.multiple_of(base_c + (1 - my_set) * 64, 64), 64)
    base_z = base_c + my_set * 64
    place_in = pl.ds(pl.multiple_of(base_z + my_place * 32, 32), 32)
    place_out = pl.ds(pl.multiple_of(base_z + (1 - my_place) * 32, 32), 32)

    def after_pair(c):
        pair_copy(c).wait()
        keep = keeps[c]
        keep[...] += precvs[c][...].astype(f32)
        psends[c][pl.ds(0, 256), :] = keep[half_a_out, :].astype(bf16)
        a_copy(c).start()

    def after_a(c):
        a_copy(c).wait()
        keep = keeps[c]
        keep[half_a, :] += rv1s[c][...].astype(f32)
        psends[c][pl.ds(256, 128), :] = keep[half_b_out, :].astype(bf16)
        b_copy(c).start()

    def after_b(c):
        b_copy(c).wait()
        keep = keeps[c]
        keep[half_b, :] += rv2s[c][...].astype(f32)
        psends[c][pl.ds(384, 64), :] = keep[half_c_out, :].astype(bf16)
        c_copy(c).start()

    def after_c(c):
        c_copy(c).wait()
        keep = keeps[c]
        keep[half_c, :] += rv3s[c][pl.ds(0, 64), :].astype(f32)
        psends[c][pl.ds(448, 32), :] = keep[place_out, :].astype(bf16)
        z_copy(c).start()

    def after_z(c, pieces):
        z_copy(c).wait()
        total = keeps[c][place_in, :] + rv3s[c][pl.ds(64, 32), :].astype(f32)
        size = total.shape[1] // len(pieces)
        for n, (out, start) in enumerate(pieces):
            out[:, start : start + size] = total[:, n * size : (n + 1) * size]

    gain_a, gain_f = gains[0:1, :], gains[1:2, :]
    loads["res"].wait()
    join_slots(ra, rb)
    gmix[...] = (res[...] + wide[...]).astype(bf16)
    apply_rows(turn, gmix, so)
    out_move = move(0, so, out_o)
    out_move.start()
    unit, inv = norm_parts(res[...])
    join_slots(ga, gb)
    grad_shared = wide[...]
    ffn_sums = jnp.sum(grad_shared * unit, axis=0, keepdims=True)
    loads["cot"].wait()
    grad = cot[...].astype(f32) + norm_back(unit, inv, gain_f, grad_shared)
    res[...] = grad
    gatt[...] = grad.astype(bf16)
    loads["mixed"].wait()
    gpk_view = gpk.at[:, pl.ds(0, width)]
    apply_rows(mixed, perm, gpk_view)
    compute(0, gpk_view, gatt, 0, width // 4, 4, width // 4)
    loads["wout"].wait()

    def mix(cols, n):
        gmix[:, cols] = mm(gatt[...], wout[cols, :], (1, 1)).astype(bf16)

    by_columns(width, 256, mix)
    after_pair(0)
    loads["probs"].wait()
    loads["packed"].wait()
    lane = lax.broadcasted_iota(jnp.int32, (PACK, 2 * HEAD), 1)
    first = lane < HEAD

    def stacked(v):
        zero = jnp.zeros_like(v)
        return jnp.concatenate([jnp.where(first, v, zero), jnp.where(first, zero, v)], axis=0)

    def head_pair(p, h):
        at = pl.ds(pl.multiple_of(p * PACK, PACK), PACK)
        lo = h * 2 * HEAD
        q = packed[at, lo : lo + 2 * HEAD]
        k = packed[at, width + lo : width + lo + 2 * HEAD]
        v = packed[at, 2 * width + lo : 2 * width + lo + 2 * HEAD]
        gs = stacked(gmix[at, lo : lo + 2 * HEAD])
        pr_lo = probs[p * (HEADS // 2) + h]
        pr = pr_lo.astype(f32)
        gp = mm(gs, v, (1, 1))
        gv = mm(pr_lo, gs, (0, 0))
        inner = jnp.sum(pr * gp, axis=1, keepdims=True)
        ds_ = (pr * (gp - inner)).astype(bf16)
        t = mm(ds_, k)
        gq = jnp.where(first, t[:PACK], t[PACK:]) * 0.125
        gk = mm(ds_, stacked(q), (0, 0)) * 0.125
        gpk[at, lo : lo + 2 * HEAD] = gq.astype(bf16)
        gpk[at, width + lo : width + lo + 2 * HEAD] = gk.astype(bf16)
        gpk[at, 2 * width + lo : 2 * width + lo + 2 * HEAD] = gv.astype(bf16)

    part = width // 4

    def group_pieces(g):
        return tuple(part * g + width * i for i in range(3))

    def group(g):
        def packs(p, carry):
            for h in range(HEADS // 8):
                head_pair(p, g * (HEADS // 8) + h)
            return carry

        lax.fori_loop(0, MICRO, packs, 0)

    def set_off(g):
        compute(1 + g, normed, gpk, part * g, width, 3, part)

    def finish(g):
        after_z(1 + g, [(gqkv_o, start) for start in group_pieces(g)])

    loads["tok"].wait()
    unit, inv = norm_parts(tok[...].astype(f32))
    so2 = gpk.at[:, pl.ds(2 * width, width)]
    so2[...] = (unit * gain_a).astype(bf16)
    apply_rows(so2, perm, normed)
    group(0)
    set_off(0)
    group(1)
    set_off(1)
    after_pair(1)
    after_a(0)
    group(2)
    set_off(2)
    after_pair(2)
    after_b(0)
    group(3)
    after_pair(3)
    after_a(1)
    after_c(0)
    loads["wqkv"].wait()

    def pull(cols, n):
        wide[:, cols] = mm(gpk[...], wqkv[cols, :], (1, 1))

    by_columns(width, 256, pull)
    grad_normed = wide[...]
    unit, inv = norm_parts(tok[...].astype(f32))
    attn_sums = jnp.sum(grad_normed * unit, axis=0, keepdims=True)
    gmix[...] = (res[...] + norm_back(unit, inv, gain_a, grad_normed)).astype(bf16)
    apply_rows(turn, gmix, si)
    ig_move = move(1, si, ig_o)
    ig_move.start()
    set_off(3)
    after_a(2)
    after_b(1)
    sums = jnp.where(lax.broadcasted_iota(jnp.int32, (128, width), 0) < 64, attn_sums, ffn_sums)
    sums_hi = sums.astype(bf16)
    sums_lo = (sums - sums_hi.astype(f32)).astype(bf16)
    place(5, mm(perm[...], sums_hi, (0, 1)) + mm(perm[...], sums_lo, (0, 1)), pl.ds(0, 128))
    pair_copy(5).start()
    after_pair(4)
    after_pair(5)
    after_z(0, [(gout_o, 0)])
    after_a(3)
    after_b(2)
    after_c(1)
    after_a(4)
    after_a(5)
    after_b(3)
    after_c(2)
    finish(0)
    after_b(4)
    after_b(5)
    after_c(3)
    finish(1)
    after_c(4)
    after_c(5)
    finish(2)
    finish(3)
    after_z(5, [(ggain_o, 0)])
    out_move.wait()
    ig_move.wait()


def run_back(experts, tail, slots, tails, grads, grad_tails, d_main, d_tail, gains, cot, residual, tok, packed, probs, mixed, w_all, done):
    rows, width = tok.shape

    def sds(*shape, dtype=bf16):
        return jax.ShapeDtypeStruct(shape, dtype)

    widths = (width,) + (3 * width // 4,) * 4 + (128,)
    scratch = [
        pltpu.VMEM(cot.shape, bf16),
        pltpu.VMEM(residual.shape, f32),
        pltpu.VMEM(tok.shape, bf16),
        pltpu.VMEM(packed.shape, bf16),
        pltpu.VMEM(probs.shape, bf16),
        pltpu.VMEM(mixed.shape, bf16),
        pltpu.VMEM((width, 3 * width), bf16),
        pltpu.VMEM((width, width), bf16),
        pltpu.VMEM((rows, width), bf16),
        pltpu.VMEM((rows, width), bf16),
        pltpu.VMEM((rows, width), bf16),
        pltpu.VMEM((rows, 3 * width), bf16),
        pltpu.VMEM((rows, width), bf16),
        pltpu.VMEM((rows, width), bf16),
        pltpu.VMEM((width, width), bf16),
        pltpu.VMEM((rows, width), f32),
        pltpu.VMEM((rows, rows), bf16),
    ]
    scratch += [pltpu.VMEM((width // 2, w), f32) for w in widths]
    for part in (2, 2, 4, 8):
        scratch += [pltpu.VMEM((width // part, w), bf16) for w in widths]
    scratch += [pltpu.VMEM((96, w), bf16) for w in widths]
    scratch += [
        DMA((8,)),
        DMA((6, 6)),
        DMA((6, 6)),
        DMA((2, experts)),
        DMA((2, experts)),
        DMA((2,)),
    ]
    return pl.pallas_call(
        functools.partial(back_kernel, experts, tail),
        out_shape=[sds(rows, width), sds(rows, width), sds(32, 3 * width, dtype=f32), sds(32, width, dtype=f32), sds(32, 128, dtype=f32)],
        in_specs=[VM] * 7 + [ANY] * 8,
        out_specs=[ANY, ANY, VM, VM, VM],
        scratch_shapes=scratch,
        compiler_params=pltpu.CompilerParams(
            collective_id=3, has_side_effects=True, vmem_limit_bytes=VMEM_MAX
        ),
        name="attention_back",
    )(slots, tails, grads, grad_tails, d_main, d_tail, gains, cot, residual, tok, packed, probs, mixed, w_all, done)


def front_kernel(experts, tail, *refs):
    (tokens, cots, routes, orders, deal, lengths, g_attn, g_ffn, w_qkv, w_out) = refs[:10]
    (slots_o, tails_o, cslots_o, ctails_o, deal_o, dm_o, dt_o, gains_o, cot_o, res_o, tok_o, packed_o, probs_o, mixed_o, w_o) = refs[10:25]
    (st, sl, rt, rl, rc, tok, cot, w, packed, probs, mixed, res, shared, dm, dt, ftm, masks, ss, stl, cs, ctl, turn) = refs[25:47]
    zs, zr, as_, ar, bs, br, ps, pr, asend, arecv, alocal, osem = refs[47:]
    me, core = lax.axis_index("expert"), lax.axis_index("hidden")
    other = 1 - core
    my_z, my_y, my_x = me // 4, lax.rem(me // 2, 2), lax.rem(me, 2)
    rows, width = tok.shape
    piece = SEQ // experts
    seats = MICRO * PER
    block = width // PARTS
    step = w_qkv.shape[0]
    per_dest = experts and dims(experts, width)[0]
    main = per_dest - tail
    capacity = per_dest // MICRO

    def iota(shape, axis):
        return lax.broadcasted_iota(jnp.int32, shape, axis)

    def one_hot(test):
        return test.astype(f32).astype(bf16)

    own_rows = pl.ds(pl.multiple_of((me * 2 + core) * step, step), step)
    gain_at, out_at = 3 * width, 3 * width + 128
    w[own_rows, :gain_at] = w_qkv[...]
    w[own_rows, out_at:] = w_out[...]
    eye = iota((step, step), 0) == iota((step, step), 1)

    def as_column(row):
        return jnp.sum(jnp.where(eye, row[...].astype(f32), 0.0), axis=1, keepdims=True)

    gain_cols = jnp.where(iota((step, 128), 1) < 64, as_column(g_attn), as_column(g_ffn))
    w[own_rows, gain_at:out_at] = gain_cols.astype(bf16)
    cuts = ((0, out_at), (out_at, width))

    line = lax.rem(me, 4)
    a_to = jnp.where(core == 0, my_z * 4 + my_y * 2 + 1 - my_x, my_z * 4 + 2 - 2 * my_y + my_x)
    b_to = jnp.where(core == 0, my_z * 4 + 2 - 2 * my_y + my_x, my_z * 4 + my_y * 2 + 1 - my_x)
    shift_a, shift_b = a_to - me, b_to - me

    def send(j, e, sem_s, sem_r, to, to_core):
        start, size = cuts[j]
        ref = w.at[pl.ds(pl.multiple_of((e * 2 + core) * step, step), step), pl.ds(start, size)]
        return pltpu.make_async_remote_copy(
            ref, ref, sem_s, sem_r, device_id=(to, to_core), device_id_type=MESH
        )

    def up(j, d):
        s = my_z - d
        return send(j, s * 4 + line, zs.at[j, d], zr.at[j, s], me + 4, core)

    def down(j, d):
        s = my_z + d
        return send(j, s * 4 + line, zs.at[j, 4 + d], zr.at[j, s], me - 4, core)

    def a_copy(j, s):
        return send(j, s * 4 + line, as_.at[j, s], ar.at[j, s], a_to, core)

    def b_copy(j, f, s):
        return send(j, s * 4 + line + f * shift_a, bs.at[j, 4 * f + s], br.at[j, 4 * f + s], b_to, core)

    def p_copy(j, f, s):
        e = s * 4 + line + (f % 2) * shift_a + (f // 2) * shift_b
        return send(j, e, ps.at[j, 4 * f + s], pr.at[j, 4 * f + s], me, other)

    def release(j, s):
        b_copy(j, 0, s).start()
        a_copy(j, s).start()
        p_copy(j, 0, s).start()

    def chain(j, d):
        @pl.when(my_z >= d)
        def _():
            if d:
                up(j, d).wait_recv()

            @pl.when(my_z < 3)
            def _():
                up(j, d).start()

            if d:
                release(j, my_z - d)

        @pl.when(my_z + d <= 3)
        def _():
            if d:
                down(j, d).wait_recv()

            @pl.when(my_z > 0)
            def _():
                down(j, d).start()

            if d:
                release(j, my_z + d)

        if not d:
            release(j, my_z)

    def places():
        return [lax.rem(my_z + k, 4) for k in (0, 1, 3, 2)]

    def fan_a(j):
        for s in places():
            a_copy(j, s).wait_recv()
            b_copy(j, 1, s).start()
            p_copy(j, 1, s).start()

    def fan_b(j):
        for f in range(2):
            for s in places():
                b_copy(j, f, s).wait_recv()
                p_copy(j, 2 + f, s).start()

    def fan_p(j):
        for f in range(4):
            for s in range(4):
                p_copy(j, f, s).wait_recv()

    def all_sent(j):
        for d in range(4):

            @pl.when((my_z >= d) & (my_z < 3))
            def _():
                up(j, d).wait_send()

            @pl.when((my_z + d <= 3) & (my_z > 0))
            def _():
                down(j, d).wait_send()

        for s in range(4):
            a_copy(j, s).wait_send()
            for f in range(2):
                b_copy(j, f, s).wait_send()
            for f in range(4):
                p_copy(j, f, s).wait_send()

    greet(experts, me, core, other)
    chain(0, 0)
    chain(1, 0)

    def move(i, src, dst):
        return Spread(experts, me, core, src, dst, asend.at[i], arecv.at[i], alocal.at[i])

    group = deal.shape[1]
    deal_row = deal[pl.ds(core, 1), :]
    length_row = lengths[pl.ds(core, 1), :]
    spread_out = one_hot(iota((group, rows), 1) // piece == iota((group, rows), 0))
    wide = jnp.broadcast_to(deal_row.astype(f32), (8, group)).astype(bf16)
    goal = mm(wide, spread_out)[0:1].astype(jnp.int32) * piece + iota((1, rows), 1) % piece
    ftm[...] = one_hot(iota((rows, rows), 0) == goal)
    apply_rows(ftm, tokens, st)
    lab = jnp.where(iota((128, rows), 0) < 64, routes[...], orders[...]).astype(f32).astype(bf16)
    sl[...] = mm(ftm[...], lab, (1, 1)).astype(bf16)
    tok_moves = (move(0, st, rt), move(1, sl, rl))
    for m in tok_moves:
        m.start()
    chain(0, 1)
    chain(1, 1)
    chain(0, 2)
    chain(1, 2)
    apply_rows(ftm, cots, cs)
    goal_col = mm(spread_out, wide, (0, 1))[:, 0:1].astype(jnp.int32) * piece + iota((rows, 1), 0) % piece
    ftm[...] = one_hot(iota((rows, rows), 1) == goal_col)
    chain(0, 3)
    chain(1, 3)
    fan_a(0)
    fan_a(1)
    for m in tok_moves:
        m.wait()

    outs = []

    def store(i, ref, out):
        copy = pltpu.make_async_copy(ref, out, osem.at[i])
        copy.start()
        outs.append(copy)

    cot_move = move(2, cs, rc)
    cot_move.start()
    store(0, ftm, deal_o)
    to, at = iota((rows, rows), 0), iota((rows, rows), 1)
    b, s, q = to // (seats * piece), to // piece % seats, to % piece
    turn[...] = one_hot(at == s * SEQ + b * piece + q)
    apply_rows(turn, rt, tok, (0, 0))
    store(1, tok, tok_o)
    lab_col = mm(turn[...], rl[...], (0, 0))
    lab_row = mm(rl[...], turn[...], (0, 0))
    ranks, heads_at, oks = [], [], []
    own = [
        jnp.sum(jnp.where(deal_row == me * seats + i, length_row, 0), axis=1, keepdims=True)
        for i in range(seats)
    ]
    posr, posc = iota((1, PACK), 1), iota((PACK, 1), 0)
    near_ = (iota((PACK, PACK), 0) // SEQ == iota((PACK, PACK), 1) // SEQ) & (
        iota((PACK, PACK), 1) <= iota((PACK, PACK), 0)
    )
    for p in range(MICRO):
        low, high = own[PER * p], own[PER * p + 1]
        here_r = posr % SEQ < jnp.where(posr < SEQ, low, high)
        here_c = posc % SEQ < jnp.where(posc < SEQ, low, high)
        masks[p] = (near_ & here_r).astype(f32)
        cols = slice(p * PACK, (p + 1) * PACK)
        route_r = lab_row[0:1, cols]
        key_r = lab_row[64:65, cols] * PER + (posr // SEQ).astype(f32)
        route_c = lab_col[cols, 0:1]
        key_c = lab_col[cols, 64:65] * PER + (posc // SEQ).astype(f32)
        ahead = jnp.sum(
            ((route_c == route_r) & (key_c < key_r) & here_c).astype(f32), axis=0, keepdims=True
        ).astype(jnp.int32)
        base = p * capacity + ahead
        good = here_r & (ahead < capacity)
        route_i = route_r.astype(jnp.int32)
        heads_at.append(jnp.where(good & (base < main), route_i * main + base, -1))
        oks.append(jnp.where(good & (base >= main), route_i * (PARTS * tail) + base - main, -PARTS * PARTS * tail))
    head_row = jnp.concatenate(heads_at, axis=1)
    tail_row = jnp.concatenate(oks, axis=1)
    dm[...] = one_hot(iota(dm.shape, 0) == head_row)
    for part in range(PARTS):
        dt[part] = one_hot(iota(dt.shape[1:], 0) == tail_row + part * tail)
    store(2, dm, dm_o)
    store(3, dt, dt_o)

    def split(ref, to_main, to_tails):
        apply_rows(dm, ref, to_main)
        total = None
        for part in range(PARTS):
            term = mm(dt[part], ref[:, part * block : (part + 1) * block])
            total = term if total is None else total + term
        to_tails[...] = total.astype(bf16)

    inputs = tok[...].astype(f32)
    unit, inv = norm_parts(inputs)
    res[...] = unit
    fan_b(0)
    fan_p(0)
    big = iota((128, 128), 0) == iota((128, 128), 1)

    def gain_row(lane):
        parts = []
        for j in range(width // 128):
            col = w[128 * j : 128 * (j + 1), gain_at:out_at].astype(f32)[:, lane : lane + 1]
            parts.append(jnp.sum(jnp.where(big, col, 0.0), axis=0, keepdims=True))
        return jnp.concatenate(parts, axis=1)

    gain_a, gain_f = gain_row(0), gain_row(64)
    gains_o[0:1, :] = gain_a
    gains_o[1:2, :] = gain_f
    shared[...] = (res[...] * gain_a).astype(bf16)

    def project(n, carry):
        cols = pl.ds(pl.multiple_of(n * 256, 256), 256)
        packed[:, cols] = mm(shared[...], w[:, cols]).astype(bf16)
        return carry

    lax.fori_loop(0, 3 * width // 256, project, 0)
    store(5, packed, packed_o)
    first = iota((PACK, 2 * HEAD), 1) < HEAD

    def pack(n, carry):
        p, half = n // 2, lax.rem(n, 2)
        at = pl.ds(pl.multiple_of(p * PACK, PACK), PACK)
        mask = masks[p] > 0.5
        mask = jnp.concatenate([mask, mask], axis=0)
        for j in range(HEADS // 4):
            h = half * (HEADS // 4) + j
            own_lanes, key_lanes, value_lanes = (
                pl.ds(pl.multiple_of(h * 2 * HEAD + n * width, 2 * HEAD), 2 * HEAD) for n in range(3)
            )
            q, k, v = packed[at, own_lanes], packed[at, key_lanes], packed[at, value_lanes]
            zero = jnp.zeros_like(q)
            qs = jnp.concatenate([jnp.where(first, q, zero), jnp.where(first, zero, q)], axis=0)
            scores = jnp.where(mask, mm(qs, k, (1, 1)) * 0.125, -1e30)
            e = jnp.exp(scores - jnp.max(scores, axis=1, keepdims=True))
            prob = (e / jnp.sum(e, axis=1, keepdims=True)).astype(bf16)
            probs[p * (HEADS // 2) + h] = prob
            t = mm(prob, v)
            mixed[at, own_lanes] = jnp.where(first, t[:PACK], t[PACK:]).astype(bf16)
        return carry

    fan_b(1)
    lax.fori_loop(0, 2 * MICRO, pack, 0)
    store(6, probs, probs_o)
    fan_p(1)
    store(4, w, w_o)
    store(7, mixed, mixed_o)
    apply_rows(mixed, w.at[:, pl.ds(out_at, width)], res)
    residual = tok[...].astype(f32) + res[...]
    res[...] = residual
    store(8, res, res_o)
    unit, inv = norm_parts(residual)
    shared[...] = (unit * gain_f).astype(bf16)
    split(shared, ss, stl)
    slot_moves = (move(3, ss, slots_o), move(4, stl, tails_o))
    cot_move.wait()
    for m in slot_moves:
        m.start()
    apply_rows(turn, rc, cot, (0, 0))
    store(9, cot, cot_o)
    split(cot, cs, ctl)
    store(10, cs, cslots_o)
    store(11, ctl, ctails_o)
    all_sent(0)
    all_sent(1)
    for copy in outs:
        copy.wait()
    for m in slot_moves:
        m.wait()


def run_front(experts, tail, tokens, cots, routes, orders, deal, lengths, g_attn, g_ffn, w_qkv, w_out):
    rows, width = tokens.shape
    per_dest = dims(experts, width)[0]
    main = (per_dest - tail) * experts
    side = experts * PARTS * tail

    def sds(*shape, dtype=bf16):
        return jax.ShapeDtypeStruct(shape, dtype)

    tails = (side, width // PARTS)
    out_shape = [
        sds(main, width),
        sds(*tails),
        sds(main, width),
        sds(*tails),
        sds(rows, rows),
        sds(main, rows),
        sds(PARTS, side, rows),
        sds(2, width, dtype=f32),
        sds(rows, width),
        sds(rows, width, dtype=f32),
        sds(rows, width),
        sds(rows, 3 * width),
        sds(MICRO * HEADS // 2, 2 * PACK, PACK),
        sds(rows, width),
        sds(width, 4 * width + 128),
    ]
    vm = pltpu.VMEM
    return pl.pallas_call(
        functools.partial(front_kernel, experts, tail),
        out_shape=out_shape,
        in_specs=[VM] * 10,
        out_specs=[ANY] * 7 + [VM] + [ANY] * 7,
        scratch_shapes=[
            vm((rows, width), bf16),
            vm((rows, 128), bf16),
            vm((rows, width), bf16),
            vm((rows, 128), bf16),
            vm((rows, width), bf16),
            vm((rows, width), bf16),
            vm((rows, width), bf16),
            vm((width, 4 * width + 128), bf16),
            vm((rows, 3 * width), bf16),
            vm((MICRO * HEADS // 2, 2 * PACK, PACK), bf16),
            vm((rows, width), bf16),
            vm((rows, width), f32),
            vm((rows, width), bf16),
            vm((main, rows), bf16),
            vm((PARTS, side, rows), bf16),
            vm((rows, rows), bf16),
            vm((MICRO, PACK, PACK), f32),
            vm((main, width), bf16),
            vm(tails, bf16),
            vm((main, width), bf16),
            vm(tails, bf16),
            vm((rows, rows), bf16),
            DMA((2, 8)),
            DMA((2, 4)),
            DMA((2, 4)),
            DMA((2, 4)),
            DMA((2, 8)),
            DMA((2, 8)),
            DMA((2, 16)),
            DMA((2, 16)),
            DMA((5, experts)),
            DMA((5, experts)),
            DMA((5,)),
            DMA((12,)),
        ],
        compiler_params=pltpu.CompilerParams(
            collective_id=1, has_side_effects=True, vmem_limit_bytes=VMEM_MAX
        ),
        name="attention_front",
    )(tokens, cots, routes, orders, deal, lengths, g_attn, g_ffn, w_qkv, w_out)


def finish_kernel(f, out_r, ig_r, qkv, proj, gain, cent, out_o, ig_o, qkv_o, proj_o, cent_o, ga_o, gf_o):
    qkv_o[...], proj_o[...], cent_o[...] = qkv[...], proj[...], cent[...]
    n = gain.shape[0]
    eye = lax.broadcasted_iota(jnp.int32, (n, n), 0) == lax.broadcasted_iota(jnp.int32, (n, n), 1)
    for row, lane in ((ga_o, 0), (gf_o, 64)):
        row[...] = jnp.sum(jnp.where(eye, gain[:, lane : lane + 1], 0.0), axis=0, keepdims=True)
    out_o[...] = mm(f[...], out_r[...]).astype(bf16)
    ig_o[...] = mm(f[...], ig_r[...])


def run_finish(f, out_r, ig_r, qkv, proj, gain, cent):
    steps = 2
    rows, width = out_r.shape

    def cut(shape):
        return pl.BlockSpec((shape[0] // steps, shape[1]), lambda i: (i, 0))

    def whole(shape):
        return pl.BlockSpec(shape, lambda i: (0, 0))

    outs = [
        jax.ShapeDtypeStruct((rows, width), bf16),
        jax.ShapeDtypeStruct((rows, width), f32),
    ]
    small = [jax.ShapeDtypeStruct(g.shape, f32) for g in (qkv, proj, cent)]
    small += [jax.ShapeDtypeStruct((1, gain.shape[0]), f32)] * 2
    return pl.pallas_call(
        finish_kernel,
        grid=(steps,),
        out_shape=outs + small,
        in_specs=[cut(f.shape)] + [whole(x.shape) for x in (out_r, ig_r, qkv, proj, gain, cent)],
        out_specs=[cut(o.shape) for o in outs] + [whole(o.shape) for o in small],
        name="finish",
    )(f, out_r, ig_r, qkv, proj, gain, cent)


def widen_kernel(ups, downs, up_first, down_first, up_second, down_second, done):
    i = pl.program_id(0)
    for k, (up, down) in enumerate(((up_first, down_first), (up_second, down_second))):
        for narrow, full in ((ups, up), (downs, down)):
            size = full.shape[0]
            full[...] = narrow[k, pl.ds(pl.multiple_of(i * size, size), size), :].astype(f32)
    done[...] = jnp.zeros_like(done)


def run_widen(ups, downs):
    steps = 16

    def cut(shape):
        return pl.BlockSpec((shape[0] // steps, shape[1]), lambda i: (i, 0))

    outs = [jax.ShapeDtypeStruct(g.shape[1:], f32) for g in (ups, downs)] * 2
    return pl.pallas_call(
        widen_kernel,
        grid=(steps,),
        out_shape=outs + [jax.ShapeDtypeStruct((8, 128), f32)],
        in_specs=[VM, VM],
        out_specs=[cut(o.shape) for o in outs] + [pl.BlockSpec((8, 128), lambda i: (0, 0))],
        compiler_params=pltpu.CompilerParams(vmem_limit_bytes=24 << 20),
        name="widen",
    )(ups, downs)


def fast_shards(
    tokens,
    lengths,
    deal,
    routes,
    slot_order,
    gain_attn,
    gain_ffn,
    w_qkv,
    w_out,
    centroids,
    expert_in,
    expert_out,
    second_in,
    second_out,
    cotangent,
):
    width = tokens.shape[1]
    experts = lax.axis_size("expert")
    tail = dims(experts, width)[2]
    (slots, tails, cots, cot_tails, dealt, d_main, d_tail, gains, grad_output, residual, tok,
     packed, probs, mixed, w_all) = run_front(
        experts, tail, tokens, cotangent, routes.reshape(1, -1), slot_order.reshape(1, -1), deal, lengths,
        gain_attn[None], gain_ffn[None], w_qkv, w_out,
    )
    ra, rb, ga, gb, g_cent, ups, downs = run_experts(
        experts, slots, tails, cots, cot_tails, centroids,
        (expert_in[0], expert_out[0], second_in[0], second_out[0]),
    )
    *g_experts, done = run_widen(ups, downs)
    out_r, ig_r, g_qkv, g_out, g_gain = run_back(
        experts, tail, ra, rb, ga, gb, d_main, d_tail, gains, grad_output, residual, tok,
        packed, probs, mixed, w_all, done,
    )
    output, input_grad, g_qkv, g_out, g_cent, ga_attn, ga_ffn = run_finish(
        dealt, out_r, ig_r, g_qkv, g_out, g_gain, g_cent
    )
    return (
        output,
        input_grad,
        ga_attn[0],
        ga_ffn[0],
        g_qkv,
        g_out,
        g_cent,
        *(g[None] for g in g_experts),
    )


def gather_hidden(rows):
    return lax.all_gather(rows, "hidden", axis=0, tiled=True)


def sum_hidden(terms):
    return lax.psum_scatter(terms, "hidden", scatter_dimension=0, tiled=True)


def swap(blocks):
    return lax.all_to_all(blocks, "expert", split_axis=0, concat_axis=0, tiled=True)


def plain_shards(
    tokens,
    lengths,
    deal,
    routes,
    slot_order,
    gain_attn,
    gain_ffn,
    w_qkv,
    w_out,
    centroids,
    expert_in,
    expert_out,
    second_in,
    second_out,
    cotangent,
):
    width = tokens.shape[1]
    experts = lax.axis_size("expert")
    piece = SEQ // experts
    seats = MICRO * PER
    group = experts * seats
    rows = seats * SEQ
    capacity = (9 * PACK + 8 * experts - 1) // (8 * experts)
    per_dest = MICRO * capacity
    my_expert = lax.axis_index("expert")
    my_hidden = lax.axis_index("hidden")

    deal_row = lax.dynamic_index_in_dim(deal, my_hidden, 0, keepdims=False)
    length_row = lax.dynamic_index_in_dim(lengths, my_hidden, 0, keepdims=False)
    ids = jnp.arange(group, dtype=jnp.int32)
    inverse = jnp.sum(jnp.where(deal_row[None, :] == ids[:, None], ids[None, :], 0), axis=1)
    own = my_expert * seats + jnp.arange(seats, dtype=jnp.int32)
    own_lengths = jnp.sum(
        jnp.where(deal_row[None, :] == own[:, None], length_row[None, :], 0), axis=1
    )

    def to_dealt(flat):
        pieces = jnp.take(flat.reshape(group, piece, flat.shape[1]), inverse, axis=0)
        return lax.all_to_all(
            pieces.reshape(experts, seats, piece, flat.shape[1]),
            "expert",
            split_axis=0,
            concat_axis=2,
            tiled=True,
        ).reshape(rows, flat.shape[1])

    labels = jnp.concatenate([routes, slot_order], axis=1)
    lab = to_dealt(labels)
    tok = to_dealt(tokens)
    grad_output = to_dealt(cotangent)

    cat = jnp.concatenate(
        [w_qkv, w_out, gain_attn[:, None], gain_ffn[:, None], jnp.zeros((w_qkv.shape[0], 126), bf16)],
        axis=1,
    )
    cat = lax.all_gather(cat, ("expert", "hidden"), axis=0, tiled=True)
    qkv_w = cat[:, : 3 * width]
    out_w = cat[:, 3 * width : 4 * width]
    attn_gain = cat[:, 4 * width].astype(f32)[None, :]
    ffn_gain = cat[:, 4 * width + 1].astype(f32)[None, :]

    route = lab[:, 0].reshape(MICRO, PACK)
    order = lab[:, 1].reshape(MICRO, PACK)
    positions = jnp.arange(PACK, dtype=jnp.int32)
    seat = positions // SEQ
    pack_lengths = own_lengths.reshape(MICRO, PER)
    limit = jnp.repeat(pack_lengths, SEQ, axis=1)
    present = (positions % SEQ)[None, :] < limit
    priority = order * PER + seat[None, :]
    ahead = jnp.sum(
        (
            (route[:, :, None] == route[:, None, :])
            & (priority[:, None, :] < priority[:, :, None])
            & present[:, None, :]
        ).astype(jnp.int32),
        axis=2,
    )
    accepted = (present & (ahead < capacity)).reshape(rows)
    target = (
        route * per_dest + jnp.arange(MICRO, dtype=jnp.int32)[:, None] * capacity + ahead
    ).reshape(rows)
    target = jnp.where(accepted, target, -1)
    slot_ids = jnp.arange(experts * per_dest, dtype=jnp.int32)
    dispatch = (slot_ids[:, None] == target[None, :]).astype(bf16)

    def to_experts(values):
        out = mm(dispatch, values).astype(bf16)
        return swap(out.reshape(experts, per_dest, width)).reshape(experts * per_dest, width)

    cot_arrived = to_experts(grad_output)

    inputs = tok.astype(f32)
    unit_a, inv_a = norm_parts(inputs)
    normed = (unit_a * attn_gain).astype(bf16)
    packed = mm(normed, qkv_w).astype(bf16)
    allowed = (
        (seat[:, None] == seat[None, :]) & (positions[None, :] <= positions[:, None])
    )[None] & present[:, None, :]

    def heads(block):
        return block.reshape(MICRO, PACK, HEADS, HEAD)

    queries = heads(packed[:, :width])
    keys_all = heads(packed[:, width : 2 * width])
    values_all = heads(packed[:, 2 * width :])
    scores = jnp.einsum("pqhd,pkhd->phqk", queries, keys_all, preferred_element_type=f32) * 0.125
    masked = jnp.where(allowed[:, None], scores, -1e30)
    peaks = jnp.max(masked, axis=-1, keepdims=True)
    log_total = peaks + jnp.log(jnp.sum(jnp.exp(masked - peaks), axis=-1, keepdims=True))
    probs = jnp.exp(masked - log_total)
    probs_lo = probs.astype(bf16)
    mixed = (
        jnp.einsum("phqk,pkhd->pqhd", probs_lo, values_all, preferred_element_type=f32)
        .reshape(rows, width)
        .astype(bf16)
    )
    residual = inputs + mm(mixed, out_w)
    unit_f, inv_f = norm_parts(residual)
    shared = (unit_f * ffn_gain).astype(bf16)
    arrived = to_experts(shared)

    centroid_row = centroids[0]
    w_in, w_back = expert_in[0], expert_out[0]
    s_in, s_back = second_in[0], second_out[0]
    count = arrived.shape[0]
    arrived_f = arrived.astype(f32)
    gate_vals = jax.nn.sigmoid(
        jnp.sum(arrived_f * centroid_row.astype(f32)[None, :], axis=1, keepdims=True)
    )
    grad_result_own = (gate_vals * cot_arrived.astype(f32)).astype(bf16)
    gathered = gather_hidden(arrived)
    grad_result = gather_hidden(grad_result_own)
    pre_first = mm(gathered, w_in)
    act_first, pull_first = jax.vjp(gelu_act, pre_first)
    act_first = act_first.astype(bf16)
    middle = arrived_f + sum_hidden(mm(act_first, w_back).astype(bf16)).astype(f32)
    middle_lo = gather_hidden(middle.astype(bf16))
    pre_second = mm(middle_lo, s_in)
    act_second, pull_second = jax.vjp(gelu_act, pre_second)
    act_second = act_second.astype(bf16)
    expert_sum = middle + sum_hidden(mm(act_second, s_back).astype(bf16)).astype(f32)
    returned = (gate_vals * expert_sum).astype(bf16)
    came_back = swap(returned.reshape(experts, per_dest, width)).reshape(count, width)

    grad_logit = (
        jnp.sum(cot_arrived.astype(f32) * expert_sum, axis=1, keepdims=True)
        * gate_vals
        * (1.0 - gate_vals)
    )
    grad_pre_second = pull_second(mm(grad_result, s_back, (1, 1)))[0].astype(bf16)
    grad_middle_own = (
        grad_result_own.astype(f32)
        + sum_hidden(mm(grad_pre_second, s_in, (1, 1)).astype(bf16)).astype(f32)
    ).astype(bf16)
    grad_middle = gather_hidden(grad_middle_own)
    grad_pre = pull_first(mm(grad_middle, w_back, (1, 1)))[0].astype(bf16)
    grad_slots = (
        sum_hidden(mm(grad_pre, w_in, (1, 1)).astype(bf16)).astype(f32)
        + grad_middle_own.astype(f32)
        + grad_logit * centroid_row.astype(f32)[None, :]
    ).astype(bf16)
    grad_back = swap(grad_slots.reshape(experts, per_dest, width)).reshape(count, width)
    g_sec_out = mm(act_second, grad_result, (0, 0))
    g_sec_in = mm(middle_lo, grad_pre_second, (0, 0))
    g_exp_out = mm(act_first, grad_middle, (0, 0))
    g_exp_in = mm(gathered, grad_pre, (0, 0))
    g_cent = jnp.sum(grad_logit * arrived_f, axis=0, keepdims=True)

    combined = (residual + mm(dispatch, came_back, (0, 0))).astype(bf16)

    grad_shared = mm(dispatch, grad_back, (0, 0))
    g_gain_ffn = jnp.sum(grad_shared * unit_f, axis=0)
    grad_residual = grad_output.astype(f32) + norm_back(unit_f, inv_f, ffn_gain, grad_shared)
    grad_attended = grad_residual.astype(bf16)
    g_out_w = mm(mixed, grad_attended, (0, 0))
    grad_mixed = heads(mm(grad_attended, out_w, (1, 1)).astype(bf16))
    grad_probs = jnp.einsum("pqhd,pkhd->phqk", grad_mixed, values_all, preferred_element_type=f32)
    grad_values = jnp.einsum("phqk,pqhd->pkhd", probs_lo, grad_mixed, preferred_element_type=f32)
    inner = jnp.sum(probs * grad_probs, axis=-1, keepdims=True)
    grad_scores = (probs * (grad_probs - inner)).astype(bf16)
    grad_queries = (
        jnp.einsum("phqk,pkhd->pqhd", grad_scores, keys_all, preferred_element_type=f32) * 0.125
    )
    grad_keys = (
        jnp.einsum("phqk,pqhd->pkhd", grad_scores, queries, preferred_element_type=f32) * 0.125
    )
    grad_packed = jnp.concatenate(
        [g.reshape(rows, width) for g in (grad_queries, grad_keys, grad_values)], axis=1
    ).astype(bf16)
    g_qkv = mm(normed, grad_packed, (0, 0))
    grad_normed = mm(grad_packed, qkv_w, (1, 1))
    g_gain_attn = jnp.sum(grad_normed * unit_a, axis=0)
    input_grad = (grad_residual + norm_back(unit_a, inv_a, attn_gain, grad_normed)).astype(bf16)

    def scatter(partial):
        return lax.psum_scatter(
            partial, ("expert", "hidden"), scatter_dimension=0, tiled=True
        )

    g_cat = jnp.concatenate([g_qkv, g_out_w, g_gain_attn[:, None], g_gain_ffn[:, None], jnp.zeros((width, 126), f32)], axis=1)
    g_cat = scatter(g_cat)
    g_cent = lax.psum(g_cent, "hidden")

    def from_dealt(dealt):
        received = lax.all_to_all(
            dealt.reshape(1, seats, SEQ, width), "expert", split_axis=2, concat_axis=0, tiled=True
        ).reshape(group, piece, width)
        return jnp.take(received, deal_row, axis=0).reshape(group * piece, width)

    return (
        from_dealt(combined),
        from_dealt(input_grad).astype(f32),
        g_cat[:, 4 * width],
        g_cat[:, 4 * width + 1],
        g_cat[:, : 3 * width],
        g_cat[:, 3 * width : 4 * width],
        g_cent,
        g_exp_in[None],
        g_exp_out[None],
        g_sec_in[None],
        g_sec_out[None],
    )


def solution(mesh):
    both = ("expert", "hidden")
    fast = mesh.shape["expert"] == 16 and mesh.shape["hidden"] == 2
    return jax.shard_map(
        fast_shards if fast else plain_shards,
        mesh=mesh,
        in_specs=(
            P(both, None),
            P(),
            P(),
            P(both, None),
            P(both, None),
            P(both),
            P(both),
            P(both, None),
            P(both, None),
            P("expert", None),
            P("expert", None, "hidden"),
            P("expert", "hidden", None),
            P("expert", None, "hidden"),
            P("expert", "hidden", None),
            P(both, None),
        ),
        out_specs=(
            P(both, None),
            P(both, None),
            P(both),
            P(both),
            P(both, None),
            P(both, None),
            P("expert", None),
            P("expert", None, "hidden"),
            P("expert", "hidden", None),
            P("expert", None, "hidden"),
            P("expert", "hidden", None),
        ),
        check_vma=False,
    )
```
